32 devices in a mesh: bucket: 16 (over z, y, core), seq: 2 (over x).
Axes of the slice: x: 2, y: 2, z: 4, core: 2. Of those that a mesh axis runs over, the one named last changes fastest.
Arguments:
- tokens: bfloat16 [4096, 1536], P(('bucket', 'seq')), may hold values from -6 to 6
- cotangent: bfloat16 [4096, 1536], P(('bucket', 'seq')), may hold values from -6 to 6
- clip_slices: int32 [4], replicated, may hold values from 1 to 10, 16 in all
- caption_lengths: int32 [4], replicated, may hold values from 1 to 128, as said below
- caption: bfloat16 [4, 128, 4096], replicated, may hold values from -6 to 6
- cond: float32 [4, 1024], replicated, may hold values from -6 to 6
- ada_w: bfloat16 [9216, 1024], P('seq'), may hold values from -0.1875 to 0.1875
- norm_gain: float32 [1536], replicated, may hold values from 0.5 to 1.5
- w_qkv: bfloat16 [4608, 1536], P('seq'), may hold values from -0.15625 to 0.15625
- q_gain: float32 [1536], replicated, may hold values from 0.5 to 1.5
- k_gain: float32 [1536], replicated, may hold values from 0.5 to 1.5
- w_caption: bfloat16 [2, 1536, 4096], P(None, 'seq'), may hold values from -0.09375 to 0.09375
- ky_gain: float32 [1536], replicated, may hold values from 0.5 to 1.5
- cross_gate: float32 [24], replicated, may hold values from -1.5 to 1.5
- w_out: bfloat16 [1536, 1536], P('seq'), may hold values from -1.5 to 1.5
- ffn_gain: float32 [1536], replicated, may hold values from 0.5 to 1.5
- w_gate_up: bfloat16 [8192, 1536], P('seq'), may hold values from -0.15625 to 0.15625
- w_down: bfloat16 [4096, 1536], P('seq'), may hold values from -0.09375 to 0.09375
Outputs:
- out: bfloat16 [4096, 1536], P(('bucket', 'seq'))
- d_tokens: float32 [4096, 1536], P(('bucket', 'seq'))
- d_cond: float32 [4, 1024], replicated
- d_ada: float32 [9216, 1024], P('seq', 'bucket')
- d_norm_gain: float32 [1536], replicated
- d_qkv: float32 [4608, 1536], P('seq', 'bucket')
- d_q_gain: float32 [1536], replicated
- d_k_gain: float32 [1536], replicated
- d_caption_w: float32 [2, 1536, 4096], P(None, 'seq', 'bucket')
- d_ky_gain: float32 [1536], replicated
- d_cross_gate: float32 [24], replicated
- d_out_w: float32 [1536, 1536], P('seq', 'bucket')
- d_ffn_gain: float32 [1536], replicated
- d_gate_up: float32 [8192, 1536], P('seq', 'bucket')
- d_down: float32 [4096, 1536], P('seq', 'bucket')
The draws below stay inside these ranges and needn't reach their ends.
Inputs may be any that keep to these rules, and one draw needn't show every extreme that they name: Clip c covers 256 * clip_slices[c] consecutive tokens, clips in order; the counts add up to the bucket indices; the longest has 10. `caption_lengths`: some clip has 128 caption tokens.
All inputs are finite; a program needn't handle non-finite values.
Results may differ from the reference program's by a relative error of at most 0.02.
Values may be sent and summed in bfloat16 or wider, within the bound.
No kernel may reach another device: no remote copies, remote signals or barrier semaphores. Data moves between devices by JAX's collectives and lax.ppermute only.
A program may use at most 576 MiB of HBM per device.

```python
import math
import jax
import jax.numpy as jnp
import numpy as np
from jax import lax

H = 24
HD = 64
D = 1536
FF = 4096
YD = 4096
CD = 1024
CAP = 128
CLIPS = 4
SLICE = 256
MOST = 10
TOKENS = 4096
N_BUCKET = 16


def draw_caption_lengths(key, part):
    first_key, second_key = jax.random.split(key)
    lengths = jax.random.randint(first_key, (CLIPS,), 1, CAP + 1)
    longest = jax.random.randint(second_key, (), 0, CLIPS)
    return jnp.where(jnp.arange(CLIPS) == longest, CAP, lengths).astype(jnp.int32)


def levels(key, shape, shards, smallest, top_value):
    def one(dim, blocks):
        draws = jax.random.uniform(jax.random.fold_in(jax.random.fold_in(key, 6), dim), (blocks,), jnp.float32, smallest / len(shards), top_value / len(shards))
        return jnp.repeat(jnp.exp(draws), shape[dim] // blocks).reshape((-1,) + (1,) * (len(shape) - dim - 1))

    gain = one(*shards[0])
    for cut in shards[1:]:
        gain = gain * one(*cut)
    return gain


def split_up(number_of, total, limit, skew):
    portions = [(1 << 20) // math.isqrt(grade ** skew) + 1 for grade in range(2, number_of + 1)]
    rest, counts = total - limit - (number_of - 1), [1] * (number_of - 1)
    while rest > 0:
        free = [i for i in range(number_of - 1) if counts[i] < limit]
        whole, budget = sum([portions[i] for i in free]), rest
        for i in free:
            extra = min(limit - counts[i], max(1, budget * portions[i] // whole), rest)
            counts[i] = counts[i] + extra
            rest = rest - extra
    return np.array([limit] + counts)


def ragged(stream_key, amount, total, most, slope):
    if amount == 2:
        one = jax.random.randint(stream_key, (), max(1, total - most), min(most, total - 1) + 1)
        return jnp.stack([one, total - one])
    sizes = jnp.asarray(split_up(amount, total, most, slope), jnp.int32)
    pairs = (amount - 1) // 2
    giver, taker = sizes[1:1 + 2 * pairs:2], sizes[2:2 + 2 * pairs:2]
    slack = jnp.minimum(giver - 1, most - taker)
    shifted = jax.random.randint(jax.random.fold_in(stream_key, 1), (pairs,), 0, 1 << 20) % (slack + 1)
    sizes = sizes.at[1:1 + 2 * pairs:2].set(giver - shifted).at[2:2 + 2 * pairs:2].set(taker + shifted)
    return sizes[jax.random.permutation(jax.random.fold_in(stream_key, 2), amount)]


def noise(stream_key, dims, deviation, limit, cuts=(), held_as=jnp.bfloat16):
    factor_of = levels(stream_key, dims, cuts, -0.22, 0.18) if cuts else 1.0
    entries = jax.random.normal(stream_key, dims, jnp.float32) * deviation * factor_of
    return jnp.minimum(jnp.maximum(entries, -limit), limit).astype(held_as)


def setup_inputs(seed: int = 0) -> dict:
    seeds = jax.random.split(jax.random.key(seed), 19)
    tokens = noise(seeds[0], (TOKENS, D), 1.0, 6.0, ((0, 32),))
    cotangent = noise(seeds[1], (TOKENS, D), 1.0, 6.0, ((0, 32),))
    clip_slices = ragged(seeds[2], CLIPS, N_BUCKET, MOST, 2).astype(jnp.int32)
    caption_lengths = draw_caption_lengths(jax.random.fold_in(seeds[18], 71), 0)
    caption = noise(seeds[4], (CLIPS, CAP, YD), 1.0, 6.0)
    cond = noise(seeds[5], (CLIPS, CD), 1.0, 6.0, (), jnp.float32)
    ada_w = noise(seeds[6], (6 * D, CD), CD ** -0.5, 0.1875, ((0, 2),))
    norm_gain = jnp.clip(1.0 + 0.1 * jax.random.normal(seeds[7], (D,), jnp.float32), 0.5, 1.5)
    w_qkv = noise(seeds[8], (3 * D, D), D ** -0.5, 0.15625, ((0, 2),))
    q_gain = jnp.clip(1.0 + 0.1 * jax.random.normal(seeds[9], (D,), jnp.float32), 0.5, 1.5)
    k_gain = jnp.clip(1.0 + 0.1 * jax.random.normal(seeds[10], (D,), jnp.float32), 0.5, 1.5)
    w_caption = noise(seeds[11], (2, D, YD), YD ** -0.5, 0.09375, ((1, 2),))
    ky_gain = jnp.clip(1.0 + 0.1 * jax.random.normal(seeds[12], (D,), jnp.float32), 0.5, 1.5)
    cross_gate = jnp.clip(jax.random.uniform(seeds[13], (H,), jnp.float32, -1.5, 1.5), -1.5, 1.5)
    w_out = noise(seeds[14], (D, D), (max(D // 96, 1)) ** -0.5, 1.5, ((0, 2),))
    ffn_gain = jnp.clip(1.0 + 0.1 * jax.random.normal(seeds[15], (D,), jnp.float32), 0.5, 1.5)
    w_gate_up = noise(seeds[16], (2 * FF, D), D ** -0.5, 0.15625, ((0, 2),))
    w_down = noise(seeds[17], (FF, D), FF ** -0.5, 0.09375, ((0, 2),))
    return {"tokens": tokens, "cotangent": cotangent, "clip_slices": clip_slices, "caption_lengths": caption_lengths, "caption": caption, "cond": cond, "ada_w": ada_w, "norm_gain": norm_gain, "w_qkv": w_qkv, "q_gain": q_gain, "k_gain": k_gain, "w_caption": w_caption, "ky_gain": ky_gain, "cross_gate": cross_gate, "w_out": w_out, "ffn_gain": ffn_gain, "w_gate_up": w_gate_up, "w_down": w_down}


@jax.custom_vjp
def low(v):
    return lax.optimization_barrier(v.astype(jnp.bfloat16)).astype(jnp.float32)

@jax.custom_vjp
def low_back(v):
    return v

def low_keep(v):
    return (low(v), None)

def low_pass(kept, grad):
    return (grad,)

def back_keep(v):
    return (v, None)

def back_low(kept, grad):
    return (low(grad),)
low.defvjp(low_keep, low_pass)
low_back.defvjp(back_keep, back_low)
EPSILON = 1e-06
MASKED = -1e+30
HIGHEST = lax.Precision.HIGHEST

def clip_bounds(clip_slices, slice_rows):
    ends = (jnp.cumsum(clip_slices) * slice_rows).astype(jnp.int32)
    starts = (ends - clip_slices * slice_rows).astype(jnp.int32)
    return (starts, ends)

def clip_of(rows, ends):
    return lax.optimization_barrier(jnp.sum((rows[:, None] >= ends[None, :]).astype(jnp.int32), axis=1)).astype(jnp.int32)

def head_norm(values, gains, head_count):
    row_count = values.shape[0]
    split = values.reshape(row_count, head_count, -1)
    unit_rows = split * lax.rsqrt(lax.optimization_barrier(jnp.mean(split * split, axis=-1, keepdims=True)) + EPSILON)
    return unit_rows.reshape(row_count, -1) * gains

def rotate(values, positions, head_count):
    row_count = values.shape[0]
    split = values.reshape(row_count, head_count, -1)
    half_width = split.shape[-1] // 2
    frequency = jnp.exp(jnp.arange(half_width, dtype=jnp.float32) * (-2.0 * math.log(10000.0) / (2 * half_width)))
    angles = positions[:, None] * frequency[None, :]
    cosine = jnp.cos(angles)[:, None, :]
    sine = jnp.sin(angles)[:, None, :]
    first_half = split[..., :half_width]
    second_half = split[..., half_width:]
    turned = jnp.concatenate([first_half * cosine - second_half * sine, first_half * sine + second_half * cosine], axis=-1)
    return turned.reshape(row_count, -1)

def forward(inputs, cond, ada_w, norm_gain, w_qkv, q_gain, k_gain, w_caption, ky_gain, cross_gate, w_out, ffn_gain, w_gate_up, w_down, caption, clip_slices, caption_lengths):
    starts, ends = clip_bounds(clip_slices, SLICE)
    rows = jnp.arange(TOKENS, dtype=jnp.int32)
    clips = clip_of(rows, ends)
    activation = low(jax.nn.silu(cond))
    modulation = low_back(jnp.dot(activation, ada_w.T, precision=HIGHEST))
    shift_rows = modulation[:, :D][clips]
    scale_rows = modulation[:, D:2 * D][clips]
    gate_rows = modulation[:, 2 * D:3 * D][clips]
    shift_mlp = modulation[:, 3 * D:4 * D][clips]
    scale_mlp = modulation[:, 4 * D:5 * D][clips]
    gate_mlp = modulation[:, 5 * D:][clips]
    unit_rows = inputs * lax.rsqrt(lax.optimization_barrier(jnp.mean(inputs * inputs, axis=-1, keepdims=True)) + EPSILON)
    hidden = low(unit_rows * norm_gain * (1.0 + scale_rows) + shift_rows)
    projected = low_back(jnp.dot(hidden, w_qkv.T, precision=HIGHEST))
    positions = (rows - starts[clips]).astype(jnp.float32)
    queries = low(low_back(rotate(head_norm(projected[:, :D], q_gain, H), positions, H)))
    keys_all = low(low_back(rotate(head_norm(projected[:, D:2 * D], k_gain, H), positions, H)))
    values_all = low(low_back(projected[:, 2 * D:]))
    caption_raw = low_back(jnp.einsum('cty,jdy->cjtd', caption, w_caption, precision=HIGHEST))
    caption_keys = low(head_norm(caption_raw[:, 0].reshape(CLIPS * CAP, D), ky_gain, H)).reshape(CLIPS, CAP, H, HD)
    caption_values = low(caption_raw[:, 1]).reshape(CLIPS, CAP, H, HD)
    gates = jnp.tanh(cross_gate)
    score_scale = HD ** (-0.5)
    window = MOST * SLICE
    block_rows = min(256, SLICE)

    def attend(first_row):
        clip_index = clips[first_row]
        block_queries = lax.dynamic_slice_in_dim(queries, first_row, block_rows, 0).reshape(block_rows, H, HD)
        key_first = jnp.minimum(starts[clip_index], TOKENS - window).astype(jnp.int32)
        block_keys = lax.dynamic_slice_in_dim(keys_all, key_first, window, 0).reshape(window, H, HD)
        block_values = lax.dynamic_slice_in_dim(values_all, key_first, window, 0).reshape(window, H, HD)
        usable = lax.dynamic_slice_in_dim(clips, key_first, window, 0) == clip_index
        scores = low_back(jnp.einsum('qhd,khd->hqk', block_queries, block_keys, precision=HIGHEST) * score_scale)
        probability = jax.nn.softmax(jnp.where(usable[None, None, :], scores, MASKED), axis=-1)
        own = jnp.einsum('hqk,khd->qhd', low(probability), block_values, precision=HIGHEST)
        caption_usable = jnp.arange(CAP) < caption_lengths[clip_index]
        cross_scores = low_back(jnp.einsum('qhd,khd->hqk', block_queries, caption_keys[clip_index], precision=HIGHEST) * score_scale)
        cross_prob = jax.nn.softmax(jnp.where(caption_usable[None, None, :], cross_scores, MASKED), axis=-1)
        other = low_back(jnp.einsum('hqk,khd->qhd', low(cross_prob), caption_values[clip_index], precision=HIGHEST))
        return low(low_back(own + gates[None, :, None] * other)).reshape(block_rows, D)
    blocks = lax.map(jax.checkpoint(attend), jnp.arange(0, TOKENS, block_rows, dtype=jnp.int32))
    attention = blocks.reshape(TOKENS, D)
    branch = low_back(jnp.dot(attention, w_out.T, precision=HIGHEST))
    middle = inputs + gate_rows * branch
    mid_unit = middle * lax.rsqrt(lax.optimization_barrier(jnp.mean(middle * middle, axis=-1, keepdims=True)) + EPSILON)
    mlp_in = low(mid_unit * ffn_gain * (1.0 + scale_mlp) + shift_mlp)
    gate_up = low_back(jnp.dot(mlp_in, w_gate_up.T, precision=HIGHEST))
    inner = low(jax.nn.silu(gate_up[:, :FF]) * gate_up[:, FF:])
    mlp_branch = low_back(jnp.dot(inner, w_down, precision=HIGHEST))
    return middle + gate_mlp * mlp_branch

def reference(tokens, cotangent, clip_slices, caption_lengths, caption, cond, ada_w, norm_gain, w_qkv, q_gain, k_gain, w_caption, ky_gain, cross_gate, w_out, ffn_gain, w_gate_up, w_down):
    primals = (tokens.astype(jnp.float32), cond, ada_w.astype(jnp.float32), norm_gain, w_qkv.astype(jnp.float32), q_gain, k_gain, w_caption.astype(jnp.float32), ky_gain, cross_gate, w_out.astype(jnp.float32), ffn_gain, w_gate_up.astype(jnp.float32), w_down.astype(jnp.float32))
    caption_rows = caption.astype(jnp.float32)

    def layer(*params):
        return forward(*params, caption_rows, clip_slices, caption_lengths)
    output, pull = jax.vjp(layer, *primals)
    grads = pull(cotangent.astype(jnp.float32))
    return (output.astype(jnp.bfloat16), grads[0], grads[1], grads[2], grads[3], grads[4], grads[5], grads[6], grads[7], grads[8], grads[9], grads[10], grads[11], grads[12], grads[13])
```

```python
import functools
import math

import jax
import jax.numpy as jnp
from jax import lax
from jax.experimental import pallas as pl
from jax.experimental.pallas import tpu as pltpu
from jax.sharding import PartitionSpec as P

H = 24
HD = 64
D = 1536
FF = 4096
YD = 4096
CD = 1024
CAP = 128
CLIPS = 4

EPSILON = 1e-06
MASKED = -1e30
BF = jnp.bfloat16
F32 = jnp.float32
NN = (((1,), (0,)), ((), ()))
NT = (((1,), (1,)), ((), ()))
TN = (((0,), (0,)), ((), ()))


def mm(a, b, dims):
    return lax.dot_general(a, b, dims, preferred_element_type=F32)


def norm_rope(raw, gain, cosine, sine):
    inverse = lax.rsqrt(jnp.mean(raw * raw, axis=0, keepdims=True) + EPSILON)
    normed = raw * inverse * gain
    half = raw.shape[0] // 2
    first, second = normed[:half], normed[half:]
    return jnp.concatenate(
        [first * cosine - second * sine, first * sine + second * cosine], axis=0
    )


def norm_rope_back(grad, raw, gain, cosine, sine):
    inverse = lax.rsqrt(jnp.mean(raw * raw, axis=0, keepdims=True) + EPSILON)
    unit = raw * inverse
    half = raw.shape[0] // 2
    first, second = grad[:half], grad[half:]
    turned = jnp.concatenate(
        [first * cosine + second * sine, second * cosine - first * sine], axis=0
    )
    gain_grad = jnp.sum(turned * unit, axis=1, keepdims=True)
    unit_grad = turned * gain
    raw_grad = inverse * (unit_grad - unit * jnp.mean(unit_grad * unit, axis=0, keepdims=True))
    return raw_grad, gain_grad


def attend_kernel(
    heads, pieces, meta, gates, q_ref, *refs
):
    kv_refs = refs[:pieces]
    (cap_ref, qg_ref, kg_ref, cos_ref, sin_ref) = refs[pieces : pieces + 5]
    (comb_ref, own_ref, other_ref, stat_ref, qs_ref, ks_ref, vs_ref) = refs[pieces + 5 :]
    width = heads * HD
    count = q_ref.shape[0]
    rows = q_ref.shape[2]
    scale = HD**-0.5

    for j, kv_ref in enumerate(kv_refs):
        for k in range(kv_ref.shape[0]):
            slot = meta[8 * count + j * kv_ref.shape[0] + k]
            cosine, sine = cos_ref[slot], sin_ref[slot]
            for h in range(heads):
                at = slice(h * HD, h * HD + HD)
                raw = kv_ref[k, at, :].astype(F32)
                ks_ref[slot, at, :] = norm_rope(raw, kg_ref[at, :], cosine, sine).astype(BF)
            vs_ref[slot] = kv_ref[k, width:, :]

    def per_slice(i, carry):
        slot = meta[8 * i + 4]
        cosine, sine = cos_ref[slot], sin_ref[slot]
        first, last = meta[8 * i], meta[8 * i + 1]
        clip, length = meta[8 * i + 2], meta[8 * i + 3]
        queries = []
        for h in range(heads):
            at = slice(h * HD, h * HD + HD)
            raw = q_ref[i, at, :].astype(F32)
            turned = norm_rope(raw, qg_ref[at, :], cosine, sine).astype(BF)
            turned = (turned.astype(F32) * scale).astype(BF)
            qs_ref[i, at, :] = turned
            queries.append(turned)

        def step(b, state):
            totals, sums = state
            new_totals, new_sums = [], []
            for h in range(heads):
                at = slice(h * HD, h * HD + HD)
                weights = jnp.exp(mm(ks_ref[b, at, :], queries[h], TN))
                new_totals.append(totals[h] + jnp.sum(weights, axis=0, keepdims=True))
                new_sums.append(sums[h] + mm(vs_ref[b, at, :], weights.astype(BF), NN))
            return tuple(new_totals), tuple(new_sums)

        zero_total = tuple(jnp.zeros((1, rows), F32) for _ in range(heads))
        zero_sum = tuple(jnp.zeros((HD, rows), F32) for _ in range(heads))
        totals, sums = lax.fori_loop(first, last, step, (zero_total, zero_sum))
        usable = lax.broadcasted_iota(jnp.int32, (CAP, rows), 0) < length
        for h in range(heads):
            at = slice(h * HD, h * HD + HD)
            inverse = 1.0 / totals[h]
            own = sums[h] * inverse
            weights = jnp.where(usable, jnp.exp(mm(cap_ref[clip, at, :], queries[h], TN)), 0.0)
            cap_inverse = 1.0 / jnp.sum(weights, axis=0, keepdims=True)
            at_value = slice(width + h * HD, width + h * HD + HD)
            other = mm(cap_ref[clip, at_value, :], weights.astype(BF), NN) * cap_inverse
            own_ref[i, at, :] = own
            other_ref[i, at, :] = other
            comb_ref[i, at, :] = (own + gates[h] * other).astype(BF)
            stat_ref[i, h : h + 1, :] = inverse
            stat_ref[i, 4 + h : 5 + h, :] = cap_inverse
        return carry

    lax.fori_loop(0, count, per_slice, 0)


def attend_back_kernel(heads, pieces, meta, gates, q_ref, *refs):
    (g_ref, own_ref, other_ref, stat_ref, qs_ref, ks_ref, vs_ref) = refs[:7]
    (cap_ref, qg_ref, cos_ref, sin_ref) = refs[7:11]
    gq_ref, qgain_ref, dcap_ref, dgate_ref = refs[11:15]
    dkv_refs = refs[15 : 15 + pieces]
    acc_ref = refs[15 + pieces]
    width = heads * HD
    count = q_ref.shape[0]
    rows = q_ref.shape[2]
    scale = HD**-0.5
    acc_ref[...] = jnp.zeros_like(acc_ref)
    dcap_ref[...] = jnp.zeros_like(dcap_ref)
    dgate_ref[...] = jnp.zeros_like(dgate_ref)
    qgain_ref[...] = jnp.zeros_like(qgain_ref)

    def per_slice(i, carry):
        slot = meta[8 * i + 4]
        first, last = meta[8 * i], meta[8 * i + 1]
        clip, length = meta[8 * i + 2], meta[8 * i + 3]
        queries, grads, deltas, inverses = [], [], [], []
        for h in range(heads):
            at = slice(h * HD, h * HD + HD)
            grad = g_ref[i, at, :]
            queries.append(qs_ref[i, at, :])
            grads.append(grad)
            deltas.append(jnp.sum(grad.astype(F32) * own_ref[i, at, :], axis=0, keepdims=True))
            inverses.append(stat_ref[i, h : h + 1, :])

        def step(b, state):
            out = []
            for h in range(heads):
                at = slice(h * HD, h * HD + HD)
                at_value = slice(width + h * HD, width + h * HD + HD)
                keys, values = ks_ref[b, at, :], vs_ref[b, at, :]
                prob = jnp.exp(mm(keys, queries[h], TN)) * inverses[h]
                grad_prob = mm(values, grads[h], TN)
                grad_score = (prob * (grad_prob - deltas[h])).astype(BF)
                acc_ref[b, at_value, :] += mm(grads[h], prob.astype(BF), NT)
                acc_ref[b, at, :] += mm(queries[h], grad_score, NT)
                out.append(state[h] + mm(keys, grad_score, NN))
            return tuple(out)

        query_grads = lax.fori_loop(
            first, last, step, tuple(jnp.zeros((HD, rows), F32) for _ in range(heads))
        )
        usable = lax.broadcasted_iota(jnp.int32, (CAP, rows), 0) < length
        cosine, sine = cos_ref[slot], sin_ref[slot]
        for h in range(heads):
            at = slice(h * HD, h * HD + HD)
            at_value = slice(width + h * HD, width + h * HD + HD)
            cap_keys, cap_values = cap_ref[clip, at, :], cap_ref[clip, at_value, :]
            grad = grads[h].astype(F32)
            grad_other = (grad * gates[h]).astype(BF)
            prob = (
                jnp.where(usable, jnp.exp(mm(cap_keys, queries[h], TN)), 0.0)
                * stat_ref[i, 4 + h : 5 + h, :]
            )
            grad_prob = mm(cap_values, grad_other, TN)
            inner = jnp.sum(prob * grad_prob, axis=0, keepdims=True)
            grad_score = (prob * (grad_prob - inner)).astype(BF)
            query_grad = (query_grads[h] + mm(cap_keys, grad_score, NN)) * scale
            dcap_ref[clip, at, :] += mm(queries[h], grad_score, NT)
            dcap_ref[clip, at_value, :] += mm(grad_other, prob.astype(BF), NT)
            part = jnp.sum(grad * other_ref[i, at, :], axis=0, keepdims=True)
            dgate_ref[h : h + 1, :] += part
            raw_grad, gain_grad = norm_rope_back(
                query_grad.astype(BF).astype(F32), q_ref[i, at, :].astype(F32), qg_ref[at, :], cosine, sine
            )
            gq_ref[i, at, :] = raw_grad.astype(BF)
            qgain_ref[at, :] += gain_grad
        return carry

    lax.fori_loop(0, count, per_slice, 0)
    for j, dkv_ref in enumerate(dkv_refs):
        for k in range(dkv_ref.shape[0]):
            slot = meta[8 * count + j * dkv_ref.shape[0] + k]
            dkv_ref[k] = acc_ref[slot].astype(BF)


def vmem_specs(n):
    return [pl.BlockSpec(memory_space=pltpu.VMEM) for _ in range(n)]


SMEM = pl.BlockSpec(memory_space=pltpu.SMEM)


def attend(heads, meta, gates, queries, kv_pieces, cap_kv, q_gain, k_gain, cosine, sine):
    count, width, rows = queries.shape
    slots = cosine.shape[0]
    shape = jax.ShapeDtypeStruct
    return pl.pallas_call(
        functools.partial(attend_kernel, heads, len(kv_pieces)),
        in_specs=[SMEM, SMEM] + vmem_specs(1 + len(kv_pieces) + 5),
        out_specs=vmem_specs(7),
        out_shape=[
            shape((count, width, rows), BF),
            shape((count, width, rows), F32),
            shape((count, width, rows), F32),
            shape((count, 8, rows), F32),
            shape((count, width, rows), BF),
            shape((slots, width, rows), BF),
            shape((slots, width, rows), BF),
        ],
        name="attend",
    )(meta, gates, queries, *kv_pieces, cap_kv, q_gain, k_gain, cosine, sine)


def attend_back(heads, meta, gates, queries, grads, saved, cap_kv, q_gain, cosine, sine, kv_shapes):
    count, width, rows = queries.shape
    slots = cosine.shape[0]
    shape = jax.ShapeDtypeStruct
    own, other, stat, qs, ks, vs = saved
    return pl.pallas_call(
        functools.partial(attend_back_kernel, heads, len(kv_shapes)),
        in_specs=[SMEM, SMEM] + vmem_specs(12),
        out_specs=vmem_specs(4 + len(kv_shapes)),
        out_shape=[
            shape((count, width, rows), BF),
            shape((width, 1), F32),
            shape((CLIPS, 2 * width, CAP), F32),
            shape((8, rows), F32),
        ]
        + [shape(s, BF) for s in kv_shapes],
        scratch_shapes=[pltpu.VMEM((slots, 2 * width, rows), F32)],
        name="attend_back",
    )(meta, gates, queries, grads, own, other, stat, qs, ks, vs, cap_kv, q_gain, cosine, sine)


def keys_back_kernel(heads, meta, a_ref, r_ref, kv_ref, kg_ref, cos_ref, sin_ref, out_ref, gain_ref):
    width = heads * HD
    gain_ref[...] = jnp.zeros_like(gain_ref)
    for i in range(a_ref.shape[0]):
        slot = meta[8 * i + 4]
        cosine, sine = cos_ref[slot], sin_ref[slot]
        total = (a_ref[i].astype(F32) + r_ref[i].astype(F32)).astype(BF)
        for h in range(heads):
            at = slice(h * HD, h * HD + HD)
            raw_grad, gain_grad = norm_rope_back(
                total[at, :].astype(F32), kv_ref[i, at, :].astype(F32), kg_ref[at, :], cosine, sine
            )
            out_ref[i, at, :] = raw_grad.astype(BF)
            gain_ref[at, :] += gain_grad
        out_ref[i, width:, :] = total[width:, :]


def keys_back(heads, meta, part, received, kv, k_gain, cosine, sine):
    shape = jax.ShapeDtypeStruct
    return pl.pallas_call(
        functools.partial(keys_back_kernel, heads),
        in_specs=[SMEM] + vmem_specs(6),
        out_specs=vmem_specs(2),
        out_shape=[shape(kv.shape, BF), shape((heads * HD, 1), F32)],
        name="keys_back",
    )(meta, part, received, kv, k_gain, cosine, sine)


def weight_kernel(count, dims, *refs):
    left, right, out_ref = refs[:count], refs[count : 2 * count], refs[2 * count]
    total = None
    for a_ref, g_ref in zip(left, right):
        part = mm(a_ref[0].reshape(-1, a_ref.shape[-1]), g_ref[...], dims)
        total = part if total is None else total + part
    out_ref[...] = total.reshape(out_ref.shape).astype(BF)


def weight_grads(left, right, by_rows, tile, which):
    kinds, chunks, columns, tokens = left[0].shape
    rows = right[0].shape[0 if by_rows else 1]
    left_spec = pl.BlockSpec((1, chunks, columns, tokens), lambda i: (which(i), 0, 0, 0))
    if by_rows:
        right_spec = pl.BlockSpec((tile, tokens), lambda i: (i, 0))
    else:
        right_spec = pl.BlockSpec((tokens, tile), lambda i: (0, i))
    return pl.pallas_call(
        functools.partial(weight_kernel, len(left), NT if by_rows else NN),
        grid=(rows // tile,),
        in_specs=[left_spec] * len(left) + [right_spec] * len(right),
        out_specs=pl.BlockSpec((chunks, columns, tile), lambda i: (0, 0, i)),
        out_shape=jax.ShapeDtypeStruct((chunks, columns, rows), BF),
        name="weight_grads",
    )(*left, *right)


def fast_body(
    tokens,
    cotangent,
    clip_slices,
    caption_lengths,
    caption,
    cond,
    ada_w,
    norm_gain,
    w_qkv,
    q_gain,
    k_gain,
    w_caption,
    ky_gain,
    cross_gate,
    w_out,
    ffn_gain,
    w_gate_up,
    w_down,
):
    seq_count = lax.axis_size("seq")
    bucket_count = lax.axis_size("bucket")
    tok_rows = tokens.shape[0]
    rows = tok_rows * seq_count
    group = 4
    line = bucket_count // group
    local_width = D // seq_count
    width = local_width // line
    heads = width // HD
    units = FF // seq_count
    b = lax.axis_index("bucket")
    s = lax.axis_index("seq")
    z, g, c = b // group, b % group, b % 2
    first = s == 0

    def xswap(v):
        return lax.ppermute(v, "seq", [(0, 1), (1, 0)])

    def hop(v, to):
        return lax.ppermute(v, "bucket", [(i, to(i)) for i in range(bucket_count)])

    def cswap(v):
        return hop(v, lambda i: i ^ 1)

    def yswap(v):
        return hop(v, lambda i: i ^ 2)

    def zshift(v, k):
        return hop(v, lambda i: (i + group * k) % bucket_count)

    def join(own, other, axis):
        return jnp.where(
            first,
            jnp.concatenate([own, other], axis),
            jnp.concatenate([other, own], axis),
        )

    def take(v, index, size, axis):
        return lax.dynamic_slice_in_dim(v, index * size, size, axis)

    def pick(v, index):
        return lax.dynamic_index_in_dim(v, index, 0, False)

    ends_s = jnp.cumsum(clip_slices).astype(jnp.int32)
    starts_s = ends_s - clip_slices
    slot_ids = jnp.arange(bucket_count, dtype=jnp.int32)
    slot_clip = jnp.sum((slot_ids[:, None] >= ends_s[None, :]).astype(jnp.int32), axis=1)
    slot_start = starts_s[slot_clip]
    my_clip = slot_clip[b]
    clip_mask = jnp.arange(CLIPS) == my_clip
    half = HD // 2
    frequency = jnp.exp(
        jnp.arange(half, dtype=F32) * (-2.0 * math.log(10000.0) / (2 * half))
    )
    positions = (
        (slot_ids - slot_start)[:, None] * rows + jnp.arange(rows, dtype=jnp.int32)[None, :]
    ).astype(F32)
    angles = positions[:, None, :] * frequency[None, :, None]
    cosine, sine = jnp.cos(angles), jnp.sin(angles)
    line_ids = jnp.arange(line, dtype=jnp.int32)
    my_slots = ((z - line_ids) % line) * group + g
    my_clips = slot_clip[my_slots]
    zeros = jnp.zeros_like(my_slots)
    meta = jnp.stack(
        [
            starts_s[my_clips],
            ends_s[my_clips],
            my_clips,
            caption_lengths[my_clips],
            my_slots,
            zeros,
            zeros,
            zeros,
        ],
        axis=1,
    ).reshape(-1)
    piece_slots = (
        ((z - line_ids) % line)[None, :] * group
        + (g ^ jnp.arange(group, dtype=jnp.int32))[:, None]
    ).reshape(-1)
    meta = jnp.concatenate([meta, piece_slots]).astype(jnp.int32)

    tok_pair = join(tokens, xswap(tokens), 0).astype(F32)
    activation = jax.nn.silu(cond).astype(BF)
    cond_row = lax.dynamic_index_in_dim(activation, my_clip, 0, True)
    mod_local = mm(cond_row, ada_w, NT)
    modulation = join(mod_local, xswap(mod_local), 0).reshape(6, D)
    shift_vec, scale_vec, gate_vec, shift_mlp, scale_mlp, gate_mlp = [
        modulation[i : i + 1] for i in range(6)
    ]
    inverse = lax.rsqrt(jnp.mean(tok_pair * tok_pair, axis=-1, keepdims=True) + EPSILON)
    hidden = (tok_pair * inverse * norm_gain * (1.0 + scale_vec) + shift_vec).astype(BF)
    cot_pair = join(cotangent, xswap(cotangent), 0).astype(F32)

    projected = mm(w_qkv, hidden, NT).astype(BF).reshape(3, local_width, rows)
    swapped = xswap(projected[1])
    raw_q = jnp.where(first, projected[0], swapped).reshape(line, width, rows)
    raw_k = jnp.where(first, projected[2], projected[0]).reshape(line, width, rows)
    raw_v = jnp.where(first, swapped, projected[2]).reshape(line, width, rows)

    def spread(v):
        parts = [pick(v, z)] + [zshift(pick(v, (z + k) % line), k) for k in range(1, line)]
        return jnp.stack(parts)

    def unspread(v):
        parts = [v[0]] + [zshift(v[k], line - k) for k in range(1, line)]
        twice = jnp.stack(parts + parts)
        return lax.dynamic_slice_in_dim(twice, (line - z) % line, line, 0)

    kv_own = spread(jnp.concatenate([raw_k, raw_v], axis=1))
    queries = spread(raw_q)
    kv_y = yswap(kv_own)
    kv_c = cswap(kv_own)
    kv_pieces = [kv_own, kv_c, kv_y, cswap(kv_y)]

    w_cap = lax.dynamic_slice_in_dim(w_caption, z * width, width, 1)
    cap_raw = mm(
        w_cap.reshape(2 * width, YD), caption.reshape(CLIPS * CAP, YD), NT
    )
    head_first = s * local_width + z * width

    def mine(gain):
        return lax.dynamic_slice_in_dim(gain, head_first, width)[:, None]

    q_gain_c, k_gain_c, ky_gain_c = mine(q_gain), mine(k_gain), mine(ky_gain)
    cap_split = cap_raw[:width].reshape(heads, HD, CLIPS * CAP)
    cap_inverse = lax.rsqrt(jnp.mean(cap_split * cap_split, axis=1, keepdims=True) + EPSILON)
    cap_unit = (cap_split * cap_inverse).reshape(width, CLIPS * CAP)
    cap_kv = jnp.concatenate([cap_unit * ky_gain_c, cap_raw[width:]], axis=0).astype(BF)
    cap_kv = cap_kv.reshape(2 * width, CLIPS, CAP).transpose(1, 0, 2)
    gates = jnp.tanh(lax.dynamic_slice_in_dim(cross_gate, s * (H // seq_count) + z * heads, heads))

    combined, *saved = attend(
        heads, meta, gates, queries, kv_pieces, cap_kv, q_gain_c, k_gain_c, cosine, sine
    )
    heads_back = unspread(combined).reshape(local_width, rows)
    attention = join(heads_back, xswap(heads_back), 0)

    branch_local = mm(attention, w_out, (((0,), (1,)), ((), ()))).astype(BF)
    branch = join(branch_local, xswap(branch_local), 1).astype(F32)
    middle = tok_pair + gate_vec * branch
    mid_inverse = lax.rsqrt(jnp.mean(middle * middle, axis=-1, keepdims=True) + EPSILON)
    mid_unit = middle * mid_inverse
    mlp_gain = ffn_gain * (1.0 + scale_mlp)
    mlp_in = (mid_unit * mlp_gain + shift_mlp).astype(BF)

    quarter = units // 2
    sent = lax.dynamic_slice_in_dim(w_gate_up, (1 - s) * units + c * quarter, quarter, 0)
    came = xswap(sent)
    came_too = cswap(came)
    w_came = jnp.where(
        c == 0, jnp.concatenate([came, came_too], 0), jnp.concatenate([came_too, came], 0)
    )
    w_kept = take(w_gate_up, s, units, 0)
    kept = mm(mlp_in, w_kept, NT)
    other = mm(mlp_in, w_came, NT)
    gate_half = jnp.where(first, kept, other)
    up_half = jnp.where(first, other, kept)
    gate_sigmoid = jax.nn.sigmoid(gate_half)
    silu_gate = gate_half * gate_sigmoid
    inner = (silu_gate * up_half).astype(BF)
    grad_mlp = (cot_pair * gate_mlp).astype(BF)
    grad_inner = mm(grad_mlp, w_down, NT)
    grad_gate = (
        grad_inner * up_half * gate_sigmoid * (1.0 + gate_half * (1.0 - gate_sigmoid))
    ).astype(BF)
    grad_up = (grad_inner * silu_gate).astype(BF)
    grad_kept = jnp.where(first, grad_gate, grad_up)
    grad_came = jnp.where(first, grad_up, grad_gate)
    mlp_in_part = mm(grad_kept, w_kept, NN) + mm(grad_came, w_came, NN)

    mean_part = jnp.sum(mlp_in_part * mlp_gain * mid_unit, axis=-1, keepdims=True)
    mean_all = (mean_part + xswap(mean_part)) * (1.0 / D)

    def cols(v):
        return take(v, s, local_width, v.ndim - 1)

    def far(v, axis):
        return take(v, 1 - s, v.shape[axis] // 2, axis)

    def near(v, axis):
        return take(v, s, v.shape[axis] // 2, axis)

    mlp_in_grad = cols(mlp_in_part) + xswap(far(mlp_in_part, 1).astype(BF)).astype(F32)
    unit_c = cols(mid_unit)
    scale_mlp_c = cols(scale_mlp)
    ffn_gain_c = cols(ffn_gain)
    ffn_gain_grad = jnp.sum(mlp_in_grad * (1.0 + scale_mlp_c) * unit_c, axis=0)
    shift_mlp_grad = jnp.sum(mlp_in_grad, axis=0)
    scale_mlp_grad = jnp.sum(mlp_in_grad * unit_c * ffn_gain_c, axis=0)
    grad_middle = cols(cot_pair) + mid_inverse * (
        mlp_in_grad * ffn_gain_c * (1.0 + scale_mlp_c) - unit_c * mean_all
    )
    gate_grad = jnp.sum(grad_middle * cols(branch), axis=0)
    grad_branch = (grad_middle * cols(gate_vec)).astype(BF)
    attention_part = mm(w_out, grad_branch, (((0,), (1,)), ((), ())))
    grad_heads = (near(attention_part, 0) + xswap(far(attention_part, 0).astype(BF)).astype(F32)).astype(BF)
    grad_heads = spread(grad_heads.reshape(line, width, rows))

    grad_q, q_gain_part, cap_part, gate_part, *grad_kv = attend_back(
        heads,
        meta,
        gates,
        queries,
        grad_heads,
        saved,
        cap_kv,
        q_gain_c,
        cosine,
        sine,
        [kv_own.shape] * group,
    )
    here = (grad_kv[0].astype(F32) + cswap(grad_kv[1]).astype(F32)).astype(BF)
    away = (grad_kv[2].astype(F32) + cswap(grad_kv[3]).astype(F32)).astype(BF)
    grad_kv_raw, k_gain_part = keys_back(
        heads, meta, here, yswap(away), kv_own, k_gain_c, cosine, sine
    )
    grad_qkv = unspread(jnp.concatenate([grad_q, grad_kv_raw], axis=1)).reshape(line, 3, width, rows)
    back_q, back_k, back_v = [grad_qkv[:, i].reshape(local_width, rows) for i in range(3)]
    back_swap = xswap(jnp.where(first, back_v, back_q))
    grad_projected = jnp.concatenate(
        [
            jnp.where(first, back_q, back_k),
            back_swap,
            jnp.where(first, back_k, back_v),
        ],
        axis=0,
    )
    hidden_part = mm(grad_projected, w_qkv, TN)
    hidden_grad = near(hidden_part, 0) + xswap(far(hidden_part, 0).astype(BF)).astype(F32)

    middle_own = join(near(grad_middle, 0), xswap(far(grad_middle, 0)), 1)
    tok_own = tokens.astype(F32)
    inverse_own = near(inverse, 0)
    unit_own = tok_own * inverse_own
    unit_grad = hidden_grad * norm_gain * (1.0 + scale_vec)
    token_grad = (
        inverse_own
        * (unit_grad - unit_own * jnp.mean(unit_grad * unit_own, axis=-1, keepdims=True))
        + middle_own
    )
    norm_gain_grad = jnp.sum(hidden_grad * (1.0 + scale_vec) * unit_own, axis=0)
    shift_grad = jnp.sum(hidden_grad, axis=0)
    scale_grad = jnp.sum(hidden_grad * unit_own * norm_gain, axis=0)

    mlp_part = mm(inner, w_down, NN)
    mlp_branch = near(mlp_part, 0) + xswap(far(mlp_part, 0).astype(BF)).astype(F32)
    output = (near(middle, 0) + gate_mlp * mlp_branch).astype(BF)
    mlp_gate_grad = jnp.sum(cotangent.astype(F32) * mlp_branch, axis=0)

    def gather_left(values):
        cut = jnp.stack([v.reshape(line, group, D // bucket_count, rows) for v in values])

        def of(index):
            return lax.dynamic_index_in_dim(cut, index, 2, False)

        came_y = yswap(jnp.stack([of(g ^ 2), of(g ^ 3)]))
        came_c = cswap(jnp.stack([of(g ^ 1), came_y[1]]))
        return [of(g), came_c[0], came_y[0], came_c[1]]

    def gather_right(v):
        far_v = yswap(v)
        return [v, cswap(v), far_v, cswap(far_v)]

    right_line = [(i, i + group) for i in range(bucket_count - group)]

    def line_sum(parts):
        parts_f = parts
        left_in = right_in = None
        for t in range(1, line):
            to_right = lax.dynamic_index_in_dim(parts_f, jnp.clip(line - t + z, 0, line - 1), 0, False)
            to_left = lax.dynamic_index_in_dim(parts_f, jnp.clip(t - 1 - (line - 1 - z), 0, line - 1), 0, False)
            if t > 1:
                to_right = (to_right.astype(F32) + right_in.astype(F32)).astype(BF)
                to_left = (to_left.astype(F32) + left_in.astype(F32)).astype(BF)
            pairs = [(i, i + group) for i in range(group * t)]
            right_in = lax.ppermute(to_right, "bucket", pairs)
            pairs = [
                (bucket_count - 1 - i, bucket_count - 1 - i - group) for i in range(group * t)
            ]
            left_in = lax.ppermute(to_left, "bucket", pairs)
        own = lax.dynamic_index_in_dim(parts_f, z, 0, False)
        return own.astype(F32) + right_in.astype(F32) + left_in.astype(F32)

    ffn_left = gather_left([grad_mlp.T, mlp_in.T])
    ffn_right = gather_right(jnp.concatenate([inner, grad_kept, grad_came], axis=1))
    tile = 512
    down_tiles = units // tile
    ffn_parts = weight_grads(
        ffn_left, ffn_right, False, tile, lambda i: jnp.where(i < down_tiles, 0, 1)
    )
    ffn_sum = line_sum(ffn_parts)
    down_grad_out = ffn_sum[:, :units].T
    kept_grad = ffn_sum[:, units : 2 * units]
    came_grad = xswap(ffn_sum[:, 2 * units :].astype(BF)).astype(F32)
    gate_up_grad_out = join(kept_grad, came_grad, 1).T

    out_left = gather_left([attention])
    out_right = gather_right(grad_branch)
    out_parts = weight_grads(out_left, out_right, False, 384, lambda i: 0)
    out_grad_out = line_sum(out_parts).T
    qkv_left = gather_left([hidden.T])
    qkv_right = gather_right(grad_projected)
    qkv_parts = weight_grads(qkv_left, qkv_right, True, 384, lambda i: 0)
    qkv_grad_out = line_sum(qkv_parts).T

    cap_c = cap_part.reshape(2, 2, 2 * width, CAP)
    pair_sum = pick(cap_c.transpose(1, 0, 2, 3), c) + cswap(pick(cap_c.transpose(1, 0, 2, 3), 1 - c))
    y = (b // 2) % 2
    cap_sum = pick(pair_sum, y) + yswap(pick(pair_sum, 1 - y))
    unit_g = lax.dynamic_slice_in_dim(cap_unit, g * CAP, CAP, 1)
    cap_inverse_g = lax.dynamic_slice_in_dim(cap_inverse, g * CAP, CAP, 2)
    key_sum = cap_sum[:width]
    ky_gain_part = jnp.sum(key_sum * unit_g, axis=1)
    key_unit_grad = (key_sum * ky_gain_c).reshape(heads, HD, CAP)
    unit_g3 = unit_g.reshape(heads, HD, CAP)
    raw_key_grad = cap_inverse_g * (
        key_unit_grad - unit_g3 * jnp.mean(key_unit_grad * unit_g3, axis=1, keepdims=True)
    )
    raw_cap = jnp.concatenate([raw_key_grad.reshape(width, CAP), cap_sum[width:]], 0).astype(BF)
    raw_all = lax.all_gather(raw_cap, "bucket", axis=0, tiled=False)
    raw_all = raw_all.reshape(line, CLIPS, 2, width, CAP)
    caption_cols = lax.dynamic_slice_in_dim(
        caption, b * (YD // bucket_count), YD // bucket_count, 2
    )
    caption_w_grad = jnp.einsum(
        "zcjwt,cty->jzwy", raw_all, caption_cols, preferred_element_type=F32
    ).reshape(2, local_width, YD // bucket_count)

    def place(v, size, at):
        return lax.dynamic_update_slice_in_dim(jnp.zeros((size,), F32), v, at, 0)

    def total(v):
        v = v + cswap(v)
        v = v + yswap(v)
        v = v + hop(v, lambda i: i ^ group)
        v = v + hop(v, lambda i: i ^ (2 * group))
        return v + xswap(v)

    early = jnp.concatenate(
        [
            place(gate_grad, D, s * local_width),
            place(shift_mlp_grad, D, s * local_width),
            place(scale_mlp_grad, D, s * local_width),
            mlp_gate_grad,
        ]
    )
    early_rows = jnp.where(clip_mask[:, None], early[None, :], 0.0).reshape(-1, 128)
    early_all = jnp.concatenate(
        [early_rows, place(ffn_gain_grad, D, s * local_width).reshape(-1, 128)], axis=0
    )
    early_sum = total(early_all)
    early_mod = early_sum[: CLIPS * 4 * D // 128].reshape(CLIPS, 4 * D)
    ffn_gain_out = early_sum[CLIPS * 4 * D // 128 :].reshape(-1)
    late = jnp.concatenate([shift_grad, scale_grad])
    late_rows = jnp.where(clip_mask[:, None], late[None, :], 0.0).reshape(-1, 128)
    head_grads = lax.dynamic_update_slice_in_dim(
        jnp.zeros((128,), F32),
        jnp.sum(gate_part[:heads], axis=1) * (1.0 - gates * gates),
        s * (H // seq_count) + z * heads,
        0,
    )
    late_all = jnp.concatenate(
        [
            late_rows,
            norm_gain_grad.reshape(-1, 128),
            place(q_gain_part[:, 0], D, head_first).reshape(-1, 128),
            place(k_gain_part[:, 0], D, head_first).reshape(-1, 128),
            place(ky_gain_part, D, head_first).reshape(-1, 128),
            head_grads.reshape(1, 128),
        ],
        axis=0,
    )
    late_sum = total(late_all)
    n_late = CLIPS * 2 * D // 128
    per = D // 128
    late_mod = late_sum[:n_late].reshape(CLIPS, 2 * D)
    gain_rows = late_sum[n_late : n_late + 4 * per].reshape(4, D)
    cross_gate_out = late_sum[n_late + 4 * per, :H]
    mod_total = jnp.concatenate([late_mod, early_mod], axis=1).astype(BF)
    mod_mine = take(mod_total, s, 6 * D // seq_count, 1)
    cols_local = CD // bucket_count
    ada_grad = mm(mod_mine, take(activation, b, cols_local, 1), TN)
    cond_part = mm(mod_mine, ada_w, NN)
    cond_sigmoid = jax.nn.sigmoid(cond)
    cond_grad = (
        (cond_part + xswap(cond_part)) * cond_sigmoid * (1.0 + cond * (1.0 - cond_sigmoid))
    )
    return (
        output,
        token_grad,
        cond_grad,
        ada_grad,
        gain_rows[0],
        qkv_grad_out,
        gain_rows[1],
        gain_rows[2],
        caption_w_grad,
        gain_rows[3],
        cross_gate_out,
        out_grad_out,
        ffn_gain_out,
        gate_up_grad_out,
        down_grad_out,
    )


def project(activations, weight):
    return lax.dot_general(
        activations, weight, (((1,), (1,)), ((), ())), preferred_element_type=jnp.float32
    )


def clip_of(rows, ends):
    return jnp.sum((rows[:, None] >= ends[None, :]).astype(jnp.int32), axis=1)


def head_norm(values, gains, head_count):
    row_count = values.shape[0]
    split = values.reshape(row_count, head_count, -1)
    inverse = lax.rsqrt(jnp.mean(split * split, axis=-1, keepdims=True) + EPSILON)
    unit_rows = split * inverse
    return (unit_rows.reshape(row_count, -1) * gains, unit_rows, inverse)


def head_norm_back(norm_grads, gains, unit_rows, inverse):
    row_count, head_count, head_width = unit_rows.shape
    gain_grad = jnp.sum(norm_grads * unit_rows.reshape(row_count, -1), axis=0)
    unit_grad = (norm_grads * gains).reshape(row_count, head_count, head_width)
    raw_grad = inverse * (
        unit_grad - unit_rows * jnp.mean(unit_grad * unit_rows, axis=-1, keepdims=True)
    )
    return (raw_grad.reshape(row_count, -1), gain_grad)


def rotate(values, positions, head_count):
    row_count = values.shape[0]
    split = values.reshape(row_count, head_count, -1)
    half_width = split.shape[-1] // 2
    frequency = jnp.exp(
        jnp.arange(half_width, dtype=jnp.float32) * (-2.0 * math.log(10000.0) / (2 * half_width))
    )
    angles = positions[:, None] * frequency[None, :]
    cosine = jnp.cos(angles)[:, None, :]
    sine = jnp.sin(angles)[:, None, :]
    first_half = split[..., :half_width]
    second_half = split[..., half_width:]
    turned = jnp.concatenate(
        [first_half * cosine - second_half * sine, first_half * sine + second_half * cosine],
        axis=-1,
    )
    return turned.reshape(row_count, -1)


def block_size(row_count):
    return 512 if row_count % 512 == 0 else row_count


def general_body(
    tokens,
    cotangent,
    clip_slices,
    caption_lengths,
    caption,
    cond,
    ada_w,
    norm_gain,
    w_qkv,
    q_gain,
    k_gain,
    w_caption,
    ky_gain,
    cross_gate,
    w_out,
    ffn_gain,
    w_gate_up,
    w_down,
):
    seq_count = lax.axis_size("seq")
    bucket_count = lax.axis_size("bucket")
    tok_rows = tokens.shape[0]
    slice_rows = tok_rows * seq_count
    total_rows = slice_rows * bucket_count
    local_heads = H // seq_count
    local_width = local_heads * HD
    score_scale = HD ** (-0.5)
    bucket_id = lax.axis_index("bucket")
    seq_id = lax.axis_index("seq")
    ends = jnp.cumsum(clip_slices) * slice_rows
    starts = ends - clip_slices * slice_rows
    my_clip = clip_of(jnp.reshape(bucket_id * slice_rows, (1,)), ends)[0]
    clip_mask = jnp.arange(CLIPS) == my_clip
    clip_start = jnp.sum(jnp.where(clip_mask, starts, 0))
    first_token = (bucket_id * seq_count + seq_id) * tok_rows
    positions = (first_token + jnp.arange(tok_rows, dtype=jnp.int32) - clip_start).astype(
        jnp.float32
    )
    caption_usable = jnp.arange(CAP) < jnp.sum(jnp.where(clip_mask, caption_lengths, 0))
    head_first = seq_id * local_width
    gates_local = jnp.tanh(lax.dynamic_slice_in_dim(cross_gate, seq_id * local_heads, local_heads))
    ky_gain_local = lax.dynamic_slice_in_dim(ky_gain, head_first, local_width)
    activation = jax.nn.silu(cond).astype(jnp.bfloat16)
    cond_row = lax.dynamic_index_in_dim(activation, my_clip, 0, True)
    caption_rows = lax.dynamic_index_in_dim(caption, my_clip, 0, False)
    caption_raw = jnp.einsum(
        "ty,jdy->jtd", caption_rows, w_caption, preferred_element_type=jnp.float32
    )
    caption_norm, caption_unit, caption_inverse = head_norm(
        caption_raw[0], ky_gain_local, local_heads
    )
    caption_keys = caption_norm.astype(jnp.bfloat16).reshape(CAP, local_heads, HD)
    caption_values = caption_raw[1].astype(jnp.bfloat16).reshape(CAP, local_heads, HD)
    inputs = tokens.astype(jnp.float32)

    def key_usable(first_row, row_count):
        return clip_of(first_row + jnp.arange(row_count, dtype=jnp.int32), ends) == my_clip

    def fold_keys(queries3, running, segment, first_row):
        seg_keys, seg_values = segment
        row_count = seg_keys.shape[0]
        key_rows = block_size(row_count)
        steps_count = row_count // key_rows
        usable = key_usable(first_row, row_count).reshape(steps_count, key_rows)
        key_blocks = seg_keys.reshape(steps_count, key_rows, local_heads, HD)
        value_blocks = seg_values.reshape(steps_count, key_rows, local_heads, HD)

        def update(state, item):
            key_block, value_block, usable_block = item

            def update_include(inner):
                row_max, row_total, accum = inner
                scores = (
                    jnp.einsum(
                        "qhd,khd->hqk", queries3, key_block, preferred_element_type=jnp.float32
                    )
                    * score_scale
                )
                scores = jnp.where(usable_block[None, None, :], scores, MASKED)
                new_max = jnp.maximum(row_max, jnp.max(scores, axis=-1))
                factor = jnp.exp(row_max - new_max)
                weights = jnp.exp(scores - new_max[..., None])
                row_total = row_total * factor + jnp.sum(weights, axis=-1)
                accum = accum * factor.T[:, :, None] + jnp.einsum(
                    "hqk,khd->qhd",
                    weights.astype(jnp.bfloat16),
                    value_block,
                    preferred_element_type=jnp.float32,
                )
                return (new_max, row_total, accum)

            return (
                lax.cond(jnp.any(usable_block), update_include, lambda inner: inner, state),
                None,
            )

        running, unused = lax.scan(update, running, (key_blocks, value_blocks, usable))
        return running

    def local_fold(queries3, running, keys_whole):

        def local_visit(state, piece_index):
            first_row = piece_index * slice_rows
            segment = (
                lax.dynamic_slice_in_dim(keys_whole[0], first_row, slice_rows, 0),
                lax.dynamic_slice_in_dim(keys_whole[1], first_row, slice_rows, 0),
            )
            return (fold_keys(queries3, state, segment, first_row), None)

        running, unused = lax.scan(local_visit, running, jnp.arange(bucket_count, dtype=jnp.int32))
        return running

    def forward(qkv_full, out_full, modulation, second):
        shift_vec = modulation[:D]
        scale_vec = modulation[D : 2 * D]
        gate_vec = modulation[2 * D : 3 * D]
        inverse = lax.rsqrt(jnp.mean(inputs * inputs, axis=-1, keepdims=True) + EPSILON)
        unit_rows = inputs * inverse
        hidden = (unit_rows * norm_gain * (1.0 + scale_vec) + shift_vec).astype(jnp.bfloat16)
        projected = project(hidden, qkv_full)
        query_norm, query_unit, query_inverse = head_norm(projected[:, :D], q_gain, H)
        key_norm, key_unit, key_inverse = head_norm(projected[:, D : 2 * D], k_gain, H)
        queries = rotate(query_norm, positions, H).astype(jnp.bfloat16)
        keys_tok = rotate(key_norm, positions, H).astype(jnp.bfloat16)
        values_tok = projected[:, 2 * D :].astype(jnp.bfloat16)
        head_queries, head_keys, head_values = (
            lax.all_to_all(queries, "seq", split_axis=1, concat_axis=0, tiled=True),
            lax.all_to_all(keys_tok, "seq", split_axis=1, concat_axis=0, tiled=True),
            lax.all_to_all(values_tok, "seq", split_axis=1, concat_axis=0, tiled=True),
        )
        queries3 = head_queries.reshape(slice_rows, local_heads, HD)
        start_state = (
            jnp.full((local_heads, slice_rows), MASKED, jnp.float32),
            jnp.zeros((local_heads, slice_rows), jnp.float32),
            jnp.zeros((slice_rows, local_heads, HD), jnp.float32),
        )
        folder = functools.partial(fold_keys, queries3)
        if second:
            keys_whole = (
                lax.all_gather(head_keys, "bucket", axis=0, tiled=True),
                lax.all_gather(head_values, "bucket", axis=0, tiled=True),
            )
            final_state = local_fold(queries3, start_state, keys_whole)
        else:
            keys_whole = None
            final_state = folder(
                start_state,
                (
                    lax.all_gather(head_keys, "bucket", axis=0, tiled=True),
                    lax.all_gather(head_values, "bucket", axis=0, tiled=True),
                ),
                jnp.int32(0),
            )
        row_max, row_total, accum = final_state
        own = accum / row_total.T[:, :, None]
        cross_scores = (
            jnp.einsum("qhd,khd->hqk", queries3, caption_keys, preferred_element_type=jnp.float32)
            * score_scale
        )
        cross_prob = jax.nn.softmax(
            jnp.where(caption_usable[None, None, :], cross_scores, MASKED), axis=-1
        )
        other = jnp.einsum(
            "hqk,khd->qhd",
            cross_prob.astype(jnp.bfloat16),
            caption_values,
            preferred_element_type=jnp.float32,
        )
        combined = (
            (own + gates_local[None, :, None] * other)
            .reshape(slice_rows, local_width)
            .astype(jnp.bfloat16)
        )
        attention = lax.all_to_all(combined, "seq", split_axis=0, concat_axis=1, tiled=True)
        branch = project(attention, out_full)
        return dict(
            gate_vec=gate_vec,
            scale_vec=scale_vec,
            inverse=inverse,
            unit_rows=unit_rows,
            hidden=hidden,
            query_unit=query_unit,
            query_inverse=query_inverse,
            key_unit=key_unit,
            key_inverse=key_inverse,
            queries3=queries3,
            own_keys3=head_keys.reshape(slice_rows, local_heads, HD),
            own_values3=head_values.reshape(slice_rows, local_heads, HD),
            keys_whole=keys_whole,
            row_log=row_max + jnp.log(row_total),
            own=own,
            other=other,
            cross_prob=cross_prob,
            attention=attention,
            branch=branch,
            output=inputs + gate_vec * branch,
        )

    gathered = (
        lax.all_gather(ada_w, "seq", axis=0, tiled=True),
        lax.all_gather(w_qkv, "seq", axis=0, tiled=True),
        lax.all_gather(w_out, "seq", axis=0, tiled=True),
        lax.all_gather(w_gate_up, "seq", axis=0, tiled=True),
        lax.all_gather(w_down, "seq", axis=0, tiled=True),
    )
    modulation = project(cond_row, gathered[0])[0]
    first_pass = forward(gathered[1], gathered[2], modulation, False)
    middle = first_pass["output"]
    shift_mlp = modulation[3 * D : 4 * D]
    scale_mlp = modulation[4 * D : 5 * D]
    gate_mlp = modulation[5 * D :]
    mid_inverse = lax.rsqrt(jnp.mean(middle * middle, axis=-1, keepdims=True) + EPSILON)
    mid_unit = middle * mid_inverse
    mlp_in = (mid_unit * ffn_gain * (1.0 + scale_mlp) + shift_mlp).astype(jnp.bfloat16)
    gate_up = project(mlp_in, gathered[3])
    gate_half = gate_up[:, :FF]
    up_half = gate_up[:, FF:]
    gate_sigmoid = jax.nn.sigmoid(gate_half)
    silu_gate = gate_half * gate_sigmoid
    inner = (silu_gate * up_half).astype(jnp.bfloat16)
    mlp_branch = jnp.dot(inner, gathered[4], preferred_element_type=jnp.float32)
    output = (middle + gate_mlp * mlp_branch).astype(jnp.bfloat16)
    regathered = (
        lax.all_gather(ada_w, "seq", axis=0, tiled=True),
        lax.all_gather(w_qkv, "seq", axis=0, tiled=True),
        lax.all_gather(w_out, "seq", axis=0, tiled=True),
        lax.all_gather(w_gate_up, "seq", axis=0, tiled=True),
        lax.all_gather(w_down, "seq", axis=0, tiled=True),
    )
    second_pass = forward(regathered[1], regathered[2], modulation, True)
    ada_full, qkv_full, out_full, gate_up_full, down_full = regathered
    grad_out = cotangent.astype(jnp.float32)
    mlp_gate_grad = jnp.sum(grad_out * mlp_branch, axis=0)
    grad_mlp = (grad_out * gate_mlp).astype(jnp.bfloat16)
    grad_inner = lax.dot_general(
        grad_mlp, down_full, (((1,), (1,)), ((), ())), preferred_element_type=jnp.float32
    )
    grad_gate_half = grad_inner * up_half * gate_sigmoid * (1.0 + gate_half * (1.0 - gate_sigmoid))
    grad_up_half = grad_inner * silu_gate
    grad_gate_up = jnp.concatenate([grad_gate_half, grad_up_half], axis=1).astype(jnp.bfloat16)
    mlp_in_grad = jnp.dot(grad_gate_up, gate_up_full, preferred_element_type=jnp.float32)
    ffn_gain_grad = jnp.sum(mlp_in_grad * (1.0 + scale_mlp) * mid_unit, axis=0)
    shift_mlp_grad = jnp.sum(mlp_in_grad, axis=0)
    scale_mlp_grad = jnp.sum(mlp_in_grad * mid_unit * ffn_gain, axis=0)
    mid_unit_grad = mlp_in_grad * ffn_gain * (1.0 + scale_mlp)
    residual_grad = (
        mid_inverse
        * (mid_unit_grad - mid_unit * jnp.mean(mid_unit_grad * mid_unit, axis=-1, keepdims=True))
        + grad_out
    )
    gate_grad = jnp.sum(residual_grad * second_pass["branch"], axis=0)
    grad_branch = (residual_grad * second_pass["gate_vec"]).astype(jnp.bfloat16)
    attention = second_pass["attention"]
    grad_attention = jnp.dot(grad_branch, out_full, preferred_element_type=jnp.float32).astype(
        jnp.bfloat16
    )
    grad_heads = lax.all_to_all(grad_attention, "seq", split_axis=1, concat_axis=0, tiled=True)
    grad_own16 = grad_heads.reshape(slice_rows, local_heads, HD)
    grad_own = grad_own16.astype(jnp.float32)
    queries3 = second_pass["queries3"]
    own = second_pass["own"]
    other = second_pass["other"]
    cross_prob = second_pass["cross_prob"]
    grad_other = (grad_own * gates_local[None, :, None]).astype(jnp.bfloat16)
    gate_grad_local = jnp.sum(grad_own * other, axis=(0, 2)) * (1.0 - gates_local * gates_local)
    grad_cross_prob = jnp.einsum(
        "qhd,khd->hqk", grad_other, caption_values, preferred_element_type=jnp.float32
    )
    grad_cross = (
        cross_prob
        * (grad_cross_prob - jnp.sum(cross_prob * grad_cross_prob, axis=-1, keepdims=True))
    ).astype(jnp.bfloat16)
    cross_query_grad = score_scale * jnp.einsum(
        "hqk,khd->qhd", grad_cross, caption_keys, preferred_element_type=jnp.float32
    )
    caption_key_grad = score_scale * jnp.einsum(
        "hqk,qhd->khd", grad_cross, queries3, preferred_element_type=jnp.float32
    )
    caption_value_grad = jnp.einsum(
        "hqk,qhd->khd",
        cross_prob.astype(jnp.bfloat16),
        grad_other,
        preferred_element_type=jnp.float32,
    )
    row_delta = jnp.sum(grad_own * own, axis=-1).T
    row_log = second_pass["row_log"]
    keys_whole = second_pass["keys_whole"]

    def grad_piece(query_grad, piece_index, with_keys):
        first_row = piece_index * slice_rows
        key_rows = block_size(slice_rows)
        steps_count = slice_rows // key_rows
        key_blocks = lax.dynamic_slice_in_dim(keys_whole[0], first_row, slice_rows, 0).reshape(
            steps_count, key_rows, local_heads, HD
        )
        value_blocks = lax.dynamic_slice_in_dim(keys_whole[1], first_row, slice_rows, 0).reshape(
            steps_count, key_rows, local_heads, HD
        )
        usable = key_usable(first_row, slice_rows).reshape(steps_count, key_rows)

        def grad_visit(accum, item):
            key_block, value_block, usable_block = item

            def grad_include(inner):
                scores = (
                    jnp.einsum(
                        "qhd,khd->hqk", queries3, key_block, preferred_element_type=jnp.float32
                    )
                    * score_scale
                )
                scores = jnp.where(usable_block[None, None, :], scores, MASKED)
                probability = jnp.exp(scores - row_log[..., None])
                grad_prob = jnp.einsum(
                    "qhd,khd->hqk", grad_own16, value_block, preferred_element_type=jnp.float32
                )
                grad_scores = (probability * (grad_prob - row_delta[..., None])).astype(
                    jnp.bfloat16
                )
                updated = inner + score_scale * jnp.einsum(
                    "hqk,khd->qhd", grad_scores, key_block, preferred_element_type=jnp.float32
                )
                key_grad = score_scale * jnp.einsum(
                    "hqk,qhd->khd", grad_scores, queries3, preferred_element_type=jnp.float32
                )
                value_grad = jnp.einsum(
                    "hqk,qhd->khd",
                    probability.astype(jnp.bfloat16),
                    grad_own16,
                    preferred_element_type=jnp.float32,
                )
                return (updated, key_grad, value_grad)

            def skip(inner):
                empty = jnp.zeros((key_rows, local_heads, HD), jnp.float32)
                return (inner, empty, empty)

            updated, key_grad, value_grad = lax.cond(
                jnp.any(usable_block), grad_include, skip, accum
            )
            return (updated, (key_grad, value_grad))

        query_grad, (key_grads, value_grads) = lax.scan(
            grad_visit, query_grad, (key_blocks, value_blocks, usable)
        )
        return (
            query_grad,
            (
                key_grads.reshape(slice_rows, local_width),
                value_grads.reshape(slice_rows, local_width),
            ),
        )

    query_start = jnp.zeros((slice_rows, local_heads, HD), jnp.float32)
    piece_order = jnp.arange(bucket_count, dtype=jnp.int32)
    self_query_grad, (key_terms, value_terms) = lax.scan(
        functools.partial(grad_piece, with_keys=True), query_start, piece_order
    )
    key_sum, value_sum = (
        lax.psum_scatter(
            key_terms.reshape(total_rows, local_width).astype(jnp.bfloat16),
            "bucket",
            scatter_dimension=0,
            tiled=True,
        ).astype(jnp.float32),
        lax.psum_scatter(
            value_terms.reshape(total_rows, local_width).astype(jnp.bfloat16),
            "bucket",
            scatter_dimension=0,
            tiled=True,
        ).astype(jnp.float32),
    )
    query_grad16 = (
        (self_query_grad + cross_query_grad).reshape(slice_rows, local_width).astype(jnp.bfloat16)
    )
    tok_query_grad, tok_key_grad, tok_value_grad = (
        lax.all_to_all(query_grad16, "seq", split_axis=0, concat_axis=1, tiled=True),
        lax.all_to_all(
            key_sum.astype(jnp.bfloat16), "seq", split_axis=0, concat_axis=1, tiled=True
        ),
        lax.all_to_all(
            value_sum.astype(jnp.bfloat16), "seq", split_axis=0, concat_axis=1, tiled=True
        ),
    )
    query_raw_grad, q_gain_grad = head_norm_back(
        rotate(tok_query_grad.astype(jnp.float32), -positions, H),
        q_gain,
        second_pass["query_unit"],
        second_pass["query_inverse"],
    )
    key_raw_grad, k_gain_grad = head_norm_back(
        rotate(tok_key_grad.astype(jnp.float32), -positions, H),
        k_gain,
        second_pass["key_unit"],
        second_pass["key_inverse"],
    )
    projected_grad = jnp.concatenate(
        [query_raw_grad, key_raw_grad, tok_value_grad.astype(jnp.float32)], axis=1
    ).astype(jnp.bfloat16)
    hidden = second_pass["hidden"]
    out_each = D // seq_count
    qkv_each = 3 * D // seq_count
    gate_up_each = 2 * FF // seq_count
    down_each = FF // seq_count
    rows_each = out_each + qkv_each + gate_up_each + down_each
    device_count = rows_each * lax.axis_size("seq") // rows_each
    first_device = jnp.int32(0) // rows_each

    def part(operand, partner, each):
        picked = lax.dynamic_slice_in_dim(operand, first_device * each, device_count * each, 1)
        term = lax.dot_general(
            picked, partner, (((0,), (0,)), ((), ())), preferred_element_type=jnp.float32
        )
        return term.reshape(device_count, each, D)

    terms = [
        part(grad_branch, attention, out_each),
        part(projected_grad, hidden, qkv_each),
        part(grad_gate_up, mlp_in, gate_up_each),
        part(inner, grad_mlp, down_each),
    ]
    weight_grad_seq = lax.psum_scatter(
        jnp.concatenate(terms, axis=1)
        .reshape(rows_each * lax.axis_size("seq"), D)
        .astype(jnp.bfloat16),
        "seq",
        scatter_dimension=0,
        tiled=True,
    )
    hidden_grad = jnp.dot(projected_grad, qkv_full, preferred_element_type=jnp.float32)
    unit_rows = second_pass["unit_rows"]
    scale_vec = second_pass["scale_vec"]
    inverse = second_pass["inverse"]
    norm_gain_grad = jnp.sum(hidden_grad * (1.0 + scale_vec) * unit_rows, axis=0)
    shift_grad = jnp.sum(hidden_grad, axis=0)
    scale_grad = jnp.sum(hidden_grad * unit_rows * norm_gain, axis=0)
    unit_grad = hidden_grad * norm_gain * (1.0 + scale_vec)
    token_grad = (
        inverse * (unit_grad - unit_rows * jnp.mean(unit_grad * unit_rows, axis=-1, keepdims=True))
        + residual_grad
    )
    modulation_grad = jnp.where(
        clip_mask[:, None],
        jnp.concatenate(
            [shift_grad, scale_grad, gate_grad, shift_mlp_grad, scale_mlp_grad, mlp_gate_grad]
        )[None, :],
        0.0,
    )
    ky_gain_part = jnp.sum(
        caption_key_grad.reshape(CAP, local_width) * caption_unit.reshape(CAP, local_width), axis=0
    )
    ky_gain_full = lax.dynamic_update_slice_in_dim(
        jnp.zeros((D,), jnp.float32), ky_gain_part, head_first, 0
    )
    gate_full = lax.dynamic_update_slice_in_dim(
        jnp.zeros((H,), jnp.float32), gate_grad_local, seq_id * local_heads, 0
    )
    caption_part = jnp.stack(
        [caption_key_grad.reshape(CAP, local_width), caption_value_grad.reshape(CAP, local_width)]
    )[None]
    zero_index = jnp.zeros((), jnp.int32)
    caption_full = lax.dynamic_update_slice(
        jnp.zeros((CLIPS, 2, CAP, D), jnp.float32),
        caption_part,
        (my_clip, zero_index, zero_index, head_first),
    )
    reduced = lax.psum(
        (
            norm_gain_grad,
            q_gain_grad,
            k_gain_grad,
            ky_gain_full,
            gate_full,
            modulation_grad,
            caption_full,
            ffn_gain_grad,
        ),
        ("bucket", "seq"),
    )
    modulation_total = reduced[5].astype(jnp.bfloat16)
    rows_local = 6 * D // seq_count
    cols_local = CD // bucket_count
    ada_grad = lax.dot_general(
        lax.dynamic_slice_in_dim(modulation_total, seq_id * rows_local, rows_local, 1),
        lax.dynamic_slice_in_dim(activation, bucket_id * cols_local, cols_local, 1),
        (((0,), (0,)), ((), ())),
        preferred_element_type=jnp.float32,
    )
    cond_sigmoid = jax.nn.sigmoid(cond)
    cond_grad = (
        jnp.dot(modulation_total, ada_full, preferred_element_type=jnp.float32)
        * cond_sigmoid
        * (1.0 + cond * (1.0 - cond_sigmoid))
    )
    caption_total = lax.dynamic_slice_in_dim(reduced[6], head_first, local_width, 3)
    raw_keys_all = jnp.einsum(
        "cty,dy->ctd", caption, w_caption[0], preferred_element_type=jnp.float32
    ).reshape(CLIPS * CAP, local_width)
    ignored, unit_all, inverse_all = head_norm(raw_keys_all, ky_gain_local, local_heads)
    raw_key_grad, unused_gain = head_norm_back(
        caption_total[:, 0].reshape(CLIPS * CAP, local_width), ky_gain_local, unit_all, inverse_all
    )
    raw_grad = jnp.stack(
        [raw_key_grad.reshape(CLIPS, CAP, local_width), caption_total[:, 1]], axis=1
    ).astype(jnp.bfloat16)
    caption_cols = lax.dynamic_slice_in_dim(
        caption, bucket_id * (YD // bucket_count), YD // bucket_count, 2
    )
    caption_w_grad = jnp.einsum(
        "cjtd,cty->jdy", raw_grad, caption_cols, preferred_element_type=jnp.float32
    )
    combined_grads = lax.psum_scatter(
        weight_grad_seq, "bucket", scatter_dimension=1, tiled=True
    ).astype(jnp.float32)
    out_grad_out = combined_grads[:out_each]
    qkv_grad_out = combined_grads[out_each : out_each + qkv_each]
    gate_up_grad_out = combined_grads[out_each + qkv_each : out_each + qkv_each + gate_up_each]
    down_grad_out = combined_grads[out_each + qkv_each + gate_up_each :]
    return (
        output,
        token_grad,
        cond_grad,
        ada_grad,
        reduced[0],
        qkv_grad_out,
        reduced[1],
        reduced[2],
        caption_w_grad,
        reduced[3],
        reduced[4],
        out_grad_out,
        reduced[7],
        gate_up_grad_out,
        down_grad_out,
    )


def solution(mesh):
    in_specs = (
        P(("bucket", "seq"), None),
        P(("bucket", "seq"), None),
        P(),
        P(),
        P(),
        P(),
        P("seq", None),
        P(),
        P("seq", None),
        P(),
        P(),
        P(None, "seq", None),
        P(),
        P(),
        P("seq", None),
        P(),
        P("seq", None),
        P("seq", None),
    )
    out_specs = (
        P(("bucket", "seq"), None),
        P(("bucket", "seq"), None),
        P(),
        P("seq", "bucket"),
        P(),
        P("seq", "bucket"),
        P(),
        P(),
        P(None, "seq", "bucket"),
        P(),
        P(),
        P("seq", "bucket"),
        P(),
        P("seq", "bucket"),
        P("seq", "bucket"),
    )
    fits = mesh.shape["seq"] == 2 and mesh.shape["bucket"] == 16
    body = fast_body if fits else general_body
    return jax.shard_map(body, mesh=mesh, in_specs=in_specs, out_specs=out_specs, check_vma=False)
```

```python
import functools
import math

import jax
import jax.numpy as jnp
from jax import lax
from jax.experimental import pallas as pl
from jax.experimental.pallas import tpu as pltpu
from jax.sharding import Mesh, PartitionSpec as P

H = 24
HD = 64
D = 1536
FF = 4096
YD = 4096
CD = 1024
CAP = 128
CLIPS = 4

EPSILON = 1e-06
MASKED = -1e30
BF = jnp.bfloat16
F32 = jnp.float32
NN = (((1,), (0,)), ((), ()))
NT = (((1,), (1,)), ((), ()))
TN = (((0,), (0,)), ((), ()))
GROUP = 4
LINE = 4
BUCKET = ("z", "y", "c")
SMEM = pl.BlockSpec(memory_space=pltpu.SMEM)
VMEM = pl.BlockSpec(memory_space=pltpu.VMEM)
shape = jax.ShapeDtypeStruct


def cost(microseconds):
    return pl.CostEstimate(
        flops=0, transcendentals=0, bytes_accessed=int(microseconds * 3_000_000)
    )


def mm(a, b, dims):
    return lax.dot_general(a, b, dims, preferred_element_type=F32)


def clip_at(slices, slot):
    ends = [slices[0]]
    for i in range(1, CLIPS):
        ends.append(ends[-1] + slices[i])
    clip = jnp.int32(0)
    first, last = jnp.int32(0), ends[0]
    for i in range(CLIPS - 1):
        later = slot >= ends[i]
        clip = jnp.where(later, i + 1, clip)
        first = jnp.where(later, ends[i], first)
        last = jnp.where(later, ends[i + 1], last)
    return clip, first, last


def slot_of(bucket, k, j):
    return lax.rem(bucket // GROUP - k + LINE, LINE) * GROUP + jnp.bitwise_xor(
        lax.rem(bucket, GROUP), j
    )


def chunk_at(bucket, k, width):
    return pl.multiple_of(lax.rem(bucket // GROUP + k, LINE) * width, HD)


def norm_rope(raw, gain, cosine, sine):
    inverse = lax.rsqrt(jnp.mean(raw * raw, axis=0, keepdims=True) + EPSILON)
    normed = raw * inverse * gain
    half = raw.shape[0] // 2
    first, second = normed[:half], normed[half:]
    return jnp.concatenate(
        [first * cosine - second * sine, first * sine + second * cosine], axis=0
    )


def norm_rope_back(grad, raw, gain, cosine, sine):
    inverse = lax.rsqrt(jnp.mean(raw * raw, axis=0, keepdims=True) + EPSILON)
    unit = raw * inverse
    half = raw.shape[0] // 2
    first, second = grad[:half], grad[half:]
    turned = jnp.concatenate(
        [first * cosine + second * sine, second * cosine - first * sine], axis=0
    )
    gain_grad = jnp.sum(turned * unit, axis=1, keepdims=True)
    unit_grad = turned * gain
    raw_grad = inverse * (unit_grad - unit * jnp.mean(unit_grad * unit, axis=0, keepdims=True))
    return raw_grad, gain_grad


def row_inverse(values):
    return lax.rsqrt(jnp.mean(values * values, axis=-1, keepdims=True) + EPSILON)


def pre_kernel(ids, slices, tok_a, tok_b, mod_a, mod_b, gain_ref, w_ref, p_ref, hid_ref, mod_ref):
    @pl.when(pl.program_id(0) == 0)
    def _():
        s = ids[1]
        clip, _, _ = clip_at(slices, ids[0])
        row_a, row_b = mod_a[pl.ds(clip, 1), :], mod_b[pl.ds(clip, 1), :]
        low, high = jnp.where(s == 0, row_a, row_b), jnp.where(s == 0, row_b, row_a)
        mod_ref[...] = jnp.zeros_like(mod_ref)
        for i in range(3):
            mod_ref[i : i + 1, :] = low[:, i * D : (i + 1) * D]
            mod_ref[3 + i : 4 + i, :] = high[:, i * D : (i + 1) * D]
        shift, scale = mod_ref[0:1, :], mod_ref[1:2, :]
        count = tok_a.shape[0]
        for place, ref in ((s, tok_a), (1 - s, tok_b)):
            values = ref[...].astype(F32)
            hidden = values * row_inverse(values) * gain_ref[...] * (1.0 + scale) + shift
            hid_ref[pl.ds(pl.multiple_of(place * count, count), count), :] = hidden.astype(BF)

    p_ref[...] = mm(w_ref[...], hid_ref[...], NT).astype(BF)


def pre(ids, slices, tok_a, tok_b, mod_a, mod_b, gain, w_qkv):
    rows = 2 * tok_a.shape[0]
    tile = w_qkv.shape[0] // 3
    full = lambda v: pl.BlockSpec(v.shape, lambda i: (0,) * v.ndim)
    return pl.pallas_call(
        pre_kernel,
        grid=(w_qkv.shape[0] // tile,),
        in_specs=[SMEM, SMEM]
        + [full(v) for v in (tok_a, tok_b, mod_a, mod_b, gain)]
        + [pl.BlockSpec((tile, D), lambda i: (i, 0))],
        out_specs=[
            pl.BlockSpec((tile, rows), lambda i: (i, 0)),
            pl.BlockSpec((rows, D), lambda i: (0, 0)),
            pl.BlockSpec((8, D), lambda i: (0, 0)),
        ],
        out_shape=[shape((w_qkv.shape[0], rows), BF), shape((rows, D), BF), shape((8, D), F32)],
        name="pre",
        cost_estimate=cost(6),
    )(ids, slices, tok_a, tok_b, mod_a, mod_b, gain, w_qkv)


def route_kernel(ids, p_ref, r_ref, *outs):
    b, s = ids[0], ids[1]
    local = r_ref.shape[0]
    width = local // LINE
    for k in range(LINE):
        at = chunk_at(b, k, width)
        kv_ref, q_ref = outs[k], outs[LINE + k]

        @pl.when(s == 0)
        def _():
            q_ref[...] = p_ref[pl.ds(at, width), :]
            kv_ref[:width, :] = p_ref[pl.ds(2 * local + at, width), :]
            kv_ref[width:, :] = r_ref[pl.ds(at, width), :]

        @pl.when(s == 1)
        def _():
            q_ref[...] = r_ref[pl.ds(at, width), :]
            kv_ref[:width, :] = p_ref[pl.ds(at, width), :]
            kv_ref[width:, :] = p_ref[pl.ds(2 * local + at, width), :]


def route(ids, projected, received):
    local, rows = received.shape
    width = local // LINE
    outs = pl.pallas_call(
        route_kernel,
        in_specs=[SMEM, VMEM, VMEM],
        out_specs=[VMEM] * (2 * LINE),
        out_shape=[shape((2 * width, rows), BF)] * LINE + [shape((width, rows), BF)] * LINE,
        name="route",
        cost_estimate=cost(2.5),
    )(ids, projected, received)
    return outs[:LINE], outs[LINE:]


def caption_kernel(ids, w_ref, cap_ref, gains_ref, raw_ref, kv_ref):
    step = pl.program_id(0)
    width = w_ref.shape[1]

    @pl.when(step == 0)
    def _():
        raw_ref[...] = jnp.zeros_like(raw_ref)

    for j in range(2):
        raw_ref[j * width : (j + 1) * width, :] += mm(w_ref[j], cap_ref[...], NT)

    @pl.when(step == pl.num_programs(0) - 1)
    def _():
        base = ids[1] * LINE * width + ids[0] // GROUP * width
        for h in range(width // HD):
            at = slice(h * HD, h * HD + HD)
            raw = raw_ref[at, :]
            inverse = lax.rsqrt(jnp.mean(raw * raw, axis=0, keepdims=True) + EPSILON)
            gain = gains_ref[pl.ds(pl.multiple_of(base + h * HD, HD), HD), 2:3]
            keys = (raw * inverse * gain).astype(BF)
            for c in range(CLIPS):
                kv_ref[c, at, :] = keys[:, c * CAP : (c + 1) * CAP]
        for c in range(CLIPS):
            kv_ref[c, width:, :] = raw_ref[width:, c * CAP : (c + 1) * CAP].astype(BF)


def caption_keys(ids, w_caption, caption, gains):
    width = w_caption.shape[1] // LINE
    tile = 1024
    count = caption.shape[0]
    return pl.pallas_call(
        caption_kernel,
        grid_spec=pltpu.PrefetchScalarGridSpec(
            num_scalar_prefetch=1,
            grid=(YD // tile,),
            in_specs=[
                pl.BlockSpec((2, width, tile), lambda i, ids: (0, ids[0] // GROUP, i)),
                pl.BlockSpec((count, tile), lambda i, ids: (0, i)),
                pl.BlockSpec(gains.shape, lambda i, ids: (0, 0)),
            ],
            out_specs=[
                pl.BlockSpec((2 * width, count), lambda i, ids: (0, 0)),
                pl.BlockSpec((CLIPS, 2 * width, CAP), lambda i, ids: (0, 0, 0)),
            ],
        ),
        out_shape=[shape((2 * width, count), F32), shape((CLIPS, 2 * width, CAP), BF)],
        name="caption_keys",
        cost_estimate=cost(8),
    )(ids, w_caption, caption, gains)


def attend_kernel(ids, slices, lengths, gates, *refs):
    q_refs = refs[:LINE]
    kv_refs = refs[LINE : LINE + GROUP]
    cap_ref, gains_ref, cos_ref, sin_ref = refs[LINE + GROUP : LINE + GROUP + 4]
    outs = refs[LINE + GROUP + 4 :]
    comb_refs = outs[:LINE]
    own_ref, other_ref, stat_ref, qs_ref, ks_ref, vs_ref = outs[LINE:]
    b, s = ids[0], ids[1]
    width, rows = q_refs[0].shape
    heads = width // HD
    scale = HD**-0.5
    base = s * LINE * width + b // GROUP * width

    def gain_of(h, column):
        return gains_ref[pl.ds(pl.multiple_of(base + h * HD, HD), HD), column : column + 1]

    key_gains = [gain_of(h, 1) for h in range(heads)]
    query_gains = [gain_of(h, 0) for h in range(heads)]
    for j, kv_ref in enumerate(kv_refs):
        for k in range(LINE):
            slot = slot_of(b, k, j)
            _, start, _ = clip_at(slices, slot)
            cosine, sine = cos_ref[slot - start], sin_ref[slot - start]
            for h in range(heads):
                at = slice(h * HD, h * HD + HD)
                raw = kv_ref[k, at, :].astype(F32)
                ks_ref[slot, at, :] = norm_rope(raw, key_gains[h], cosine, sine).astype(BF)
            vs_ref[slot] = kv_ref[k, width:, :]

    for i in range(LINE):
        slot = slot_of(b, i, 0)
        clip, first, last = clip_at(slices, slot)
        cosine, sine = cos_ref[slot - first], sin_ref[slot - first]
        queries = []
        for h in range(heads):
            at = slice(h * HD, h * HD + HD)
            raw = q_refs[i][at, :].astype(F32)
            turned = norm_rope(raw, query_gains[h], cosine, sine).astype(BF)
            turned = (turned.astype(F32) * scale).astype(BF)
            qs_ref[i, at, :] = turned
            queries.append(turned)

        def step(n, state):
            totals, sums = state
            new_totals, new_sums = [], []
            for h in range(heads):
                at = slice(h * HD, h * HD + HD)
                weights = jnp.exp(mm(ks_ref[n, at, :], queries[h], TN))
                new_totals.append(totals[h] + jnp.sum(weights, axis=0, keepdims=True))
                new_sums.append(sums[h] + mm(vs_ref[n, at, :], weights.astype(BF), NN))
            return tuple(new_totals), tuple(new_sums)

        zero_total = tuple(jnp.zeros((1, rows), F32) for _ in range(heads))
        zero_sum = tuple(jnp.zeros((HD, rows), F32) for _ in range(heads))
        totals, sums = lax.fori_loop(first, last, step, (zero_total, zero_sum))
        usable = lax.broadcasted_iota(jnp.int32, (CAP, rows), 0) < lengths[clip]
        for h in range(heads):
            at = slice(h * HD, h * HD + HD)
            inverse = 1.0 / totals[h]
            own = sums[h] * inverse
            weights = jnp.where(usable, jnp.exp(mm(cap_ref[clip, at, :], queries[h], TN)), 0.0)
            cap_inverse = 1.0 / jnp.sum(weights, axis=0, keepdims=True)
            at_value = slice(width + h * HD, width + h * HD + HD)
            other = mm(cap_ref[clip, at_value, :], weights.astype(BF), NN) * cap_inverse
            own_ref[i, at, :] = own
            other_ref[i, at, :] = other
            gate = gates[(s * LINE + b // GROUP) * heads + h]
            comb_refs[i][at, :] = (own + gate * other).astype(BF)
            stat_ref[i, h : h + 1, :] = inverse
            stat_ref[i, 4 + h : 5 + h, :] = cap_inverse


def attend(ids, slices, lengths, gates, queries, kv_pieces, cap_kv, gains, cosine, sine):
    width, rows = queries[0].shape
    slots = LINE * GROUP
    outs = pl.pallas_call(
        attend_kernel,
        in_specs=[SMEM] * 4 + [VMEM] * (LINE + GROUP + 4),
        out_specs=[VMEM] * (LINE + 6),
        out_shape=[shape((width, rows), BF)] * LINE
        + [
            shape((LINE, width, rows), F32),
            shape((LINE, width, rows), F32),
            shape((LINE, 8, rows), F32),
            shape((LINE, width, rows), BF),
            shape((slots, width, rows), BF),
            shape((slots, width, rows), BF),
        ],
        name="attend",
        cost_estimate=cost(33),
    )(ids, slices, lengths, gates, *queries, *kv_pieces, cap_kv, gains, cosine, sine)
    return outs[:LINE], outs[LINE:]


def out_kernel(ids, *refs):
    own, other = refs[:LINE], refs[LINE : 2 * LINE]
    w_ref, att_ref, branch_ref = refs[2 * LINE :]
    b, s = ids[0], ids[1]
    width = own[0].shape[0]
    for k in range(LINE):
        at = chunk_at(b, k, width)
        att_ref[pl.ds(pl.multiple_of(s * LINE * width + at, HD), width), :] = own[k][...]
        att_ref[pl.ds(pl.multiple_of((1 - s) * LINE * width + at, HD), width), :] = other[k][...]
    branch_ref[...] = mm(w_ref[...], att_ref[...], NN).T.astype(BF)


def out_proj(ids, own, other, w_out):
    rows = own[0].shape[1]
    return pl.pallas_call(
        out_kernel,
        in_specs=[SMEM] + [VMEM] * (2 * LINE + 1),
        out_specs=[VMEM, VMEM],
        out_shape=[shape((D, rows), BF), shape((rows, w_out.shape[0]), BF)],
        name="out_proj",
        cost_estimate=cost(3.5),
    )(ids, *own, *other, w_out)


def cut_kernel(turned, ids, *refs):
    count = len(turned)
    ins = refs[:count]
    own_ref, c_ref, y_ref, scratch = refs[count:]
    place = lax.rem(ids[0], GROUP)
    columns = own_ref.shape[3]
    for n in range(count):
        if turned[n]:
            source = ins[n]
        else:
            scratch[...] = ins[n][...].astype(F32).T
            source = scratch
        for k in range(LINE):
            for j, (ref, i) in enumerate(((own_ref, 0), (c_ref, 0), (y_ref, 0), (y_ref, 1))):
                at = (k * GROUP + jnp.bitwise_xor(place, j)) * columns
                ref[i, n, k] = source[pl.ds(pl.multiple_of(at, 32), columns), :].astype(BF)


def cut(ids, values, turned):
    rows = values[0].shape[1 if turned[0] else 0]
    columns = D // (LINE * GROUP)
    count = len(values)
    return pl.pallas_call(
        functools.partial(cut_kernel, tuple(turned)),
        in_specs=[SMEM] + [VMEM] * count,
        out_specs=[VMEM] * 3,
        out_shape=[shape((n, count, LINE, columns, rows), BF) for n in (1, 1, 2)],
        scratch_shapes=[pltpu.VMEM((D, rows), F32)],
        name="cut",
        cost_estimate=cost(2.4),
    )(ids, *values)


def ffn_kernel(
    ids,
    tok_a,
    tok_b,
    br_a,
    br_b,
    out16_ref,
    mod_ref,
    gain_ref,
    kept_ref,
    came_ref,
    down_ref,
    inner_ref,
    gkept_ref,
    gcame_ref,
    in16_ref,
    mid_ref,
    near_ref,
    far_ref,
    mean_ref,
    near_out_ref,
    far_out_ref,
    acc_in,
    acc_out,
):
    step = pl.program_id(0)
    steps = pl.num_programs(0)
    s = ids[1]
    count = tok_a.shape[0]
    half = br_a.shape[1]
    gate, shift2, scale2 = [mod_ref[i : i + 1, :] for i in (2, 3, 4)]
    mlp_gain = gain_ref[...] * (1.0 + scale2)

    @pl.when(step == 0)
    def _():
        for place, tok in ((s, tok_a), (1 - s, tok_b)):
            at = pl.ds(pl.multiple_of(place * count, count), count)
            mid_ref[at, :] = tok[...].astype(F32)
        low = jnp.where(s == 0, br_a[...].astype(F32), br_b[...].astype(F32))
        high = jnp.where(s == 0, br_b[...].astype(F32), br_a[...].astype(F32))
        mid_ref[:, :half] += gate[:, :half] * low
        mid_ref[:, half:] += gate[:, half:] * high
        middle = mid_ref[...]
        in16_ref[...] = (middle * row_inverse(middle) * mlp_gain + shift2).astype(BF)
        acc_in[...] = jnp.zeros_like(acc_in)
        acc_out[...] = jnp.zeros_like(acc_out)

    w_kept, w_came, w_down = kept_ref[...], came_ref[...], down_ref[...]
    kept = mm(in16_ref[...], w_kept, NT)
    other = mm(in16_ref[...], w_came, NT)
    grad_inner = mm(out16_ref[...], w_down, NT)
    gate_half = jnp.where(s == 0, kept, other)
    up_half = jnp.where(s == 0, other, kept)
    sigmoid = jax.nn.sigmoid(gate_half)
    silu = gate_half * sigmoid
    inner = (silu * up_half).astype(BF)
    grad_gate = grad_inner * up_half * sigmoid * (1.0 + gate_half * (1.0 - sigmoid))
    grad_up = grad_inner * silu
    grad_kept = jnp.where(s == 0, grad_gate, grad_up).astype(BF)
    grad_came = jnp.where(s == 0, grad_up, grad_gate).astype(BF)
    inner_ref[...] = inner
    gkept_ref[...] = grad_kept
    gcame_ref[...] = grad_came
    acc_in[...] += mm(grad_kept, w_kept, NN) + mm(grad_came, w_came, NN)
    acc_out[...] += mm(inner, w_down, NN)

    @pl.when(step == steps - 1)
    def _():
        middle = mid_ref[...]
        part = jnp.sum(
            acc_in[...] * mlp_gain * (middle * row_inverse(middle)), axis=-1, keepdims=True
        )
        mean_ref[...] = jnp.broadcast_to(part, (part.shape[0], 128)).T[:8]
        near_ref[...] = acc_in[:, pl.ds(pl.multiple_of(s * half, half), half)]
        far_ref[...] = acc_in[:, pl.ds(pl.multiple_of((1 - s) * half, half), half)].astype(BF)
        near_out_ref[...] = acc_out[pl.ds(pl.multiple_of(s * count, count), count), :]
        far_out_ref[...] = acc_out[pl.ds(pl.multiple_of((1 - s) * count, count), count), :].astype(BF)


def ffn(ids, toks, branches, grad_mlp, mod, gain, w_gate_up, came, w_down):
    count = toks[0].shape[0]
    rows = 2 * count
    half = D // 2
    units = w_down.shape[0]
    tile = 512
    steps = units // tile
    full = lambda v: pl.BlockSpec(v.shape, lambda i, ids: (0,) * v.ndim)

    def fixed(r, c):
        return pl.BlockSpec((r, c), lambda i, ids: (0, 0))

    small = [*toks, *branches, grad_mlp, mod, gain]
    return pl.pallas_call(
        ffn_kernel,
        grid_spec=pltpu.PrefetchScalarGridSpec(
            num_scalar_prefetch=1,
            grid=(steps,),
            in_specs=[full(v) for v in small]
            + [
                pl.BlockSpec((tile, D), lambda i, ids: (ids[1] * steps + i, 0)),
                pl.BlockSpec((tile, D), lambda i, ids: ((1 - ids[1]) * steps + i, 0)),
                pl.BlockSpec((tile, D), lambda i, ids: (i, 0)),
            ],
            out_specs=[pl.BlockSpec((rows, tile), lambda i, ids: (0, i))] * 3
            + [
                fixed(rows, D),
                fixed(rows, D),
                fixed(rows, half),
                fixed(rows, half),
                fixed(8, rows),
                fixed(count, D),
                fixed(count, D),
            ],
            scratch_shapes=[pltpu.VMEM((rows, D), F32), pltpu.VMEM((rows, D), F32)],
        ),
        out_shape=[shape((rows, units), BF)] * 3
        + [
            shape((rows, D), BF),
            shape((rows, D), F32),
            shape((rows, half), F32),
            shape((rows, half), BF),
            shape((8, rows), F32),
            shape((count, D), F32),
            shape((count, D), BF),
        ],
        name="ffn",
        cost_estimate=cost(18),
    )(ids, *small, w_gate_up, came, w_down)


def mid_kernel(
    ids,
    near_ref,
    recv_ref,
    mean_a,
    mean_b,
    mid_ref,
    cot_a,
    cot_b,
    br_ref,
    mod_ref,
    gain_ref,
    w_ref,
    sums_ref,
    gbr_ref,
    near_mid_ref,
    far_mid_ref,
    *refs,
):
    near_refs, far_refs, scratch = refs[:LINE], refs[LINE : 2 * LINE], refs[2 * LINE]
    b, s = ids[0], ids[1]
    half = near_ref.shape[1]
    count = cot_a.shape[0]
    cols = pl.ds(pl.multiple_of(s * half, half), half)
    gate, scale2 = mod_ref[2:3, cols], mod_ref[4:5, cols]
    gain = gain_ref[:, cols]
    middle = mid_ref[...]
    inverse = row_inverse(middle)
    unit = mid_ref[:, cols] * inverse
    means = (mean_a[...] + mean_b[...]) * (1.0 / D)
    mean = jnp.concatenate([means] * 16, axis=0).T[:, 0:1]
    grad_in = near_ref[...] + recv_ref[...].astype(F32)
    cot_own, cot_far = cot_a[:, cols].astype(F32), cot_b[:, cols].astype(F32)
    cot = jnp.concatenate(
        [jnp.where(s == 0, cot_own, cot_far), jnp.where(s == 0, cot_far, cot_own)], axis=0
    )
    scaled = grad_in * (1.0 + scale2)
    grad_mid = cot + inverse * (scaled * gain - unit * mean)
    sums_ref[...] = jnp.zeros_like(sums_ref)
    sums_ref[0:1, :] = jnp.sum(grad_mid * br_ref[...].astype(F32), axis=0, keepdims=True)
    sums_ref[1:2, :] = jnp.sum(grad_in, axis=0, keepdims=True)
    sums_ref[2:3, :] = jnp.sum(grad_in * unit, axis=0, keepdims=True) * gain
    sums_ref[3:4, :] = jnp.sum(scaled * unit, axis=0, keepdims=True)
    grad_branch = (grad_mid * gate).astype(BF)
    gbr_ref[...] = grad_branch
    top, low = grad_mid[:count], grad_mid[count:]
    near_mid_ref[...] = jnp.where(s == 0, top, low)
    far_mid_ref[...] = jnp.where(s == 0, low, top).astype(BF)
    scratch[...] = mm(grad_branch, w_ref[...], NN).T
    width = near_refs[0].shape[0]
    for k in range(LINE):
        at = chunk_at(b, k, width)
        near_refs[k][...] = scratch[pl.ds(pl.multiple_of(s * half + at, HD), width), :]
        far_refs[k][...] = scratch[pl.ds(pl.multiple_of((1 - s) * half + at, HD), width), :].astype(BF)


def mid_back(ids, near, received, mean_a, mean_b, middle, cots, branch, mod, gain, w_out):
    rows, half = near.shape
    width = half // LINE
    count = cots[0].shape[0]
    outs = pl.pallas_call(
        mid_kernel,
        in_specs=[SMEM] + [VMEM] * 11,
        out_specs=[VMEM] * (4 + 2 * LINE),
        out_shape=[
            shape((8, half), F32),
            shape((rows, half), BF),
            shape((count, half), F32),
            shape((count, half), BF),
        ]
        + [shape((width, rows), F32)] * LINE
        + [shape((width, rows), BF)] * LINE,
        scratch_shapes=[pltpu.VMEM((D, rows), F32)],
        name="mid_back",
        cost_estimate=cost(5.5),
    )(ids, near, received, mean_a, mean_b, middle, *cots, branch, mod, gain, w_out)
    return outs[:4], outs[4 : 4 + LINE], outs[4 + LINE :]


def place_row(b, column):
    width = column.shape[0]
    row = jnp.broadcast_to(column, (width, 128)).T[0:1]
    z = b // GROUP
    return jnp.concatenate([jnp.where(z == k, row, 0.0) for k in range(LINE)], axis=1)


def output_kernel(ids, slices, near_ref, recv_ref, mid_ref, cot_ref, mod_ref, sums_ref, out_ref, early_ref):
    s = ids[1]
    count, half = near_ref.shape[0], sums_ref.shape[1]
    clip, _, _ = clip_at(slices, ids[0])
    branch = near_ref[...] + recv_ref[...].astype(F32)
    middle = mid_ref[pl.ds(pl.multiple_of(s * count, count), count), :]
    out_ref[...] = (middle + mod_ref[5:6, :] * branch).astype(BF)
    gate2 = jnp.sum(cot_ref[...].astype(F32) * branch, axis=0, keepdims=True)
    rows = [sums_ref[i : i + 1, :] for i in range(3)] + [gate2[:, :half], gate2[:, half:]]
    early_ref[...] = jnp.zeros_like(early_ref)
    for c in range(CLIPS):
        for i, row in enumerate(rows):
            early_ref[5 * c + i : 5 * c + i + 1, :] = jnp.where(clip == c, row, 0.0)
    early_ref[20:21, :] = sums_ref[3:4, :]


def output_sums(ids, slices, near, received, middle, cot, mod, sums):
    count = near.shape[0]
    return pl.pallas_call(
        output_kernel,
        in_specs=[SMEM, SMEM] + [VMEM] * 6,
        out_specs=[VMEM, VMEM],
        out_shape=[shape((count, D), BF), shape((24, D // 2), F32)],
        name="output_sums",
        cost_estimate=cost(3),
    )(ids, slices, near, received, middle, cot, mod, sums)


def attend_back_kernel(ids, slices, lengths, gates, *refs):
    q_refs, g_refs = refs[:LINE], refs[LINE : 2 * LINE]
    (own_ref, other_ref, stat_ref, qs_ref, ks_ref, vs_ref, cap_ref, gains_ref, cos_ref, sin_ref) = refs[
        2 * LINE : 2 * LINE + 10
    ]
    outs = refs[2 * LINE + 10 :]
    gq_refs = outs[:LINE]
    qgain_ref, keep_ref, send_ref, dgate_ref = outs[LINE : LINE + 4]
    dkv_refs = outs[LINE + 4 : LINE + 4 + GROUP]
    acc_ref, dcap_ref = outs[LINE + 4 + GROUP :]
    b, s = ids[0], ids[1]
    width, rows = q_refs[0].shape
    heads = width // HD
    scale = HD**-0.5
    base = s * LINE * width + b // GROUP * width
    acc_ref[...] = jnp.zeros_like(acc_ref)
    dcap_ref[...] = jnp.zeros_like(dcap_ref)
    dgate_ref[...] = jnp.zeros_like(dgate_ref)
    qgain_ref[...] = jnp.zeros_like(qgain_ref)

    for i in range(LINE):
        slot = slot_of(b, i, 0)
        clip, first, last = clip_at(slices, slot)
        queries, grads, deltas, inverses = [], [], [], []
        for h in range(heads):
            at = slice(h * HD, h * HD + HD)
            grad = g_refs[i][at, :]
            queries.append(qs_ref[i, at, :])
            grads.append(grad)
            deltas.append(jnp.sum(grad.astype(F32) * own_ref[i, at, :], axis=0, keepdims=True))
            inverses.append(stat_ref[i, h : h + 1, :])

        def step(n, state):
            out = []
            for h in range(heads):
                at = slice(h * HD, h * HD + HD)
                at_value = slice(width + h * HD, width + h * HD + HD)
                keys, values = ks_ref[n, at, :], vs_ref[n, at, :]
                prob = jnp.exp(mm(keys, queries[h], TN)) * inverses[h]
                grad_prob = mm(values, grads[h], TN)
                grad_score = (prob * (grad_prob - deltas[h])).astype(BF)
                acc_ref[n, at_value, :] += mm(grads[h], prob.astype(BF), NT)
                acc_ref[n, at, :] += mm(queries[h], grad_score, NT)
                out.append(state[h] + mm(keys, grad_score, NN))
            return tuple(out)

        query_grads = lax.fori_loop(
            first, last, step, tuple(jnp.zeros((HD, rows), F32) for _ in range(heads))
        )
        usable = lax.broadcasted_iota(jnp.int32, (CAP, rows), 0) < lengths[clip]
        cosine, sine = cos_ref[slot - first], sin_ref[slot - first]
        for h in range(heads):
            at = slice(h * HD, h * HD + HD)
            at_value = slice(width + h * HD, width + h * HD + HD)
            gate = gates[(s * LINE + b // GROUP) * heads + h]
            cap_keys, cap_values = cap_ref[clip, at, :], cap_ref[clip, at_value, :]
            grad = grads[h].astype(F32)
            grad_other = (grad * gate).astype(BF)
            prob = (
                jnp.where(usable, jnp.exp(mm(cap_keys, queries[h], TN)), 0.0)
                * stat_ref[i, 4 + h : 5 + h, :]
            )
            grad_prob = mm(cap_values, grad_other, TN)
            inner = jnp.sum(prob * grad_prob, axis=0, keepdims=True)
            grad_score = (prob * (grad_prob - inner)).astype(BF)
            query_grad = (query_grads[h] + mm(cap_keys, grad_score, NN)) * scale
            dcap_ref[clip, at, :] += mm(queries[h], grad_score, NT)
            dcap_ref[clip, at_value, :] += mm(grad_other, prob.astype(BF), NT)
            part = jnp.sum(grad * other_ref[i, at, :], axis=0, keepdims=True)
            dgate_ref[h : h + 1, :] += part * (1.0 - gate * gate)
            gain = gains_ref[pl.ds(pl.multiple_of(base + h * HD, HD), HD), 0:1]
            raw_grad, gain_grad = norm_rope_back(
                query_grad.astype(BF).astype(F32), q_refs[i][at, :].astype(F32), gain, cosine, sine
            )
            gq_refs[i][at, :] = raw_grad.astype(BF)
            qgain_ref[at, :] += gain_grad

    for j, dkv_ref in enumerate(dkv_refs):
        for k in range(LINE):
            dkv_ref[k] = acc_ref[slot_of(b, k, j)].astype(BF)
    core = lax.rem(b, 2)
    for i in range(2):
        keep_ref[i] = dcap_ref[2 * i + core]
        send_ref[i] = dcap_ref[2 * i + 1 - core]


def attend_back(ids, slices, lengths, gates, queries, grads, saved, cap_kv, gains, cosine, sine):
    width, rows = queries[0].shape
    outs = pl.pallas_call(
        attend_back_kernel,
        in_specs=[SMEM] * 4 + [VMEM] * (2 * LINE + 10),
        out_specs=[VMEM] * (LINE + 4 + GROUP),
        out_shape=[shape((width, rows), BF)] * LINE
        + [
            shape((width, 1), F32),
            shape((2, 2 * width, CAP), F32),
            shape((2, 2 * width, CAP), F32),
            shape((8, rows), F32),
        ]
        + [shape((LINE, 2 * width, rows), BF)] * GROUP,
        scratch_shapes=[
            pltpu.VMEM((LINE * GROUP, 2 * width, rows), F32),
            pltpu.VMEM((CLIPS, 2 * width, CAP), F32),
        ],
        name="attend_back",
        cost_estimate=cost(40),
    )(ids, slices, lengths, gates, *queries, *grads, *saved, cap_kv, gains, cosine, sine)
    return outs[:LINE], outs[LINE : LINE + 4], outs[LINE + 4 :]


def keys_back_kernel(ids, slices, a_ref, r_ref, kv_ref, gains_ref, cos_ref, sin_ref, *outs):
    out_refs, gain_ref = outs[:LINE], outs[LINE]
    b, s = ids[0], ids[1]
    width = gain_ref.shape[0]
    base = s * LINE * width + b // GROUP * width
    gain_ref[...] = jnp.zeros_like(gain_ref)
    for i in range(LINE):
        slot = slot_of(b, i, 0)
        _, first, _ = clip_at(slices, slot)
        cosine, sine = cos_ref[slot - first], sin_ref[slot - first]
        total = (a_ref[i].astype(F32) + r_ref[i].astype(F32)).astype(BF)
        for h in range(width // HD):
            at = slice(h * HD, h * HD + HD)
            gain = gains_ref[pl.ds(pl.multiple_of(base + h * HD, HD), HD), 1:2]
            raw_grad, gain_grad = norm_rope_back(
                total[at, :].astype(F32), kv_ref[i, at, :].astype(F32), gain, cosine, sine
            )
            out_refs[i][at, :] = raw_grad.astype(BF)
            gain_ref[at, :] += gain_grad
        out_refs[i][width:, :] = total[width:, :]


def keys_back(ids, slices, part, received, kv, gains, cosine, sine):
    _, both, rows = kv.shape
    outs = pl.pallas_call(
        keys_back_kernel,
        in_specs=[SMEM, SMEM] + [VMEM] * 6,
        out_specs=[VMEM] * (LINE + 1),
        out_shape=[shape((both, rows), BF)] * LINE + [shape((both // 2, 1), F32)],
        name="keys_back",
        cost_estimate=cost(3.7),
    )(ids, slices, part, received, kv, gains, cosine, sine)
    return outs[:LINE], outs[LINE]


def pack_kernel(ids, *refs):
    q_refs, kv_refs = refs[:LINE], refs[LINE : 2 * LINE]
    own_ref, send_ref = refs[2 * LINE :]
    b, s = ids[0], ids[1]
    width = q_refs[0].shape[0]
    local = LINE * width
    for k in range(LINE):
        at = chunk_at(b, k, width)

        @pl.when(s == 0)
        def _():
            own_ref[pl.ds(at, width), :] = q_refs[k][...]
            own_ref[pl.ds(local + at, width), :] = kv_refs[k][:width, :]
            send_ref[pl.ds(at, width), :] = kv_refs[k][width:, :]

        @pl.when(s == 1)
        def _():
            own_ref[pl.ds(at, width), :] = kv_refs[k][:width, :]
            own_ref[pl.ds(local + at, width), :] = kv_refs[k][width:, :]
            send_ref[pl.ds(at, width), :] = q_refs[k][...]


def pack(ids, grads_q, grads_kv):
    width, rows = grads_q[0].shape
    return pl.pallas_call(
        pack_kernel,
        in_specs=[SMEM] + [VMEM] * (2 * LINE),
        out_specs=[VMEM, VMEM],
        out_shape=[shape((2 * LINE * width, rows), BF), shape((LINE * width, rows), BF)],
        name="pack",
        cost_estimate=cost(2.5),
    )(ids, *grads_q, *grads_kv)


def qkv_back_kernel(ids, own_ref, recv_ref, w_ref, near_ref, far_ref, acc_ref):
    step = pl.program_id(0)
    third = pl.num_programs(0) // 3
    count = near_ref.shape[0]
    s = ids[1]

    @pl.when(step == 0)
    def _():
        acc_ref[...] = jnp.zeros_like(acc_ref)

    middle = jnp.logical_and(step >= third, step < 2 * third)
    grads = jnp.where(middle, recv_ref[...], own_ref[...])
    acc_ref[...] += mm(grads, w_ref[...], TN)

    @pl.when(step == pl.num_programs(0) - 1)
    def _():
        near_ref[...] = acc_ref[pl.ds(pl.multiple_of(s * count, count), count), :]
        far_ref[...] = acc_ref[pl.ds(pl.multiple_of((1 - s) * count, count), count), :].astype(BF)


def qkv_back(ids, own, received, w_qkv):
    local, rows = received.shape
    count = rows // 2
    tile = local
    third = local // tile

    def own_at(i, ids):
        return (jnp.where(i < third, i, jnp.clip(i - third, third - 1, 2 * third - 1)), 0)

    return pl.pallas_call(
        qkv_back_kernel,
        grid_spec=pltpu.PrefetchScalarGridSpec(
            num_scalar_prefetch=1,
            grid=(3 * third,),
            in_specs=[
                pl.BlockSpec((tile, rows), own_at),
                pl.BlockSpec((tile, rows), lambda i, ids: (jnp.clip(i - third, 0, third - 1), 0)),
                pl.BlockSpec((tile, D), lambda i, ids: (i, 0)),
            ],
            out_specs=[pl.BlockSpec((count, D), lambda i, ids: (0, 0))] * 2,
            scratch_shapes=[pltpu.VMEM((rows, D), F32)],
        ),
        out_shape=[shape((count, D), F32), shape((count, D), BF)],
        name="qkv_back",
        cost_estimate=cost(6),
    )(ids, own, received, w_qkv)


def tokens_kernel(
    ids, slices, tok_ref, near_ref, recv_ref, mid_near, mid_far, mod_ref, gain_ref, *refs
):
    qgain_ref, kgain_ref, cgain_ref, dgate_ref, early_ref, out_ref, late_ref = refs
    b, s = ids[0], ids[1]
    half = mid_near.shape[1]
    clip, _, _ = clip_at(slices, b)
    values = tok_ref[...].astype(F32)
    inverse = row_inverse(values)
    unit = values * inverse
    scale = 1.0 + mod_ref[1:2, :]
    gain = gain_ref[...]
    grad = near_ref[...] + recv_ref[...].astype(F32)
    scaled = grad * scale
    unit_grad = scaled * gain
    mean = jnp.mean(unit_grad * unit, axis=-1, keepdims=True)
    mid_own, mid_other = mid_near[...], mid_far[...].astype(F32)
    middle = jnp.concatenate(
        [jnp.where(s == 0, mid_own, mid_other), jnp.where(s == 0, mid_other, mid_own)], axis=1
    )
    out_ref[...] = inverse * (unit_grad - unit * mean) + middle
    shift_row = jnp.sum(grad, axis=0, keepdims=True)
    with_unit = grad * unit
    scale_row = jnp.sum(with_unit, axis=0, keepdims=True) * gain
    norm_row = jnp.sum(scaled * unit, axis=0, keepdims=True)
    rows = [shift_row[:, :half], shift_row[:, half:], scale_row[:, :half], scale_row[:, half:]]
    late_ref[...] = jnp.zeros_like(late_ref)
    for c in range(CLIPS):
        for i, row in enumerate(rows):
            late_ref[4 * c + i : 4 * c + i + 1, :] = jnp.where(clip == c, row, 0.0)
    late_ref[16:17, :] = norm_row[:, :half]
    late_ref[17:18, :] = norm_row[:, half:]
    for i, ref in enumerate((qgain_ref, kgain_ref, cgain_ref)):
        late_ref[18 + i : 19 + i, :] = place_row(b, ref[...])
    heads = qgain_ref.shape[0] // HD
    lane = lax.broadcasted_iota(jnp.int32, (1, half), 1)
    gate_row = jnp.zeros((1, half), F32)
    for h in range(heads):
        value = jnp.sum(dgate_ref[h : h + 1, :], axis=1, keepdims=True)
        gate_row = gate_row + jnp.where(lane == b // GROUP * heads + h, value, 0.0)
    late_ref[21:22, :] = gate_row
    late_ref[24:, :] = early_ref[...]


def tokens_back(ids, slices, tok, near, received, mid_near, mid_far, mod, gain, parts):
    return pl.pallas_call(
        tokens_kernel,
        in_specs=[SMEM, SMEM] + [VMEM] * 12,
        out_specs=[VMEM, VMEM],
        out_shape=[shape(tok.shape, F32), shape((48, D // 2), F32)],
        name="tokens_back",
        cost_estimate=cost(3.5),
    )(ids, slices, tok, near, received, mid_near, mid_far, mod, gain, *parts)


def finish_kernel(ids, late_a, late_b, mod_ref, gains_ref):
    s = ids[1]
    early_a, early_b = late_a.at[pl.ds(24, 24)], late_b.at[pl.ds(24, 24)]

    def joined(a, b, i):
        own, other = a[i : i + 1, :], b[i : i + 1, :]
        return jnp.concatenate(
            [jnp.where(s == 0, own, other), jnp.where(s == 0, other, own)], axis=1
        )

    def added(a, b, i):
        both = a[i : i + 2, :] + b[i : i + 2, :]
        return jnp.concatenate([both[0:1], both[1:2]], axis=1)

    for c in range(CLIPS):
        low = [added(late_a, late_b, 4 * c), added(late_a, late_b, 4 * c + 2), joined(early_a, early_b, 5 * c)]
        high = [
            joined(early_a, early_b, 5 * c + 1),
            joined(early_a, early_b, 5 * c + 2),
            added(early_a, early_b, 5 * c + 3),
        ]
        for i in range(3):
            mod_ref[c : c + 1, i * D : (i + 1) * D] = jnp.where(s == 0, low[i], high[i])
    gains_ref[...] = jnp.zeros_like(gains_ref)
    gains_ref[0:1, :] = added(late_a, late_b, 16)
    for i in range(3):
        gains_ref[1 + i : 2 + i, :] = joined(late_a, late_b, 18 + i)
    gains_ref[4:5, :] = joined(early_a, early_b, 20)
    gains_ref[5:6, :] = joined(late_a, late_b, 21)


def finish(ids, late_a, late_b):
    return pl.pallas_call(
        finish_kernel,
        in_specs=[SMEM] + [VMEM] * 2,
        out_specs=[VMEM, VMEM],
        out_shape=[shape((CLIPS, 3 * D), F32), shape((8, D), F32)],
        name="finish",
        cost_estimate=cost(1.7),
    )(ids, late_a, late_b)


def caption_back_kernel(ids, sum_ref, raw_ref, gains_ref, out_ref, gain_ref):
    b, s = ids[0], ids[1]
    width = gain_ref.shape[0]
    base = s * LINE * width + b // GROUP * width
    cols = pl.ds(pl.multiple_of(lax.rem(b, GROUP) * CAP, CAP), CAP)
    for h in range(width // HD):
        at = slice(h * HD, h * HD + HD)
        gain = gains_ref[pl.ds(pl.multiple_of(base + h * HD, HD), HD), 2:3]
        raw = raw_ref[at, cols]
        inverse = lax.rsqrt(jnp.mean(raw * raw, axis=0, keepdims=True) + EPSILON)
        unit = raw * inverse
        grad = sum_ref[at, :]
        gain_ref[at, :] = jnp.sum(grad * unit, axis=1, keepdims=True)
        unit_grad = grad * gain
        out_ref[at, :] = (
            inverse * (unit_grad - unit * jnp.mean(unit_grad * unit, axis=0, keepdims=True))
        ).astype(BF)
    out_ref[width:, :] = sum_ref[width:, :].astype(BF)


def caption_back(ids, total, raw, gains):
    return pl.pallas_call(
        caption_back_kernel,
        in_specs=[SMEM] + [VMEM] * 3,
        out_specs=[VMEM, VMEM],
        out_shape=[shape(total.shape, BF), shape((total.shape[0] // 2, 1), F32)],
        name="caption_back",
        cost_estimate=cost(2.3),
    )(ids, total, raw, gains)


def caption_weight_kernel(ids, *refs):
    raw_refs, cap_ref, out_refs = refs[:GROUP], refs[GROUP], refs[GROUP + 1 :]
    b = ids[0]
    each = out_refs[0].shape[1]
    place = lax.rem(b, GROUP)
    for k in range(LINE):
        at = pl.multiple_of((lax.rem(b // GROUP - k + LINE, LINE) * GROUP + place) * each, each)
        total = None
        for j in range(GROUP):
            rows = pl.ds(pl.multiple_of(jnp.bitwise_xor(place, j) * CAP, CAP), CAP)
            part = mm(raw_refs[j][...], cap_ref[rows, pl.ds(at, each)], NN)
            total = part if total is None else total + part
        out_refs[k][...] = total.astype(BF)


def caption_weights(ids, raws, caption):
    rows = raws[0].shape[0]
    return pl.pallas_call(
        caption_weight_kernel,
        in_specs=[SMEM] + [VMEM] * (GROUP + 1),
        out_specs=[VMEM] * LINE,
        out_shape=[shape((rows, YD // (LINE * GROUP)), BF)] * LINE,
        name="caption_weights",
        cost_estimate=cost(4),
    )(ids, *raws, caption)


def caption_join_kernel(ids, *refs):
    parts, out_ref = refs[:LINE], refs[LINE]
    width = parts[0].shape[0] // 2
    for k in range(LINE):
        at = chunk_at(ids[0], k, width)
        for j in range(2):
            out_ref[j, pl.ds(at, width), :] = parts[k][j * width : (j + 1) * width, :].astype(F32)


def caption_join(ids, parts):
    both, each = parts[0].shape
    return pl.pallas_call(
        caption_join_kernel,
        in_specs=[SMEM] + [VMEM] * LINE,
        out_specs=VMEM,
        out_shape=shape((2, both // 2 * LINE, each), F32),
        name="caption_join",
        cost_estimate=cost(2),
    )(ids, *parts)


def weight_kernel(count, dims, *refs):
    left, right, out_ref = refs[:count], refs[count : 2 * count], refs[-1]
    total = None
    for a_ref, g_ref in zip(left, right):
        part = mm(a_ref[0, 0].reshape(-1, a_ref.shape[-1]), g_ref[...], dims)
        total = part if total is None else total + part
    out_ref[...] = total.reshape(out_ref.shape).astype(BF)


def weight_grads(left, right, by_rows, tile, kind, total, place, into=None):
    _, _, chunks, columns, tokens = left[0][0].shape
    rows = right[0].shape[0 if by_rows else 1]
    left_specs = [
        pl.BlockSpec((1, 1, chunks, columns, tokens), lambda i, n=n: (n, kind, 0, 0, 0))
        for _, n in left
    ]
    if by_rows:
        right_spec = pl.BlockSpec((tile, tokens), lambda i: (i, 0))
    else:
        right_spec = pl.BlockSpec((tokens, tile), lambda i: (0, i))
    args = [a for a, _ in left] + list(right)
    specs = left_specs + [right_spec] * len(right)
    aliases = {}
    if into is not None:
        aliases = {len(args): 0}
        args.append(into)
        specs.append(pl.BlockSpec(memory_space=pl.ANY))
    return pl.pallas_call(
        functools.partial(weight_kernel, len(left), NT if by_rows else NN),
        grid=(rows // tile,),
        in_specs=specs,
        out_specs=pl.BlockSpec((chunks, columns, tile), lambda i: (0, 0, place(i))),
        out_shape=shape((chunks, columns, total), BF),
        input_output_aliases=aliases,
        name="weight_grads",
        cost_estimate=cost(5),
    )(*args)


def fast_body(
    tokens,
    cotangent,
    clip_slices,
    caption_lengths,
    caption,
    cond,
    ada_w,
    norm_gain,
    w_qkv,
    q_gain,
    k_gain,
    w_caption,
    ky_gain,
    cross_gate,
    w_out,
    ffn_gain,
    w_gate_up,
    w_down,
):
    bucket_count = LINE * GROUP
    seq_count = lax.axis_size("seq")
    local_width = D // seq_count
    units = FF // seq_count
    b = lax.axis_index(BUCKET)
    s = lax.axis_index("seq")
    z, g, c, y = b // GROUP, b % GROUP, b % 2, (b // 2) % 2
    ids = jnp.stack([b, s]).astype(jnp.int32)

    def xswap(v):
        return lax.ppermute(v, "seq", [(0, 1), (1, 0)])

    def hop(v, to):
        return lax.ppermute(v, BUCKET, [(i, to(i)) for i in range(bucket_count)])

    def cswap(v):
        return hop(v, lambda i: i ^ 1)

    def yswap(v):
        return hop(v, lambda i: i ^ 2)

    def zshift(v, k):
        return hop(v, lambda i: (i + GROUP * k) % bucket_count)

    def after(v, *others):
        return lax.optimization_barrier((v, *others))[0]

    def pick(v, index):
        return lax.dynamic_index_in_dim(v, index, 0, False)

    def spread(parts):
        return [parts[0]] + [zshift(parts[k], k) for k in range(1, LINE)]

    def unspread(parts):
        return [parts[0]] + [zshift(parts[k], LINE - k) for k in range(1, LINE)]

    half = HD // 2
    rows = tokens.shape[0] * seq_count
    frequency = jnp.exp(jnp.arange(half, dtype=F32) * (-2.0 * math.log(10000.0) / (2 * half)))
    positions = jnp.arange(bucket_count * rows, dtype=F32).reshape(bucket_count, 1, rows)
    angles = positions * frequency[None, :, None]
    cosine, sine = jnp.cos(angles), jnp.sin(angles)
    gains = jnp.stack([q_gain, k_gain, ky_gain], axis=1)
    gates = jnp.tanh(cross_gate)
    norm_row, ffn_row = norm_gain[None], ffn_gain[None]

    tok_far = xswap(tokens)
    activation = jax.nn.silu(cond).astype(BF)
    mod_near = mm(activation, ada_w, NT)
    mod_far = xswap(mod_near)
    each = units // 2
    sent = lax.dynamic_slice_in_dim(w_gate_up, (1 - s) * units + c * each, each, 0)
    tok_far, sent = lax.optimization_barrier((tok_far, sent))
    projected, hidden, mod = pre(
        ids, clip_slices, tokens, tok_far, mod_near, mod_far, norm_row, w_qkv
    )
    local = lax.slice_in_dim(projected, local_width, 2 * local_width, axis=0)
    swapped = xswap(local)
    hid_own, hid_c, hid_y = cut(ids, [hidden], [False])
    came = lax.all_gather(after(sent, swapped), ("seq", "c"), axis=0, tiled=True)
    swapped = after(swapped, hid_own)
    kv_parts, q_parts = route(ids, projected, swapped)
    kv_here = spread(kv_parts)
    q_here = spread(q_parts)
    caption_rows = caption.reshape(CLIPS * CAP, YD)
    cap_raw, cap_kv = caption_keys(ids, w_caption, after(caption_rows, kv_parts[0]), gains)
    kv_here[1] = after(kv_here[1], cap_kv, cosine, sine)
    cot_far = xswap(after(cotangent, cap_kv))
    kv_own = jnp.stack(kv_here)
    kv_y = yswap(kv_own)
    kv_c = cswap(kv_own)
    kv_cy = cswap(kv_y)
    kv_pieces = [kv_own, kv_c, kv_y, kv_cy]
    grad_mlp = (
        jnp.where(
            s == 0,
            jnp.concatenate([cotangent, cot_far], 0),
            jnp.concatenate([cot_far, cotangent], 0),
        ).astype(F32)
        * mod[5:6]
    ).astype(BF)
    q_here[0] = after(q_here[0], grad_mlp)
    combined, saved = attend(
        ids, clip_slices, caption_lengths, gates, q_here, kv_pieces, cap_kv, gains, cosine, sine
    )
    heads_own = unspread(combined)
    heads_far = [xswap(v) for v in heads_own]
    attention, branch = out_proj(ids, heads_own, heads_far, w_out)
    branch_far = xswap(branch)
    att_own, att_c, att_y = cut(ids, [attention, grad_mlp], [True, False])
    branch_far = after(branch_far, att_own)
    (
        inner,
        grad_kept,
        grad_came,
        mlp_in,
        middle,
        near,
        far,
        mean_near,
        near_out,
        far_out,
    ) = ffn(ids, [tokens, tok_far], [branch, branch_far], grad_mlp, mod, ffn_row, w_gate_up, came, w_down)
    received = xswap(far)
    mean_far = xswap(mean_near)
    ffn_own, ffn_c, ffn_y = cut(ids, [mlp_in], [False])
    received = after(received, ffn_own)

    def left_of(own, c_part, y_part):
        came_y = yswap(y_part)
        return [(own, 0), (cswap(c_part), 0), (came_y, 0), (cswap(came_y), 1)]

    def right_of(v):
        far_v = yswap(v)
        return [v, cswap(v), far_v, cswap(far_v)]

    def line_sum(parts):
        right_in = left_in = None
        for t in range(1, LINE):
            to_right = pick(parts, jnp.clip(LINE - t + z, 0, LINE - 1))
            to_left = pick(parts, jnp.clip(t - LINE + z, 0, LINE - 1))
            if t > 1:
                to_right = (to_right.astype(F32) + right_in.astype(F32)).astype(BF)
                to_left = (to_left.astype(F32) + left_in.astype(F32)).astype(BF)
            ends = range(GROUP * t)
            right_in = lax.ppermute(to_right, BUCKET, [(i, i + GROUP) for i in ends])
            last = bucket_count - 1
            left_in = lax.ppermute(to_left, BUCKET, [(last - i, last - i - GROUP) for i in ends])
        return pick(parts, z).astype(F32) + right_in.astype(F32) + left_in.astype(F32)

    def scatter(parts):
        return lax.psum_scatter(parts, "z", scatter_dimension=0, tiled=False)

    att_left = left_of(att_own, att_c, att_y)
    inner_all = right_of(inner)
    tile = 512
    per = units // tile
    (sums, grad_branch, mid_near, mid_far), near_heads, far_heads = mid_back(
        ids, near, received, mean_near, mean_far, middle, [cotangent, cot_far], branch, mod, ffn_row, w_out
    )
    grad_heads = [
        (near_heads[k] + xswap(far_heads[k]).astype(F32)).astype(BF) for k in range(LINE)
    ]
    grad_here = spread(grad_heads)
    parts_inner = weight_grads(att_left, inner_all, False, tile, 1, units, lambda i: i)
    sum_inner = scatter(parts_inner)
    ffn_left = left_of(*[after(v, inner_all[2]) for v in (ffn_own, ffn_c, ffn_y)])
    kept_all = right_of(after(grad_kept, inner_all[2]))
    out_recv = xswap(after(far_out, grad_heads[0]))
    output, early = output_sums(ids, clip_slices, near_out, out_recv, middle, cotangent, mod, sums)
    grad_here[0] = after(grad_here[0], parts_inner)
    grads_q, (q_gain_part, cap_keep, cap_send, gate_part), grads_kv = attend_back(
        ids, clip_slices, caption_lengths, gates, q_here, grad_here, saved, cap_kv, gains, cosine, sine
    )
    came_all = right_of(after(grad_came, kept_all[2]))
    here = (grads_kv[0].astype(F32) + cswap(grads_kv[1]).astype(F32)).astype(BF)
    away = (grads_kv[2].astype(F32) + cswap(grads_kv[3]).astype(F32)).astype(BF)
    away_here = yswap(away)
    back_q = unspread(grads_q)
    pair = cap_keep + cswap(cap_send)
    mid_came = xswap(after(mid_far, away))

    kept_all[0] = after(kept_all[0], away)
    parts_a = weight_grads(ffn_left, kept_all, False, tile, 0, 2 * units, lambda i: i)
    parts_a = weight_grads(ffn_left, came_all, False, tile, 0, 2 * units, lambda i: i + per, parts_a)
    sum_a = scatter(parts_a)
    away_here = after(away_here, parts_a)
    back_kv, k_gain_part = keys_back(ids, clip_slices, here, away_here, kv_own, gains, cosine, sine)
    back_kv = unspread(back_kv)
    branch_all = right_of(after(grad_branch, away_here))
    hid_left = left_of(hid_own, hid_c, hid_y)

    cap_total = pick(pair, y) + yswap(after(pick(pair, 1 - y), away_here))
    raw_cap, cap_gain_part = caption_back(ids, cap_total, cap_raw, gains)
    raw_y = yswap(raw_cap)
    cap_parts = caption_weights(ids, [raw_cap, cswap(raw_cap), raw_y, cswap(raw_y)], caption_rows)
    parts_out = weight_grads(att_left, branch_all, False, 384, 0, local_width, lambda i: i)
    sum_out = scatter(parts_out)
    back_kv[1] = after(back_kv[1], parts_out, cap_parts[0])

    packed, send = pack(ids, back_q, back_kv)
    packed_recv = xswap(send)
    packed_all = right_of(packed)
    recv_all = right_of(packed_recv)
    cap_parts = unspread([after(v, packed) for v in cap_parts])
    tok_near, tok_send = qkv_back(ids, packed, packed_recv, w_qkv)
    tok_recv = xswap(tok_send)
    token_grad, late = tokens_back(
        ids,
        clip_slices,
        tokens,
        tok_near,
        tok_recv,
        mid_near,
        mid_came,
        mod,
        norm_row,
        [q_gain_part, k_gain_part, cap_gain_part, gate_part, early],
    )
    tile = 384
    parts_c = weight_grads(
        hid_left, packed_all, True, tile, 0, 3 * local_width, lambda i: jnp.where(i < 2, i, i + 2)
    )
    parts_c = weight_grads(
        hid_left, recv_all, True, tile, 0, 3 * local_width, lambda i: i + 2, parts_c
    )
    sum_c = line_sum(parts_c)
    caption_w_grad = caption_join(ids, cap_parts)
    def bucket_sum(v):
        v = v + cswap(v)
        v = v + yswap(v)
        v = v + hop(v, lambda i: i ^ GROUP)
        return v + hop(v, lambda i: i ^ (2 * GROUP))

    late_sum = bucket_sum(late)
    late_far = xswap(late_sum)
    mod_grad, gain_rows = finish(ids, late_sum, late_far)
    mod_mine = mod_grad.astype(BF)
    cols_local = CD // bucket_count
    act_cols = lax.dynamic_slice_in_dim(activation, b * cols_local, cols_local, 1)
    ada_grad = mm(mod_mine, act_cols, TN)
    cond_part = mm(mod_mine, ada_w, NN)
    cond_sigmoid = jax.nn.sigmoid(cond)
    cond_grad = (
        (cond_part + xswap(cond_part)) * cond_sigmoid * (1.0 + cond * (1.0 - cond_sigmoid))
    )
    heads_each = H // seq_count
    cross_out = jnp.concatenate(
        [gain_rows[5, :heads_each], gain_rows[5, local_width : local_width + heads_each]]
    )

    down_out = sum_inner.astype(F32).T
    kept_out = sum_a[:, :units].astype(F32)
    came_out = xswap(sum_a[:, units:]).astype(F32)
    gate_up_out = jnp.where(
        s == 0,
        jnp.concatenate([kept_out, came_out], 1),
        jnp.concatenate([came_out, kept_out], 1),
    ).T
    return (
        output,
        token_grad,
        cond_grad,
        ada_grad,
        gain_rows[0],
        sum_c.T,
        gain_rows[1],
        gain_rows[2],
        caption_w_grad,
        gain_rows[3],
        cross_out,
        sum_out.astype(F32).T,
        gain_rows[4],
        gate_up_out,
        down_out,
    )


def project(activations, weight):
    return lax.dot_general(
        activations, weight, (((1,), (1,)), ((), ())), preferred_element_type=jnp.float32
    )


def clip_of(rows, ends):
    return jnp.sum((rows[:, None] >= ends[None, :]).astype(jnp.int32), axis=1)


def head_norm(values, gains, head_count):
    row_count = values.shape[0]
    split = values.reshape(row_count, head_count, -1)
    inverse = lax.rsqrt(jnp.mean(split * split, axis=-1, keepdims=True) + EPSILON)
    unit_rows = split * inverse
    return (unit_rows.reshape(row_count, -1) * gains, unit_rows, inverse)


def head_norm_back(norm_grads, gains, unit_rows, inverse):
    row_count, head_count, head_width = unit_rows.shape
    gain_grad = jnp.sum(norm_grads * unit_rows.reshape(row_count, -1), axis=0)
    unit_grad = (norm_grads * gains).reshape(row_count, head_count, head_width)
    raw_grad = inverse * (
        unit_grad - unit_rows * jnp.mean(unit_grad * unit_rows, axis=-1, keepdims=True)
    )
    return (raw_grad.reshape(row_count, -1), gain_grad)


def rotate(values, positions, head_count):
    row_count = values.shape[0]
    split = values.reshape(row_count, head_count, -1)
    half_width = split.shape[-1] // 2
    frequency = jnp.exp(
        jnp.arange(half_width, dtype=jnp.float32) * (-2.0 * math.log(10000.0) / (2 * half_width))
    )
    angles = positions[:, None] * frequency[None, :]
    cosine = jnp.cos(angles)[:, None, :]
    sine = jnp.sin(angles)[:, None, :]
    first_half = split[..., :half_width]
    second_half = split[..., half_width:]
    turned = jnp.concatenate(
        [first_half * cosine - second_half * sine, first_half * sine + second_half * cosine],
        axis=-1,
    )
    return turned.reshape(row_count, -1)


def block_size(row_count):
    return 512 if row_count % 512 == 0 else row_count


def general_body(
    tokens,
    cotangent,
    clip_slices,
    caption_lengths,
    caption,
    cond,
    ada_w,
    norm_gain,
    w_qkv,
    q_gain,
    k_gain,
    w_caption,
    ky_gain,
    cross_gate,
    w_out,
    ffn_gain,
    w_gate_up,
    w_down,
):
    seq_count = lax.axis_size("seq")
    bucket_count = lax.axis_size("bucket")
    tok_rows = tokens.shape[0]
    slice_rows = tok_rows * seq_count
    total_rows = slice_rows * bucket_count
    local_heads = H // seq_count
    local_width = local_heads * HD
    score_scale = HD ** (-0.5)
    bucket_id = lax.axis_index("bucket")
    seq_id = lax.axis_index("seq")
    ends = jnp.cumsum(clip_slices) * slice_rows
    starts = ends - clip_slices * slice_rows
    my_clip = clip_of(jnp.reshape(bucket_id * slice_rows, (1,)), ends)[0]
    clip_mask = jnp.arange(CLIPS) == my_clip
    clip_start = jnp.sum(jnp.where(clip_mask, starts, 0))
    first_token = (bucket_id * seq_count + seq_id) * tok_rows
    positions = (first_token + jnp.arange(tok_rows, dtype=jnp.int32) - clip_start).astype(
        jnp.float32
    )
    caption_usable = jnp.arange(CAP) < jnp.sum(jnp.where(clip_mask, caption_lengths, 0))
    head_first = seq_id * local_width
    gates_local = jnp.tanh(lax.dynamic_slice_in_dim(cross_gate, seq_id * local_heads, local_heads))
    ky_gain_local = lax.dynamic_slice_in_dim(ky_gain, head_first, local_width)
    activation = jax.nn.silu(cond).astype(jnp.bfloat16)
    cond_row = lax.dynamic_index_in_dim(activation, my_clip, 0, True)
    caption_rows = lax.dynamic_index_in_dim(caption, my_clip, 0, False)
    caption_raw = jnp.einsum(
        "ty,jdy->jtd", caption_rows, w_caption, preferred_element_type=jnp.float32
    )
    caption_norm, caption_unit, caption_inverse = head_norm(
        caption_raw[0], ky_gain_local, local_heads
    )
    caption_keys = caption_norm.astype(jnp.bfloat16).reshape(CAP, local_heads, HD)
    caption_values = caption_raw[1].astype(jnp.bfloat16).reshape(CAP, local_heads, HD)
    inputs = tokens.astype(jnp.float32)

    def key_usable(first_row, row_count):
        return clip_of(first_row + jnp.arange(row_count, dtype=jnp.int32), ends) == my_clip

    def fold_keys(queries3, running, segment, first_row):
        seg_keys, seg_values = segment
        row_count = seg_keys.shape[0]
        key_rows = block_size(row_count)
        steps_count = row_count // key_rows
        usable = key_usable(first_row, row_count).reshape(steps_count, key_rows)
        key_blocks = seg_keys.reshape(steps_count, key_rows, local_heads, HD)
        value_blocks = seg_values.reshape(steps_count, key_rows, local_heads, HD)

        def update(state, item):
            key_block, value_block, usable_block = item

            def update_include(inner):
                row_max, row_total, accum = inner
                scores = (
                    jnp.einsum(
                        "qhd,khd->hqk", queries3, key_block, preferred_element_type=jnp.float32
                    )
                    * score_scale
                )
                scores = jnp.where(usable_block[None, None, :], scores, MASKED)
                new_max = jnp.maximum(row_max, jnp.max(scores, axis=-1))
                factor = jnp.exp(row_max - new_max)
                weights = jnp.exp(scores - new_max[..., None])
                row_total = row_total * factor + jnp.sum(weights, axis=-1)
                accum = accum * factor.T[:, :, None] + jnp.einsum(
                    "hqk,khd->qhd",
                    weights.astype(jnp.bfloat16),
                    value_block,
                    preferred_element_type=jnp.float32,
                )
                return (new_max, row_total, accum)

            return (
                lax.cond(jnp.any(usable_block), update_include, lambda inner: inner, state),
                None,
            )

        running, unused = lax.scan(update, running, (key_blocks, value_blocks, usable))
        return running

    def local_fold(queries3, running, keys_whole):

        def local_visit(state, piece_index):
            first_row = piece_index * slice_rows
            segment = (
                lax.dynamic_slice_in_dim(keys_whole[0], first_row, slice_rows, 0),
                lax.dynamic_slice_in_dim(keys_whole[1], first_row, slice_rows, 0),
            )
            return (fold_keys(queries3, state, segment, first_row), None)

        running, unused = lax.scan(local_visit, running, jnp.arange(bucket_count, dtype=jnp.int32))
        return running

    def forward(qkv_full, out_full, modulation, second):
        shift_vec = modulation[:D]
        scale_vec = modulation[D : 2 * D]
        gate_vec = modulation[2 * D : 3 * D]
        inverse = lax.rsqrt(jnp.mean(inputs * inputs, axis=-1, keepdims=True) + EPSILON)
        unit_rows = inputs * inverse
        hidden = (unit_rows * norm_gain * (1.0 + scale_vec) + shift_vec).astype(jnp.bfloat16)
        projected = project(hidden, qkv_full)
        query_norm, query_unit, query_inverse = head_norm(projected[:, :D], q_gain, H)
        key_norm, key_unit, key_inverse = head_norm(projected[:, D : 2 * D], k_gain, H)
        queries = rotate(query_norm, positions, H).astype(jnp.bfloat16)
        keys_tok = rotate(key_norm, positions, H).astype(jnp.bfloat16)
        values_tok = projected[:, 2 * D :].astype(jnp.bfloat16)
        head_queries, head_keys, head_values = (
            lax.all_to_all(queries, "seq", split_axis=1, concat_axis=0, tiled=True),
            lax.all_to_all(keys_tok, "seq", split_axis=1, concat_axis=0, tiled=True),
            lax.all_to_all(values_tok, "seq", split_axis=1, concat_axis=0, tiled=True),
        )
        queries3 = head_queries.reshape(slice_rows, local_heads, HD)
        start_state = (
            jnp.full((local_heads, slice_rows), MASKED, jnp.float32),
            jnp.zeros((local_heads, slice_rows), jnp.float32),
            jnp.zeros((slice_rows, local_heads, HD), jnp.float32),
        )
        folder = functools.partial(fold_keys, queries3)
        if second:
            keys_whole = (
                lax.all_gather(head_keys, "bucket", axis=0, tiled=True),
                lax.all_gather(head_values, "bucket", axis=0, tiled=True),
            )
            final_state = local_fold(queries3, start_state, keys_whole)
        else:
            keys_whole = None
            final_state = folder(
                start_state,
                (
                    lax.all_gather(head_keys, "bucket", axis=0, tiled=True),
                    lax.all_gather(head_values, "bucket", axis=0, tiled=True),
                ),
                jnp.int32(0),
            )
        row_max, row_total, accum = final_state
        own = accum / row_total.T[:, :, None]
        cross_scores = (
            jnp.einsum("qhd,khd->hqk", queries3, caption_keys, preferred_element_type=jnp.float32)
            * score_scale
        )
        cross_prob = jax.nn.softmax(
            jnp.where(caption_usable[None, None, :], cross_scores, MASKED), axis=-1
        )
        other = jnp.einsum(
            "hqk,khd->qhd",
            cross_prob.astype(jnp.bfloat16),
            caption_values,
            preferred_element_type=jnp.float32,
        )
        combined = (
            (own + gates_local[None, :, None] * other)
            .reshape(slice_rows, local_width)
            .astype(jnp.bfloat16)
        )
        attention = lax.all_to_all(combined, "seq", split_axis=0, concat_axis=1, tiled=True)
        branch = project(attention, out_full)
        return dict(
            gate_vec=gate_vec,
            scale_vec=scale_vec,
            inverse=inverse,
            unit_rows=unit_rows,
            hidden=hidden,
            query_unit=query_unit,
            query_inverse=query_inverse,
            key_unit=key_unit,
            key_inverse=key_inverse,
            queries3=queries3,
            own_keys3=head_keys.reshape(slice_rows, local_heads, HD),
            own_values3=head_values.reshape(slice_rows, local_heads, HD),
            keys_whole=keys_whole,
            row_log=row_max + jnp.log(row_total),
            own=own,
            other=other,
            cross_prob=cross_prob,
            attention=attention,
            branch=branch,
            output=inputs + gate_vec * branch,
        )

    gathered = (
        lax.all_gather(ada_w, "seq", axis=0, tiled=True),
        lax.all_gather(w_qkv, "seq", axis=0, tiled=True),
        lax.all_gather(w_out, "seq", axis=0, tiled=True),
        lax.all_gather(w_gate_up, "seq", axis=0, tiled=True),
        lax.all_gather(w_down, "seq", axis=0, tiled=True),
    )
    modulation = project(cond_row, gathered[0])[0]
    first_pass = forward(gathered[1], gathered[2], modulation, False)
    middle = first_pass["output"]
    shift_mlp = modulation[3 * D : 4 * D]
    scale_mlp = modulation[4 * D : 5 * D]
    gate_mlp = modulation[5 * D :]
    mid_inverse = lax.rsqrt(jnp.mean(middle * middle, axis=-1, keepdims=True) + EPSILON)
    mid_unit = middle * mid_inverse
    mlp_in = (mid_unit * ffn_gain * (1.0 + scale_mlp) + shift_mlp).astype(jnp.bfloat16)
    gate_up = project(mlp_in, gathered[3])
    gate_half = gate_up[:, :FF]
    up_half = gate_up[:, FF:]
    gate_sigmoid = jax.nn.sigmoid(gate_half)
    silu_gate = gate_half * gate_sigmoid
    inner = (silu_gate * up_half).astype(jnp.bfloat16)
    mlp_branch = jnp.dot(inner, gathered[4], preferred_element_type=jnp.float32)
    output = (middle + gate_mlp * mlp_branch).astype(jnp.bfloat16)
    regathered = (
        lax.all_gather(ada_w, "seq", axis=0, tiled=True),
        lax.all_gather(w_qkv, "seq", axis=0, tiled=True),
        lax.all_gather(w_out, "seq", axis=0, tiled=True),
        lax.all_gather(w_gate_up, "seq", axis=0, tiled=True),
        lax.all_gather(w_down, "seq", axis=0, tiled=True),
    )
    second_pass = forward(regathered[1], regathered[2], modulation, True)
    ada_full, qkv_full, out_full, gate_up_full, down_full = regathered
    grad_out = cotangent.astype(jnp.float32)
    mlp_gate_grad = jnp.sum(grad_out * mlp_branch, axis=0)
    grad_mlp = (grad_out * gate_mlp).astype(jnp.bfloat16)
    grad_inner = lax.dot_general(
        grad_mlp, down_full, (((1,), (1,)), ((), ())), preferred_element_type=jnp.float32
    )
    grad_gate_half = grad_inner * up_half * gate_sigmoid * (1.0 + gate_half * (1.0 - gate_sigmoid))
    grad_up_half = grad_inner * silu_gate
    grad_gate_up = jnp.concatenate([grad_gate_half, grad_up_half], axis=1).astype(jnp.bfloat16)
    mlp_in_grad = jnp.dot(grad_gate_up, gate_up_full, preferred_element_type=jnp.float32)
    ffn_gain_grad = jnp.sum(mlp_in_grad * (1.0 + scale_mlp) * mid_unit, axis=0)
    shift_mlp_grad = jnp.sum(mlp_in_grad, axis=0)
    scale_mlp_grad = jnp.sum(mlp_in_grad * mid_unit * ffn_gain, axis=0)
    mid_unit_grad = mlp_in_grad * ffn_gain * (1.0 + scale_mlp)
    residual_grad = (
        mid_inverse
        * (mid_unit_grad - mid_unit * jnp.mean(mid_unit_grad * mid_unit, axis=-1, keepdims=True))
        + grad_out
    )
    gate_grad = jnp.sum(residual_grad * second_pass["branch"], axis=0)
    grad_branch = (residual_grad * second_pass["gate_vec"]).astype(jnp.bfloat16)
    attention = second_pass["attention"]
    grad_attention = jnp.dot(grad_branch, out_full, preferred_element_type=jnp.float32).astype(
        jnp.bfloat16
    )
    grad_heads = lax.all_to_all(grad_attention, "seq", split_axis=1, concat_axis=0, tiled=True)
    grad_own16 = grad_heads.reshape(slice_rows, local_heads, HD)
    grad_own = grad_own16.astype(jnp.float32)
    queries3 = second_pass["queries3"]
    own = second_pass["own"]
    other = second_pass["other"]
    cross_prob = second_pass["cross_prob"]
    grad_other = (grad_own * gates_local[None, :, None]).astype(jnp.bfloat16)
    gate_grad_local = jnp.sum(grad_own * other, axis=(0, 2)) * (1.0 - gates_local * gates_local)
    grad_cross_prob = jnp.einsum(
        "qhd,khd->hqk", grad_other, caption_values, preferred_element_type=jnp.float32
    )
    grad_cross = (
        cross_prob
        * (grad_cross_prob - jnp.sum(cross_prob * grad_cross_prob, axis=-1, keepdims=True))
    ).astype(jnp.bfloat16)
    cross_query_grad = score_scale * jnp.einsum(
        "hqk,khd->qhd", grad_cross, caption_keys, preferred_element_type=jnp.float32
    )
    caption_key_grad = score_scale * jnp.einsum(
        "hqk,qhd->khd", grad_cross, queries3, preferred_element_type=jnp.float32
    )
    caption_value_grad = jnp.einsum(
        "hqk,qhd->khd",
        cross_prob.astype(jnp.bfloat16),
        grad_other,
        preferred_element_type=jnp.float32,
    )
    row_delta = jnp.sum(grad_own * own, axis=-1).T
    row_log = second_pass["row_log"]
    keys_whole = second_pass["keys_whole"]

    def grad_piece(query_grad, piece_index, with_keys):
        first_row = piece_index * slice_rows
        key_rows = block_size(slice_rows)
        steps_count = slice_rows // key_rows
        key_blocks = lax.dynamic_slice_in_dim(keys_whole[0], first_row, slice_rows, 0).reshape(
            steps_count, key_rows, local_heads, HD
        )
        value_blocks = lax.dynamic_slice_in_dim(keys_whole[1], first_row, slice_rows, 0).reshape(
            steps_count, key_rows, local_heads, HD
        )
        usable = key_usable(first_row, slice_rows).reshape(steps_count, key_rows)

        def grad_visit(accum, item):
            key_block, value_block, usable_block = item

            def grad_include(inner):
                scores = (
                    jnp.einsum(
                        "qhd,khd->hqk", queries3, key_block, preferred_element_type=jnp.float32
                    )
                    * score_scale
                )
                scores = jnp.where(usable_block[None, None, :], scores, MASKED)
                probability = jnp.exp(scores - row_log[..., None])
                grad_prob = jnp.einsum(
                    "qhd,khd->hqk", grad_own16, value_block, preferred_element_type=jnp.float32
                )
                grad_scores = (probability * (grad_prob - row_delta[..., None])).astype(
                    jnp.bfloat16
                )
                updated = inner + score_scale * jnp.einsum(
                    "hqk,khd->qhd", grad_scores, key_block, preferred_element_type=jnp.float32
                )
                key_grad = score_scale * jnp.einsum(
                    "hqk,qhd->khd", grad_scores, queries3, preferred_element_type=jnp.float32
                )
                value_grad = jnp.einsum(
                    "hqk,qhd->khd",
                    probability.astype(jnp.bfloat16),
                    grad_own16,
                    preferred_element_type=jnp.float32,
                )
                return (updated, key_grad, value_grad)

            def skip(inner):
                empty = jnp.zeros((key_rows, local_heads, HD), jnp.float32)
                return (inner, empty, empty)

            updated, key_grad, value_grad = lax.cond(
                jnp.any(usable_block), grad_include, skip, accum
            )
            return (updated, (key_grad, value_grad))

        query_grad, (key_grads, value_grads) = lax.scan(
            grad_visit, query_grad, (key_blocks, value_blocks, usable)
        )
        return (
            query_grad,
            (
                key_grads.reshape(slice_rows, local_width),
                value_grads.reshape(slice_rows, local_width),
            ),
        )

    query_start = jnp.zeros((slice_rows, local_heads, HD), jnp.float32)
    piece_order = jnp.arange(bucket_count, dtype=jnp.int32)
    self_query_grad, (key_terms, value_terms) = lax.scan(
        functools.partial(grad_piece, with_keys=True), query_start, piece_order
    )
    key_sum, value_sum = (
        lax.psum_scatter(
            key_terms.reshape(total_rows, local_width).astype(jnp.bfloat16),
            "bucket",
            scatter_dimension=0,
            tiled=True,
        ).astype(jnp.float32),
        lax.psum_scatter(
            value_terms.reshape(total_rows, local_width).astype(jnp.bfloat16),
            "bucket",
            scatter_dimension=0,
            tiled=True,
        ).astype(jnp.float32),
    )
    query_grad16 = (
        (self_query_grad + cross_query_grad).reshape(slice_rows, local_width).astype(jnp.bfloat16)
    )
    tok_query_grad, tok_key_grad, tok_value_grad = (
        lax.all_to_all(query_grad16, "seq", split_axis=0, concat_axis=1, tiled=True),
        lax.all_to_all(
            key_sum.astype(jnp.bfloat16), "seq", split_axis=0, concat_axis=1, tiled=True
        ),
        lax.all_to_all(
            value_sum.astype(jnp.bfloat16), "seq", split_axis=0, concat_axis=1, tiled=True
        ),
    )
    query_raw_grad, q_gain_grad = head_norm_back(
        rotate(tok_query_grad.astype(jnp.float32), -positions, H),
        q_gain,
        second_pass["query_unit"],
        second_pass["query_inverse"],
    )
    key_raw_grad, k_gain_grad = head_norm_back(
        rotate(tok_key_grad.astype(jnp.float32), -positions, H),
        k_gain,
        second_pass["key_unit"],
        second_pass["key_inverse"],
    )
    projected_grad = jnp.concatenate(
        [query_raw_grad, key_raw_grad, tok_value_grad.astype(jnp.float32)], axis=1
    ).astype(jnp.bfloat16)
    hidden = second_pass["hidden"]
    out_each = D // seq_count
    qkv_each = 3 * D // seq_count
    gate_up_each = 2 * FF // seq_count
    down_each = FF // seq_count
    rows_each = out_each + qkv_each + gate_up_each + down_each
    device_count = rows_each * lax.axis_size("seq") // rows_each
    first_device = jnp.int32(0) // rows_each

    def part(operand, partner, each):
        picked = lax.dynamic_slice_in_dim(operand, first_device * each, device_count * each, 1)
        term = lax.dot_general(
            picked, partner, (((0,), (0,)), ((), ())), preferred_element_type=jnp.float32
        )
        return term.reshape(device_count, each, D)

    terms = [
        part(grad_branch, attention, out_each),
        part(projected_grad, hidden, qkv_each),
        part(grad_gate_up, mlp_in, gate_up_each),
        part(inner, grad_mlp, down_each),
    ]
    weight_grad_seq = lax.psum_scatter(
        jnp.concatenate(terms, axis=1)
        .reshape(rows_each * lax.axis_size("seq"), D)
        .astype(jnp.bfloat16),
        "seq",
        scatter_dimension=0,
        tiled=True,
    )
    hidden_grad = jnp.dot(projected_grad, qkv_full, preferred_element_type=jnp.float32)
    unit_rows = second_pass["unit_rows"]
    scale_vec = second_pass["scale_vec"]
    inverse = second_pass["inverse"]
    norm_gain_grad = jnp.sum(hidden_grad * (1.0 + scale_vec) * unit_rows, axis=0)
    shift_grad = jnp.sum(hidden_grad, axis=0)
    scale_grad = jnp.sum(hidden_grad * unit_rows * norm_gain, axis=0)
    unit_grad = hidden_grad * norm_gain * (1.0 + scale_vec)
    token_grad = (
        inverse * (unit_grad - unit_rows * jnp.mean(unit_grad * unit_rows, axis=-1, keepdims=True))
        + residual_grad
    )
    modulation_grad = jnp.where(
        clip_mask[:, None],
        jnp.concatenate(
            [shift_grad, scale_grad, gate_grad, shift_mlp_grad, scale_mlp_grad, mlp_gate_grad]
        )[None, :],
        0.0,
    )
    ky_gain_part = jnp.sum(
        caption_key_grad.reshape(CAP, local_width) * caption_unit.reshape(CAP, local_width), axis=0
    )
    ky_gain_full = lax.dynamic_update_slice_in_dim(
        jnp.zeros((D,), jnp.float32), ky_gain_part, head_first, 0
    )
    gate_full = lax.dynamic_update_slice_in_dim(
        jnp.zeros((H,), jnp.float32), gate_grad_local, seq_id * local_heads, 0
    )
    caption_part = jnp.stack(
        [caption_key_grad.reshape(CAP, local_width), caption_value_grad.reshape(CAP, local_width)]
    )[None]
    zero_index = jnp.zeros((), jnp.int32)
    caption_full = lax.dynamic_update_slice(
        jnp.zeros((CLIPS, 2, CAP, D), jnp.float32),
        caption_part,
        (my_clip, zero_index, zero_index, head_first),
    )
    reduced = lax.psum(
        (
            norm_gain_grad,
            q_gain_grad,
            k_gain_grad,
            ky_gain_full,
            gate_full,
            modulation_grad,
            caption_full,
            ffn_gain_grad,
        ),
        ("bucket", "seq"),
    )
    modulation_total = reduced[5].astype(jnp.bfloat16)
    rows_local = 6 * D // seq_count
    cols_local = CD // bucket_count
    ada_grad = lax.dot_general(
        lax.dynamic_slice_in_dim(modulation_total, seq_id * rows_local, rows_local, 1),
        lax.dynamic_slice_in_dim(activation, bucket_id * cols_local, cols_local, 1),
        (((0,), (0,)), ((), ())),
        preferred_element_type=jnp.float32,
    )
    cond_sigmoid = jax.nn.sigmoid(cond)
    cond_grad = (
        jnp.dot(modulation_total, ada_full, preferred_element_type=jnp.float32)
        * cond_sigmoid
        * (1.0 + cond * (1.0 - cond_sigmoid))
    )
    caption_total = lax.dynamic_slice_in_dim(reduced[6], head_first, local_width, 3)
    raw_keys_all = jnp.einsum(
        "cty,dy->ctd", caption, w_caption[0], preferred_element_type=jnp.float32
    ).reshape(CLIPS * CAP, local_width)
    ignored, unit_all, inverse_all = head_norm(raw_keys_all, ky_gain_local, local_heads)
    raw_key_grad, unused_gain = head_norm_back(
        caption_total[:, 0].reshape(CLIPS * CAP, local_width), ky_gain_local, unit_all, inverse_all
    )
    raw_grad = jnp.stack(
        [raw_key_grad.reshape(CLIPS, CAP, local_width), caption_total[:, 1]], axis=1
    ).astype(jnp.bfloat16)
    caption_cols = lax.dynamic_slice_in_dim(
        caption, bucket_id * (YD // bucket_count), YD // bucket_count, 2
    )
    caption_w_grad = jnp.einsum(
        "cjtd,cty->jdy", raw_grad, caption_cols, preferred_element_type=jnp.float32
    )
    combined_grads = lax.psum_scatter(
        weight_grad_seq, "bucket", scatter_dimension=1, tiled=True
    ).astype(jnp.float32)
    out_grad_out = combined_grads[:out_each]
    qkv_grad_out = combined_grads[out_each : out_each + qkv_each]
    gate_up_grad_out = combined_grads[out_each + qkv_each : out_each + qkv_each + gate_up_each]
    down_grad_out = combined_grads[out_each + qkv_each + gate_up_each :]
    return (
        output,
        token_grad,
        cond_grad,
        ada_grad,
        reduced[0],
        qkv_grad_out,
        reduced[1],
        reduced[2],
        caption_w_grad,
        reduced[3],
        reduced[4],
        out_grad_out,
        reduced[7],
        gate_up_grad_out,
        down_grad_out,
    )


def solution(mesh):
    fits = mesh.shape["seq"] == 2 and mesh.shape["bucket"] == LINE * GROUP
    bucket = ("bucket",)
    if fits:
        bucket = BUCKET
        mesh = Mesh(mesh.devices.reshape(LINE, 2, GROUP // 2, 2), (*BUCKET, "seq"))
    in_specs = (
        P((*bucket, "seq"), None),
        P((*bucket, "seq"), None),
        P(),
        P(),
        P(),
        P(),
        P("seq", None),
        P(),
        P("seq", None),
        P(),
        P(),
        P(None, "seq", None),
        P(),
        P(),
        P("seq", None),
        P(),
        P("seq", None),
        P("seq", None),
    )
    out_specs = (
        P((*bucket, "seq"), None),
        P((*bucket, "seq"), None),
        P(),
        P("seq", bucket),
        P(),
        P("seq", bucket),
        P(),
        P(),
        P(None, "seq", bucket),
        P(),
        P(),
        P("seq", bucket),
        P(),
        P("seq", bucket),
        P("seq", bucket),
    )
    body = fast_body if fits else general_body
    return jax.shard_map(body, mesh=mesh, in_specs=in_specs, out_specs=out_specs, check_vma=False)
```

```python
import functools
import math

import jax
import jax.numpy as jnp
from jax import lax
from jax.experimental import pallas as pl
from jax.experimental.pallas import tpu as pltpu
from jax.sharding import Mesh, PartitionSpec as P

H = 24
HD = 64
D = 1536
FF = 4096
YD = 4096
CD = 1024
CAP = 128
CLIPS = 4

EPSILON = 1e-06
MASKED = -1e30
BF = jnp.bfloat16
F32 = jnp.float32
NN = (((1,), (0,)), ((), ()))
NT = (((1,), (1,)), ((), ()))
TN = (((0,), (0,)), ((), ()))
GROUP = 4
LINE = 4
BUCKET = ("z", "y", "c")
SENDS = (1, 2, 3, 0)
SMEM = pl.BlockSpec(memory_space=pltpu.SMEM)
VMEM = pl.BlockSpec(memory_space=pltpu.VMEM)
shape = jax.ShapeDtypeStruct


def cost(microseconds):
    return pl.CostEstimate(
        flops=0, transcendentals=0, bytes_accessed=int(microseconds * 20_000)
    )


def mm(a, b, dims):
    return lax.dot_general(a, b, dims, preferred_element_type=F32)


def clip_at(slices, slot):
    ends = [slices[0]]
    for i in range(1, CLIPS):
        ends.append(ends[-1] + slices[i])
    clip = jnp.int32(0)
    first, last = jnp.int32(0), ends[0]
    for i in range(CLIPS - 1):
        later = slot >= ends[i]
        clip = jnp.where(later, i + 1, clip)
        first = jnp.where(later, ends[i], first)
        last = jnp.where(later, ends[i + 1], last)
    return clip, first, last


def slot_of(bucket, k, j):
    return lax.rem(bucket // GROUP - k + LINE, LINE) * GROUP + jnp.bitwise_xor(
        lax.rem(bucket, GROUP), j
    )


def chunk_at(bucket, k, width):
    return pl.multiple_of(lax.rem(bucket // GROUP + k, LINE) * width, HD)


def norm_rope(raw, gain, cosine, sine):
    inverse = lax.rsqrt(jnp.mean(raw * raw, axis=0, keepdims=True) + EPSILON)
    normed = raw * inverse * gain
    half = raw.shape[0] // 2
    first, second = normed[:half], normed[half:]
    return jnp.concatenate(
        [first * cosine - second * sine, first * sine + second * cosine], axis=0
    )


def norm_rope_back(grad, raw, gain, cosine, sine):
    inverse = lax.rsqrt(jnp.mean(raw * raw, axis=0, keepdims=True) + EPSILON)
    unit = raw * inverse
    half = raw.shape[0] // 2
    first, second = grad[:half], grad[half:]
    turned = jnp.concatenate(
        [first * cosine + second * sine, second * cosine - first * sine], axis=0
    )
    gain_grad = jnp.sum(turned * unit, axis=1, keepdims=True)
    unit_grad = turned * gain
    raw_grad = inverse * (unit_grad - unit * jnp.mean(unit_grad * unit, axis=0, keepdims=True))
    return raw_grad, gain_grad


def row_inverse(values):
    return lax.rsqrt(jnp.mean(values * values, axis=-1, keepdims=True) + EPSILON)


def pre_kernel(ids, slices, tok_a, tok_b, mod_a, mod_b, gain_ref, w_ref, p_ref, hid_ref, mod_ref):
    @pl.when(pl.program_id(0) == 0)
    def _():
        s = ids[1]
        clip, _, _ = clip_at(slices, ids[0])
        row_a, row_b = mod_a[pl.ds(clip, 1), :], mod_b[pl.ds(clip, 1), :]
        low, high = jnp.where(s == 0, row_a, row_b), jnp.where(s == 0, row_b, row_a)
        mod_ref[...] = jnp.zeros_like(mod_ref)
        for i in range(3):
            mod_ref[i : i + 1, :] = low[:, i * D : (i + 1) * D]
            mod_ref[3 + i : 4 + i, :] = high[:, i * D : (i + 1) * D]
        shift, scale = mod_ref[0:1, :], mod_ref[1:2, :]
        count = tok_a.shape[0]
        for place, ref in ((s, tok_a), (1 - s, tok_b)):
            values = ref[...].astype(F32)
            hidden = values * row_inverse(values) * gain_ref[...] * (1.0 + scale) + shift
            hid_ref[pl.ds(pl.multiple_of(place * count, count), count), :] = hidden.astype(BF)

    p_ref[...] = mm(w_ref[...], hid_ref[...], NT).astype(BF)


def pre(ids, slices, tok_a, tok_b, mod_a, mod_b, gain, w_qkv):
    rows = 2 * tok_a.shape[0]
    tile = w_qkv.shape[0] // 3
    full = lambda v: pl.BlockSpec(v.shape, lambda i: (0,) * v.ndim)
    return pl.pallas_call(
        pre_kernel,
        grid=(w_qkv.shape[0] // tile,),
        in_specs=[SMEM, SMEM]
        + [full(v) for v in (tok_a, tok_b, mod_a, mod_b, gain)]
        + [pl.BlockSpec((tile, D), lambda i: (i, 0))],
        out_specs=[
            pl.BlockSpec((tile, rows), lambda i: (i, 0)),
            pl.BlockSpec((rows, D), lambda i: (0, 0)),
            pl.BlockSpec((8, D), lambda i: (0, 0)),
        ],
        out_shape=[shape((w_qkv.shape[0], rows), BF), shape((rows, D), BF), shape((8, D), F32)],
        name="pre",
        cost_estimate=cost(6),
    )(ids, slices, tok_a, tok_b, mod_a, mod_b, gain, w_qkv)


def route_kernel(ids, p_ref, r_ref, *outs):
    b, s = ids[0], ids[1]
    local = r_ref.shape[0]
    width = local // LINE
    for k in range(LINE):
        at = chunk_at(b, k, width)
        kv_ref, q_ref = outs[k], outs[LINE + k]

        @pl.when(s == 0)
        def _():
            q_ref[...] = p_ref[pl.ds(at, width), :]
            kv_ref[:width, :] = p_ref[pl.ds(2 * local + at, width), :]
            kv_ref[width:, :] = r_ref[pl.ds(at, width), :]

        @pl.when(s == 1)
        def _():
            q_ref[...] = r_ref[pl.ds(at, width), :]
            kv_ref[:width, :] = p_ref[pl.ds(at, width), :]
            kv_ref[width:, :] = p_ref[pl.ds(2 * local + at, width), :]


def route(ids, projected, received):
    local, rows = received.shape
    width = local // LINE
    outs = pl.pallas_call(
        route_kernel,
        in_specs=[SMEM, VMEM, VMEM],
        out_specs=[VMEM] * (2 * LINE),
        out_shape=[shape((2 * width, rows), BF)] * LINE + [shape((width, rows), BF)] * LINE,
        name="route",
        cost_estimate=cost(2.5),
    )(ids, projected, received)
    return outs[:LINE], outs[LINE:]


def caption_kernel(ids, w_ref, cap_ref, gains_ref, raw_ref, kv_ref):
    step = pl.program_id(0)
    width = w_ref.shape[1]

    @pl.when(step == 0)
    def _():
        raw_ref[...] = jnp.zeros_like(raw_ref)

    for j in range(2):
        raw_ref[j * width : (j + 1) * width, :] += mm(w_ref[j], cap_ref[...], NT)

    @pl.when(step == pl.num_programs(0) - 1)
    def _():
        base = ids[1] * LINE * width + ids[0] // GROUP * width
        for h in range(width // HD):
            at = slice(h * HD, h * HD + HD)
            raw = raw_ref[at, :]
            inverse = lax.rsqrt(jnp.mean(raw * raw, axis=0, keepdims=True) + EPSILON)
            gain = gains_ref[pl.ds(pl.multiple_of(base + h * HD, HD), HD), 2:3]
            keys = (raw * inverse * gain).astype(BF)
            for c in range(CLIPS):
                kv_ref[c, at, :] = keys[:, c * CAP : (c + 1) * CAP]
        for c in range(CLIPS):
            kv_ref[c, width:, :] = raw_ref[width:, c * CAP : (c + 1) * CAP].astype(BF)


def caption_keys(ids, w_caption, caption, gains):
    width = w_caption.shape[1] // LINE
    tile = 1024
    count = caption.shape[0]
    return pl.pallas_call(
        caption_kernel,
        grid_spec=pltpu.PrefetchScalarGridSpec(
            num_scalar_prefetch=1,
            grid=(YD // tile,),
            in_specs=[
                pl.BlockSpec((2, width, tile), lambda i, ids: (0, ids[0] // GROUP, i)),
                pl.BlockSpec((count, tile), lambda i, ids: (0, i)),
                pl.BlockSpec(gains.shape, lambda i, ids: (0, 0)),
            ],
            out_specs=[
                pl.BlockSpec((2 * width, count), lambda i, ids: (0, 0)),
                pl.BlockSpec((CLIPS, 2 * width, CAP), lambda i, ids: (0, 0, 0)),
            ],
        ),
        out_shape=[shape((2 * width, count), F32), shape((CLIPS, 2 * width, CAP), BF)],
        name="caption_keys",
        cost_estimate=cost(8),
    )(ids, w_caption, caption, gains)


def attend_kernel(ids, slices, lengths, gates, *refs):
    q_refs = refs[:LINE]
    kv_refs = refs[LINE : LINE + GROUP]
    cap_ref, gains_ref, cos_ref, sin_ref = refs[LINE + GROUP : LINE + GROUP + 4]
    outs = refs[LINE + GROUP + 4 :]
    comb_refs = outs[:LINE]
    own_ref, other_ref, stat_ref, qs_ref, ks_ref, pair_ref = outs[LINE : LINE + 6]
    value_ref, cap_value_ref, sum_ref = outs[LINE + 6 :]
    b, s = ids[0], ids[1]
    width, rows = q_refs[0].shape
    heads = width // HD
    scale = HD**-0.5
    base = s * LINE * width + b // GROUP * width

    def gain_of(h, column):
        return gains_ref[pl.ds(pl.multiple_of(base + h * HD, HD), HD), column : column + 1]

    key_gains = [gain_of(h, 1) for h in range(heads)]
    query_gains = [gain_of(h, 0) for h in range(heads)]
    is_one = lax.broadcasted_iota(jnp.int32, (rows, 2 * HD), 1) < HD
    for j, kv_ref in enumerate(kv_refs):
        for k in range(LINE):
            slot = slot_of(b, k, j)
            _, start, _ = clip_at(slices, slot)
            cosine, sine = cos_ref[slot - start], sin_ref[slot - start]
            for h in range(heads):
                at = slice(h * HD, h * HD + HD)
                raw = kv_ref[k, at, :].astype(F32)
                keys = norm_rope(raw, key_gains[h], cosine, sine)
                values = kv_ref[k, width + h * HD : width + h * HD + HD, :].astype(F32)
                ks_ref[slot, at, :] = keys.astype(BF)
                pair = jnp.concatenate([keys, values], axis=0).T
                pair_ref[slot, h] = pair.astype(BF)
                value_ref[slot, h] = jnp.where(is_one, 1.0, pair).astype(BF)
    cap_one = is_one[:CAP]
    for c in range(CLIPS):
        for h in range(heads):
            values = cap_ref[c, width + h * HD : width + h * HD + HD, :].astype(F32)
            both = jnp.concatenate([values, values], axis=0).T
            cap_value_ref[c, h] = jnp.where(cap_one, 1.0, both).astype(BF)

    for i in range(LINE):
        slot = slot_of(b, i, 0)
        clip, first, last = clip_at(slices, slot)
        cosine, sine = cos_ref[slot - first], sin_ref[slot - first]
        queries = []
        for h in range(heads):
            at = slice(h * HD, h * HD + HD)
            raw = q_refs[i][at, :].astype(F32)
            turned = norm_rope(raw, query_gains[h], cosine, sine).astype(BF).astype(F32) * scale
            qs_ref[i, at, :] = turned.astype(BF)
            queries.append(turned.T.astype(BF))
        sum_ref[...] = jnp.zeros_like(sum_ref)

        def step(n, carry):
            for h in range(heads):
                at = slice(h * HD, h * HD + HD)
                weights = jnp.exp(mm(queries[h], ks_ref[n, at, :], NN))
                sum_ref[h] += mm(weights.astype(BF), value_ref[n, h], NN)
            return carry

        lax.fori_loop(first, last, step, 0)
        usable = lax.broadcasted_iota(jnp.int32, (rows, CAP), 1) < lengths[clip]
        for h in range(heads):
            at = slice(h * HD, h * HD + HD)
            total = sum_ref[h].T
            inverse = 1.0 / total[0:1]
            own = total[HD:] * inverse
            weights = jnp.where(usable, jnp.exp(mm(queries[h], cap_ref[clip, at, :], NN)), 0.0)
            cap_total = mm(weights.astype(BF), cap_value_ref[clip, h], NN).T
            cap_inverse = 1.0 / cap_total[0:1]
            other = cap_total[HD:] * cap_inverse
            own_ref[i, at, :] = own
            other_ref[i, at, :] = other
            gate = gates[(s * LINE + b // GROUP) * heads + h]
            comb_refs[i][at, :] = (own + gate * other).astype(BF)
            stat_ref[i, h : h + 1, :] = inverse
            stat_ref[i, 4 + h : 5 + h, :] = cap_inverse


def attend(ids, slices, lengths, gates, queries, kv_pieces, cap_kv, gains, cosine, sine):
    width, rows = queries[0].shape
    slots = LINE * GROUP
    heads = width // HD
    outs = pl.pallas_call(
        attend_kernel,
        in_specs=[SMEM] * 4 + [VMEM] * (LINE + GROUP + 4),
        out_specs=[VMEM] * (LINE + 6),
        out_shape=[shape((width, rows), BF)] * LINE
        + [
            shape((LINE, width, rows), F32),
            shape((LINE, width, rows), F32),
            shape((LINE, 8, rows), F32),
            shape((LINE, width, rows), BF),
            shape((slots, width, rows), BF),
            shape((slots, heads, rows, 2 * HD), BF),
        ],
        scratch_shapes=[
            pltpu.VMEM((slots, heads, rows, 2 * HD), BF),
            pltpu.VMEM((CLIPS, heads, CAP, 2 * HD), BF),
            pltpu.VMEM((heads, rows, 2 * HD), F32),
        ],
        name="attend",
        cost_estimate=cost(33),
    )(ids, slices, lengths, gates, *queries, *kv_pieces, cap_kv, gains, cosine, sine)
    return outs[:LINE], outs[LINE:]


def out_kernel(ids, *refs):
    own, other = refs[:LINE], refs[LINE : 2 * LINE]
    w_ref, att_ref, branch_ref = refs[2 * LINE :]
    b, s = ids[0], ids[1]
    width = own[0].shape[0]
    for k in range(LINE):
        at = chunk_at(b, k, width)
        att_ref[pl.ds(pl.multiple_of(s * LINE * width + at, HD), width), :] = own[k][...]
        att_ref[pl.ds(pl.multiple_of((1 - s) * LINE * width + at, HD), width), :] = other[k][...]
    branch_ref[...] = mm(w_ref[...], att_ref[...], NN).T.astype(BF)


def out_proj(ids, own, other, w_out):
    rows = own[0].shape[1]
    return pl.pallas_call(
        out_kernel,
        in_specs=[SMEM] + [VMEM] * (2 * LINE + 1),
        out_specs=[VMEM, VMEM],
        out_shape=[shape((D, rows), BF), shape((rows, w_out.shape[0]), BF)],
        name="out_proj",
        cost_estimate=cost(3.5),
    )(ids, *own, *other, w_out)


def cut_kernel(turned, ids, *refs):
    count = len(turned)
    ins = refs[:count]
    own_ref, c_ref, y_ref, scratch = refs[count:]
    place = lax.rem(ids[0], GROUP)
    columns = own_ref.shape[3]
    for n in range(count):
        if turned[n]:
            source = ins[n]
        else:
            scratch[...] = ins[n][...].astype(F32).T
            source = scratch
        for k in range(LINE):
            for j, (ref, i) in enumerate(((own_ref, 0), (c_ref, 0), (y_ref, 0), (y_ref, 1))):
                at = (k * GROUP + jnp.bitwise_xor(place, j)) * columns
                ref[i, n, k] = source[pl.ds(pl.multiple_of(at, 32), columns), :].astype(BF)


def cut(ids, values, turned):
    rows = values[0].shape[1 if turned[0] else 0]
    columns = D // (LINE * GROUP)
    count = len(values)
    return pl.pallas_call(
        functools.partial(cut_kernel, tuple(turned)),
        in_specs=[SMEM] + [VMEM] * count,
        out_specs=[VMEM] * 3,
        out_shape=[shape((n, count, LINE, columns, rows), BF) for n in (1, 1, 2)],
        scratch_shapes=[pltpu.VMEM((D, rows), F32)],
        name="cut",
        cost_estimate=cost(2.4),
    )(ids, *values)


def ffn_kernel(
    ids,
    tok_a,
    tok_b,
    br_a,
    br_b,
    out16_ref,
    mod_ref,
    gain_ref,
    kept_ref,
    came_ref,
    down_ref,
    inner_ref,
    grads_ref,
    in16_ref,
    mid_ref,
    near_ref,
    far_ref,
    near_out_ref,
    far_out_ref,
    acc_in,
    acc_out,
):
    step = pl.program_id(0)
    steps = pl.num_programs(0)
    s = ids[1]
    count = tok_a.shape[0]
    half = br_a.shape[1]
    gate, shift2, scale2 = [mod_ref[i : i + 1, :] for i in (2, 3, 4)]
    mlp_gain = gain_ref[...] * (1.0 + scale2)

    @pl.when(step == 0)
    def _():
        for place, tok in ((s, tok_a), (1 - s, tok_b)):
            at = pl.ds(pl.multiple_of(place * count, count), count)
            mid_ref[at, :] = tok[...].astype(F32)
        low = jnp.where(s == 0, br_a[...].astype(F32), br_b[...].astype(F32))
        high = jnp.where(s == 0, br_b[...].astype(F32), br_a[...].astype(F32))
        mid_ref[:, :half] += gate[:, :half] * low
        mid_ref[:, half:] += gate[:, half:] * high
        middle = mid_ref[...]
        in16_ref[...] = (middle * row_inverse(middle) * mlp_gain + shift2).astype(BF)
        acc_in[...] = jnp.zeros_like(acc_in)
        acc_out[...] = jnp.zeros_like(acc_out)

    w_kept, w_came, w_down = kept_ref[...], came_ref[...], down_ref[...]
    kept = mm(in16_ref[...], w_kept, NT)
    other = mm(in16_ref[...], w_came, NT)
    grad_inner = mm(out16_ref[...], w_down, NT)
    gate_half = jnp.where(s == 0, kept, other)
    up_half = jnp.where(s == 0, other, kept)
    sigmoid = jax.nn.sigmoid(gate_half)
    silu = gate_half * sigmoid
    inner = (silu * up_half).astype(BF)
    grad_gate = grad_inner * up_half * sigmoid * (1.0 + gate_half * (1.0 - sigmoid))
    grad_up = grad_inner * silu
    grad_kept = jnp.where(s == 0, grad_gate, grad_up).astype(BF)
    grad_came = jnp.where(s == 0, grad_up, grad_gate).astype(BF)
    inner_ref[...] = inner
    grads_ref[0] = grad_kept
    grads_ref[1] = grad_came
    acc_in[...] += mm(grad_kept, w_kept, NN) + mm(grad_came, w_came, NN)
    acc_out[...] += mm(inner, w_down, NN)

    @pl.when(step == steps - 1)
    def _():
        middle = mid_ref[...]
        part = jnp.sum(
            acc_in[...] * mlp_gain * (middle * row_inverse(middle)), axis=-1, keepdims=True
        )
        near_ref[:, :half] = acc_in[:, pl.ds(pl.multiple_of(s * half, half), half)]
        near_ref[:, half:] = jnp.broadcast_to(part, (part.shape[0], 128))
        far_ref[:, :half] = acc_in[:, pl.ds(pl.multiple_of((1 - s) * half, half), half)].astype(BF)
        high = part.astype(BF).astype(F32)
        middle_part = (part - high).astype(BF).astype(F32)
        low_part = part - high - middle_part
        lane = lax.broadcasted_iota(jnp.int32, (part.shape[0], 128), 1)
        spread = jnp.where(lane == 0, high, jnp.where(lane == 1, middle_part, jnp.where(lane == 2, low_part, 0.0)))
        far_ref[:, half:] = spread.astype(BF)
        near_out_ref[...] = acc_out[pl.ds(pl.multiple_of(s * count, count), count), :]
        far_out_ref[...] = acc_out[pl.ds(pl.multiple_of((1 - s) * count, count), count), :].astype(BF)


def ffn(ids, toks, branches, grad_mlp, mod, gain, w_gate_up, came, w_down):
    count = toks[0].shape[0]
    rows = 2 * count
    half = D // 2
    units = w_down.shape[0]
    tile = 512
    steps = units // tile
    full = lambda v: pl.BlockSpec(v.shape, lambda i, ids: (0,) * v.ndim)

    def fixed(r, c):
        return pl.BlockSpec((r, c), lambda i, ids: (0, 0))

    small = [*toks, *branches, grad_mlp, mod, gain]
    return pl.pallas_call(
        ffn_kernel,
        grid_spec=pltpu.PrefetchScalarGridSpec(
            num_scalar_prefetch=1,
            grid=(steps,),
            in_specs=[full(v) for v in small]
            + [
                pl.BlockSpec((tile, D), lambda i, ids: (ids[1] * steps + i, 0)),
                pl.BlockSpec((tile, D), lambda i, ids: ((1 - ids[1]) * steps + i, 0)),
                pl.BlockSpec((tile, D), lambda i, ids: (i, 0)),
            ],
            out_specs=[
                pl.BlockSpec((rows, tile), lambda i, ids: (0, i)),
                pl.BlockSpec((2, rows, tile), lambda i, ids: (0, 0, i)),
            ]
            + [
                fixed(rows, D),
                fixed(rows, D),
                fixed(rows, half + 128),
                fixed(rows, half + 128),
                fixed(count, D),
                fixed(count, D),
            ],
            scratch_shapes=[pltpu.VMEM((rows, D), F32), pltpu.VMEM((rows, D), F32)],
        ),
        out_shape=[shape((rows, units), BF), shape((2, rows, units), BF)]
        + [
            shape((rows, D), BF),
            shape((rows, D), F32),
            shape((rows, half + 128), F32),
            shape((rows, half + 128), BF),
            shape((count, D), F32),
            shape((count, D), BF),
        ],
        name="ffn",
        cost_estimate=cost(18),
    )(ids, *small, w_gate_up, came, w_down)


def mid_kernel(
    ids,
    near_ref,
    recv_ref,
    mid_ref,
    cot_a,
    cot_b,
    br_ref,
    mod_ref,
    gain_ref,
    w_ref,
    sums_ref,
    gbr_ref,
    near_mid_ref,
    far_mid_ref,
    *refs,
):
    near_refs, far_refs, scratch = refs[:2], refs[2:4], refs[4]
    b, s = ids[0], ids[1]
    half = D // 2
    count = cot_a.shape[0]
    cols = pl.ds(pl.multiple_of(s * half, half), half)
    gate, scale2 = mod_ref[2:3, cols], mod_ref[4:5, cols]
    gain = gain_ref[:, cols]
    middle = mid_ref[...]
    inverse = row_inverse(middle)
    unit = mid_ref[:, cols] * inverse
    parts = jnp.sum(recv_ref[:, half:].astype(F32), axis=-1, keepdims=True)
    mean = (near_ref[:, half : half + 1] + parts) * (1.0 / D)
    grad_in = near_ref[:, :half] + recv_ref[:, :half].astype(F32)
    cot_own, cot_far = cot_a[:, cols].astype(F32), cot_b[:, cols].astype(F32)
    cot = jnp.concatenate(
        [jnp.where(s == 0, cot_own, cot_far), jnp.where(s == 0, cot_far, cot_own)], axis=0
    )
    scaled = grad_in * (1.0 + scale2)
    grad_mid = cot + inverse * (scaled * gain - unit * mean)
    sums_ref[...] = jnp.zeros_like(sums_ref)
    sums_ref[0:1, :] = jnp.sum(grad_mid * br_ref[...].astype(F32), axis=0, keepdims=True)
    sums_ref[1:2, :] = jnp.sum(grad_in, axis=0, keepdims=True)
    sums_ref[2:3, :] = jnp.sum(grad_in * unit, axis=0, keepdims=True) * gain
    sums_ref[3:4, :] = jnp.sum(scaled * unit, axis=0, keepdims=True)
    grad_branch = (grad_mid * gate).astype(BF)
    gbr_ref[...] = grad_branch
    top, low = grad_mid[:count], grad_mid[count:]
    near_mid_ref[...] = jnp.where(s == 0, top, low)
    far_mid_ref[...] = jnp.where(s == 0, low, top).astype(BF)
    scratch[...] = mm(grad_branch, w_ref[...], NN).T
    width = near_refs[0].shape[0] // 2
    for n, k in enumerate(SENDS):
        at = chunk_at(b, k, width)
        to = slice(n % 2 * width, n % 2 * width + width)
        near_refs[n // 2][to, :] = scratch[pl.ds(pl.multiple_of(s * half + at, HD), width), :]
        far_refs[n // 2][to, :] = scratch[
            pl.ds(pl.multiple_of((1 - s) * half + at, HD), width), :
        ].astype(BF)


def mid_back(ids, near, received, middle, cots, branch, mod, gain, w_out):
    rows, half = branch.shape
    width = half // LINE
    count = cots[0].shape[0]
    outs = pl.pallas_call(
        mid_kernel,
        in_specs=[SMEM] + [VMEM] * 9,
        out_specs=[VMEM] * 8,
        out_shape=[
            shape((8, half), F32),
            shape((rows, half), BF),
            shape((count, half), F32),
            shape((count, half), BF),
        ]
        + [shape((2 * width, rows), F32)] * 2
        + [shape((2 * width, rows), BF)] * 2,
        scratch_shapes=[pltpu.VMEM((D, rows), F32)],
        name="mid_back",
        cost_estimate=cost(5.5),
    )(ids, near, received, middle, *cots, branch, mod, gain, w_out)
    return outs[:4], outs[4:6], outs[6:]


def add_pair_kernel(near_ref, recv_ref, a_ref, b_ref):
    width = a_ref.shape[0]
    total = (near_ref[...] + recv_ref[...].astype(F32)).astype(BF)
    a_ref[...] = total[:width]
    b_ref[...] = total[width:]


def add_pair(near, received):
    both, rows = near.shape
    return pl.pallas_call(
        add_pair_kernel,
        in_specs=[VMEM, VMEM],
        out_specs=[VMEM, VMEM],
        out_shape=[shape((both // 2, rows), BF)] * 2,
        name="add_pair",
        cost_estimate=cost(1),
    )(near, received)


def place_row(b, column):
    width = column.shape[0]
    row = jnp.broadcast_to(column, (width, 128)).T[0:1]
    z = b // GROUP
    return jnp.concatenate([jnp.where(z == k, row, 0.0) for k in range(LINE)], axis=1)


def output_kernel(ids, slices, near_ref, recv_ref, mid_ref, cot_ref, mod_ref, sums_ref, out_ref, early_ref):
    s = ids[1]
    count, half = near_ref.shape[0], sums_ref.shape[1]
    clip, _, _ = clip_at(slices, ids[0])
    branch = near_ref[...] + recv_ref[...].astype(F32)
    middle = mid_ref[pl.ds(pl.multiple_of(s * count, count), count), :]
    out_ref[...] = (middle + mod_ref[5:6, :] * branch).astype(BF)
    gate2 = jnp.sum(cot_ref[...].astype(F32) * branch, axis=0, keepdims=True)
    rows = [sums_ref[i : i + 1, :] for i in range(3)] + [gate2[:, :half], gate2[:, half:]]
    early_ref[...] = jnp.zeros_like(early_ref)
    for c in range(CLIPS):
        for i, row in enumerate(rows):
            early_ref[5 * c + i : 5 * c + i + 1, :] = jnp.where(clip == c, row, 0.0)
    early_ref[20:21, :] = sums_ref[3:4, :]


def output_sums(ids, slices, near, received, middle, cot, mod, sums):
    count = near.shape[0]
    return pl.pallas_call(
        output_kernel,
        in_specs=[SMEM, SMEM] + [VMEM] * 6,
        out_specs=[VMEM, VMEM],
        out_shape=[shape((count, D), BF), shape((24, D // 2), F32)],
        name="output_sums",
        cost_estimate=cost(3),
    )(ids, slices, near, received, middle, cot, mod, sums)


def attend_back_kernel(ids, slices, lengths, gates, *refs):
    q_refs, g_refs = refs[:LINE], refs[LINE : 2 * LINE]
    (own_ref, other_ref, stat_ref, qs_ref, ks_ref, pair_ref, cap_ref, gains_ref, cos_ref, sin_ref) = refs[
        2 * LINE : 2 * LINE + 10
    ]
    outs = refs[2 * LINE + 10 :]
    gq_refs = outs[:LINE]
    qgain_ref, keep_ref, send_ref, dgate_ref = outs[LINE : LINE + 4]
    dkv_refs = outs[LINE + 4 : LINE + 4 + GROUP]
    acc_ref, dcap_ref, dq_ref = outs[LINE + 4 + GROUP :]
    b, s = ids[0], ids[1]
    width, rows = q_refs[0].shape
    heads = width // HD
    scale = HD**-0.5
    base = s * LINE * width + b // GROUP * width
    acc_ref[...] = jnp.zeros_like(acc_ref)
    dcap_ref[...] = jnp.zeros_like(dcap_ref)
    dgate_ref[...] = jnp.zeros_like(dgate_ref)
    qgain_ref[...] = jnp.zeros_like(qgain_ref)

    for i in range(LINE):
        slot = slot_of(b, i, 0)
        clip, first, last = clip_at(slices, slot)
        queries, grads, deltas, inverses = [], [], [], []
        tall_q, tall_g, wide = [], [], []
        for h in range(heads):
            at = slice(h * HD, h * HD + HD)
            grad = g_refs[i][at, :]
            queries.append(qs_ref[i, at, :])
            grads.append(grad)
            deltas.append(jnp.sum(grad.astype(F32) * own_ref[i, at, :], axis=0, keepdims=True))
            inverses.append(stat_ref[i, h : h + 1, :])
            blank = jnp.zeros((HD, rows), F32)
            query_pad = jnp.concatenate([queries[h].astype(F32), blank], axis=0)
            grad_pad = jnp.concatenate([blank, grad.astype(F32)], axis=0)
            tall_q.append(query_pad.astype(BF))
            tall_g.append(grad_pad.astype(BF))
            wide.append(jnp.concatenate([query_pad.T, grad_pad.T], axis=0).astype(BF))
        dq_ref[...] = jnp.zeros_like(dq_ref)

        def step(n, carry):
            for h in range(heads):
                at = slice(h * HD, h * HD + HD)
                pair = pair_ref[n, h]
                prob = jnp.exp(mm(pair, tall_q[h], NN)) * inverses[h]
                grad_score = (prob * (mm(pair, tall_g[h], NN) - deltas[h])).astype(BF)
                both = jnp.concatenate([grad_score, prob.astype(BF)], axis=1)
                acc_ref[n, h] += mm(both, wide[h], NN)
                dq_ref[at, :] += mm(ks_ref[n, at, :], grad_score, NN)
            return carry

        lax.fori_loop(first, last, step, 0)
        usable = lax.broadcasted_iota(jnp.int32, (CAP, rows), 0) < lengths[clip]
        cosine, sine = cos_ref[slot - first], sin_ref[slot - first]
        for h in range(heads):
            at = slice(h * HD, h * HD + HD)
            at_value = slice(width + h * HD, width + h * HD + HD)
            gate = gates[(s * LINE + b // GROUP) * heads + h]
            cap_keys, cap_values = cap_ref[clip, at, :], cap_ref[clip, at_value, :]
            grad = grads[h].astype(F32)
            grad_other = (grad * gate).astype(BF)
            prob = (
                jnp.where(usable, jnp.exp(mm(cap_keys, queries[h], TN)), 0.0)
                * stat_ref[i, 4 + h : 5 + h, :]
            )
            grad_prob = mm(cap_values, grad_other, TN)
            inner = jnp.sum(prob * grad_prob, axis=0, keepdims=True)
            grad_score = (prob * (grad_prob - inner)).astype(BF)
            query_grad = (dq_ref[at, :] + mm(cap_keys, grad_score, NN)) * scale
            dcap_ref[clip, at, :] += mm(queries[h], grad_score, NT)
            dcap_ref[clip, at_value, :] += mm(grad_other, prob.astype(BF), NT)
            part = jnp.sum(grad * other_ref[i, at, :], axis=0, keepdims=True)
            dgate_ref[h : h + 1, :] += part * (1.0 - gate * gate)
            gain = gains_ref[pl.ds(pl.multiple_of(base + h * HD, HD), HD), 0:1]
            raw_grad, gain_grad = norm_rope_back(
                query_grad.astype(BF).astype(F32), q_refs[i][at, :].astype(F32), gain, cosine, sine
            )
            gq_refs[i][at, :] = raw_grad.astype(BF)
            qgain_ref[at, :] += gain_grad

    for j, dkv_ref in enumerate(dkv_refs):
        for k in range(LINE):
            slot = slot_of(b, k, j)
            for h in range(heads):
                both = acc_ref[slot, h].T.astype(BF)
                dkv_ref[k, h * HD : h * HD + HD, :] = both[:HD]
                dkv_ref[k, width + h * HD : width + h * HD + HD, :] = both[HD:]
    core = lax.rem(b, 2)
    for i in range(2):
        keep_ref[i] = dcap_ref[2 * i + core]
        send_ref[i] = dcap_ref[2 * i + 1 - core]


def attend_back(ids, slices, lengths, gates, queries, grads, saved, cap_kv, gains, cosine, sine):
    width, rows = queries[0].shape
    outs = pl.pallas_call(
        attend_back_kernel,
        in_specs=[SMEM] * 4 + [VMEM] * (2 * LINE + 10),
        out_specs=[VMEM] * (LINE + 4 + GROUP),
        out_shape=[shape((width, rows), BF)] * LINE
        + [
            shape((width, 1), F32),
            shape((2, 2 * width, CAP), F32),
            shape((2, 2 * width, CAP), F32),
            shape((8, rows), F32),
        ]
        + [shape((LINE, 2 * width, rows), BF)] * GROUP,
        scratch_shapes=[
            pltpu.VMEM((LINE * GROUP, width // HD, rows, 2 * HD), F32),
            pltpu.VMEM((CLIPS, 2 * width, CAP), F32),
            pltpu.VMEM((width, rows), F32),
        ],
        name="attend_back",
        cost_estimate=cost(40),
    )(ids, slices, lengths, gates, *queries, *grads, *saved, cap_kv, gains, cosine, sine)
    return outs[:LINE], outs[LINE : LINE + 4], outs[LINE + 4 :]


def keys_back_kernel(ids, slices, a_ref, r_ref, kv_ref, gains_ref, cos_ref, sin_ref, *outs):
    out_refs, gain_ref = outs[:LINE], outs[LINE]
    b, s = ids[0], ids[1]
    width = gain_ref.shape[0]
    base = s * LINE * width + b // GROUP * width
    gain_ref[...] = jnp.zeros_like(gain_ref)
    for i in range(LINE):
        slot = slot_of(b, i, 0)
        _, first, _ = clip_at(slices, slot)
        cosine, sine = cos_ref[slot - first], sin_ref[slot - first]
        total = (a_ref[i].astype(F32) + r_ref[i].astype(F32)).astype(BF)
        for h in range(width // HD):
            at = slice(h * HD, h * HD + HD)
            gain = gains_ref[pl.ds(pl.multiple_of(base + h * HD, HD), HD), 1:2]
            raw_grad, gain_grad = norm_rope_back(
                total[at, :].astype(F32), kv_ref[i, at, :].astype(F32), gain, cosine, sine
            )
            out_refs[i][at, :] = raw_grad.astype(BF)
            gain_ref[at, :] += gain_grad
        out_refs[i][width:, :] = total[width:, :]


def keys_back(ids, slices, part, received, kv, gains, cosine, sine):
    _, both, rows = kv.shape
    outs = pl.pallas_call(
        keys_back_kernel,
        in_specs=[SMEM, SMEM] + [VMEM] * 6,
        out_specs=[VMEM] * (LINE + 1),
        out_shape=[shape((both, rows), BF)] * LINE + [shape((both // 2, 1), F32)],
        name="keys_back",
        cost_estimate=cost(3.7),
    )(ids, slices, part, received, kv, gains, cosine, sine)
    return outs[:LINE], outs[LINE]


def pack_kernel(ids, *refs):
    q_refs, kv_refs = refs[:LINE], refs[LINE : 2 * LINE]
    own_ref, send_ref = refs[2 * LINE :]
    b, s = ids[0], ids[1]
    width = q_refs[0].shape[0]
    local = LINE * width
    for k in range(LINE):
        at = chunk_at(b, k, width)

        @pl.when(s == 0)
        def _():
            own_ref[pl.ds(at, width), :] = q_refs[k][...]
            own_ref[pl.ds(local + at, width), :] = kv_refs[k][:width, :]
            send_ref[pl.ds(at, width), :] = kv_refs[k][width:, :]

        @pl.when(s == 1)
        def _():
            own_ref[pl.ds(at, width), :] = kv_refs[k][:width, :]
            own_ref[pl.ds(local + at, width), :] = kv_refs[k][width:, :]
            send_ref[pl.ds(at, width), :] = q_refs[k][...]


def pack(ids, grads_q, grads_kv):
    width, rows = grads_q[0].shape
    return pl.pallas_call(
        pack_kernel,
        in_specs=[SMEM] + [VMEM] * (2 * LINE),
        out_specs=[VMEM, VMEM],
        out_shape=[shape((2 * LINE * width, rows), BF), shape((LINE * width, rows), BF)],
        name="pack",
        cost_estimate=cost(2.5),
    )(ids, *grads_q, *grads_kv)


def qkv_back_kernel(ids, own_ref, recv_ref, w_ref, near_ref, far_ref, acc_ref):
    step = pl.program_id(0)
    third = pl.num_programs(0) // 3
    count = near_ref.shape[0]
    s = ids[1]

    @pl.when(step == 0)
    def _():
        acc_ref[...] = jnp.zeros_like(acc_ref)

    middle = jnp.logical_and(step >= third, step < 2 * third)
    grads = jnp.where(middle, recv_ref[...], own_ref[...])
    acc_ref[...] += mm(grads, w_ref[...], TN)

    @pl.when(step == pl.num_programs(0) - 1)
    def _():
        near_ref[...] = acc_ref[pl.ds(pl.multiple_of(s * count, count), count), :]
        far_ref[...] = acc_ref[pl.ds(pl.multiple_of((1 - s) * count, count), count), :].astype(BF)


def qkv_back(ids, own, received, w_qkv):
    local, rows = received.shape
    count = rows // 2
    tile = local
    third = local // tile

    def own_at(i, ids):
        return (jnp.where(i < third, i, jnp.clip(i - third, third - 1, 2 * third - 1)), 0)

    return pl.pallas_call(
        qkv_back_kernel,
        grid_spec=pltpu.PrefetchScalarGridSpec(
            num_scalar_prefetch=1,
            grid=(3 * third,),
            in_specs=[
                pl.BlockSpec((tile, rows), own_at),
                pl.BlockSpec((tile, rows), lambda i, ids: (jnp.clip(i - third, 0, third - 1), 0)),
                pl.BlockSpec((tile, D), lambda i, ids: (i, 0)),
            ],
            out_specs=[pl.BlockSpec((count, D), lambda i, ids: (0, 0))] * 2,
            scratch_shapes=[pltpu.VMEM((rows, D), F32)],
        ),
        out_shape=[shape((count, D), F32), shape((count, D), BF)],
        name="qkv_back",
        cost_estimate=cost(6),
    )(ids, own, received, w_qkv)


def tokens_kernel(
    ids, slices, tok_ref, near_ref, recv_ref, mid_near, mid_far, mod_ref, gain_ref, *refs
):
    qgain_ref, kgain_ref, cgain_ref, dgate_ref, early_ref, out_ref, late_ref = refs
    b, s = ids[0], ids[1]
    half = mid_near.shape[1]
    clip, _, _ = clip_at(slices, b)
    values = tok_ref[...].astype(F32)
    inverse = row_inverse(values)
    unit = values * inverse
    scale = 1.0 + mod_ref[1:2, :]
    gain = gain_ref[...]
    grad = near_ref[...] + recv_ref[...].astype(F32)
    scaled = grad * scale
    unit_grad = scaled * gain
    mean = jnp.mean(unit_grad * unit, axis=-1, keepdims=True)
    mid_own, mid_other = mid_near[...], mid_far[...].astype(F32)
    middle = jnp.concatenate(
        [jnp.where(s == 0, mid_own, mid_other), jnp.where(s == 0, mid_other, mid_own)], axis=1
    )
    out_ref[...] = inverse * (unit_grad - unit * mean) + middle
    shift_row = jnp.sum(grad, axis=0, keepdims=True)
    with_unit = grad * unit
    scale_row = jnp.sum(with_unit, axis=0, keepdims=True) * gain
    norm_row = jnp.sum(scaled * unit, axis=0, keepdims=True)
    rows = [shift_row[:, :half], shift_row[:, half:], scale_row[:, :half], scale_row[:, half:]]
    late_ref[...] = jnp.zeros_like(late_ref)
    for c in range(CLIPS):
        for i, row in enumerate(rows):
            late_ref[4 * c + i : 4 * c + i + 1, :] = jnp.where(clip == c, row, 0.0)
    late_ref[16:17, :] = norm_row[:, :half]
    late_ref[17:18, :] = norm_row[:, half:]
    for i, ref in enumerate((qgain_ref, kgain_ref, cgain_ref)):
        late_ref[18 + i : 19 + i, :] = place_row(b, ref[...])
    heads = qgain_ref.shape[0] // HD
    lane = lax.broadcasted_iota(jnp.int32, (1, half), 1)
    gate_row = jnp.zeros((1, half), F32)
    for h in range(heads):
        value = jnp.sum(dgate_ref[h : h + 1, :], axis=1, keepdims=True)
        gate_row = gate_row + jnp.where(lane == b // GROUP * heads + h, value, 0.0)
    late_ref[21:22, :] = gate_row
    late_ref[24:, :] = early_ref[...]


def tokens_back(ids, slices, tok, near, received, mid_near, mid_far, mod, gain, parts):
    return pl.pallas_call(
        tokens_kernel,
        in_specs=[SMEM, SMEM] + [VMEM] * 12,
        out_specs=[VMEM, VMEM],
        out_shape=[shape(tok.shape, F32), shape((48, D // 2), F32)],
        name="tokens_back",
        cost_estimate=cost(3.5),
    )(ids, slices, tok, near, received, mid_near, mid_far, mod, gain, *parts)


def finish_kernel(ids, late_a, late_b, mod_ref, gains_ref):
    s = ids[1]
    early_a, early_b = late_a.at[pl.ds(24, 24)], late_b.at[pl.ds(24, 24)]

    def joined(a, b, i):
        own, other = a[i : i + 1, :], b[i : i + 1, :]
        return jnp.concatenate(
            [jnp.where(s == 0, own, other), jnp.where(s == 0, other, own)], axis=1
        )

    def added(a, b, i):
        both = a[i : i + 2, :] + b[i : i + 2, :]
        return jnp.concatenate([both[0:1], both[1:2]], axis=1)

    for c in range(CLIPS):
        low = [added(late_a, late_b, 4 * c), added(late_a, late_b, 4 * c + 2), joined(early_a, early_b, 5 * c)]
        high = [
            joined(early_a, early_b, 5 * c + 1),
            joined(early_a, early_b, 5 * c + 2),
            added(early_a, early_b, 5 * c + 3),
        ]
        for i in range(3):
            mod_ref[c : c + 1, i * D : (i + 1) * D] = jnp.where(s == 0, low[i], high[i])
    gains_ref[...] = jnp.zeros_like(gains_ref)
    gains_ref[0:1, :] = added(late_a, late_b, 16)
    for i in range(3):
        gains_ref[1 + i : 2 + i, :] = joined(late_a, late_b, 18 + i)
    gains_ref[4:5, :] = joined(early_a, early_b, 20)
    gains_ref[5:6, :] = joined(late_a, late_b, 21)


def finish(ids, late_a, late_b):
    return pl.pallas_call(
        finish_kernel,
        in_specs=[SMEM] + [VMEM] * 2,
        out_specs=[VMEM, VMEM],
        out_shape=[shape((CLIPS, 3 * D), F32), shape((8, D), F32)],
        name="finish",
        cost_estimate=cost(1.7),
    )(ids, late_a, late_b)


def caption_back_kernel(ids, sum_ref, raw_ref, gains_ref, out_ref, gain_ref):
    b, s = ids[0], ids[1]
    width = gain_ref.shape[0]
    base = s * LINE * width + b // GROUP * width
    cols = pl.ds(pl.multiple_of(lax.rem(b, GROUP) * CAP, CAP), CAP)
    for h in range(width // HD):
        at = slice(h * HD, h * HD + HD)
        gain = gains_ref[pl.ds(pl.multiple_of(base + h * HD, HD), HD), 2:3]
        raw = raw_ref[at, cols]
        inverse = lax.rsqrt(jnp.mean(raw * raw, axis=0, keepdims=True) + EPSILON)
        unit = raw * inverse
        grad = sum_ref[at, :]
        gain_ref[at, :] = jnp.sum(grad * unit, axis=1, keepdims=True)
        unit_grad = grad * gain
        out_ref[at, :] = (
            inverse * (unit_grad - unit * jnp.mean(unit_grad * unit, axis=0, keepdims=True))
        ).astype(BF)
    out_ref[width:, :] = sum_ref[width:, :].astype(BF)


def caption_back(ids, total, raw, gains):
    return pl.pallas_call(
        caption_back_kernel,
        in_specs=[SMEM] + [VMEM] * 3,
        out_specs=[VMEM, VMEM],
        out_shape=[shape(total.shape, BF), shape((total.shape[0] // 2, 1), F32)],
        name="caption_back",
        cost_estimate=cost(2.3),
    )(ids, total, raw, gains)


def caption_weight_kernel(ids, *refs):
    raw_refs, cap_ref, out_refs = refs[:GROUP], refs[GROUP], refs[GROUP + 1 :]
    b = ids[0]
    each = out_refs[0].shape[1]
    place = lax.rem(b, GROUP)
    for k in range(LINE):
        at = pl.multiple_of((lax.rem(b // GROUP - k + LINE, LINE) * GROUP + place) * each, each)
        total = None
        for j in range(GROUP):
            rows = pl.ds(pl.multiple_of(jnp.bitwise_xor(place, j) * CAP, CAP), CAP)
            part = mm(raw_refs[j][...], cap_ref[rows, pl.ds(at, each)], NN)
            total = part if total is None else total + part
        out_refs[k][...] = total.astype(BF)


def caption_weights(ids, raws, caption):
    rows = raws[0].shape[0]
    return pl.pallas_call(
        caption_weight_kernel,
        in_specs=[SMEM] + [VMEM] * (GROUP + 1),
        out_specs=[VMEM] * LINE,
        out_shape=[shape((rows, YD // (LINE * GROUP)), BF)] * LINE,
        name="caption_weights",
        cost_estimate=cost(4),
    )(ids, *raws, caption)


def caption_join_kernel(ids, *refs):
    parts, out_ref = refs[:LINE], refs[LINE]
    width = parts[0].shape[0] // 2
    for k in range(LINE):
        at = chunk_at(ids[0], k, width)
        for j in range(2):
            out_ref[j, pl.ds(at, width), :] = parts[k][j * width : (j + 1) * width, :].astype(F32)


def caption_join(ids, parts):
    both, each = parts[0].shape
    return pl.pallas_call(
        caption_join_kernel,
        in_specs=[SMEM] + [VMEM] * LINE,
        out_specs=VMEM,
        out_shape=shape((2, both // 2 * LINE, each), F32),
        name="caption_join",
        cost_estimate=cost(2),
    )(ids, *parts)


def weight_kernel(count, dims, *refs):
    left, right, out_ref = refs[:count], refs[count : 2 * count], refs[-1]
    total = None
    for a_ref, g_ref in zip(left, right):
        block = g_ref[...].reshape(g_ref.shape[-2:])
        part = mm(a_ref[0, 0].reshape(-1, a_ref.shape[-1]), block, dims)
        total = part if total is None else total + part
    out_ref[...] = total.reshape(out_ref.shape).astype(BF)


def weight_grads(left, right, by_rows, tile, kind, total, place, into=None):
    _, _, chunks, columns, tokens = left[0][0].shape
    rows = right[0].shape[-2 if by_rows else -1]
    stack = right[0].shape[0] if right[0].ndim == 3 else 1
    per = rows // tile
    left_specs = [
        pl.BlockSpec((1, 1, chunks, columns, tokens), lambda i, n=n: (n, kind, 0, 0, 0))
        for _, n in left
    ]
    if by_rows:
        right_spec = pl.BlockSpec((tile, tokens), lambda i: (i, 0))
    elif stack == 1:
        right_spec = pl.BlockSpec((tokens, tile), lambda i: (0, i))
    else:
        right_spec = pl.BlockSpec((1, tokens, tile), lambda i: (i // per, 0, i % per))
    args = [a for a, _ in left] + list(right)
    specs = left_specs + [right_spec] * len(right)
    aliases = {}
    if into is not None:
        aliases = {len(args): 0}
        args.append(into)
        specs.append(pl.BlockSpec(memory_space=pl.ANY))
    return pl.pallas_call(
        functools.partial(weight_kernel, len(left), NT if by_rows else NN),
        grid=(stack * per,),
        in_specs=specs,
        out_specs=pl.BlockSpec((chunks, columns, tile), lambda i: (0, 0, place(i))),
        out_shape=shape((chunks, columns, total), BF),
        input_output_aliases=aliases,
        name="weight_grads",
        cost_estimate=cost(5),
    )(*args)


def fast_body(
    tokens,
    cotangent,
    clip_slices,
    caption_lengths,
    caption,
    cond,
    ada_w,
    norm_gain,
    w_qkv,
    q_gain,
    k_gain,
    w_caption,
    ky_gain,
    cross_gate,
    w_out,
    ffn_gain,
    w_gate_up,
    w_down,
):
    bucket_count = LINE * GROUP
    seq_count = lax.axis_size("seq")
    local_width = D // seq_count
    units = FF // seq_count
    b = lax.axis_index(BUCKET)
    s = lax.axis_index("seq")
    z, g, c, y = b // GROUP, b % GROUP, b % 2, (b // 2) % 2
    ids = jnp.stack([b, s]).astype(jnp.int32)

    def xswap(v):
        return lax.ppermute(v, "seq", [(0, 1), (1, 0)])

    def hop(v, to):
        return lax.ppermute(v, BUCKET, [(i, to(i)) for i in range(bucket_count)])

    def cswap(v):
        return hop(v, lambda i: i ^ 1)

    def yswap(v):
        return hop(v, lambda i: i ^ 2)

    def zshift(v, k):
        return hop(v, lambda i: (i + GROUP * k) % bucket_count)

    def after(v, *others):
        return lax.optimization_barrier((v, *others))[0]

    def fence(*values):
        return lax.optimization_barrier(values)

    def pick(v, index):
        return lax.dynamic_index_in_dim(v, index, 0, False)

    def spread(parts):
        return [parts[0]] + [zshift(parts[k], k) for k in range(1, LINE)]

    def unspread(parts):
        return [parts[0]] + [zshift(parts[k], LINE - k) for k in range(1, LINE)]

    half = HD // 2
    rows = tokens.shape[0] * seq_count
    frequency = jnp.exp(jnp.arange(half, dtype=F32) * (-2.0 * math.log(10000.0) / (2 * half)))
    positions = jnp.arange(bucket_count * rows, dtype=F32).reshape(bucket_count, 1, rows)
    angles = positions * frequency[None, :, None]
    cosine, sine = jnp.cos(angles), jnp.sin(angles)
    gains = jnp.stack([q_gain, k_gain, ky_gain], axis=1)
    gates = jnp.tanh(cross_gate)
    norm_row, ffn_row = norm_gain[None], ffn_gain[None]

    tok_far = xswap(tokens)
    activation = jax.nn.silu(cond).astype(BF)
    mod_near = mm(activation, ada_w, NT)
    mod_far = xswap(mod_near)
    each = units // 2
    sent = lax.dynamic_slice_in_dim(w_gate_up, (1 - s) * units + c * each, each, 0)
    tok_far, sent = lax.optimization_barrier((tok_far, sent))
    projected, hidden, mod = pre(
        ids, clip_slices, tokens, tok_far, mod_near, mod_far, norm_row, w_qkv
    )
    local = lax.slice_in_dim(projected, local_width, 2 * local_width, axis=0)
    swapped = xswap(local)
    def scatter(parts):
        return lax.psum_scatter(parts, "z", scatter_dimension=0, tiled=False)

    hid_own, hid_c, hid_y = cut(ids, [hidden], [False])
    swapped, hid_own, hid_c, hid_y, gains = fence(swapped, hid_own, hid_c, hid_y, gains)
    kv_parts, q_parts = route(ids, projected, swapped)
    came = lax.all_gather(after(sent, swapped), ("seq", "c"), axis=0, tiled=True)
    kv_here = spread(kv_parts)
    q_here = spread(q_parts)
    caption_rows = caption.reshape(CLIPS * CAP, YD)
    cap_raw, cap_kv = caption_keys(ids, w_caption, after(caption_rows, kv_parts[0]), gains)
    cap_raw, cap_kv, cosine, sine, *kv_here = fence(cap_raw, cap_kv, cosine, sine, *kv_here)
    kv_own = jnp.stack(kv_here)
    kv_y = yswap(kv_own)
    kv_c = cswap(kv_own)
    cot_far = xswap(after(cotangent, kv_own))
    kv_y = after(kv_y, kv_c, *q_here[1:], cot_far)
    kv_cy = cswap(kv_y)
    kv_pieces = [kv_own, kv_c, kv_y, kv_cy]
    grad_mlp = (
        jnp.where(
            s == 0,
            jnp.concatenate([cotangent, cot_far], 0),
            jnp.concatenate([cot_far, cotangent], 0),
        ).astype(F32)
        * mod[5:6]
    ).astype(BF)
    q_here[0], hid_y, hid_c = fence(q_here[0], hid_y, hid_c, grad_mlp)[:3]
    hid_came_y, hid_came_c = yswap(hid_y), cswap(hid_c)
    combined, saved = attend(
        ids, clip_slices, caption_lengths, gates, q_here, kv_pieces, cap_kv, gains, cosine, sine
    )
    combined, saved, hid_came_y, hid_came_c = fence(combined, saved, hid_came_y, hid_came_c)
    heads_own = unspread(combined)
    heads_far = [xswap(v) for v in heads_own]
    attention, branch = out_proj(ids, heads_own, heads_far, w_out)
    branch_far = xswap(branch)
    att_own, att_c, att_y = cut(ids, [attention, grad_mlp], [True, False])
    branch_far, att_own, att_c, att_y = fence(branch_far, att_own, att_c, att_y)
    att_came_y = yswap(att_y)
    att_came_c = cswap(att_c)
    hid_came_yc = cswap(after(hid_came_y, branch_far))
    hid_left = [(hid_own, 0), (hid_came_c, 0), (hid_came_y, 0), (hid_came_yc, 1)]
    inner, grads_in, mlp_in, middle, near, far, near_out, far_out = ffn(
        ids, [tokens, tok_far], [branch, branch_far], grad_mlp, mod, ffn_row, w_gate_up, came, w_down
    )
    inner, grads_in, mlp_in, near, far, att_came_y, att_came_c, hid_came_yc = fence(
        inner, grads_in, mlp_in, near, far, att_came_y, att_came_c, hid_came_yc
    )
    hid_left[3] = (hid_came_yc, 1)

    received = xswap(far)
    inner_y = yswap(inner)
    inner_c = cswap(inner)
    grads_c = cswap(grads_in)
    att_came_yc = cswap(att_came_y)
    att_left = [(att_own, 0), (att_came_c, 0), (att_came_y, 0), (att_came_yc, 1)]
    ffn_own, ffn_c, ffn_y = cut(ids, [mlp_in], [False])
    received, ffn_own, inner_c, grads_c, att_came_yc = fence(
        received, ffn_own, inner_c, grads_c, att_came_yc
    )
    att_left[3] = (att_came_yc, 1)
    (sums, grad_branch, mid_near, mid_far), near_heads, far_heads = mid_back(
        ids, near, received, middle, [cotangent, cot_far], branch, mod, ffn_row, w_out
    )
    recv_a = xswap(far_heads[0])
    recv_b = xswap(far_heads[1])
    ffn_came_c = cswap(after(ffn_c, far_heads[0]))
    branch_c = cswap(after(grad_branch, far_heads[0]))
    recv_a, ffn_came_c, branch_c = fence(recv_a, ffn_came_c, branch_c)
    grad_1, grad_2 = add_pair(near_heads[0], recv_a)
    grad_3, grad_0 = add_pair(near_heads[1], after(recv_b, grad_1))
    inner_y = after(inner_y, grad_0)
    inner_yc = cswap(inner_y)
    branch_y = yswap(after(grad_branch, inner_y))
    ffn_came_y = yswap(after(ffn_y, inner_y))
    inner_all = [inner, inner_c, inner_y, inner_yc]
    tile = 512
    per = units // tile
    grad_here = spread([grad_0, grad_1, grad_2, grad_3])
    total = units + local_width
    parts_inner = weight_grads(att_left, inner_all, False, tile, 1, total, lambda i: i)
    parts_inner, branch_y, ffn_came_y, *grad_here = fence(
        parts_inner, branch_y, ffn_came_y, *grad_here
    )
    ffn_came_yc = cswap(ffn_came_y)
    branch_all = [grad_branch, branch_c, branch_y, cswap(branch_y)]
    step = 256
    parts_inner = weight_grads(
        att_left, branch_all, False, step, 0, total, lambda i: i + units // step, parts_inner
    )
    sum_inner = scatter(parts_inner)
    ffn_left = [(ffn_own, 0), (ffn_came_c, 0), (ffn_came_y, 0), (ffn_came_yc, 1)]
    grads_op, out_op, mid_op, grad_here[0], ffn_came_yc, _ = fence(
        grads_in, far_out, mid_far, grad_here[0], ffn_came_yc, parts_inner
    )
    grads_y = yswap(grads_op)
    out_recv = xswap(out_op)
    mid_came = xswap(mid_op)
    grads_q, (q_gain_part, cap_keep, cap_send, gate_part), grads_kv = attend_back(
        ids, clip_slices, caption_lengths, gates, q_here, grad_here, saved, cap_kv, gains, cosine, sine
    )
    grads_q, grads_kv, cap_send, grads_y, out_recv, mid_came = fence(
        grads_q, grads_kv, cap_send, grads_y, out_recv, mid_came
    )

    kv_c3, grads_yc = cswap(grads_kv[3]), cswap(grads_y)
    kv_c1, cap_c = cswap(grads_kv[1]), cswap(cap_send)
    away = (grads_kv[2].astype(F32) + kv_c3.astype(F32)).astype(BF)
    away, grads_yc, kv_c1, cap_c, *grads_q = fence(away, grads_yc, kv_c1, cap_c, *grads_q)
    away_here = yswap(away)
    back_q = unspread(grads_q)
    here = (grads_kv[0].astype(F32) + kv_c1.astype(F32)).astype(BF)
    pair = cap_keep + cap_c
    grads_all = [grads_in, grads_c, grads_y, grads_yc]
    parts_a = weight_grads(ffn_left, grads_all, False, tile, 0, 2 * units, lambda i: i)
    output, early = output_sums(ids, clip_slices, near_out, out_recv, middle, cotangent, mod, sums)
    away_here, output, parts_a, here, pair, sum_inner, *back_q = fence(
        away_here, output, parts_a, here, pair, sum_inner, *back_q
    )
    back_kv, k_gain_part = keys_back(ids, clip_slices, here, away_here, kv_own, gains, cosine, sine)
    back_kv, k_gain_part = fence(back_kv, k_gain_part)
    back_kv = fence(*unspread(back_kv))
    sum_a = scatter(after(parts_a, *back_kv))

    packed, send = pack(ids, back_q, back_kv)
    packed, send = fence(packed, send)
    packed_recv = xswap(send)
    packed_y = yswap(packed)
    packed_c = cswap(packed)
    cap_y = yswap(after(pick(pair, 1 - y), packed))
    cap_total = pick(pair, y) + cap_y
    raw_cap, cap_gain_part = caption_back(ids, cap_total, cap_raw, gains)
    packed_recv, packed_c, raw_cap, cap_gain_part = fence(packed_recv, packed_c, raw_cap, cap_gain_part)
    recv_y = yswap(packed_recv)
    recv_c = cswap(packed_recv)
    tok_near, tok_send = qkv_back(ids, packed, packed_recv, w_qkv)
    packed_y, recv_c, tok_near, tok_send, raw_cap = fence(
        packed_y, recv_c, tok_near, tok_send, raw_cap
    )
    tok_recv = xswap(tok_send)
    raw_y, raw_c = yswap(raw_cap), cswap(raw_cap)
    packed_all = [packed, packed_c, packed_y, cswap(packed_y)]
    tile = 384
    parts_c = weight_grads(
        hid_left, packed_all, True, tile, 0, 3 * local_width, lambda i: jnp.where(i < 2, i, i + 2)
    )
    recv_y = after(recv_y, parts_c)
    recv_all = [packed_recv, recv_c, recv_y, cswap(recv_y)]
    parts_c = weight_grads(
        hid_left, recv_all, True, tile, 0, 3 * local_width, lambda i: i + 2, parts_c
    )
    tok_recv, parts_c, raw_y, raw_c = fence(tok_recv, parts_c, raw_y, raw_c)

    def line_first(parts):
        to_right, to_left = pick(parts, LINE - 1), pick(parts, 0)
        ends, last = range(GROUP), bucket_count - 1
        right_in = lax.ppermute(to_right, BUCKET, [(i, i + GROUP) for i in ends])
        left_in = lax.ppermute(to_left, BUCKET, [(last - i, last - i - GROUP) for i in ends])
        return right_in, left_in

    def line_next(parts, t, right_in, left_in):
        to_right = pick(parts, jnp.clip(LINE - t + z, 0, LINE - 1))
        to_left = pick(parts, jnp.clip(t - LINE + z, 0, LINE - 1))
        to_right = (to_right.astype(F32) + right_in.astype(F32)).astype(BF)
        to_left = (to_left.astype(F32) + left_in.astype(F32)).astype(BF)
        ends, last = range(GROUP * t), bucket_count - 1
        right_in = lax.ppermute(to_right, BUCKET, [(i, i + GROUP) for i in ends])
        left_in = lax.ppermute(to_left, BUCKET, [(last - i, last - i - GROUP) for i in ends])
        return right_in, left_in

    line = line_first(parts_c)
    token_grad, late = tokens_back(
        ids,
        clip_slices,
        tokens,
        tok_near,
        tok_recv,
        mid_near,
        mid_came,
        mod,
        norm_row,
        [q_gain_part, k_gain_part, cap_gain_part, gate_part, early],
    )
    token_grad, late, *line = fence(token_grad, late, *line)
    line = line_next(parts_c, 2, *line)
    late = late + cswap(late)
    late = late + yswap(late)
    late = late + hop(late, lambda i: i ^ GROUP)
    raw_yc = cswap(after(raw_y, late))
    late, raw_yc, *line = fence(late, raw_yc, *line)
    line = line_next(parts_c, 3, *line)
    late = late + hop(late, lambda i: i ^ (2 * GROUP))
    late_far = xswap(late)
    late_far, sum_a, *line = fence(late_far, sum_a, *line)
    sum_c = pick(parts_c, z).astype(F32) + line[0].astype(F32) + line[1].astype(F32)
    cap_parts = caption_weights(ids, [after(raw_cap, late), raw_c, raw_y, raw_yc], caption_rows)
    cap_parts = unspread(cap_parts)
    caption_w_grad = caption_join(ids, cap_parts)
    late_sum = late

    mod_grad, gain_rows = finish(ids, late_sum, late_far)
    mod_mine = mod_grad.astype(BF)
    cols_local = CD // bucket_count
    act_cols = lax.dynamic_slice_in_dim(activation, b * cols_local, cols_local, 1)
    ada_grad = mm(mod_mine, act_cols, TN)
    cond_part = mm(mod_mine, ada_w, NN)
    cond_sigmoid = jax.nn.sigmoid(cond)
    cond_grad = (
        (cond_part + xswap(cond_part)) * cond_sigmoid * (1.0 + cond * (1.0 - cond_sigmoid))
    )
    heads_each = H // seq_count
    cross_out = jnp.concatenate(
        [gain_rows[5, :heads_each], gain_rows[5, local_width : local_width + heads_each]]
    )

    down_out = sum_inner[:, :units].astype(F32).T
    kept_out = sum_a[:, :units].astype(F32)
    came_out = xswap(sum_a[:, units:]).astype(F32)
    gate_up_out = jnp.where(
        s == 0,
        jnp.concatenate([kept_out, came_out], 1),
        jnp.concatenate([came_out, kept_out], 1),
    ).T
    return (
        output,
        token_grad,
        cond_grad,
        ada_grad,
        gain_rows[0],
        sum_c.T,
        gain_rows[1],
        gain_rows[2],
        caption_w_grad,
        gain_rows[3],
        cross_out,
        sum_inner[:, units:].astype(F32).T,
        gain_rows[4],
        gate_up_out,
        down_out,
    )


def project(activations, weight):
    return lax.dot_general(
        activations, weight, (((1,), (1,)), ((), ())), preferred_element_type=jnp.float32
    )


def clip_of(rows, ends):
    return jnp.sum((rows[:, None] >= ends[None, :]).astype(jnp.int32), axis=1)


def head_norm(values, gains, head_count):
    row_count = values.shape[0]
    split = values.reshape(row_count, head_count, -1)
    inverse = lax.rsqrt(jnp.mean(split * split, axis=-1, keepdims=True) + EPSILON)
    unit_rows = split * inverse
    return (unit_rows.reshape(row_count, -1) * gains, unit_rows, inverse)


def head_norm_back(norm_grads, gains, unit_rows, inverse):
    row_count, head_count, head_width = unit_rows.shape
    gain_grad = jnp.sum(norm_grads * unit_rows.reshape(row_count, -1), axis=0)
    unit_grad = (norm_grads * gains).reshape(row_count, head_count, head_width)
    raw_grad = inverse * (
        unit_grad - unit_rows * jnp.mean(unit_grad * unit_rows, axis=-1, keepdims=True)
    )
    return (raw_grad.reshape(row_count, -1), gain_grad)


def rotate(values, positions, head_count):
    row_count = values.shape[0]
    split = values.reshape(row_count, head_count, -1)
    half_width = split.shape[-1] // 2
    frequency = jnp.exp(
        jnp.arange(half_width, dtype=jnp.float32) * (-2.0 * math.log(10000.0) / (2 * half_width))
    )
    angles = positions[:, None] * frequency[None, :]
    cosine = jnp.cos(angles)[:, None, :]
    sine = jnp.sin(angles)[:, None, :]
    first_half = split[..., :half_width]
    second_half = split[..., half_width:]
    turned = jnp.concatenate(
        [first_half * cosine - second_half * sine, first_half * sine + second_half * cosine],
        axis=-1,
    )
    return turned.reshape(row_count, -1)


def block_size(row_count):
    return 512 if row_count % 512 == 0 else row_count


def general_body(
    tokens,
    cotangent,
    clip_slices,
    caption_lengths,
    caption,
    cond,
    ada_w,
    norm_gain,
    w_qkv,
    q_gain,
    k_gain,
    w_caption,
    ky_gain,
    cross_gate,
    w_out,
    ffn_gain,
    w_gate_up,
    w_down,
):
    seq_count = lax.axis_size("seq")
    bucket_count = lax.axis_size("bucket")
    tok_rows = tokens.shape[0]
    slice_rows = tok_rows * seq_count
    total_rows = slice_rows * bucket_count
    local_heads = H // seq_count
    local_width = local_heads * HD
    score_scale = HD ** (-0.5)
    bucket_id = lax.axis_index("bucket")
    seq_id = lax.axis_index("seq")
    ends = jnp.cumsum(clip_slices) * slice_rows
    starts = ends - clip_slices * slice_rows
    my_clip = clip_of(jnp.reshape(bucket_id * slice_rows, (1,)), ends)[0]
    clip_mask = jnp.arange(CLIPS) == my_clip
    clip_start = jnp.sum(jnp.where(clip_mask, starts, 0))
    first_token = (bucket_id * seq_count + seq_id) * tok_rows
    positions = (first_token + jnp.arange(tok_rows, dtype=jnp.int32) - clip_start).astype(
        jnp.float32
    )
    caption_usable = jnp.arange(CAP) < jnp.sum(jnp.where(clip_mask, caption_lengths, 0))
    head_first = seq_id * local_width
    gates_local = jnp.tanh(lax.dynamic_slice_in_dim(cross_gate, seq_id * local_heads, local_heads))
    ky_gain_local = lax.dynamic_slice_in_dim(ky_gain, head_first, local_width)
    activation = jax.nn.silu(cond).astype(jnp.bfloat16)
    cond_row = lax.dynamic_index_in_dim(activation, my_clip, 0, True)
    caption_rows = lax.dynamic_index_in_dim(caption, my_clip, 0, False)
    caption_raw = jnp.einsum(
        "ty,jdy->jtd", caption_rows, w_caption, preferred_element_type=jnp.float32
    )
    caption_norm, caption_unit, caption_inverse = head_norm(
        caption_raw[0], ky_gain_local, local_heads
    )
    caption_keys = caption_norm.astype(jnp.bfloat16).reshape(CAP, local_heads, HD)
    caption_values = caption_raw[1].astype(jnp.bfloat16).reshape(CAP, local_heads, HD)
    inputs = tokens.astype(jnp.float32)

    def key_usable(first_row, row_count):
        return clip_of(first_row + jnp.arange(row_count, dtype=jnp.int32), ends) == my_clip

    def fold_keys(queries3, running, segment, first_row):
        seg_keys, seg_values = segment
        row_count = seg_keys.shape[0]
        key_rows = block_size(row_count)
        steps_count = row_count // key_rows
        usable = key_usable(first_row, row_count).reshape(steps_count, key_rows)
        key_blocks = seg_keys.reshape(steps_count, key_rows, local_heads, HD)
        value_blocks = seg_values.reshape(steps_count, key_rows, local_heads, HD)

        def update(state, item):
            key_block, value_block, usable_block = item

            def update_include(inner):
                row_max, row_total, accum = inner
                scores = (
                    jnp.einsum(
                        "qhd,khd->hqk", queries3, key_block, preferred_element_type=jnp.float32
                    )
                    * score_scale
                )
                scores = jnp.where(usable_block[None, None, :], scores, MASKED)
                new_max = jnp.maximum(row_max, jnp.max(scores, axis=-1))
                factor = jnp.exp(row_max - new_max)
                weights = jnp.exp(scores - new_max[..., None])
                row_total = row_total * factor + jnp.sum(weights, axis=-1)
                accum = accum * factor.T[:, :, None] + jnp.einsum(
                    "hqk,khd->qhd",
                    weights.astype(jnp.bfloat16),
                    value_block,
                    preferred_element_type=jnp.float32,
                )
                return (new_max, row_total, accum)

            return (
                lax.cond(jnp.any(usable_block), update_include, lambda inner: inner, state),
                None,
            )

        running, unused = lax.scan(update, running, (key_blocks, value_blocks, usable))
        return running

    def local_fold(queries3, running, keys_whole):

        def local_visit(state, piece_index):
            first_row = piece_index * slice_rows
            segment = (
                lax.dynamic_slice_in_dim(keys_whole[0], first_row, slice_rows, 0),
                lax.dynamic_slice_in_dim(keys_whole[1], first_row, slice_rows, 0),
            )
            return (fold_keys(queries3, state, segment, first_row), None)

        running, unused = lax.scan(local_visit, running, jnp.arange(bucket_count, dtype=jnp.int32))
        return running

    def forward(qkv_full, out_full, modulation, second):
        shift_vec = modulation[:D]
        scale_vec = modulation[D : 2 * D]
        gate_vec = modulation[2 * D : 3 * D]
        inverse = lax.rsqrt(jnp.mean(inputs * inputs, axis=-1, keepdims=True) + EPSILON)
        unit_rows = inputs * inverse
        hidden = (unit_rows * norm_gain * (1.0 + scale_vec) + shift_vec).astype(jnp.bfloat16)
        projected = project(hidden, qkv_full)
        query_norm, query_unit, query_inverse = head_norm(projected[:, :D], q_gain, H)
        key_norm, key_unit, key_inverse = head_norm(projected[:, D : 2 * D], k_gain, H)
        queries = rotate(query_norm, positions, H).astype(jnp.bfloat16)
        keys_tok = rotate(key_norm, positions, H).astype(jnp.bfloat16)
        values_tok = projected[:, 2 * D :].astype(jnp.bfloat16)
        head_queries, head_keys, head_values = (
            lax.all_to_all(queries, "seq", split_axis=1, concat_axis=0, tiled=True),
            lax.all_to_all(keys_tok, "seq", split_axis=1, concat_axis=0, tiled=True),
            lax.all_to_all(values_tok, "seq", split_axis=1, concat_axis=0, tiled=True),
        )
        queries3 = head_queries.reshape(slice_rows, local_heads, HD)
        start_state = (
            jnp.full((local_heads, slice_rows), MASKED, jnp.float32),
            jnp.zeros((local_heads, slice_rows), jnp.float32),
            jnp.zeros((slice_rows, local_heads, HD), jnp.float32),
        )
        folder = functools.partial(fold_keys, queries3)
        if second:
            keys_whole = (
                lax.all_gather(head_keys, "bucket", axis=0, tiled=True),
                lax.all_gather(head_values, "bucket", axis=0, tiled=True),
            )
            final_state = local_fold(queries3, start_state, keys_whole)
        else:
            keys_whole = None
            final_state = folder(
                start_state,
                (
                    lax.all_gather(head_keys, "bucket", axis=0, tiled=True),
                    lax.all_gather(head_values, "bucket", axis=0, tiled=True),
                ),
                jnp.int32(0),
            )
        row_max, row_total, accum = final_state
        own = accum / row_total.T[:, :, None]
        cross_scores = (
            jnp.einsum("qhd,khd->hqk", queries3, caption_keys, preferred_element_type=jnp.float32)
            * score_scale
        )
        cross_prob = jax.nn.softmax(
            jnp.where(caption_usable[None, None, :], cross_scores, MASKED), axis=-1
        )
        other = jnp.einsum(
            "hqk,khd->qhd",
            cross_prob.astype(jnp.bfloat16),
            caption_values,
            preferred_element_type=jnp.float32,
        )
        combined = (
            (own + gates_local[None, :, None] * other)
            .reshape(slice_rows, local_width)
            .astype(jnp.bfloat16)
        )
        attention = lax.all_to_all(combined, "seq", split_axis=0, concat_axis=1, tiled=True)
        branch = project(attention, out_full)
        return dict(
            gate_vec=gate_vec,
            scale_vec=scale_vec,
            inverse=inverse,
            unit_rows=unit_rows,
            hidden=hidden,
            query_unit=query_unit,
            query_inverse=query_inverse,
            key_unit=key_unit,
            key_inverse=key_inverse,
            queries3=queries3,
            own_keys3=head_keys.reshape(slice_rows, local_heads, HD),
            own_values3=head_values.reshape(slice_rows, local_heads, HD),
            keys_whole=keys_whole,
            row_log=row_max + jnp.log(row_total),
            own=own,
            other=other,
            cross_prob=cross_prob,
            attention=attention,
            branch=branch,
            output=inputs + gate_vec * branch,
        )

    gathered = (
        lax.all_gather(ada_w, "seq", axis=0, tiled=True),
        lax.all_gather(w_qkv, "seq", axis=0, tiled=True),
        lax.all_gather(w_out, "seq", axis=0, tiled=True),
        lax.all_gather(w_gate_up, "seq", axis=0, tiled=True),
        lax.all_gather(w_down, "seq", axis=0, tiled=True),
    )
    modulation = project(cond_row, gathered[0])[0]
    first_pass = forward(gathered[1], gathered[2], modulation, False)
    middle = first_pass["output"]
    shift_mlp = modulation[3 * D : 4 * D]
    scale_mlp = modulation[4 * D : 5 * D]
    gate_mlp = modulation[5 * D :]
    mid_inverse = lax.rsqrt(jnp.mean(middle * middle, axis=-1, keepdims=True) + EPSILON)
    mid_unit = middle * mid_inverse
    mlp_in = (mid_unit * ffn_gain * (1.0 + scale_mlp) + shift_mlp).astype(jnp.bfloat16)
    gate_up = project(mlp_in, gathered[3])
    gate_half = gate_up[:, :FF]
    up_half = gate_up[:, FF:]
    gate_sigmoid = jax.nn.sigmoid(gate_half)
    silu_gate = gate_half * gate_sigmoid
    inner = (silu_gate * up_half).astype(jnp.bfloat16)
    mlp_branch = jnp.dot(inner, gathered[4], preferred_element_type=jnp.float32)
    output = (middle + gate_mlp * mlp_branch).astype(jnp.bfloat16)
    regathered = (
        lax.all_gather(ada_w, "seq", axis=0, tiled=True),
        lax.all_gather(w_qkv, "seq", axis=0, tiled=True),
        lax.all_gather(w_out, "seq", axis=0, tiled=True),
        lax.all_gather(w_gate_up, "seq", axis=0, tiled=True),
        lax.all_gather(w_down, "seq", axis=0, tiled=True),
    )
    second_pass = forward(regathered[1], regathered[2], modulation, True)
    ada_full, qkv_full, out_full, gate_up_full, down_full = regathered
    grad_out = cotangent.astype(jnp.float32)
    mlp_gate_grad = jnp.sum(grad_out * mlp_branch, axis=0)
    grad_mlp = (grad_out * gate_mlp).astype(jnp.bfloat16)
    grad_inner = lax.dot_general(
        grad_mlp, down_full, (((1,), (1,)), ((), ())), preferred_element_type=jnp.float32
    )
    grad_gate_half = grad_inner * up_half * gate_sigmoid * (1.0 + gate_half * (1.0 - gate_sigmoid))
    grad_up_half = grad_inner * silu_gate
    grad_gate_up = jnp.concatenate([grad_gate_half, grad_up_half], axis=1).astype(jnp.bfloat16)
    mlp_in_grad = jnp.dot(grad_gate_up, gate_up_full, preferred_element_type=jnp.float32)
    ffn_gain_grad = jnp.sum(mlp_in_grad * (1.0 + scale_mlp) * mid_unit, axis=0)
    shift_mlp_grad = jnp.sum(mlp_in_grad, axis=0)
    scale_mlp_grad = jnp.sum(mlp_in_grad * mid_unit * ffn_gain, axis=0)
    mid_unit_grad = mlp_in_grad * ffn_gain * (1.0 + scale_mlp)
    residual_grad = (
        mid_inverse
        * (mid_unit_grad - mid_unit * jnp.mean(mid_unit_grad * mid_unit, axis=-1, keepdims=True))
        + grad_out
    )
    gate_grad = jnp.sum(residual_grad * second_pass["branch"], axis=0)
    grad_branch = (residual_grad * second_pass["gate_vec"]).astype(jnp.bfloat16)
    attention = second_pass["attention"]
    grad_attention = jnp.dot(grad_branch, out_full, preferred_element_type=jnp.float32).astype(
        jnp.bfloat16
    )
    grad_heads = lax.all_to_all(grad_attention, "seq", split_axis=1, concat_axis=0, tiled=True)
    grad_own16 = grad_heads.reshape(slice_rows, local_heads, HD)
    grad_own = grad_own16.astype(jnp.float32)
    queries3 = second_pass["queries3"]
    own = second_pass["own"]
    other = second_pass["other"]
    cross_prob = second_pass["cross_prob"]
    grad_other = (grad_own * gates_local[None, :, None]).astype(jnp.bfloat16)
    gate_grad_local = jnp.sum(grad_own * other, axis=(0, 2)) * (1.0 - gates_local * gates_local)
    grad_cross_prob = jnp.einsum(
        "qhd,khd->hqk", grad_other, caption_values, preferred_element_type=jnp.float32
    )
    grad_cross = (
        cross_prob
        * (grad_cross_prob - jnp.sum(cross_prob * grad_cross_prob, axis=-1, keepdims=True))
    ).astype(jnp.bfloat16)
    cross_query_grad = score_scale * jnp.einsum(
        "hqk,khd->qhd", grad_cross, caption_keys, preferred_element_type=jnp.float32
    )
    caption_key_grad = score_scale * jnp.einsum(
        "hqk,qhd->khd", grad_cross, queries3, preferred_element_type=jnp.float32
    )
    caption_value_grad = jnp.einsum(
        "hqk,qhd->khd",
        cross_prob.astype(jnp.bfloat16),
        grad_other,
        preferred_element_type=jnp.float32,
    )
    row_delta = jnp.sum(grad_own * own, axis=-1).T
    row_log = second_pass["row_log"]
    keys_whole = second_pass["keys_whole"]

    def grad_piece(query_grad, piece_index, with_keys):
        first_row = piece_index * slice_rows
        key_rows = block_size(slice_rows)
        steps_count = slice_rows // key_rows
        key_blocks = lax.dynamic_slice_in_dim(keys_whole[0], first_row, slice_rows, 0).reshape(
            steps_count, key_rows, local_heads, HD
        )
        value_blocks = lax.dynamic_slice_in_dim(keys_whole[1], first_row, slice_rows, 0).reshape(
            steps_count, key_rows, local_heads, HD
        )
        usable = key_usable(first_row, slice_rows).reshape(steps_count, key_rows)

        def grad_visit(accum, item):
            key_block, value_block, usable_block = item

            def grad_include(inner):
                scores = (
                    jnp.einsum(
                        "qhd,khd->hqk", queries3, key_block, preferred_element_type=jnp.float32
                    )
                    * score_scale
                )
                scores = jnp.where(usable_block[None, None, :], scores, MASKED)
                probability = jnp.exp(scores - row_log[..., None])
                grad_prob = jnp.einsum(
                    "qhd,khd->hqk", grad_own16, value_block, preferred_element_type=jnp.float32
                )
                grad_scores = (probability * (grad_prob - row_delta[..., None])).astype(
                    jnp.bfloat16
                )
                updated = inner + score_scale * jnp.einsum(
                    "hqk,khd->qhd", grad_scores, key_block, preferred_element_type=jnp.float32
                )
                key_grad = score_scale * jnp.einsum(
                    "hqk,qhd->khd", grad_scores, queries3, preferred_element_type=jnp.float32
                )
                value_grad = jnp.einsum(
                    "hqk,qhd->khd",
                    probability.astype(jnp.bfloat16),
                    grad_own16,
                    preferred_element_type=jnp.float32,
                )
                return (updated, key_grad, value_grad)

            def skip(inner):
                empty = jnp.zeros((key_rows, local_heads, HD), jnp.float32)
                return (inner, empty, empty)

            updated, key_grad, value_grad = lax.cond(
                jnp.any(usable_block), grad_include, skip, accum
            )
            return (updated, (key_grad, value_grad))

        query_grad, (key_grads, value_grads) = lax.scan(
            grad_visit, query_grad, (key_blocks, value_blocks, usable)
        )
        return (
            query_grad,
            (
                key_grads.reshape(slice_rows, local_width),
                value_grads.reshape(slice_rows, local_width),
            ),
        )

    query_start = jnp.zeros((slice_rows, local_heads, HD), jnp.float32)
    piece_order = jnp.arange(bucket_count, dtype=jnp.int32)
    self_query_grad, (key_terms, value_terms) = lax.scan(
        functools.partial(grad_piece, with_keys=True), query_start, piece_order
    )
    key_sum, value_sum = (
        lax.psum_scatter(
            key_terms.reshape(total_rows, local_width).astype(jnp.bfloat16),
            "bucket",
            scatter_dimension=0,
            tiled=True,
        ).astype(jnp.float32),
        lax.psum_scatter(
            value_terms.reshape(total_rows, local_width).astype(jnp.bfloat16),
            "bucket",
            scatter_dimension=0,
            tiled=True,
        ).astype(jnp.float32),
    )
    query_grad16 = (
        (self_query_grad + cross_query_grad).reshape(slice_rows, local_width).astype(jnp.bfloat16)
    )
    tok_query_grad, tok_key_grad, tok_value_grad = (
        lax.all_to_all(query_grad16, "seq", split_axis=0, concat_axis=1, tiled=True),
        lax.all_to_all(
            key_sum.astype(jnp.bfloat16), "seq", split_axis=0, concat_axis=1, tiled=True
        ),
        lax.all_to_all(
            value_sum.astype(jnp.bfloat16), "seq", split_axis=0, concat_axis=1, tiled=True
        ),
    )
    query_raw_grad, q_gain_grad = head_norm_back(
        rotate(tok_query_grad.astype(jnp.float32), -positions, H),
        q_gain,
        second_pass["query_unit"],
        second_pass["query_inverse"],
    )
    key_raw_grad, k_gain_grad = head_norm_back(
        rotate(tok_key_grad.astype(jnp.float32), -positions, H),
        k_gain,
        second_pass["key_unit"],
        second_pass["key_inverse"],
    )
    projected_grad = jnp.concatenate(
        [query_raw_grad, key_raw_grad, tok_value_grad.astype(jnp.float32)], axis=1
    ).astype(jnp.bfloat16)
    hidden = second_pass["hidden"]
    out_each = D // seq_count
    qkv_each = 3 * D // seq_count
    gate_up_each = 2 * FF // seq_count
    down_each = FF // seq_count
    rows_each = out_each + qkv_each + gate_up_each + down_each
    device_count = rows_each * lax.axis_size("seq") // rows_each
    first_device = jnp.int32(0) // rows_each

    def part(operand, partner, each):
        picked = lax.dynamic_slice_in_dim(operand, first_device * each, device_count * each, 1)
        term = lax.dot_general(
            picked, partner, (((0,), (0,)), ((), ())), preferred_element_type=jnp.float32
        )
        return term.reshape(device_count, each, D)

    terms = [
        part(grad_branch, attention, out_each),
        part(projected_grad, hidden, qkv_each),
        part(grad_gate_up, mlp_in, gate_up_each),
        part(inner, grad_mlp, down_each),
    ]
    weight_grad_seq = lax.psum_scatter(
        jnp.concatenate(terms, axis=1)
        .reshape(rows_each * lax.axis_size("seq"), D)
        .astype(jnp.bfloat16),
        "seq",
        scatter_dimension=0,
        tiled=True,
    )
    hidden_grad = jnp.dot(projected_grad, qkv_full, preferred_element_type=jnp.float32)
    unit_rows = second_pass["unit_rows"]
    scale_vec = second_pass["scale_vec"]
    inverse = second_pass["inverse"]
    norm_gain_grad = jnp.sum(hidden_grad * (1.0 + scale_vec) * unit_rows, axis=0)
    shift_grad = jnp.sum(hidden_grad, axis=0)
    scale_grad = jnp.sum(hidden_grad * unit_rows * norm_gain, axis=0)
    unit_grad = hidden_grad * norm_gain * (1.0 + scale_vec)
    token_grad = (
        inverse * (unit_grad - unit_rows * jnp.mean(unit_grad * unit_rows, axis=-1, keepdims=True))
        + residual_grad
    )
    modulation_grad = jnp.where(
        clip_mask[:, None],
        jnp.concatenate(
            [shift_grad, scale_grad, gate_grad, shift_mlp_grad, scale_mlp_grad, mlp_gate_grad]
        )[None, :],
        0.0,
    )
    ky_gain_part = jnp.sum(
        caption_key_grad.reshape(CAP, local_width) * caption_unit.reshape(CAP, local_width), axis=0
    )
    ky_gain_full = lax.dynamic_update_slice_in_dim(
        jnp.zeros((D,), jnp.float32), ky_gain_part, head_first, 0
    )
    gate_full = lax.dynamic_update_slice_in_dim(
        jnp.zeros((H,), jnp.float32), gate_grad_local, seq_id * local_heads, 0
    )
    caption_part = jnp.stack(
        [caption_key_grad.reshape(CAP, local_width), caption_value_grad.reshape(CAP, local_width)]
    )[None]
    zero_index = jnp.zeros((), jnp.int32)
    caption_full = lax.dynamic_update_slice(
        jnp.zeros((CLIPS, 2, CAP, D), jnp.float32),
        caption_part,
        (my_clip, zero_index, zero_index, head_first),
    )
    reduced = lax.psum(
        (
            norm_gain_grad,
            q_gain_grad,
            k_gain_grad,
            ky_gain_full,
            gate_full,
            modulation_grad,
            caption_full,
            ffn_gain_grad,
        ),
        ("bucket", "seq"),
    )
    modulation_total = reduced[5].astype(jnp.bfloat16)
    rows_local = 6 * D // seq_count
    cols_local = CD // bucket_count
    ada_grad = lax.dot_general(
        lax.dynamic_slice_in_dim(modulation_total, seq_id * rows_local, rows_local, 1),
        lax.dynamic_slice_in_dim(activation, bucket_id * cols_local, cols_local, 1),
        (((0,), (0,)), ((), ())),
        preferred_element_type=jnp.float32,
    )
    cond_sigmoid = jax.nn.sigmoid(cond)
    cond_grad = (
        jnp.dot(modulation_total, ada_full, preferred_element_type=jnp.float32)
        * cond_sigmoid
        * (1.0 + cond * (1.0 - cond_sigmoid))
    )
    caption_total = lax.dynamic_slice_in_dim(reduced[6], head_first, local_width, 3)
    raw_keys_all = jnp.einsum(
        "cty,dy->ctd", caption, w_caption[0], preferred_element_type=jnp.float32
    ).reshape(CLIPS * CAP, local_width)
    ignored, unit_all, inverse_all = head_norm(raw_keys_all, ky_gain_local, local_heads)
    raw_key_grad, unused_gain = head_norm_back(
        caption_total[:, 0].reshape(CLIPS * CAP, local_width), ky_gain_local, unit_all, inverse_all
    )
    raw_grad = jnp.stack(
        [raw_key_grad.reshape(CLIPS, CAP, local_width), caption_total[:, 1]], axis=1
    ).astype(jnp.bfloat16)
    caption_cols = lax.dynamic_slice_in_dim(
        caption, bucket_id * (YD // bucket_count), YD // bucket_count, 2
    )
    caption_w_grad = jnp.einsum(
        "cjtd,cty->jdy", raw_grad, caption_cols, preferred_element_type=jnp.float32
    )
    combined_grads = lax.psum_scatter(
        weight_grad_seq, "bucket", scatter_dimension=1, tiled=True
    ).astype(jnp.float32)
    out_grad_out = combined_grads[:out_each]
    qkv_grad_out = combined_grads[out_each : out_each + qkv_each]
    gate_up_grad_out = combined_grads[out_each + qkv_each : out_each + qkv_each + gate_up_each]
    down_grad_out = combined_grads[out_each + qkv_each + gate_up_each :]
    return (
        output,
        token_grad,
        cond_grad,
        ada_grad,
        reduced[0],
        qkv_grad_out,
        reduced[1],
        reduced[2],
        caption_w_grad,
        reduced[3],
        reduced[4],
        out_grad_out,
        reduced[7],
        gate_up_grad_out,
        down_grad_out,
    )


def solution(mesh):
    fits = mesh.shape["seq"] == 2 and mesh.shape["bucket"] == LINE * GROUP
    bucket = ("bucket",)
    if fits:
        bucket = BUCKET
        mesh = Mesh(mesh.devices.reshape(LINE, 2, GROUP // 2, 2), (*BUCKET, "seq"))
    in_specs = (
        P((*bucket, "seq"), None),
        P((*bucket, "seq"), None),
        P(),
        P(),
        P(),
        P(),
        P("seq", None),
        P(),
        P("seq", None),
        P(),
        P(),
        P(None, "seq", None),
        P(),
        P(),
        P("seq", None),
        P(),
        P("seq", None),
        P("seq", None),
    )
    out_specs = (
        P((*bucket, "seq"), None),
        P((*bucket, "seq"), None),
        P(),
        P("seq", bucket),
        P(),
        P("seq", bucket),
        P(),
        P(),
        P(None, "seq", bucket),
        P(),
        P(),
        P("seq", bucket),
        P(),
        P("seq", bucket),
        P("seq", bucket),
    )
    body = fast_body if fits else general_body
    return jax.shard_map(body, mesh=mesh, in_specs=in_specs, out_specs=out_specs, check_vma=False)
```

```python
import functools
import math

import jax
import jax.numpy as jnp
from jax import lax
from jax.experimental import pallas as pl
from jax.experimental.pallas import tpu as pltpu
from jax.sharding import Mesh, PartitionSpec as P

H = 24
HD = 64
D = 1536
FF = 4096
YD = 4096
CD = 1024
CAP = 128
CLIPS = 4

EPSILON = 1e-06
MASKED = -1e30
BF = jnp.bfloat16
F32 = jnp.float32
NN = (((1,), (0,)), ((), ()))
NT = (((1,), (1,)), ((), ()))
TN = (((0,), (0,)), ((), ()))
GROUP = 4
LINE = 4
BUCKET = ("z", "y", "c")
SENDS = (1, 2, 3, 0)
SMEM = pl.BlockSpec(memory_space=pltpu.SMEM)
VMEM = pl.BlockSpec(memory_space=pltpu.VMEM)
shape = jax.ShapeDtypeStruct


def cost(microseconds):
    return pl.CostEstimate(
        flops=0, transcendentals=0, bytes_accessed=int(microseconds * 20_000)
    )


def mm(a, b, dims):
    return lax.dot_general(a, b, dims, preferred_element_type=F32)


def clip_at(slices, slot):
    ends = [slices[0]]
    for i in range(1, CLIPS):
        ends.append(ends[-1] + slices[i])
    clip = jnp.int32(0)
    first, last = jnp.int32(0), ends[0]
    for i in range(CLIPS - 1):
        later = slot >= ends[i]
        clip = jnp.where(later, i + 1, clip)
        first = jnp.where(later, ends[i], first)
        last = jnp.where(later, ends[i + 1], last)
    return clip, first, last


def slot_of(bucket, k, j):
    return lax.rem(bucket // GROUP - k + LINE, LINE) * GROUP + jnp.bitwise_xor(
        lax.rem(bucket, GROUP), j
    )


def chunk_at(bucket, k, width):
    return pl.multiple_of(lax.rem(bucket // GROUP + k, LINE) * width, HD)


def norm_rope(raw, gain, cosine, sine):
    inverse = lax.rsqrt(jnp.mean(raw * raw, axis=0, keepdims=True) + EPSILON)
    normed = raw * inverse * gain
    half = raw.shape[0] // 2
    first, second = normed[:half], normed[half:]
    return jnp.concatenate(
        [first * cosine - second * sine, first * sine + second * cosine], axis=0
    )


def norm_rope_back(grad, raw, gain, cosine, sine):
    inverse = lax.rsqrt(jnp.mean(raw * raw, axis=0, keepdims=True) + EPSILON)
    unit = raw * inverse
    half = raw.shape[0] // 2
    first, second = grad[:half], grad[half:]
    turned = jnp.concatenate(
        [first * cosine + second * sine, second * cosine - first * sine], axis=0
    )
    gain_grad = jnp.sum(turned * unit, axis=1, keepdims=True)
    unit_grad = turned * gain
    raw_grad = inverse * (unit_grad - unit * jnp.mean(unit_grad * unit, axis=0, keepdims=True))
    return raw_grad, gain_grad


def row_inverse(values):
    return lax.rsqrt(jnp.mean(values * values, axis=-1, keepdims=True) + EPSILON)


def pre_kernel(ids, slices, tok_a, tok_b, mod_a, mod_b, gain_ref, w_ref, p_ref, hid_ref, mod_ref):
    @pl.when(pl.program_id(0) == 0)
    def _():
        s = ids[1]
        clip, _, _ = clip_at(slices, ids[0])
        row_a, row_b = mod_a[pl.ds(clip, 1), :], mod_b[pl.ds(clip, 1), :]
        low, high = jnp.where(s == 0, row_a, row_b), jnp.where(s == 0, row_b, row_a)
        mod_ref[...] = jnp.zeros_like(mod_ref)
        for i in range(3):
            mod_ref[i : i + 1, :] = low[:, i * D : (i + 1) * D]
            mod_ref[3 + i : 4 + i, :] = high[:, i * D : (i + 1) * D]
        shift, scale = mod_ref[0:1, :], mod_ref[1:2, :]
        count = tok_a.shape[0]
        for place, ref in ((s, tok_a), (1 - s, tok_b)):
            values = ref[...].astype(F32)
            hidden = values * row_inverse(values) * gain_ref[...] * (1.0 + scale) + shift
            hid_ref[pl.ds(pl.multiple_of(place * count, count), count), :] = hidden.astype(BF)

    p_ref[...] = mm(w_ref[...], hid_ref[...], NT).astype(BF)


def pre(ids, slices, tok_a, tok_b, mod_a, mod_b, gain, w_qkv):
    rows = 2 * tok_a.shape[0]
    tile = w_qkv.shape[0] // 3
    full = lambda v: pl.BlockSpec(v.shape, lambda i: (0,) * v.ndim)
    return pl.pallas_call(
        pre_kernel,
        grid=(w_qkv.shape[0] // tile,),
        in_specs=[SMEM, SMEM]
        + [full(v) for v in (tok_a, tok_b, mod_a, mod_b, gain)]
        + [pl.BlockSpec((tile, D), lambda i: (i, 0))],
        out_specs=[
            pl.BlockSpec((tile, rows), lambda i: (i, 0)),
            pl.BlockSpec((rows, D), lambda i: (0, 0)),
            pl.BlockSpec((8, D), lambda i: (0, 0)),
        ],
        out_shape=[shape((w_qkv.shape[0], rows), BF), shape((rows, D), BF), shape((8, D), F32)],
        name="pre",
        cost_estimate=cost(6),
    )(ids, slices, tok_a, tok_b, mod_a, mod_b, gain, w_qkv)


def route_kernel(ids, p_ref, r_ref, *outs):
    b, s = ids[0], ids[1]
    local = r_ref.shape[0]
    width = local // LINE
    for k in range(LINE):
        at = chunk_at(b, k, width)
        kv_ref, q_ref = outs[k], outs[LINE + k]

        @pl.when(s == 0)
        def _():
            q_ref[...] = p_ref[pl.ds(at, width), :]
            kv_ref[:width, :] = p_ref[pl.ds(2 * local + at, width), :]
            kv_ref[width:, :] = r_ref[pl.ds(at, width), :]

        @pl.when(s == 1)
        def _():
            q_ref[...] = r_ref[pl.ds(at, width), :]
            kv_ref[:width, :] = p_ref[pl.ds(at, width), :]
            kv_ref[width:, :] = p_ref[pl.ds(2 * local + at, width), :]


def route(ids, projected, received):
    local, rows = received.shape
    width = local // LINE
    outs = pl.pallas_call(
        route_kernel,
        in_specs=[SMEM, VMEM, VMEM],
        out_specs=[VMEM] * (2 * LINE),
        out_shape=[shape((2 * width, rows), BF)] * LINE + [shape((width, rows), BF)] * LINE,
        name="route",
        cost_estimate=cost(2.5),
    )(ids, projected, received)
    return outs[:LINE], outs[LINE:]


def caption_kernel(ids, w_ref, cap_ref, gains_ref, raw_ref, kv_ref):
    step = pl.program_id(0)
    width = w_ref.shape[1]

    @pl.when(step == 0)
    def _():
        raw_ref[...] = jnp.zeros_like(raw_ref)

    for j in range(2):
        raw_ref[j * width : (j + 1) * width, :] += mm(w_ref[j], cap_ref[...], NT)

    @pl.when(step == pl.num_programs(0) - 1)
    def _():
        base = ids[1] * LINE * width + ids[0] // GROUP * width
        for h in range(width // HD):
            at = slice(h * HD, h * HD + HD)
            raw = raw_ref[at, :]
            inverse = lax.rsqrt(jnp.mean(raw * raw, axis=0, keepdims=True) + EPSILON)
            gain = gains_ref[pl.ds(pl.multiple_of(base + h * HD, HD), HD), 2:3]
            keys = (raw * inverse * gain).astype(BF)
            for c in range(CLIPS):
                kv_ref[c, at, :] = keys[:, c * CAP : (c + 1) * CAP]
        for c in range(CLIPS):
            kv_ref[c, width:, :] = raw_ref[width:, c * CAP : (c + 1) * CAP].astype(BF)


def caption_keys(ids, w_caption, caption, gains):
    width = w_caption.shape[1] // LINE
    tile = 1024
    count = caption.shape[0]
    return pl.pallas_call(
        caption_kernel,
        grid_spec=pltpu.PrefetchScalarGridSpec(
            num_scalar_prefetch=1,
            grid=(YD // tile,),
            in_specs=[
                pl.BlockSpec((2, width, tile), lambda i, ids: (0, ids[0] // GROUP, i)),
                pl.BlockSpec((count, tile), lambda i, ids: (0, i)),
                pl.BlockSpec(gains.shape, lambda i, ids: (0, 0)),
            ],
            out_specs=[
                pl.BlockSpec((2 * width, count), lambda i, ids: (0, 0)),
                pl.BlockSpec((CLIPS, 2 * width, CAP), lambda i, ids: (0, 0, 0)),
            ],
        ),
        out_shape=[shape((2 * width, count), F32), shape((CLIPS, 2 * width, CAP), BF)],
        name="caption_keys",
        cost_estimate=cost(8),
    )(ids, w_caption, caption, gains)


def attend_kernel(ids, slices, lengths, gates, *refs):
    q_refs = refs[:LINE]
    kv_refs = refs[LINE : LINE + GROUP]
    cap_ref, gains_ref, cos_ref, sin_ref = refs[LINE + GROUP : LINE + GROUP + 4]
    outs = refs[LINE + GROUP + 4 :]
    comb_refs = outs[:LINE]
    own_ref, other_ref, stat_ref, qs_ref, ks_ref, pair_ref = outs[LINE : LINE + 6]
    value_ref, cap_value_ref, sum_ref = outs[LINE + 6 :]
    b, s = ids[0], ids[1]
    width, rows = q_refs[0].shape
    heads = width // HD
    scale = HD**-0.5
    base = s * LINE * width + b // GROUP * width

    def gain_of(h, column):
        return gains_ref[pl.ds(pl.multiple_of(base + h * HD, HD), HD), column : column + 1]

    key_gains = [gain_of(h, 1) for h in range(heads)]
    query_gains = [gain_of(h, 0) for h in range(heads)]
    is_one = lax.broadcasted_iota(jnp.int32, (rows, 2 * HD), 1) < HD
    for j, kv_ref in enumerate(kv_refs):
        for k in range(LINE):
            slot = slot_of(b, k, j)
            _, start, _ = clip_at(slices, slot)
            cosine, sine = cos_ref[slot - start], sin_ref[slot - start]
            for h in range(heads):
                at = slice(h * HD, h * HD + HD)
                raw = kv_ref[k, at, :].astype(F32)
                keys = norm_rope(raw, key_gains[h], cosine, sine)
                values = kv_ref[k, width + h * HD : width + h * HD + HD, :].astype(F32)
                ks_ref[slot, at, :] = keys.astype(BF)
                pair = jnp.concatenate([keys, values], axis=0).T
                pair_ref[slot, h] = pair.astype(BF)
                value_ref[slot, h] = jnp.where(is_one, 1.0, pair).astype(BF)
    cap_one = is_one[:CAP]
    for c in range(CLIPS):
        for h in range(heads):
            values = cap_ref[c, width + h * HD : width + h * HD + HD, :].astype(F32)
            both = jnp.concatenate([values, values], axis=0).T
            cap_value_ref[c, h] = jnp.where(cap_one, 1.0, both).astype(BF)

    for i in range(LINE):
        slot = slot_of(b, i, 0)
        clip, first, last = clip_at(slices, slot)
        cosine, sine = cos_ref[slot - first], sin_ref[slot - first]
        queries = []
        for h in range(heads):
            at = slice(h * HD, h * HD + HD)
            raw = q_refs[i][at, :].astype(F32)
            turned = norm_rope(raw, query_gains[h], cosine, sine).astype(BF).astype(F32) * scale
            qs_ref[i, at, :] = turned.astype(BF)
            queries.append(turned.T.astype(BF))
        sum_ref[...] = jnp.zeros_like(sum_ref)

        def step(n, carry):
            for h in range(heads):
                at = slice(h * HD, h * HD + HD)
                weights = jnp.exp(mm(queries[h], ks_ref[n, at, :], NN))
                sum_ref[h] += mm(weights.astype(BF), value_ref[n, h], NN)
            return carry

        lax.fori_loop(first, last, step, 0)
        usable = lax.broadcasted_iota(jnp.int32, (rows, CAP), 1) < lengths[clip]
        for h in range(heads):
            at = slice(h * HD, h * HD + HD)
            total = sum_ref[h].T
            inverse = 1.0 / total[0:1]
            own = total[HD:] * inverse
            weights = jnp.where(usable, jnp.exp(mm(queries[h], cap_ref[clip, at, :], NN)), 0.0)
            cap_total = mm(weights.astype(BF), cap_value_ref[clip, h], NN).T
            cap_inverse = 1.0 / cap_total[0:1]
            other = cap_total[HD:] * cap_inverse
            own_ref[i, at, :] = own
            other_ref[i, at, :] = other
            gate = gates[(s * LINE + b // GROUP) * heads + h]
            comb_refs[i][at, :] = (own + gate * other).astype(BF)
            stat_ref[i, h : h + 1, :] = inverse
            stat_ref[i, 4 + h : 5 + h, :] = cap_inverse


def attend(ids, slices, lengths, gates, queries, kv_pieces, cap_kv, gains, cosine, sine):
    width, rows = queries[0].shape
    slots = LINE * GROUP
    heads = width // HD
    outs = pl.pallas_call(
        attend_kernel,
        in_specs=[SMEM] * 4 + [VMEM] * (LINE + GROUP + 4),
        out_specs=[VMEM] * (LINE + 6),
        out_shape=[shape((width, rows), BF)] * LINE
        + [
            shape((LINE, width, rows), F32),
            shape((LINE, width, rows), F32),
            shape((LINE, 8, rows), F32),
            shape((LINE, width, rows), BF),
            shape((slots, width, rows), BF),
            shape((slots, heads, rows, 2 * HD), BF),
        ],
        scratch_shapes=[
            pltpu.VMEM((slots, heads, rows, 2 * HD), BF),
            pltpu.VMEM((CLIPS, heads, CAP, 2 * HD), BF),
            pltpu.VMEM((heads, rows, 2 * HD), F32),
        ],
        name="attend",
        cost_estimate=cost(33),
    )(ids, slices, lengths, gates, *queries, *kv_pieces, cap_kv, gains, cosine, sine)
    return outs[:LINE], outs[LINE:]


def out_kernel(ids, *refs):
    own, other = refs[:LINE], refs[LINE : 2 * LINE]
    w_ref, att_ref, branch_ref = refs[2 * LINE :]
    b, s = ids[0], ids[1]
    width = own[0].shape[0]
    for k in range(LINE):
        at = chunk_at(b, k, width)
        att_ref[pl.ds(pl.multiple_of(s * LINE * width + at, HD), width), :] = own[k][...]
        att_ref[pl.ds(pl.multiple_of((1 - s) * LINE * width + at, HD), width), :] = other[k][...]
    branch_ref[...] = mm(w_ref[...], att_ref[...], NN).T.astype(BF)


def out_proj(ids, own, other, w_out):
    rows = own[0].shape[1]
    return pl.pallas_call(
        out_kernel,
        in_specs=[SMEM] + [VMEM] * (2 * LINE + 1),
        out_specs=[VMEM, VMEM],
        out_shape=[shape((D, rows), BF), shape((rows, w_out.shape[0]), BF)],
        name="out_proj",
        cost_estimate=cost(3.5),
    )(ids, *own, *other, w_out)


def cut_kernel(turned, ids, *refs):
    count = len(turned)
    ins = refs[:count]
    own_ref, c_ref, y_ref, scratch = refs[count:]
    place = lax.rem(ids[0], GROUP)
    columns = own_ref.shape[3]
    for n in range(count):
        if turned[n]:
            source = ins[n]
        else:
            scratch[...] = ins[n][...].astype(F32).T
            source = scratch
        for k in range(LINE):
            for j, (ref, i) in enumerate(((own_ref, 0), (c_ref, 0), (y_ref, 0), (y_ref, 1))):
                at = (k * GROUP + jnp.bitwise_xor(place, j)) * columns
                ref[i, n, k] = source[pl.ds(pl.multiple_of(at, 32), columns), :].astype(BF)


def cut(ids, values, turned):
    rows = values[0].shape[1 if turned[0] else 0]
    columns = D // (LINE * GROUP)
    count = len(values)
    return pl.pallas_call(
        functools.partial(cut_kernel, tuple(turned)),
        in_specs=[SMEM] + [VMEM] * count,
        out_specs=[VMEM] * 3,
        out_shape=[shape((n, count, LINE, columns, rows), BF) for n in (1, 1, 2)],
        scratch_shapes=[pltpu.VMEM((D, rows), F32)],
        name="cut",
        cost_estimate=cost(2.4),
    )(ids, *values)


def ffn_kernel(
    ids,
    tok_a,
    tok_b,
    br_a,
    br_b,
    out16_ref,
    mod_ref,
    gain_ref,
    kept_ref,
    came_ref,
    down_ref,
    inner_a_ref,
    inner_b_ref,
    gkept_ref,
    gcame_ref,
    in16_ref,
    mid_ref,
    near_ref,
    far_ref,
    near_out_ref,
    far_out_ref,
    acc_in,
    acc_out,
):
    step = pl.program_id(0)
    steps = pl.num_programs(0)
    s = ids[1]
    count = tok_a.shape[0]
    half = br_a.shape[1]
    gate, shift2, scale2 = [mod_ref[i : i + 1, :] for i in (2, 3, 4)]
    mlp_gain = gain_ref[...] * (1.0 + scale2)

    @pl.when(step == 0)
    def _():
        for place, tok in ((s, tok_a), (1 - s, tok_b)):
            at = pl.ds(pl.multiple_of(place * count, count), count)
            mid_ref[at, :] = tok[...].astype(F32)
        low = jnp.where(s == 0, br_a[...].astype(F32), br_b[...].astype(F32))
        high = jnp.where(s == 0, br_b[...].astype(F32), br_a[...].astype(F32))
        mid_ref[:, :half] += gate[:, :half] * low
        mid_ref[:, half:] += gate[:, half:] * high
        middle = mid_ref[...]
        in16_ref[...] = (middle * row_inverse(middle) * mlp_gain + shift2).astype(BF)
        acc_in[...] = jnp.zeros_like(acc_in)
        acc_out[...] = jnp.zeros_like(acc_out)

    w_kept, w_came, w_down = kept_ref[...], came_ref[...], down_ref[...]
    kept = mm(in16_ref[...], w_kept, NT)
    other = mm(in16_ref[...], w_came, NT)
    grad_inner = mm(out16_ref[...], w_down, NT)
    gate_half = jnp.where(s == 0, kept, other)
    up_half = jnp.where(s == 0, other, kept)
    sigmoid = jax.nn.sigmoid(gate_half)
    silu = gate_half * sigmoid
    inner = (silu * up_half).astype(BF)
    grad_gate = grad_inner * up_half * sigmoid * (1.0 + gate_half * (1.0 - sigmoid))
    grad_up = grad_inner * silu
    grad_kept = jnp.where(s == 0, grad_gate, grad_up).astype(BF)
    grad_came = jnp.where(s == 0, grad_up, grad_gate).astype(BF)
    @pl.when(step < steps // 2)
    def _():
        inner_a_ref[...] = inner

    @pl.when(step >= steps // 2)
    def _():
        inner_b_ref[...] = inner

    gkept_ref[...] = grad_kept
    gcame_ref[...] = grad_came
    acc_in[...] += mm(grad_kept, w_kept, NN) + mm(grad_came, w_came, NN)
    acc_out[...] += mm(inner, w_down, NN)

    @pl.when(step == steps - 1)
    def _():
        middle = mid_ref[...]
        part = jnp.sum(
            acc_in[...] * mlp_gain * (middle * row_inverse(middle)), axis=-1, keepdims=True
        )
        near_ref[:, :half] = acc_in[:, pl.ds(pl.multiple_of(s * half, half), half)]
        near_ref[:, half:] = jnp.broadcast_to(part, (part.shape[0], 128))
        far_ref[:, :half] = acc_in[:, pl.ds(pl.multiple_of((1 - s) * half, half), half)].astype(BF)
        high = part.astype(BF).astype(F32)
        middle_part = (part - high).astype(BF).astype(F32)
        low_part = part - high - middle_part
        lane = lax.broadcasted_iota(jnp.int32, (part.shape[0], 128), 1)
        spread = jnp.where(lane == 0, high, jnp.where(lane == 1, middle_part, jnp.where(lane == 2, low_part, 0.0)))
        far_ref[:, half:] = spread.astype(BF)
        near_out_ref[...] = acc_out[pl.ds(pl.multiple_of(s * count, count), count), :]
        far_out_ref[...] = acc_out[pl.ds(pl.multiple_of((1 - s) * count, count), count), :].astype(BF)


def ffn(ids, toks, branches, grad_mlp, mod, gain, w_gate_up, came, w_down):
    count = toks[0].shape[0]
    rows = 2 * count
    half = D // 2
    units = w_down.shape[0]
    tile = 512
    steps = units // tile
    full = lambda v: pl.BlockSpec(v.shape, lambda i, ids: (0,) * v.ndim)

    def fixed(r, c):
        return pl.BlockSpec((r, c), lambda i, ids: (0, 0))

    small = [*toks, *branches, grad_mlp, mod, gain]
    return pl.pallas_call(
        ffn_kernel,
        grid_spec=pltpu.PrefetchScalarGridSpec(
            num_scalar_prefetch=1,
            grid=(steps,),
            in_specs=[full(v) for v in small]
            + [
                pl.BlockSpec((tile, D), lambda i, ids: (ids[1] * steps + i, 0)),
                pl.BlockSpec((tile, D), lambda i, ids: ((1 - ids[1]) * steps + i, 0)),
                pl.BlockSpec((tile, D), lambda i, ids: (i, 0)),
            ],
            out_specs=[
                pl.BlockSpec((rows, tile), lambda i, ids: (0, jnp.minimum(i, steps // 2 - 1))),
                pl.BlockSpec((rows, tile), lambda i, ids: (0, jnp.maximum(i - steps // 2, 0))),
            ]
            + [pl.BlockSpec((rows, tile), lambda i, ids: (0, i))] * 2
            + [
                fixed(rows, D),
                fixed(rows, D),
                fixed(rows, half + 128),
                fixed(rows, half + 128),
                fixed(count, D),
                fixed(count, D),
            ],
            scratch_shapes=[pltpu.VMEM((rows, D), F32), pltpu.VMEM((rows, D), F32)],
        ),
        out_shape=[shape((rows, units // 2), BF)] * 2
        + [shape((rows, units), BF)] * 2
        + [
            shape((rows, D), BF),
            shape((rows, D), F32),
            shape((rows, half + 128), F32),
            shape((rows, half + 128), BF),
            shape((count, D), F32),
            shape((count, D), BF),
        ],
        name="ffn",
        cost_estimate=cost(18),
    )(ids, *small, w_gate_up, came, w_down)


def mid_kernel(
    ids,
    near_ref,
    recv_ref,
    mid_ref,
    cot_a,
    cot_b,
    br_ref,
    mod_ref,
    gain_ref,
    w_ref,
    sums_ref,
    gbr_ref,
    near_mid_ref,
    far_mid_ref,
    *refs,
):
    near_refs, far_refs, scratch = refs[:2], refs[2:4], refs[4]
    b, s = ids[0], ids[1]
    half = D // 2
    count = cot_a.shape[0]
    cols = pl.ds(pl.multiple_of(s * half, half), half)
    gate, scale2 = mod_ref[2:3, cols], mod_ref[4:5, cols]
    gain = gain_ref[:, cols]
    middle = mid_ref[...]
    inverse = row_inverse(middle)
    unit = mid_ref[:, cols] * inverse
    parts = jnp.sum(recv_ref[:, half:].astype(F32), axis=-1, keepdims=True)
    mean = (near_ref[:, half : half + 1] + parts) * (1.0 / D)
    grad_in = near_ref[:, :half] + recv_ref[:, :half].astype(F32)
    cot_own, cot_far = cot_a[:, cols].astype(F32), cot_b[:, cols].astype(F32)
    cot = jnp.concatenate(
        [jnp.where(s == 0, cot_own, cot_far), jnp.where(s == 0, cot_far, cot_own)], axis=0
    )
    scaled = grad_in * (1.0 + scale2)
    grad_mid = cot + inverse * (scaled * gain - unit * mean)
    sums_ref[...] = jnp.zeros_like(sums_ref)
    sums_ref[0:1, :] = jnp.sum(grad_mid * br_ref[...].astype(F32), axis=0, keepdims=True)
    sums_ref[1:2, :] = jnp.sum(grad_in, axis=0, keepdims=True)
    sums_ref[2:3, :] = jnp.sum(grad_in * unit, axis=0, keepdims=True) * gain
    sums_ref[3:4, :] = jnp.sum(scaled * unit, axis=0, keepdims=True)
    grad_branch = (grad_mid * gate).astype(BF)
    gbr_ref[...] = grad_branch
    top, low = grad_mid[:count], grad_mid[count:]
    near_mid_ref[...] = jnp.where(s == 0, top, low)
    far_mid_ref[...] = jnp.where(s == 0, low, top).astype(BF)
    scratch[...] = mm(grad_branch, w_ref[...], NN).T
    width = near_refs[0].shape[0] // 2
    for n, k in enumerate(SENDS):
        at = chunk_at(b, k, width)
        to = slice(n % 2 * width, n % 2 * width + width)
        near_refs[n // 2][to, :] = scratch[pl.ds(pl.multiple_of(s * half + at, HD), width), :]
        far_refs[n // 2][to, :] = scratch[
            pl.ds(pl.multiple_of((1 - s) * half + at, HD), width), :
        ].astype(BF)


def mid_back(ids, near, received, middle, cots, branch, mod, gain, w_out):
    rows, half = branch.shape
    width = half // LINE
    count = cots[0].shape[0]
    outs = pl.pallas_call(
        mid_kernel,
        in_specs=[SMEM] + [VMEM] * 9,
        out_specs=[VMEM] * 8,
        out_shape=[
            shape((8, half), F32),
            shape((rows, half), BF),
            shape((count, half), F32),
            shape((count, half), BF),
        ]
        + [shape((2 * width, rows), F32)] * 2
        + [shape((2 * width, rows), BF)] * 2,
        scratch_shapes=[pltpu.VMEM((D, rows), F32)],
        name="mid_back",
        cost_estimate=cost(5.5),
    )(ids, near, received, middle, *cots, branch, mod, gain, w_out)
    return outs[:4], outs[4:6], outs[6:]


def add_pair_kernel(near_ref, recv_ref, a_ref, b_ref):
    width = a_ref.shape[0]
    total = (near_ref[...] + recv_ref[...].astype(F32)).astype(BF)
    a_ref[...] = total[:width]
    b_ref[...] = total[width:]


def add_pair(near, received):
    both, rows = near.shape
    return pl.pallas_call(
        add_pair_kernel,
        in_specs=[VMEM, VMEM],
        out_specs=[VMEM, VMEM],
        out_shape=[shape((both // 2, rows), BF)] * 2,
        name="add_pair",
        cost_estimate=cost(1),
    )(near, received)


def place_row(b, column):
    width = column.shape[0]
    row = jnp.broadcast_to(column, (width, 128)).T[0:1]
    z = b // GROUP
    return jnp.concatenate([jnp.where(z == k, row, 0.0) for k in range(LINE)], axis=1)


def output_kernel(ids, slices, near_ref, recv_ref, mid_ref, cot_ref, mod_ref, sums_ref, out_ref, early_ref):
    s = ids[1]
    count, half = near_ref.shape[0], sums_ref.shape[1]
    clip, _, _ = clip_at(slices, ids[0])
    branch = near_ref[...] + recv_ref[...].astype(F32)
    middle = mid_ref[pl.ds(pl.multiple_of(s * count, count), count), :]
    out_ref[...] = (middle + mod_ref[5:6, :] * branch).astype(BF)
    gate2 = jnp.sum(cot_ref[...].astype(F32) * branch, axis=0, keepdims=True)
    rows = [sums_ref[i : i + 1, :] for i in range(3)] + [gate2[:, :half], gate2[:, half:]]
    early_ref[...] = jnp.zeros_like(early_ref)
    for c in range(CLIPS):
        for i, row in enumerate(rows):
            early_ref[5 * c + i : 5 * c + i + 1, :] = jnp.where(clip == c, row, 0.0)
    early_ref[20:21, :] = sums_ref[3:4, :]


def output_sums(ids, slices, near, received, middle, cot, mod, sums):
    count = near.shape[0]
    return pl.pallas_call(
        output_kernel,
        in_specs=[SMEM, SMEM] + [VMEM] * 6,
        out_specs=[VMEM, VMEM],
        out_shape=[shape((count, D), BF), shape((24, D // 2), F32)],
        name="output_sums",
        cost_estimate=cost(3),
    )(ids, slices, near, received, middle, cot, mod, sums)


def attend_back_kernel(ids, slices, lengths, gates, *refs):
    q_refs, g_refs = refs[:LINE], refs[LINE : 2 * LINE]
    (own_ref, other_ref, stat_ref, qs_ref, ks_ref, pair_ref, cap_ref, gains_ref, cos_ref, sin_ref) = refs[
        2 * LINE : 2 * LINE + 10
    ]
    outs = refs[2 * LINE + 10 :]
    gq_refs = outs[:LINE]
    qgain_ref, keep_ref, send_ref, dgate_ref = outs[LINE : LINE + 4]
    dkv_refs = outs[LINE + 4 : LINE + 4 + GROUP]
    acc_ref, dcap_ref, dq_ref = outs[LINE + 4 + GROUP :]
    b, s = ids[0], ids[1]
    width, rows = q_refs[0].shape
    heads = width // HD
    scale = HD**-0.5
    base = s * LINE * width + b // GROUP * width
    acc_ref[...] = jnp.zeros_like(acc_ref)
    dcap_ref[...] = jnp.zeros_like(dcap_ref)
    dgate_ref[...] = jnp.zeros_like(dgate_ref)
    qgain_ref[...] = jnp.zeros_like(qgain_ref)

    for i in range(LINE):
        slot = slot_of(b, i, 0)
        clip, first, last = clip_at(slices, slot)
        queries, grads, deltas, inverses = [], [], [], []
        tall_q, tall_g, wide = [], [], []
        for h in range(heads):
            at = slice(h * HD, h * HD + HD)
            grad = g_refs[i][at, :]
            queries.append(qs_ref[i, at, :])
            grads.append(grad)
            deltas.append(jnp.sum(grad.astype(F32) * own_ref[i, at, :], axis=0, keepdims=True))
            inverses.append(stat_ref[i, h : h + 1, :])
            blank = jnp.zeros((HD, rows), F32)
            query_pad = jnp.concatenate([queries[h].astype(F32), blank], axis=0)
            grad_pad = jnp.concatenate([blank, grad.astype(F32)], axis=0)
            tall_q.append(query_pad.astype(BF))
            tall_g.append(grad_pad.astype(BF))
            wide.append(jnp.concatenate([query_pad.T, grad_pad.T], axis=0).astype(BF))
        dq_ref[...] = jnp.zeros_like(dq_ref)

        def step(n, carry):
            for h in range(heads):
                at = slice(h * HD, h * HD + HD)
                pair = pair_ref[n, h]
                prob = jnp.exp(mm(pair, tall_q[h], NN)) * inverses[h]
                grad_score = (prob * (mm(pair, tall_g[h], NN) - deltas[h])).astype(BF)
                both = jnp.concatenate([grad_score, prob.astype(BF)], axis=1)
                acc_ref[n, h] += mm(both, wide[h], NN)
                dq_ref[at, :] += mm(ks_ref[n, at, :], grad_score, NN)
            return carry

        lax.fori_loop(first, last, step, 0)
        usable = lax.broadcasted_iota(jnp.int32, (CAP, rows), 0) < lengths[clip]
        cosine, sine = cos_ref[slot - first], sin_ref[slot - first]
        for h in range(heads):
            at = slice(h * HD, h * HD + HD)
            at_value = slice(width + h * HD, width + h * HD + HD)
            gate = gates[(s * LINE + b // GROUP) * heads + h]
            cap_keys, cap_values = cap_ref[clip, at, :], cap_ref[clip, at_value, :]
            grad = grads[h].astype(F32)
            grad_other = (grad * gate).astype(BF)
            prob = (
                jnp.where(usable, jnp.exp(mm(cap_keys, queries[h], TN)), 0.0)
                * stat_ref[i, 4 + h : 5 + h, :]
            )
            grad_prob = mm(cap_values, grad_other, TN)
            inner = jnp.sum(prob * grad_prob, axis=0, keepdims=True)
            grad_score = (prob * (grad_prob - inner)).astype(BF)
            query_grad = (dq_ref[at, :] + mm(cap_keys, grad_score, NN)) * scale
            dcap_ref[clip, at, :] += mm(queries[h], grad_score, NT)
            dcap_ref[clip, at_value, :] += mm(grad_other, prob.astype(BF), NT)
            part = jnp.sum(grad * other_ref[i, at, :], axis=0, keepdims=True)
            dgate_ref[h : h + 1, :] += part * (1.0 - gate * gate)
            gain = gains_ref[pl.ds(pl.multiple_of(base + h * HD, HD), HD), 0:1]
            raw_grad, gain_grad = norm_rope_back(
                query_grad.astype(BF).astype(F32), q_refs[i][at, :].astype(F32), gain, cosine, sine
            )
            gq_refs[i][at, :] = raw_grad.astype(BF)
            qgain_ref[at, :] += gain_grad

    for j, dkv_ref in enumerate(dkv_refs):
        for k in range(LINE):
            slot = slot_of(b, k, j)
            for h in range(heads):
                both = acc_ref[slot, h].T.astype(BF)
                dkv_ref[k, h * HD : h * HD + HD, :] = both[:HD]
                dkv_ref[k, width + h * HD : width + h * HD + HD, :] = both[HD:]
    core = lax.rem(b, 2)
    for i in range(2):
        keep_ref[i] = dcap_ref[2 * i + core]
        send_ref[i] = dcap_ref[2 * i + 1 - core]


def attend_back(ids, slices, lengths, gates, queries, grads, saved, cap_kv, gains, cosine, sine):
    width, rows = queries[0].shape
    outs = pl.pallas_call(
        attend_back_kernel,
        in_specs=[SMEM] * 4 + [VMEM] * (2 * LINE + 10),
        out_specs=[VMEM] * (LINE + 4 + GROUP),
        out_shape=[shape((width, rows), BF)] * LINE
        + [
            shape((width, 1), F32),
            shape((2, 2 * width, CAP), F32),
            shape((2, 2 * width, CAP), F32),
            shape((8, rows), F32),
        ]
        + [shape((LINE, 2 * width, rows), BF)] * GROUP,
        scratch_shapes=[
            pltpu.VMEM((LINE * GROUP, width // HD, rows, 2 * HD), F32),
            pltpu.VMEM((CLIPS, 2 * width, CAP), F32),
            pltpu.VMEM((width, rows), F32),
        ],
        name="attend_back",
        cost_estimate=cost(40),
    )(ids, slices, lengths, gates, *queries, *grads, *saved, cap_kv, gains, cosine, sine)
    return outs[:LINE], outs[LINE : LINE + 4], outs[LINE + 4 :]


def keys_back_kernel(ids, slices, a_ref, r_ref, kv_ref, gains_ref, cos_ref, sin_ref, *outs):
    out_refs, gain_ref = outs[:LINE], outs[LINE]
    b, s = ids[0], ids[1]
    width = gain_ref.shape[0]
    base = s * LINE * width + b // GROUP * width
    gain_ref[...] = jnp.zeros_like(gain_ref)
    for i in range(LINE):
        slot = slot_of(b, i, 0)
        _, first, _ = clip_at(slices, slot)
        cosine, sine = cos_ref[slot - first], sin_ref[slot - first]
        total = (a_ref[i].astype(F32) + r_ref[i].astype(F32)).astype(BF)
        for h in range(width // HD):
            at = slice(h * HD, h * HD + HD)
            gain = gains_ref[pl.ds(pl.multiple_of(base + h * HD, HD), HD), 1:2]
            raw_grad, gain_grad = norm_rope_back(
                total[at, :].astype(F32), kv_ref[i, at, :].astype(F32), gain, cosine, sine
            )
            out_refs[i][at, :] = raw_grad.astype(BF)
            gain_ref[at, :] += gain_grad
        out_refs[i][width:, :] = total[width:, :]


def keys_back(ids, slices, part, received, kv, gains, cosine, sine):
    _, both, rows = kv.shape
    outs = pl.pallas_call(
        keys_back_kernel,
        in_specs=[SMEM, SMEM] + [VMEM] * 6,
        out_specs=[VMEM] * (LINE + 1),
        out_shape=[shape((both, rows), BF)] * LINE + [shape((both // 2, 1), F32)],
        name="keys_back",
        cost_estimate=cost(3.7),
    )(ids, slices, part, received, kv, gains, cosine, sine)
    return outs[:LINE], outs[LINE]


def pack_kernel(ids, *refs):
    q_refs, kv_refs = refs[:LINE], refs[LINE : 2 * LINE]
    first_ref, second_ref, send_ref = refs[2 * LINE :]
    b, s = ids[0], ids[1]
    width = q_refs[0].shape[0]
    for k in range(LINE):
        at = chunk_at(b, k, width)

        @pl.when(s == 0)
        def _():
            first_ref[pl.ds(at, width), :] = q_refs[k][...]
            second_ref[pl.ds(at, width), :] = kv_refs[k][:width, :]
            send_ref[pl.ds(at, width), :] = kv_refs[k][width:, :]

        @pl.when(s == 1)
        def _():
            first_ref[pl.ds(at, width), :] = kv_refs[k][:width, :]
            second_ref[pl.ds(at, width), :] = kv_refs[k][width:, :]
            send_ref[pl.ds(at, width), :] = q_refs[k][...]


def pack(ids, grads_q, grads_kv):
    width, rows = grads_q[0].shape
    return pl.pallas_call(
        pack_kernel,
        in_specs=[SMEM] + [VMEM] * (2 * LINE),
        out_specs=[VMEM] * 3,
        out_shape=[shape((LINE * width, rows), BF)] * 3,
        name="pack",
        cost_estimate=cost(2.5),
    )(ids, *grads_q, *grads_kv)


def qkv_back_kernel(ids, first_ref, recv_ref, second_ref, w_ref, near_ref, far_ref, acc_ref):
    step = pl.program_id(0)
    count = near_ref.shape[0]
    s = ids[1]

    for n, ref in enumerate((first_ref, recv_ref, second_ref)):

        @pl.when(step == n)
        def _():
            part = mm(ref[...], w_ref[...], TN)
            acc_ref[...] = part if n == 0 else acc_ref[...] + part

    @pl.when(step == pl.num_programs(0) - 1)
    def _():
        near_ref[...] = acc_ref[pl.ds(pl.multiple_of(s * count, count), count), :]
        far_ref[...] = acc_ref[pl.ds(pl.multiple_of((1 - s) * count, count), count), :].astype(BF)


def qkv_back(ids, first, received, second, w_qkv):
    local, rows = received.shape
    count = rows // 2
    whole = pl.BlockSpec((local, rows), lambda i, ids: (0, 0))
    return pl.pallas_call(
        qkv_back_kernel,
        grid_spec=pltpu.PrefetchScalarGridSpec(
            num_scalar_prefetch=1,
            grid=(3,),
            in_specs=[whole] * 3 + [pl.BlockSpec((local, D), lambda i, ids: (i, 0))],
            out_specs=[pl.BlockSpec((count, D), lambda i, ids: (0, 0))] * 2,
            scratch_shapes=[pltpu.VMEM((rows, D), F32)],
        ),
        out_shape=[shape((count, D), F32), shape((count, D), BF)],
        name="qkv_back",
        cost_estimate=cost(6),
    )(ids, first, received, second, w_qkv)


def tokens_kernel(
    ids, slices, tok_ref, near_ref, recv_ref, mid_near, mid_far, mod_ref, gain_ref, *refs
):
    qgain_ref, kgain_ref, cgain_ref, dgate_ref, early_ref, out_ref, late_ref = refs
    b, s = ids[0], ids[1]
    half = mid_near.shape[1]
    clip, _, _ = clip_at(slices, b)
    values = tok_ref[...].astype(F32)
    inverse = row_inverse(values)
    unit = values * inverse
    scale = 1.0 + mod_ref[1:2, :]
    gain = gain_ref[...]
    grad = near_ref[...] + recv_ref[...].astype(F32)
    scaled = grad * scale
    unit_grad = scaled * gain
    mean = jnp.mean(unit_grad * unit, axis=-1, keepdims=True)
    mid_own, mid_other = mid_near[...], mid_far[...].astype(F32)
    middle = jnp.concatenate(
        [jnp.where(s == 0, mid_own, mid_other), jnp.where(s == 0, mid_other, mid_own)], axis=1
    )
    out_ref[...] = inverse * (unit_grad - unit * mean) + middle
    shift_row = jnp.sum(grad, axis=0, keepdims=True)
    with_unit = grad * unit
    scale_row = jnp.sum(with_unit, axis=0, keepdims=True) * gain
    norm_row = jnp.sum(scaled * unit, axis=0, keepdims=True)
    rows = [shift_row[:, :half], shift_row[:, half:], scale_row[:, :half], scale_row[:, half:]]
    late_ref[...] = jnp.zeros_like(late_ref)
    for c in range(CLIPS):
        for i, row in enumerate(rows):
            late_ref[4 * c + i : 4 * c + i + 1, :] = jnp.where(clip == c, row, 0.0)
    late_ref[16:17, :] = norm_row[:, :half]
    late_ref[17:18, :] = norm_row[:, half:]
    for i, ref in enumerate((qgain_ref, kgain_ref, cgain_ref)):
        late_ref[18 + i : 19 + i, :] = place_row(b, ref[...])
    heads = qgain_ref.shape[0] // HD
    lane = lax.broadcasted_iota(jnp.int32, (1, half), 1)
    gate_row = jnp.zeros((1, half), F32)
    for h in range(heads):
        value = jnp.sum(dgate_ref[h : h + 1, :], axis=1, keepdims=True)
        gate_row = gate_row + jnp.where(lane == b // GROUP * heads + h, value, 0.0)
    late_ref[21:22, :] = gate_row
    late_ref[24:, :] = early_ref[...]


def tokens_back(ids, slices, tok, near, received, mid_near, mid_far, mod, gain, parts):
    return pl.pallas_call(
        tokens_kernel,
        in_specs=[SMEM, SMEM] + [VMEM] * 12,
        out_specs=[VMEM, VMEM],
        out_shape=[shape(tok.shape, F32), shape((48, D // 2), F32)],
        name="tokens_back",
        cost_estimate=cost(3.5),
    )(ids, slices, tok, near, received, mid_near, mid_far, mod, gain, *parts)


def finish_kernel(ids, late_a, late_b, mod_ref, gains_ref):
    s = ids[1]
    early_a, early_b = late_a.at[pl.ds(24, 24)], late_b.at[pl.ds(24, 24)]

    def joined(a, b, i):
        own, other = a[i : i + 1, :], b[i : i + 1, :]
        return jnp.concatenate(
            [jnp.where(s == 0, own, other), jnp.where(s == 0, other, own)], axis=1
        )

    def added(a, b, i):
        both = a[i : i + 2, :] + b[i : i + 2, :]
        return jnp.concatenate([both[0:1], both[1:2]], axis=1)

    for c in range(CLIPS):
        low = [added(late_a, late_b, 4 * c), added(late_a, late_b, 4 * c + 2), joined(early_a, early_b, 5 * c)]
        high = [
            joined(early_a, early_b, 5 * c + 1),
            joined(early_a, early_b, 5 * c + 2),
            added(early_a, early_b, 5 * c + 3),
        ]
        for i in range(3):
            mod_ref[c : c + 1, i * D : (i + 1) * D] = jnp.where(s == 0, low[i], high[i])
    gains_ref[...] = jnp.zeros_like(gains_ref)
    gains_ref[0:1, :] = added(late_a, late_b, 16)
    for i in range(3):
        gains_ref[1 + i : 2 + i, :] = joined(late_a, late_b, 18 + i)
    gains_ref[4:5, :] = joined(early_a, early_b, 20)
    gains_ref[5:6, :] = joined(late_a, late_b, 21)


def finish(ids, late_a, late_b):
    return pl.pallas_call(
        finish_kernel,
        in_specs=[SMEM] + [VMEM] * 2,
        out_specs=[VMEM, VMEM],
        out_shape=[shape((CLIPS, 3 * D), F32), shape((8, D), F32)],
        name="finish",
        cost_estimate=cost(1.7),
    )(ids, late_a, late_b)


def caption_back_kernel(ids, sum_ref, raw_ref, gains_ref, out_ref, gain_ref):
    b, s = ids[0], ids[1]
    width = gain_ref.shape[0]
    base = s * LINE * width + b // GROUP * width
    cols = pl.ds(pl.multiple_of(lax.rem(b, GROUP) * CAP, CAP), CAP)
    for h in range(width // HD):
        at = slice(h * HD, h * HD + HD)
        gain = gains_ref[pl.ds(pl.multiple_of(base + h * HD, HD), HD), 2:3]
        raw = raw_ref[at, cols]
        inverse = lax.rsqrt(jnp.mean(raw * raw, axis=0, keepdims=True) + EPSILON)
        unit = raw * inverse
        grad = sum_ref[at, :]
        gain_ref[at, :] = jnp.sum(grad * unit, axis=1, keepdims=True)
        unit_grad = grad * gain
        out_ref[at, :] = (
            inverse * (unit_grad - unit * jnp.mean(unit_grad * unit, axis=0, keepdims=True))
        ).astype(BF)
    out_ref[width:, :] = sum_ref[width:, :].astype(BF)


def caption_back(ids, total, raw, gains):
    return pl.pallas_call(
        caption_back_kernel,
        in_specs=[SMEM] + [VMEM] * 3,
        out_specs=[VMEM, VMEM],
        out_shape=[shape(total.shape, BF), shape((total.shape[0] // 2, 1), F32)],
        name="caption_back",
        cost_estimate=cost(2.3),
    )(ids, total, raw, gains)


def caption_weight_kernel(ids, *refs):
    raw_refs, cap_ref, out_refs = refs[:GROUP], refs[GROUP], refs[GROUP + 1 :]
    b = ids[0]
    each = out_refs[0].shape[1]
    place = lax.rem(b, GROUP)
    for k in range(LINE):
        at = pl.multiple_of((lax.rem(b // GROUP - k + LINE, LINE) * GROUP + place) * each, each)
        total = None
        for j in range(GROUP):
            rows = pl.ds(pl.multiple_of(jnp.bitwise_xor(place, j) * CAP, CAP), CAP)
            part = mm(raw_refs[j][...], cap_ref[rows, pl.ds(at, each)], NN)
            total = part if total is None else total + part
        out_refs[k][...] = total.astype(BF)


def caption_weights(ids, raws, caption):
    rows = raws[0].shape[0]
    return pl.pallas_call(
        caption_weight_kernel,
        in_specs=[SMEM] + [VMEM] * (GROUP + 1),
        out_specs=[VMEM] * LINE,
        out_shape=[shape((rows, YD // (LINE * GROUP)), BF)] * LINE,
        name="caption_weights",
        cost_estimate=cost(4),
    )(ids, *raws, caption)


def caption_join_kernel(ids, *refs):
    parts, out_ref = refs[:LINE], refs[LINE]
    width = parts[0].shape[0] // 2
    for k in range(LINE):
        at = chunk_at(ids[0], k, width)
        for j in range(2):
            out_ref[j, pl.ds(at, width), :] = parts[k][j * width : (j + 1) * width, :].astype(F32)


def caption_join(ids, parts):
    both, each = parts[0].shape
    return pl.pallas_call(
        caption_join_kernel,
        in_specs=[SMEM] + [VMEM] * LINE,
        out_specs=VMEM,
        out_shape=shape((2, both // 2 * LINE, each), F32),
        name="caption_join",
        cost_estimate=cost(2),
    )(ids, *parts)


def weight_kernel(count, dims, *refs):
    left, right, out_ref = refs[:count], refs[count : 2 * count], refs[-1]
    total = None
    for a_ref, g_ref in zip(left, right):
        block = g_ref[...].reshape(g_ref.shape[-2:])
        part = mm(a_ref[0, 0].reshape(-1, a_ref.shape[-1]), block, dims)
        total = part if total is None else total + part
    out_ref[...] = total.reshape(out_ref.shape).astype(BF)


def weight_grads(left, right, by_rows, tile, kind, total, place, into=None):
    _, _, chunks, columns, tokens = left[0][0].shape
    rows = right[0].shape[-2 if by_rows else -1]
    stack = right[0].shape[0] if right[0].ndim == 3 else 1
    per = rows // tile
    left_specs = [
        pl.BlockSpec((1, 1, chunks, columns, tokens), lambda i, n=n: (n, kind, 0, 0, 0))
        for _, n in left
    ]
    if by_rows:
        right_spec = pl.BlockSpec((tile, tokens), lambda i: (i, 0))
    elif stack == 1:
        right_spec = pl.BlockSpec((tokens, tile), lambda i: (0, i))
    else:
        right_spec = pl.BlockSpec((1, tokens, tile), lambda i: (i // per, 0, i % per))
    args = [a for a, _ in left] + list(right)
    specs = left_specs + [right_spec] * len(right)
    aliases = {}
    if into is not None:
        aliases = {len(args): 0}
        args.append(into)
        specs.append(pl.BlockSpec(memory_space=pl.ANY))
    return pl.pallas_call(
        functools.partial(weight_kernel, len(left), NT if by_rows else NN),
        grid=(stack * per,),
        in_specs=specs,
        out_specs=pl.BlockSpec((chunks, columns, tile), lambda i: (0, 0, place(i))),
        out_shape=shape((chunks, columns, total), BF),
        input_output_aliases=aliases,
        name="weight_grads",
        cost_estimate=cost(5),
    )(*args)


def fast_body(
    tokens,
    cotangent,
    clip_slices,
    caption_lengths,
    caption,
    cond,
    ada_w,
    norm_gain,
    w_qkv,
    q_gain,
    k_gain,
    w_caption,
    ky_gain,
    cross_gate,
    w_out,
    ffn_gain,
    w_gate_up,
    w_down,
):
    bucket_count = LINE * GROUP
    seq_count = lax.axis_size("seq")
    local_width = D // seq_count
    units = FF // seq_count
    b = lax.axis_index(BUCKET)
    s = lax.axis_index("seq")
    z, g, c, y = b // GROUP, b % GROUP, b % 2, (b // 2) % 2
    ids = jnp.stack([b, s]).astype(jnp.int32)

    def xswap(v):
        return lax.ppermute(v, "seq", [(0, 1), (1, 0)])

    def hop(v, to):
        return lax.ppermute(v, BUCKET, [(i, to(i)) for i in range(bucket_count)])

    def cswap(v):
        return hop(v, lambda i: i ^ 1)

    def yswap(v):
        return hop(v, lambda i: i ^ 2)

    def zshift(v, k):
        return hop(v, lambda i: (i + GROUP * k) % bucket_count)

    def after(v, *others):
        return lax.optimization_barrier((v, *others))[0]

    def fence(*values):
        return lax.optimization_barrier(values)

    def pick(v, index):
        return lax.dynamic_index_in_dim(v, index, 0, False)

    def spread(parts):
        return [parts[0]] + [zshift(parts[k], k) for k in range(1, LINE)]

    def unspread(parts):
        return [parts[0]] + [zshift(parts[k], LINE - k) for k in range(1, LINE)]

    half = HD // 2
    rows = tokens.shape[0] * seq_count
    frequency = jnp.exp(jnp.arange(half, dtype=F32) * (-2.0 * math.log(10000.0) / (2 * half)))
    positions = jnp.arange(bucket_count * rows, dtype=F32).reshape(bucket_count, 1, rows)
    angles = positions * frequency[None, :, None]
    cosine, sine = jnp.cos(angles), jnp.sin(angles)
    gains = jnp.stack([q_gain, k_gain, ky_gain], axis=1)
    gates = jnp.tanh(cross_gate)
    norm_row, ffn_row = norm_gain[None], ffn_gain[None]

    tok_far = xswap(tokens)
    activation = jax.nn.silu(cond).astype(BF)
    mod_near = mm(activation, ada_w, NT)
    mod_far = xswap(mod_near)
    each = units // 2
    sent = lax.dynamic_slice_in_dim(w_gate_up, (1 - s) * units + c * each, each, 0)
    tok_far, sent = lax.optimization_barrier((tok_far, sent))
    projected, hidden, mod = pre(
        ids, clip_slices, tokens, tok_far, mod_near, mod_far, norm_row, w_qkv
    )
    local = lax.slice_in_dim(projected, local_width, 2 * local_width, axis=0)
    swapped = xswap(local)
    def scatter(parts):
        return lax.psum_scatter(parts, "z", scatter_dimension=0, tiled=False)

    hid_own, hid_c, hid_y = cut(ids, [hidden], [False])
    swapped, hid_own, hid_c, hid_y, gains = fence(swapped, hid_own, hid_c, hid_y, gains)
    kv_parts, q_parts = route(ids, projected, swapped)
    came = lax.all_gather(after(sent, swapped), ("seq", "c"), axis=0, tiled=True)
    kv_here = spread(kv_parts)
    q_here = spread(q_parts)
    caption_rows = caption.reshape(CLIPS * CAP, YD)
    cap_raw, cap_kv = caption_keys(ids, w_caption, after(caption_rows, kv_parts[0]), gains)
    cap_raw, cap_kv, cosine, sine, *kv_here = fence(cap_raw, cap_kv, cosine, sine, *kv_here)
    kv_own = jnp.stack(kv_here)
    kv_y = yswap(kv_own)
    kv_c = cswap(kv_own)
    cot_far = xswap(after(cotangent, kv_own))
    kv_y = after(kv_y, kv_c, *q_here[1:], cot_far)
    kv_cy = cswap(kv_y)
    kv_pieces = [kv_own, kv_c, kv_y, kv_cy]
    grad_mlp = (
        jnp.where(
            s == 0,
            jnp.concatenate([cotangent, cot_far], 0),
            jnp.concatenate([cot_far, cotangent], 0),
        ).astype(F32)
        * mod[5:6]
    ).astype(BF)
    q_here[0], hid_y, hid_c = fence(q_here[0], hid_y, hid_c, grad_mlp)[:3]
    hid_came_y, hid_came_c = yswap(hid_y), cswap(hid_c)
    combined, saved = attend(
        ids, clip_slices, caption_lengths, gates, q_here, kv_pieces, cap_kv, gains, cosine, sine
    )
    combined, saved, hid_came_y, hid_came_c = fence(combined, saved, hid_came_y, hid_came_c)
    heads_own = unspread(combined)
    heads_far = [xswap(v) for v in heads_own]
    attention, branch = out_proj(ids, heads_own, heads_far, w_out)
    branch_far = xswap(branch)
    att_own, att_c, att_y = cut(ids, [attention, grad_mlp], [True, False])
    branch_far, att_own, att_c, att_y = fence(branch_far, att_own, att_c, att_y)
    att_came_y = yswap(att_y)
    att_came_c = cswap(att_c)
    hid_came_yc = cswap(after(hid_came_y, branch_far))
    hid_left = [(hid_own, 0), (hid_came_c, 0), (hid_came_y, 0), (hid_came_yc, 1)]
    inner, inner_2, grad_kept, grad_came, mlp_in, middle, near, far, near_out, far_out = ffn(
        ids, [tokens, tok_far], [branch, branch_far], grad_mlp, mod, ffn_row, w_gate_up, came, w_down
    )
    inner, inner_2, grad_kept, grad_came, mlp_in, near, far = fence(
        inner, inner_2, grad_kept, grad_came, mlp_in, near, far
    )
    att_came_y, att_came_c, hid_came_yc, far = fence(att_came_y, att_came_c, hid_came_yc, far)
    hid_left[3] = (hid_came_yc, 1)

    received = xswap(far)
    inner_y = yswap(inner)
    inner_c = cswap(inner)
    kept_c = cswap(grad_kept)
    att_came_yc = cswap(att_came_y)
    att_left = [(att_own, 0), (att_came_c, 0), (att_came_y, 0), (att_came_yc, 1)]
    ffn_own, ffn_c, ffn_y = cut(ids, [mlp_in], [False])
    received, ffn_own, ffn_c, ffn_y, inner_c, inner_y, kept_c, att_came_yc, came_op, inner_op = fence(
        received, ffn_own, ffn_c, ffn_y, inner_c, inner_y, kept_c, att_came_yc, grad_came, inner_2
    )
    att_left[3] = (att_came_yc, 1)
    inner_2y = yswap(inner_op)
    inner_2c = cswap(inner_op)
    inner_yc = cswap(inner_y)
    ffn_came_c = cswap(ffn_c)
    (sums, grad_branch, mid_near, mid_far), near_heads, far_heads = mid_back(
        ids, near, received, middle, [cotangent, cot_far], branch, mod, ffn_row, w_out
    )
    grad_branch, ffn_came_c, inner_yc, inner_2c, *far_heads = fence(
        grad_branch, ffn_came_c, inner_yc, inner_2c, *far_heads
    )
    recv_a = xswap(far_heads[0])
    recv_b = xswap(far_heads[1])
    branch_c = cswap(grad_branch)
    recv_a, branch_c, inner_2y, ffn_y, branch_op, came_op = fence(
        recv_a, branch_c, inner_2y, ffn_y, grad_branch, came_op
    )
    ffn_came_y = yswap(ffn_y)
    inner_2yc = cswap(inner_2y)
    grad_1, grad_2 = add_pair(near_heads[0], recv_a)
    grad_3, grad_0 = add_pair(near_heads[1], after(recv_b, grad_1))
    grad_here = spread([grad_0, grad_1, grad_2, grad_3])
    tile = 512
    per = units // tile
    parts_inner = weight_grads(
        att_left, [after(inner, grad_0), inner_c, inner_y, inner_yc], False, tile, 1, units, lambda i: i
    )
    parts_inner = weight_grads(
        att_left,
        [inner_2, inner_2c, inner_2y, inner_2yc],
        False,
        tile,
        1,
        units,
        lambda i: i + per // 2,
        parts_inner,
    )
    parts_inner, ffn_came_y, *grad_here = fence(parts_inner, ffn_came_y, *grad_here)
    sum_inner = scatter(parts_inner)
    grad_here[0], kept_op, came_op, out_op, mid_op = fence(
        grad_here[0], grad_kept, grad_came, far_out, mid_far
    )
    kept_y = yswap(kept_op)
    came_y = yswap(came_op)
    came_c = cswap(came_op)
    out_recv = xswap(out_op)
    mid_came = xswap(mid_op)
    grads_q, (q_gain_part, cap_keep, cap_send, gate_part), grads_kv = attend_back(
        ids, clip_slices, caption_lengths, gates, q_here, grad_here, saved, cap_kv, gains, cosine, sine
    )
    grads_q, grads_kv, cap_send, kept_y, came_y, came_c, out_recv, mid_came = fence(
        grads_q, grads_kv, cap_send, kept_y, came_y, came_c, out_recv, mid_came
    )

    kv_c3 = cswap(grads_kv[3])
    kv_c1, cap_c = cswap(grads_kv[1]), cswap(cap_send)
    away = (grads_kv[2].astype(F32) + kv_c3.astype(F32)).astype(BF)
    away, kv_c1, cap_c, *grads_q = fence(away, kv_c1, cap_c, *grads_q)
    away_here = yswap(away)
    ffn_came_yc, kept_yc, came_yc = fence(ffn_came_y, kept_y, came_y, away)[:3]
    ffn_came_yc, kept_yc, came_yc = cswap(ffn_came_yc), cswap(kept_yc), cswap(came_yc)
    ffn_came_yc, kept_yc, came_yc, *grads_q = fence(ffn_came_yc, kept_yc, came_yc, *grads_q)
    ffn_left = [(ffn_own, 0), (ffn_came_c, 0), (ffn_came_y, 0), (ffn_came_yc, 1)]
    kept_all = [grad_kept, kept_c, kept_y, kept_yc]
    came_all = [grad_came, came_c, came_y, came_yc]
    back_q = unspread(grads_q)
    here = (grads_kv[0].astype(F32) + kv_c1.astype(F32)).astype(BF)
    pair = cap_keep + cap_c
    parts_a = weight_grads(ffn_left, kept_all, False, tile, 0, 2 * units, lambda i: i)
    parts_a = weight_grads(ffn_left, came_all, False, tile, 0, 2 * units, lambda i: i + per, parts_a)
    output, early = output_sums(ids, clip_slices, near_out, out_recv, middle, cotangent, mod, sums)
    away_here, output, parts_a, here, pair, sum_inner, *back_q = fence(
        away_here, output, parts_a, here, pair, sum_inner, *back_q
    )
    back_kv, k_gain_part = keys_back(ids, clip_slices, here, away_here, kv_own, gains, cosine, sine)
    back_kv, k_gain_part, branch_op = fence(back_kv, k_gain_part, branch_op)
    branch_y = yswap(branch_op)
    back_kv = unspread(back_kv)
    *back_kv, parts_a, branch_y = fence(*back_kv, parts_a, branch_y)
    sum_a = scatter(parts_a)

    first, second, send = fence(*pack(ids, back_q, back_kv))
    packed_recv = xswap(send)
    first_y = yswap(first)
    first_c = cswap(first)
    branch_all = [grad_branch, branch_c, branch_y, cswap(after(branch_y, first))]
    tile, total = 384, 4 * local_width
    parts_c = weight_grads(att_left, branch_all, False, tile, 0, total, lambda i: i + 6)
    cap_y = yswap(after(pick(pair, 1 - y), first))
    cap_total = pick(pair, y) + cap_y
    raw_cap, cap_gain_part = caption_back(ids, cap_total, cap_raw, gains)
    packed_recv, first_y, first_c, raw_cap, cap_gain_part, second, parts_c = fence(
        packed_recv, first_y, first_c, raw_cap, cap_gain_part, second, parts_c
    )
    second_y = yswap(second)
    second_c = cswap(second)
    recv_c = cswap(packed_recv)
    first_yc = cswap(first_y)
    tok_near, tok_send = qkv_back(ids, first, packed_recv, second, w_qkv)
    tok_near, tok_send, second_y, second_c, recv_c, first_yc, recv_op, raw_cap = fence(
        tok_near, tok_send, second_y, second_c, recv_c, first_yc, packed_recv, raw_cap
    )
    tok_recv = xswap(tok_send)
    recv_y = yswap(recv_op)
    second_yc = cswap(second_y)
    raw_c = cswap(raw_cap)
    parts_c = weight_grads(
        hid_left, [first, first_c, first_y, first_yc], True, tile, 0, total, lambda i: i, parts_c
    )
    parts_c = weight_grads(
        hid_left, [second, second_c, second_y, second_yc], True, tile, 0, total, lambda i: i + 4, parts_c
    )
    tok_recv, parts_c, recv_y, raw_c = fence(tok_recv, parts_c, recv_y, raw_c)
    recv_yc = cswap(recv_y)
    raw_y = yswap(raw_cap)
    parts_c = weight_grads(
        hid_left, [packed_recv, recv_c, recv_y, recv_yc], True, tile, 0, total, lambda i: i + 2, parts_c
    )
    parts_c, raw_y = fence(parts_c, raw_y)
    sum_c = scatter(parts_c)
    token_grad, late = tokens_back(
        ids,
        clip_slices,
        tokens,
        tok_near,
        tok_recv,
        mid_near,
        mid_came,
        mod,
        norm_row,
        [q_gain_part, k_gain_part, cap_gain_part, gate_part, early],
    )
    raw_yc = cswap(raw_y)
    late = late + cswap(late)
    cap_parts = caption_weights(ids, [raw_cap, raw_c, raw_y, raw_yc], caption_rows)
    late_y = yswap(late)
    late_y, cap_parts = fence(late_y, cap_parts)
    late = late + late_y
    late_z = hop(late, lambda i: i ^ GROUP)
    late_z, sum_a = fence(late_z, sum_a)
    late = late + late_z
    late = late + hop(late, lambda i: i ^ (2 * GROUP))
    late, *cap_parts = fence(late, *cap_parts)
    cap_parts = unspread(cap_parts)
    late_far = xswap(late)
    came_out = xswap(sum_a[:, units:])
    late_sum = late

    mod_grad, gain_rows = finish(ids, late_sum, late_far)
    mod_mine = mod_grad.astype(BF)
    caption_w_grad = caption_join(ids, fence(*cap_parts, mod_mine)[:LINE])
    cols_local = CD // bucket_count
    act_cols = lax.dynamic_slice_in_dim(activation, b * cols_local, cols_local, 1)
    ada_grad = mm(mod_mine, act_cols, TN)
    cond_part = mm(mod_mine, ada_w, NN)
    cond_sigmoid = jax.nn.sigmoid(cond)
    cond_grad = (
        (cond_part + xswap(cond_part)) * cond_sigmoid * (1.0 + cond * (1.0 - cond_sigmoid))
    )
    heads_each = H // seq_count
    cross_out = jnp.concatenate(
        [gain_rows[5, :heads_each], gain_rows[5, local_width : local_width + heads_each]]
    )

    down_out = sum_inner.astype(F32).T
    kept_out = sum_a[:, :units].astype(F32)
    came_out = came_out.astype(F32)
    gate_up_out = jnp.where(
        s == 0,
        jnp.concatenate([kept_out, came_out], 1),
        jnp.concatenate([came_out, kept_out], 1),
    ).T
    sum_c = after(sum_c, gate_up_out)
    return (
        output,
        token_grad,
        cond_grad,
        ada_grad,
        gain_rows[0],
        sum_c[:, : 3 * local_width].astype(F32).T,
        gain_rows[1],
        gain_rows[2],
        caption_w_grad,
        gain_rows[3],
        cross_out,
        sum_c[:, 3 * local_width :].astype(F32).T,
        gain_rows[4],
        gate_up_out,
        down_out,
    )


def project(activations, weight):
    return lax.dot_general(
        activations, weight, (((1,), (1,)), ((), ())), preferred_element_type=jnp.float32
    )


def clip_of(rows, ends):
    return jnp.sum((rows[:, None] >= ends[None, :]).astype(jnp.int32), axis=1)


def head_norm(values, gains, head_count):
    row_count = values.shape[0]
    split = values.reshape(row_count, head_count, -1)
    inverse = lax.rsqrt(jnp.mean(split * split, axis=-1, keepdims=True) + EPSILON)
    unit_rows = split * inverse
    return (unit_rows.reshape(row_count, -1) * gains, unit_rows, inverse)


def head_norm_back(norm_grads, gains, unit_rows, inverse):
    row_count, head_count, head_width = unit_rows.shape
    gain_grad = jnp.sum(norm_grads * unit_rows.reshape(row_count, -1), axis=0)
    unit_grad = (norm_grads * gains).reshape(row_count, head_count, head_width)
    raw_grad = inverse * (
        unit_grad - unit_rows * jnp.mean(unit_grad * unit_rows, axis=-1, keepdims=True)
    )
    return (raw_grad.reshape(row_count, -1), gain_grad)


def rotate(values, positions, head_count):
    row_count = values.shape[0]
    split = values.reshape(row_count, head_count, -1)
    half_width = split.shape[-1] // 2
    frequency = jnp.exp(
        jnp.arange(half_width, dtype=jnp.float32) * (-2.0 * math.log(10000.0) / (2 * half_width))
    )
    angles = positions[:, None] * frequency[None, :]
    cosine = jnp.cos(angles)[:, None, :]
    sine = jnp.sin(angles)[:, None, :]
    first_half = split[..., :half_width]
    second_half = split[..., half_width:]
    turned = jnp.concatenate(
        [first_half * cosine - second_half * sine, first_half * sine + second_half * cosine],
        axis=-1,
    )
    return turned.reshape(row_count, -1)


def block_size(row_count):
    return 512 if row_count % 512 == 0 else row_count


def general_body(
    tokens,
    cotangent,
    clip_slices,
    caption_lengths,
    caption,
    cond,
    ada_w,
    norm_gain,
    w_qkv,
    q_gain,
    k_gain,
    w_caption,
    ky_gain,
    cross_gate,
    w_out,
    ffn_gain,
    w_gate_up,
    w_down,
):
    seq_count = lax.axis_size("seq")
    bucket_count = lax.axis_size("bucket")
    tok_rows = tokens.shape[0]
    slice_rows = tok_rows * seq_count
    total_rows = slice_rows * bucket_count
    local_heads = H // seq_count
    local_width = local_heads * HD
    score_scale = HD ** (-0.5)
    bucket_id = lax.axis_index("bucket")
    seq_id = lax.axis_index("seq")
    ends = jnp.cumsum(clip_slices) * slice_rows
    starts = ends - clip_slices * slice_rows
    my_clip = clip_of(jnp.reshape(bucket_id * slice_rows, (1,)), ends)[0]
    clip_mask = jnp.arange(CLIPS) == my_clip
    clip_start = jnp.sum(jnp.where(clip_mask, starts, 0))
    first_token = (bucket_id * seq_count + seq_id) * tok_rows
    positions = (first_token + jnp.arange(tok_rows, dtype=jnp.int32) - clip_start).astype(
        jnp.float32
    )
    caption_usable = jnp.arange(CAP) < jnp.sum(jnp.where(clip_mask, caption_lengths, 0))
    head_first = seq_id * local_width
    gates_local = jnp.tanh(lax.dynamic_slice_in_dim(cross_gate, seq_id * local_heads, local_heads))
    ky_gain_local = lax.dynamic_slice_in_dim(ky_gain, head_first, local_width)
    activation = jax.nn.silu(cond).astype(jnp.bfloat16)
    cond_row = lax.dynamic_index_in_dim(activation, my_clip, 0, True)
    caption_rows = lax.dynamic_index_in_dim(caption, my_clip, 0, False)
    caption_raw = jnp.einsum(
        "ty,jdy->jtd", caption_rows, w_caption, preferred_element_type=jnp.float32
    )
    caption_norm, caption_unit, caption_inverse = head_norm(
        caption_raw[0], ky_gain_local, local_heads
    )
    caption_keys = caption_norm.astype(jnp.bfloat16).reshape(CAP, local_heads, HD)
    caption_values = caption_raw[1].astype(jnp.bfloat16).reshape(CAP, local_heads, HD)
    inputs = tokens.astype(jnp.float32)

    def key_usable(first_row, row_count):
        return clip_of(first_row + jnp.arange(row_count, dtype=jnp.int32), ends) == my_clip

    def fold_keys(queries3, running, segment, first_row):
        seg_keys, seg_values = segment
        row_count = seg_keys.shape[0]
        key_rows = block_size(row_count)
        steps_count = row_count // key_rows
        usable = key_usable(first_row, row_count).reshape(steps_count, key_rows)
        key_blocks = seg_keys.reshape(steps_count, key_rows, local_heads, HD)
        value_blocks = seg_values.reshape(steps_count, key_rows, local_heads, HD)

        def update(state, item):
            key_block, value_block, usable_block = item

            def update_include(inner):
                row_max, row_total, accum = inner
                scores = (
                    jnp.einsum(
                        "qhd,khd->hqk", queries3, key_block, preferred_element_type=jnp.float32
                    )
                    * score_scale
                )
                scores = jnp.where(usable_block[None, None, :], scores, MASKED)
                new_max = jnp.maximum(row_max, jnp.max(scores, axis=-1))
                factor = jnp.exp(row_max - new_max)
                weights = jnp.exp(scores - new_max[..., None])
                row_total = row_total * factor + jnp.sum(weights, axis=-1)
                accum = accum * factor.T[:, :, None] + jnp.einsum(
                    "hqk,khd->qhd",
                    weights.astype(jnp.bfloat16),
                    value_block,
                    preferred_element_type=jnp.float32,
                )
                return (new_max, row_total, accum)

            return (
                lax.cond(jnp.any(usable_block), update_include, lambda inner: inner, state),
                None,
            )

        running, unused = lax.scan(update, running, (key_blocks, value_blocks, usable))
        return running

    def local_fold(queries3, running, keys_whole):

        def local_visit(state, piece_index):
            first_row = piece_index * slice_rows
            segment = (
                lax.dynamic_slice_in_dim(keys_whole[0], first_row, slice_rows, 0),
                lax.dynamic_slice_in_dim(keys_whole[1], first_row, slice_rows, 0),
            )
            return (fold_keys(queries3, state, segment, first_row), None)

        running, unused = lax.scan(local_visit, running, jnp.arange(bucket_count, dtype=jnp.int32))
        return running

    def forward(qkv_full, out_full, modulation, second):
        shift_vec = modulation[:D]
        scale_vec = modulation[D : 2 * D]
        gate_vec = modulation[2 * D : 3 * D]
        inverse = lax.rsqrt(jnp.mean(inputs * inputs, axis=-1, keepdims=True) + EPSILON)
        unit_rows = inputs * inverse
        hidden = (unit_rows * norm_gain * (1.0 + scale_vec) + shift_vec).astype(jnp.bfloat16)
        projected = project(hidden, qkv_full)
        query_norm, query_unit, query_inverse = head_norm(projected[:, :D], q_gain, H)
        key_norm, key_unit, key_inverse = head_norm(projected[:, D : 2 * D], k_gain, H)
        queries = rotate(query_norm, positions, H).astype(jnp.bfloat16)
        keys_tok = rotate(key_norm, positions, H).astype(jnp.bfloat16)
        values_tok = projected[:, 2 * D :].astype(jnp.bfloat16)
        head_queries, head_keys, head_values = (
            lax.all_to_all(queries, "seq", split_axis=1, concat_axis=0, tiled=True),
            lax.all_to_all(keys_tok, "seq", split_axis=1, concat_axis=0, tiled=True),
            lax.all_to_all(values_tok, "seq", split_axis=1, concat_axis=0, tiled=True),
        )
        queries3 = head_queries.reshape(slice_rows, local_heads, HD)
        start_state = (
            jnp.full((local_heads, slice_rows), MASKED, jnp.float32),
            jnp.zeros((local_heads, slice_rows), jnp.float32),
            jnp.zeros((slice_rows, local_heads, HD), jnp.float32),
        )
        folder = functools.partial(fold_keys, queries3)
        if second:
            keys_whole = (
                lax.all_gather(head_keys, "bucket", axis=0, tiled=True),
                lax.all_gather(head_values, "bucket", axis=0, tiled=True),
            )
            final_state = local_fold(queries3, start_state, keys_whole)
        else:
            keys_whole = None
            final_state = folder(
                start_state,
                (
                    lax.all_gather(head_keys, "bucket", axis=0, tiled=True),
                    lax.all_gather(head_values, "bucket", axis=0, tiled=True),
                ),
                jnp.int32(0),
            )
        row_max, row_total, accum = final_state
        own = accum / row_total.T[:, :, None]
        cross_scores = (
            jnp.einsum("qhd,khd->hqk", queries3, caption_keys, preferred_element_type=jnp.float32)
            * score_scale
        )
        cross_prob = jax.nn.softmax(
            jnp.where(caption_usable[None, None, :], cross_scores, MASKED), axis=-1
        )
        other = jnp.einsum(
            "hqk,khd->qhd",
            cross_prob.astype(jnp.bfloat16),
            caption_values,
            preferred_element_type=jnp.float32,
        )
        combined = (
            (own + gates_local[None, :, None] * other)
            .reshape(slice_rows, local_width)
            .astype(jnp.bfloat16)
        )
        attention = lax.all_to_all(combined, "seq", split_axis=0, concat_axis=1, tiled=True)
        branch = project(attention, out_full)
        return dict(
            gate_vec=gate_vec,
            scale_vec=scale_vec,
            inverse=inverse,
            unit_rows=unit_rows,
            hidden=hidden,
            query_unit=query_unit,
            query_inverse=query_inverse,
            key_unit=key_unit,
            key_inverse=key_inverse,
            queries3=queries3,
            own_keys3=head_keys.reshape(slice_rows, local_heads, HD),
            own_values3=head_values.reshape(slice_rows, local_heads, HD),
            keys_whole=keys_whole,
            row_log=row_max + jnp.log(row_total),
            own=own,
            other=other,
            cross_prob=cross_prob,
            attention=attention,
            branch=branch,
            output=inputs + gate_vec * branch,
        )

    gathered = (
        lax.all_gather(ada_w, "seq", axis=0, tiled=True),
        lax.all_gather(w_qkv, "seq", axis=0, tiled=True),
        lax.all_gather(w_out, "seq", axis=0, tiled=True),
        lax.all_gather(w_gate_up, "seq", axis=0, tiled=True),
        lax.all_gather(w_down, "seq", axis=0, tiled=True),
    )
    modulation = project(cond_row, gathered[0])[0]
    first_pass = forward(gathered[1], gathered[2], modulation, False)
    middle = first_pass["output"]
    shift_mlp = modulation[3 * D : 4 * D]
    scale_mlp = modulation[4 * D : 5 * D]
    gate_mlp = modulation[5 * D :]
    mid_inverse = lax.rsqrt(jnp.mean(middle * middle, axis=-1, keepdims=True) + EPSILON)
    mid_unit = middle * mid_inverse
    mlp_in = (mid_unit * ffn_gain * (1.0 + scale_mlp) + shift_mlp).astype(jnp.bfloat16)
    gate_up = project(mlp_in, gathered[3])
    gate_half = gate_up[:, :FF]
    up_half = gate_up[:, FF:]
    gate_sigmoid = jax.nn.sigmoid(gate_half)
    silu_gate = gate_half * gate_sigmoid
    inner = (silu_gate * up_half).astype(jnp.bfloat16)
    mlp_branch = jnp.dot(inner, gathered[4], preferred_element_type=jnp.float32)
    output = (middle + gate_mlp * mlp_branch).astype(jnp.bfloat16)
    regathered = (
        lax.all_gather(ada_w, "seq", axis=0, tiled=True),
        lax.all_gather(w_qkv, "seq", axis=0, tiled=True),
        lax.all_gather(w_out, "seq", axis=0, tiled=True),
        lax.all_gather(w_gate_up, "seq", axis=0, tiled=True),
        lax.all_gather(w_down, "seq", axis=0, tiled=True),
    )
    second_pass = forward(regathered[1], regathered[2], modulation, True)
    ada_full, qkv_full, out_full, gate_up_full, down_full = regathered
    grad_out = cotangent.astype(jnp.float32)
    mlp_gate_grad = jnp.sum(grad_out * mlp_branch, axis=0)
    grad_mlp = (grad_out * gate_mlp).astype(jnp.bfloat16)
    grad_inner = lax.dot_general(
        grad_mlp, down_full, (((1,), (1,)), ((), ())), preferred_element_type=jnp.float32
    )
    grad_gate_half = grad_inner * up_half * gate_sigmoid * (1.0 + gate_half * (1.0 - gate_sigmoid))
    grad_up_half = grad_inner * silu_gate
    grad_gate_up = jnp.concatenate([grad_gate_half, grad_up_half], axis=1).astype(jnp.bfloat16)
    mlp_in_grad = jnp.dot(grad_gate_up, gate_up_full, preferred_element_type=jnp.float32)
    ffn_gain_grad = jnp.sum(mlp_in_grad * (1.0 + scale_mlp) * mid_unit, axis=0)
    shift_mlp_grad = jnp.sum(mlp_in_grad, axis=0)
    scale_mlp_grad = jnp.sum(mlp_in_grad * mid_unit * ffn_gain, axis=0)
    mid_unit_grad = mlp_in_grad * ffn_gain * (1.0 + scale_mlp)
    residual_grad = (
        mid_inverse
        * (mid_unit_grad - mid_unit * jnp.mean(mid_unit_grad * mid_unit, axis=-1, keepdims=True))
        + grad_out
    )
    gate_grad = jnp.sum(residual_grad * second_pass["branch"], axis=0)
    grad_branch = (residual_grad * second_pass["gate_vec"]).astype(jnp.bfloat16)
    attention = second_pass["attention"]
    grad_attention = jnp.dot(grad_branch, out_full, preferred_element_type=jnp.float32).astype(
        jnp.bfloat16
    )
    grad_heads = lax.all_to_all(grad_attention, "seq", split_axis=1, concat_axis=0, tiled=True)
    grad_own16 = grad_heads.reshape(slice_rows, local_heads, HD)
    grad_own = grad_own16.astype(jnp.float32)
    queries3 = second_pass["queries3"]
    own = second_pass["own"]
    other = second_pass["other"]
    cross_prob = second_pass["cross_prob"]
    grad_other = (grad_own * gates_local[None, :, None]).astype(jnp.bfloat16)
    gate_grad_local = jnp.sum(grad_own * other, axis=(0, 2)) * (1.0 - gates_local * gates_local)
    grad_cross_prob = jnp.einsum(
        "qhd,khd->hqk", grad_other, caption_values, preferred_element_type=jnp.float32
    )
    grad_cross = (
        cross_prob
        * (grad_cross_prob - jnp.sum(cross_prob * grad_cross_prob, axis=-1, keepdims=True))
    ).astype(jnp.bfloat16)
    cross_query_grad = score_scale * jnp.einsum(
        "hqk,khd->qhd", grad_cross, caption_keys, preferred_element_type=jnp.float32
    )
    caption_key_grad = score_scale * jnp.einsum(
        "hqk,qhd->khd", grad_cross, queries3, preferred_element_type=jnp.float32
    )
    caption_value_grad = jnp.einsum(
        "hqk,qhd->khd",
        cross_prob.astype(jnp.bfloat16),
        grad_other,
        preferred_element_type=jnp.float32,
    )
    row_delta = jnp.sum(grad_own * own, axis=-1).T
    row_log = second_pass["row_log"]
    keys_whole = second_pass["keys_whole"]

    def grad_piece(query_grad, piece_index, with_keys):
        first_row = piece_index * slice_rows
        key_rows = block_size(slice_rows)
        steps_count = slice_rows // key_rows
        key_blocks = lax.dynamic_slice_in_dim(keys_whole[0], first_row, slice_rows, 0).reshape(
            steps_count, key_rows, local_heads, HD
        )
        value_blocks = lax.dynamic_slice_in_dim(keys_whole[1], first_row, slice_rows, 0).reshape(
            steps_count, key_rows, local_heads, HD
        )
        usable = key_usable(first_row, slice_rows).reshape(steps_count, key_rows)

        def grad_visit(accum, item):
            key_block, value_block, usable_block = item

            def grad_include(inner):
                scores = (
                    jnp.einsum(
                        "qhd,khd->hqk", queries3, key_block, preferred_element_type=jnp.float32
                    )
                    * score_scale
                )
                scores = jnp.where(usable_block[None, None, :], scores, MASKED)
                probability = jnp.exp(scores - row_log[..., None])
                grad_prob = jnp.einsum(
                    "qhd,khd->hqk", grad_own16, value_block, preferred_element_type=jnp.float32
                )
                grad_scores = (probability * (grad_prob - row_delta[..., None])).astype(
                    jnp.bfloat16
                )
                updated = inner + score_scale * jnp.einsum(
                    "hqk,khd->qhd", grad_scores, key_block, preferred_element_type=jnp.float32
                )
                key_grad = score_scale * jnp.einsum(
                    "hqk,qhd->khd", grad_scores, queries3, preferred_element_type=jnp.float32
                )
                value_grad = jnp.einsum(
                    "hqk,qhd->khd",
                    probability.astype(jnp.bfloat16),
                    grad_own16,
                    preferred_element_type=jnp.float32,
                )
                return (updated, key_grad, value_grad)

            def skip(inner):
                empty = jnp.zeros((key_rows, local_heads, HD), jnp.float32)
                return (inner, empty, empty)

            updated, key_grad, value_grad = lax.cond(
                jnp.any(usable_block), grad_include, skip, accum
            )
            return (updated, (key_grad, value_grad))

        query_grad, (key_grads, value_grads) = lax.scan(
            grad_visit, query_grad, (key_blocks, value_blocks, usable)
        )
        return (
            query_grad,
            (
                key_grads.reshape(slice_rows, local_width),
                value_grads.reshape(slice_rows, local_width),
            ),
        )

    query_start = jnp.zeros((slice_rows, local_heads, HD), jnp.float32)
    piece_order = jnp.arange(bucket_count, dtype=jnp.int32)
    self_query_grad, (key_terms, value_terms) = lax.scan(
        functools.partial(grad_piece, with_keys=True), query_start, piece_order
    )
    key_sum, value_sum = (
        lax.psum_scatter(
            key_terms.reshape(total_rows, local_width).astype(jnp.bfloat16),
            "bucket",
            scatter_dimension=0,
            tiled=True,
        ).astype(jnp.float32),
        lax.psum_scatter(
            value_terms.reshape(total_rows, local_width).astype(jnp.bfloat16),
            "bucket",
            scatter_dimension=0,
            tiled=True,
        ).astype(jnp.float32),
    )
    query_grad16 = (
        (self_query_grad + cross_query_grad).reshape(slice_rows, local_width).astype(jnp.bfloat16)
    )
    tok_query_grad, tok_key_grad, tok_value_grad = (
        lax.all_to_all(query_grad16, "seq", split_axis=0, concat_axis=1, tiled=True),
        lax.all_to_all(
            key_sum.astype(jnp.bfloat16), "seq", split_axis=0, concat_axis=1, tiled=True
        ),
        lax.all_to_all(
            value_sum.astype(jnp.bfloat16), "seq", split_axis=0, concat_axis=1, tiled=True
        ),
    )
    query_raw_grad, q_gain_grad = head_norm_back(
        rotate(tok_query_grad.astype(jnp.float32), -positions, H),
        q_gain,
        second_pass["query_unit"],
        second_pass["query_inverse"],
    )
    key_raw_grad, k_gain_grad = head_norm_back(
        rotate(tok_key_grad.astype(jnp.float32), -positions, H),
        k_gain,
        second_pass["key_unit"],
        second_pass["key_inverse"],
    )
    projected_grad = jnp.concatenate(
        [query_raw_grad, key_raw_grad, tok_value_grad.astype(jnp.float32)], axis=1
    ).astype(jnp.bfloat16)
    hidden = second_pass["hidden"]
    out_each = D // seq_count
    qkv_each = 3 * D // seq_count
    gate_up_each = 2 * FF // seq_count
    down_each = FF // seq_count
    rows_each = out_each + qkv_each + gate_up_each + down_each
    device_count = rows_each * lax.axis_size("seq") // rows_each
    first_device = jnp.int32(0) // rows_each

    def part(operand, partner, each):
        picked = lax.dynamic_slice_in_dim(operand, first_device * each, device_count * each, 1)
        term = lax.dot_general(
            picked, partner, (((0,), (0,)), ((), ())), preferred_element_type=jnp.float32
        )
        return term.reshape(device_count, each, D)

    terms = [
        part(grad_branch, attention, out_each),
        part(projected_grad, hidden, qkv_each),
        part(grad_gate_up, mlp_in, gate_up_each),
        part(inner, grad_mlp, down_each),
    ]
    weight_grad_seq = lax.psum_scatter(
        jnp.concatenate(terms, axis=1)
        .reshape(rows_each * lax.axis_size("seq"), D)
        .astype(jnp.bfloat16),
        "seq",
        scatter_dimension=0,
        tiled=True,
    )
    hidden_grad = jnp.dot(projected_grad, qkv_full, preferred_element_type=jnp.float32)
    unit_rows = second_pass["unit_rows"]
    scale_vec = second_pass["scale_vec"]
    inverse = second_pass["inverse"]
    norm_gain_grad = jnp.sum(hidden_grad * (1.0 + scale_vec) * unit_rows, axis=0)
    shift_grad = jnp.sum(hidden_grad, axis=0)
    scale_grad = jnp.sum(hidden_grad * unit_rows * norm_gain, axis=0)
    unit_grad = hidden_grad * norm_gain * (1.0 + scale_vec)
    token_grad = (
        inverse * (unit_grad - unit_rows * jnp.mean(unit_grad * unit_rows, axis=-1, keepdims=True))
        + residual_grad
    )
    modulation_grad = jnp.where(
        clip_mask[:, None],
        jnp.concatenate(
            [shift_grad, scale_grad, gate_grad, shift_mlp_grad, scale_mlp_grad, mlp_gate_grad]
        )[None, :],
        0.0,
    )
    ky_gain_part = jnp.sum(
        caption_key_grad.reshape(CAP, local_width) * caption_unit.reshape(CAP, local_width), axis=0
    )
    ky_gain_full = lax.dynamic_update_slice_in_dim(
        jnp.zeros((D,), jnp.float32), ky_gain_part, head_first, 0
    )
    gate_full = lax.dynamic_update_slice_in_dim(
        jnp.zeros((H,), jnp.float32), gate_grad_local, seq_id * local_heads, 0
    )
    caption_part = jnp.stack(
        [caption_key_grad.reshape(CAP, local_width), caption_value_grad.reshape(CAP, local_width)]
    )[None]
    zero_index = jnp.zeros((), jnp.int32)
    caption_full = lax.dynamic_update_slice(
        jnp.zeros((CLIPS, 2, CAP, D), jnp.float32),
        caption_part,
        (my_clip, zero_index, zero_index, head_first),
    )
    reduced = lax.psum(
        (
            norm_gain_grad,
            q_gain_grad,
            k_gain_grad,
            ky_gain_full,
            gate_full,
            modulation_grad,
            caption_full,
            ffn_gain_grad,
        ),
        ("bucket", "seq"),
    )
    modulation_total = reduced[5].astype(jnp.bfloat16)
    rows_local = 6 * D // seq_count
    cols_local = CD // bucket_count
    ada_grad = lax.dot_general(
        lax.dynamic_slice_in_dim(modulation_total, seq_id * rows_local, rows_local, 1),
        lax.dynamic_slice_in_dim(activation, bucket_id * cols_local, cols_local, 1),
        (((0,), (0,)), ((), ())),
        preferred_element_type=jnp.float32,
    )
    cond_sigmoid = jax.nn.sigmoid(cond)
    cond_grad = (
        jnp.dot(modulation_total, ada_full, preferred_element_type=jnp.float32)
        * cond_sigmoid
        * (1.0 + cond * (1.0 - cond_sigmoid))
    )
    caption_total = lax.dynamic_slice_in_dim(reduced[6], head_first, local_width, 3)
    raw_keys_all = jnp.einsum(
        "cty,dy->ctd", caption, w_caption[0], preferred_element_type=jnp.float32
    ).reshape(CLIPS * CAP, local_width)
    ignored, unit_all, inverse_all = head_norm(raw_keys_all, ky_gain_local, local_heads)
    raw_key_grad, unused_gain = head_norm_back(
        caption_total[:, 0].reshape(CLIPS * CAP, local_width), ky_gain_local, unit_all, inverse_all
    )
    raw_grad = jnp.stack(
        [raw_key_grad.reshape(CLIPS, CAP, local_width), caption_total[:, 1]], axis=1
    ).astype(jnp.bfloat16)
    caption_cols = lax.dynamic_slice_in_dim(
        caption, bucket_id * (YD // bucket_count), YD // bucket_count, 2
    )
    caption_w_grad = jnp.einsum(
        "cjtd,cty->jdy", raw_grad, caption_cols, preferred_element_type=jnp.float32
    )
    combined_grads = lax.psum_scatter(
        weight_grad_seq, "bucket", scatter_dimension=1, tiled=True
    ).astype(jnp.float32)
    out_grad_out = combined_grads[:out_each]
    qkv_grad_out = combined_grads[out_each : out_each + qkv_each]
    gate_up_grad_out = combined_grads[out_each + qkv_each : out_each + qkv_each + gate_up_each]
    down_grad_out = combined_grads[out_each + qkv_each + gate_up_each :]
    return (
        output,
        token_grad,
        cond_grad,
        ada_grad,
        reduced[0],
        qkv_grad_out,
        reduced[1],
        reduced[2],
        caption_w_grad,
        reduced[3],
        reduced[4],
        out_grad_out,
        reduced[7],
        gate_up_grad_out,
        down_grad_out,
    )


def solution(mesh):
    fits = mesh.shape["seq"] == 2 and mesh.shape["bucket"] == LINE * GROUP
    bucket = ("bucket",)
    if fits:
        bucket = BUCKET
        mesh = Mesh(mesh.devices.reshape(LINE, 2, GROUP // 2, 2), (*BUCKET, "seq"))
    in_specs = (
        P((*bucket, "seq"), None),
        P((*bucket, "seq"), None),
        P(),
        P(),
        P(),
        P(),
        P("seq", None),
        P(),
        P("seq", None),
        P(),
        P(),
        P(None, "seq", None),
        P(),
        P(),
        P("seq", None),
        P(),
        P("seq", None),
        P("seq", None),
    )
    out_specs = (
        P((*bucket, "seq"), None),
        P((*bucket, "seq"), None),
        P(),
        P("seq", bucket),
        P(),
        P("seq", bucket),
        P(),
        P(),
        P(None, "seq", bucket),
        P(),
        P(),
        P("seq", bucket),
        P(),
        P("seq", bucket),
        P("seq", bucket),
    )
    body = fast_body if fits else general_body
    return jax.shard_map(body, mesh=mesh, in_specs=in_specs, out_specs=out_specs, check_vma=False)
```

```python
import functools
import math

import jax
import jax.numpy as jnp
from jax import lax
from jax.experimental import pallas as pl
from jax.experimental.pallas import tpu as pltpu
from jax.sharding import Mesh, PartitionSpec as P

H = 24
HD = 64
D = 1536
FF = 4096
YD = 4096
CD = 1024
CAP = 128
CLIPS = 4

EPSILON = 1e-06
MASKED = -1e30
BF = jnp.bfloat16
F32 = jnp.float32
NN = (((1,), (0,)), ((), ()))
NT = (((1,), (1,)), ((), ()))
TN = (((0,), (0,)), ((), ()))
GROUP = 4
LINE = 4
BUCKET = ("z", "y", "c")
SENDS = (1, 2, 3, 0)
SMEM = pl.BlockSpec(memory_space=pltpu.SMEM)
VMEM = pl.BlockSpec(memory_space=pltpu.VMEM)
shape = jax.ShapeDtypeStruct


def cost(microseconds):
    return pl.CostEstimate(
        flops=0, transcendentals=0, bytes_accessed=int(microseconds * 20_000)
    )


def mm(a, b, dims):
    return lax.dot_general(a, b, dims, preferred_element_type=F32)


def clip_at(slices, slot):
    ends = [slices[0]]
    for i in range(1, CLIPS):
        ends.append(ends[-1] + slices[i])
    clip = jnp.int32(0)
    first, last = jnp.int32(0), ends[0]
    for i in range(CLIPS - 1):
        later = slot >= ends[i]
        clip = jnp.where(later, i + 1, clip)
        first = jnp.where(later, ends[i], first)
        last = jnp.where(later, ends[i + 1], last)
    return clip, first, last


def slot_of(bucket, k, j):
    return lax.rem(bucket // GROUP - k + LINE, LINE) * GROUP + jnp.bitwise_xor(
        lax.rem(bucket, GROUP), j
    )


def chunk_at(bucket, k, width):
    return pl.multiple_of(lax.rem(bucket // GROUP + k, LINE) * width, HD)


def norm_rope(raw, gain, cosine, sine):
    inverse = lax.rsqrt(jnp.mean(raw * raw, axis=0, keepdims=True) + EPSILON)
    normed = raw * inverse * gain
    half = raw.shape[0] // 2
    first, second = normed[:half], normed[half:]
    return jnp.concatenate(
        [first * cosine - second * sine, first * sine + second * cosine], axis=0
    )


def norm_rope_back(grad, raw, gain, cosine, sine):
    inverse = lax.rsqrt(jnp.mean(raw * raw, axis=0, keepdims=True) + EPSILON)
    unit = raw * inverse
    half = raw.shape[0] // 2
    first, second = grad[:half], grad[half:]
    turned = jnp.concatenate(
        [first * cosine + second * sine, second * cosine - first * sine], axis=0
    )
    gain_grad = jnp.sum(turned * unit, axis=1, keepdims=True)
    unit_grad = turned * gain
    raw_grad = inverse * (unit_grad - unit * jnp.mean(unit_grad * unit, axis=0, keepdims=True))
    return raw_grad, gain_grad


def row_inverse(values):
    return lax.rsqrt(jnp.mean(values * values, axis=-1, keepdims=True) + EPSILON)


def pre_kernel(ids, slices, tok_a, tok_b, mod_a, mod_b, gain_ref, w_ref, p_ref, hid_ref, mod_ref):
    @pl.when(pl.program_id(0) == 0)
    def _():
        s = ids[1]
        clip, _, _ = clip_at(slices, ids[0])
        row_a, row_b = mod_a[pl.ds(clip, 1), :], mod_b[pl.ds(clip, 1), :]
        low, high = jnp.where(s == 0, row_a, row_b), jnp.where(s == 0, row_b, row_a)
        mod_ref[...] = jnp.zeros_like(mod_ref)
        for i in range(3):
            mod_ref[i : i + 1, :] = low[:, i * D : (i + 1) * D]
            mod_ref[3 + i : 4 + i, :] = high[:, i * D : (i + 1) * D]
        shift, scale = mod_ref[0:1, :], mod_ref[1:2, :]
        count = tok_a.shape[0]
        for place, ref in ((s, tok_a), (1 - s, tok_b)):
            values = ref[...].astype(F32)
            hidden = values * row_inverse(values) * gain_ref[...] * (1.0 + scale) + shift
            hid_ref[pl.ds(pl.multiple_of(place * count, count), count), :] = hidden.astype(BF)

    p_ref[...] = mm(w_ref[...], hid_ref[...], NT).astype(BF)


def pre(ids, slices, tok_a, tok_b, mod_a, mod_b, gain, w_qkv):
    rows = 2 * tok_a.shape[0]
    tile = w_qkv.shape[0] // 3
    full = lambda v: pl.BlockSpec(v.shape, lambda i: (0,) * v.ndim)
    return pl.pallas_call(
        pre_kernel,
        grid=(w_qkv.shape[0] // tile,),
        in_specs=[SMEM, SMEM]
        + [full(v) for v in (tok_a, tok_b, mod_a, mod_b, gain)]
        + [pl.BlockSpec((tile, D), lambda i: (i, 0))],
        out_specs=[
            pl.BlockSpec((tile, rows), lambda i: (i, 0)),
            pl.BlockSpec((rows, D), lambda i: (0, 0)),
            pl.BlockSpec((8, D), lambda i: (0, 0)),
        ],
        out_shape=[shape((w_qkv.shape[0], rows), BF), shape((rows, D), BF), shape((8, D), F32)],
        name="pre",
        cost_estimate=cost(6),
    )(ids, slices, tok_a, tok_b, mod_a, mod_b, gain, w_qkv)


def route_kernel(ids, p_ref, r_ref, *outs):
    b, s = ids[0], ids[1]
    local = r_ref.shape[0]
    width = local // LINE
    for k in range(LINE):
        at = chunk_at(b, k, width)
        kv_ref, q_ref = outs[k], outs[LINE + k]

        @pl.when(s == 0)
        def _():
            q_ref[...] = p_ref[pl.ds(at, width), :]
            kv_ref[:width, :] = p_ref[pl.ds(2 * local + at, width), :]
            kv_ref[width:, :] = r_ref[pl.ds(at, width), :]

        @pl.when(s == 1)
        def _():
            q_ref[...] = r_ref[pl.ds(at, width), :]
            kv_ref[:width, :] = p_ref[pl.ds(at, width), :]
            kv_ref[width:, :] = p_ref[pl.ds(2 * local + at, width), :]


def route(ids, projected, received):
    local, rows = received.shape
    width = local // LINE
    outs = pl.pallas_call(
        route_kernel,
        in_specs=[SMEM, VMEM, VMEM],
        out_specs=[VMEM] * (2 * LINE),
        out_shape=[shape((2 * width, rows), BF)] * LINE + [shape((width, rows), BF)] * LINE,
        name="route",
        cost_estimate=cost(2.5),
    )(ids, projected, received)
    return outs[:LINE], outs[LINE:]


def caption_kernel(ids, w_ref, cap_ref, gains_ref, raw_ref, kv_ref):
    step = pl.program_id(0)
    width = w_ref.shape[1]

    @pl.when(step == 0)
    def _():
        raw_ref[...] = jnp.zeros_like(raw_ref)

    for j in range(2):
        raw_ref[j * width : (j + 1) * width, :] += mm(w_ref[j], cap_ref[...], NT)

    @pl.when(step == pl.num_programs(0) - 1)
    def _():
        base = ids[1] * LINE * width + ids[0] // GROUP * width
        for h in range(width // HD):
            at = slice(h * HD, h * HD + HD)
            raw = raw_ref[at, :]
            inverse = lax.rsqrt(jnp.mean(raw * raw, axis=0, keepdims=True) + EPSILON)
            gain = gains_ref[pl.ds(pl.multiple_of(base + h * HD, HD), HD), 2:3]
            keys = (raw * inverse * gain).astype(BF)
            for c in range(CLIPS):
                kv_ref[c, at, :] = keys[:, c * CAP : (c + 1) * CAP]
        for c in range(CLIPS):
            kv_ref[c, width:, :] = raw_ref[width:, c * CAP : (c + 1) * CAP].astype(BF)


def caption_keys(ids, w_caption, caption, gains):
    width = w_caption.shape[1] // LINE
    tile = 1024
    count = caption.shape[0]
    return pl.pallas_call(
        caption_kernel,
        grid_spec=pltpu.PrefetchScalarGridSpec(
            num_scalar_prefetch=1,
            grid=(YD // tile,),
            in_specs=[
                pl.BlockSpec((2, width, tile), lambda i, ids: (0, ids[0] // GROUP, i)),
                pl.BlockSpec((count, tile), lambda i, ids: (0, i)),
                pl.BlockSpec(gains.shape, lambda i, ids: (0, 0)),
            ],
            out_specs=[
                pl.BlockSpec((2 * width, count), lambda i, ids: (0, 0)),
                pl.BlockSpec((CLIPS, 2 * width, CAP), lambda i, ids: (0, 0, 0)),
            ],
        ),
        out_shape=[shape((2 * width, count), F32), shape((CLIPS, 2 * width, CAP), BF)],
        name="caption_keys",
        cost_estimate=cost(8),
    )(ids, w_caption, caption, gains)


def attend_kernel(ids, slices, lengths, gates, *refs):
    q_refs = refs[:LINE]
    kv_refs = refs[LINE : LINE + GROUP]
    cap_ref, gains_ref, cos_ref, sin_ref = refs[LINE + GROUP : LINE + GROUP + 4]
    outs = refs[LINE + GROUP + 4 :]
    comb_refs = outs[:LINE]
    own_ref, other_ref, stat_ref, qs_ref, ks_ref, pair_ref = outs[LINE : LINE + 6]
    value_ref, cap_value_ref, sum_ref = outs[LINE + 6 :]
    b, s = ids[0], ids[1]
    width, rows = q_refs[0].shape
    heads = width // HD
    scale = HD**-0.5
    base = s * LINE * width + b // GROUP * width

    def gain_of(h, column):
        return gains_ref[pl.ds(pl.multiple_of(base + h * HD, HD), HD), column : column + 1]

    key_gains = [gain_of(h, 1) for h in range(heads)]
    query_gains = [gain_of(h, 0) for h in range(heads)]
    is_one = lax.broadcasted_iota(jnp.int32, (rows, 2 * HD), 1) < HD
    for j, kv_ref in enumerate(kv_refs):
        for k in range(LINE):
            slot = slot_of(b, k, j)
            _, start, _ = clip_at(slices, slot)
            cosine, sine = cos_ref[slot - start], sin_ref[slot - start]
            for h in range(heads):
                at = slice(h * HD, h * HD + HD)
                raw = kv_ref[k, at, :].astype(F32)
                keys = norm_rope(raw, key_gains[h], cosine, sine)
                values = kv_ref[k, width + h * HD : width + h * HD + HD, :].astype(F32)
                ks_ref[slot, at, :] = keys.astype(BF)
                pair = jnp.concatenate([keys, values], axis=0).T
                pair_ref[slot, h] = pair.astype(BF)
                value_ref[slot, h] = jnp.where(is_one, 1.0, pair).astype(BF)
    cap_one = is_one[:CAP]
    for c in range(CLIPS):
        for h in range(heads):
            values = cap_ref[c, width + h * HD : width + h * HD + HD, :].astype(F32)
            both = jnp.concatenate([values, values], axis=0).T
            cap_value_ref[c, h] = jnp.where(cap_one, 1.0, both).astype(BF)

    for i in range(LINE):
        slot = slot_of(b, i, 0)
        clip, first, last = clip_at(slices, slot)
        cosine, sine = cos_ref[slot - first], sin_ref[slot - first]
        queries = []
        for h in range(heads):
            at = slice(h * HD, h * HD + HD)
            raw = q_refs[i][at, :].astype(F32)
            turned = norm_rope(raw, query_gains[h], cosine, sine).astype(BF).astype(F32) * scale
            qs_ref[i, at, :] = turned.astype(BF)
            queries.append(turned.T.astype(BF))
        sum_ref[...] = jnp.zeros_like(sum_ref)

        def step(n, carry):
            for h in range(heads):
                at = slice(h * HD, h * HD + HD)
                weights = jnp.exp(mm(queries[h], ks_ref[n, at, :], NN))
                sum_ref[h] += mm(weights.astype(BF), value_ref[n, h], NN)
            return carry

        lax.fori_loop(first, last, step, 0)
        usable = lax.broadcasted_iota(jnp.int32, (rows, CAP), 1) < lengths[clip]
        for h in range(heads):
            at = slice(h * HD, h * HD + HD)
            total = sum_ref[h].T
            inverse = 1.0 / total[0:1]
            own = total[HD:] * inverse
            weights = jnp.where(usable, jnp.exp(mm(queries[h], cap_ref[clip, at, :], NN)), 0.0)
            cap_total = mm(weights.astype(BF), cap_value_ref[clip, h], NN).T
            cap_inverse = 1.0 / cap_total[0:1]
            other = cap_total[HD:] * cap_inverse
            own_ref[i, at, :] = own
            other_ref[i, at, :] = other
            gate = gates[(s * LINE + b // GROUP) * heads + h]
            comb_refs[i][at, :] = (own + gate * other).astype(BF)
            stat_ref[i, h : h + 1, :] = inverse
            stat_ref[i, 4 + h : 5 + h, :] = cap_inverse


def attend(ids, slices, lengths, gates, queries, kv_pieces, cap_kv, gains, cosine, sine):
    width, rows = queries[0].shape
    slots = LINE * GROUP
    heads = width // HD
    outs = pl.pallas_call(
        attend_kernel,
        in_specs=[SMEM] * 4 + [VMEM] * (LINE + GROUP + 4),
        out_specs=[VMEM] * (LINE + 6),
        out_shape=[shape((width, rows), BF)] * LINE
        + [
            shape((LINE, width, rows), F32),
            shape((LINE, width, rows), F32),
            shape((LINE, 8, rows), F32),
            shape((LINE, width, rows), BF),
            shape((slots, width, rows), BF),
            shape((slots, heads, rows, 2 * HD), BF),
        ],
        scratch_shapes=[
            pltpu.VMEM((slots, heads, rows, 2 * HD), BF),
            pltpu.VMEM((CLIPS, heads, CAP, 2 * HD), BF),
            pltpu.VMEM((heads, rows, 2 * HD), F32),
        ],
        name="attend",
        cost_estimate=cost(33),
    )(ids, slices, lengths, gates, *queries, *kv_pieces, cap_kv, gains, cosine, sine)
    return outs[:LINE], outs[LINE:]


def out_kernel(ids, *refs):
    own, other = refs[:LINE], refs[LINE : 2 * LINE]
    w_ref, att_ref, branch_ref = refs[2 * LINE :]
    b, s = ids[0], ids[1]
    width = own[0].shape[0]
    for k in range(LINE):
        at = chunk_at(b, k, width)
        att_ref[pl.ds(pl.multiple_of(s * LINE * width + at, HD), width), :] = own[k][...]
        att_ref[pl.ds(pl.multiple_of((1 - s) * LINE * width + at, HD), width), :] = other[k][...]
    branch_ref[...] = mm(w_ref[...], att_ref[...], NN).T.astype(BF)


def out_proj(ids, own, other, w_out):
    rows = own[0].shape[1]
    return pl.pallas_call(
        out_kernel,
        in_specs=[SMEM] + [VMEM] * (2 * LINE + 1),
        out_specs=[VMEM, VMEM],
        out_shape=[shape((D, rows), BF), shape((rows, w_out.shape[0]), BF)],
        name="out_proj",
        cost_estimate=cost(3.5),
    )(ids, *own, *other, w_out)


def cut_kernel(turned, ids, *refs):
    count = len(turned)
    ins = refs[:count]
    own_ref, c_ref, y_ref, scratch = refs[count:]
    place = lax.rem(ids[0], GROUP)
    columns = own_ref.shape[3]
    for n in range(count):
        if turned[n]:
            source = ins[n]
        else:
            scratch[...] = ins[n][...].astype(F32).T
            source = scratch
        for k in range(LINE):
            for j, (ref, i) in enumerate(((own_ref, 0), (c_ref, 0), (y_ref, 0), (y_ref, 1))):
                at = (k * GROUP + jnp.bitwise_xor(place, j)) * columns
                ref[i, n, k] = source[pl.ds(pl.multiple_of(at, 32), columns), :].astype(BF)


def cut(ids, values, turned):
    rows = values[0].shape[1 if turned[0] else 0]
    columns = D // (LINE * GROUP)
    count = len(values)
    return pl.pallas_call(
        functools.partial(cut_kernel, tuple(turned)),
        in_specs=[SMEM] + [VMEM] * count,
        out_specs=[VMEM] * 3,
        out_shape=[shape((n, count, LINE, columns, rows), BF) for n in (1, 1, 2)],
        scratch_shapes=[pltpu.VMEM((D, rows), F32)],
        name="cut",
        cost_estimate=cost(2.4),
    )(ids, *values)


def ffn_kernel(
    ids,
    tok_a,
    tok_b,
    br_a,
    br_b,
    out16_ref,
    mod_ref,
    gain_ref,
    kept_ref,
    came_ref,
    too_ref,
    down_ref,
    inner_a_ref,
    inner_b_ref,
    gkept_ref,
    gcame_ref,
    in16_ref,
    mid_ref,
    near_ref,
    far_ref,
    near_out_ref,
    far_out_ref,
    acc_in,
    acc_out,
):
    step = pl.program_id(0)
    steps = pl.num_programs(0)
    s = ids[1]
    count = tok_a.shape[0]
    half = br_a.shape[1]
    gate, shift2, scale2 = [mod_ref[i : i + 1, :] for i in (2, 3, 4)]
    mlp_gain = gain_ref[...] * (1.0 + scale2)

    @pl.when(step == 0)
    def _():
        for place, tok in ((s, tok_a), (1 - s, tok_b)):
            at = pl.ds(pl.multiple_of(place * count, count), count)
            mid_ref[at, :] = tok[...].astype(F32)
        low = jnp.where(s == 0, br_a[...].astype(F32), br_b[...].astype(F32))
        high = jnp.where(s == 0, br_b[...].astype(F32), br_a[...].astype(F32))
        mid_ref[:, :half] += gate[:, :half] * low
        mid_ref[:, half:] += gate[:, half:] * high
        middle = mid_ref[...]
        in16_ref[...] = (middle * row_inverse(middle) * mlp_gain + shift2).astype(BF)
        acc_in[...] = jnp.zeros_like(acc_in)
        acc_out[...] = jnp.zeros_like(acc_out)

    w_kept, w_down = kept_ref[...], down_ref[...]
    mine = step // (steps // 2) == lax.rem(ids[0], 2)
    w_came = jnp.where(mine, came_ref[0], too_ref[0])
    kept = mm(in16_ref[...], w_kept, NT)
    other = mm(in16_ref[...], w_came, NT)
    grad_inner = mm(out16_ref[...], w_down, NT)
    gate_half = jnp.where(s == 0, kept, other)
    up_half = jnp.where(s == 0, other, kept)
    sigmoid = jax.nn.sigmoid(gate_half)
    silu = gate_half * sigmoid
    inner = (silu * up_half).astype(BF)
    grad_gate = grad_inner * up_half * sigmoid * (1.0 + gate_half * (1.0 - sigmoid))
    grad_up = grad_inner * silu
    grad_kept = jnp.where(s == 0, grad_gate, grad_up).astype(BF)
    grad_came = jnp.where(s == 0, grad_up, grad_gate).astype(BF)
    @pl.when(step < steps // 2)
    def _():
        inner_a_ref[...] = inner

    @pl.when(step >= steps // 2)
    def _():
        inner_b_ref[...] = inner

    gkept_ref[...] = grad_kept
    gcame_ref[...] = grad_came
    acc_in[...] += mm(grad_kept, w_kept, NN) + mm(grad_came, w_came, NN)
    acc_out[...] += mm(inner, w_down, NN)

    @pl.when(step == steps - 1)
    def _():
        middle = mid_ref[...]
        part = jnp.sum(
            acc_in[...] * mlp_gain * (middle * row_inverse(middle)), axis=-1, keepdims=True
        )
        near_ref[:, :half] = acc_in[:, pl.ds(pl.multiple_of(s * half, half), half)]
        near_ref[:, half:] = jnp.broadcast_to(part, (part.shape[0], 128))
        far_ref[:, :half] = acc_in[:, pl.ds(pl.multiple_of((1 - s) * half, half), half)].astype(BF)
        high = part.astype(BF).astype(F32)
        middle_part = (part - high).astype(BF).astype(F32)
        low_part = part - high - middle_part
        lane = lax.broadcasted_iota(jnp.int32, (part.shape[0], 128), 1)
        spread = jnp.where(lane == 0, high, jnp.where(lane == 1, middle_part, jnp.where(lane == 2, low_part, 0.0)))
        far_ref[:, half:] = spread.astype(BF)
        near_out_ref[...] = acc_out[pl.ds(pl.multiple_of(s * count, count), count), :]
        far_out_ref[...] = acc_out[pl.ds(pl.multiple_of((1 - s) * count, count), count), :].astype(BF)


def ffn(ids, toks, branches, grad_mlp, mod, gain, w_gate_up, came, too, w_down):
    count = toks[0].shape[0]
    rows = 2 * count
    half = D // 2
    units = w_down.shape[0]
    tile = 512
    steps = units // tile
    full = lambda v: pl.BlockSpec(v.shape, lambda i, ids: (0,) * v.ndim)

    def fixed(r, c):
        return pl.BlockSpec((r, c), lambda i, ids: (0, 0))

    def part(i, ids, flip):
        core = jnp.bitwise_xor(lax.rem(ids[0], 2), flip)
        return jnp.clip(i - core * (steps // 2), 0, steps // 2 - 1)

    small = [*toks, *branches, grad_mlp, mod, gain]
    return pl.pallas_call(
        ffn_kernel,
        grid_spec=pltpu.PrefetchScalarGridSpec(
            num_scalar_prefetch=1,
            grid=(steps,),
            in_specs=[full(v) for v in small]
            + [
                pl.BlockSpec((tile, D), lambda i, ids: (ids[1] * steps + i, 0)),
                pl.BlockSpec((1, tile, D), lambda i, ids: (1 - ids[1], part(i, ids, 0), 0)),
                pl.BlockSpec((1, tile, D), lambda i, ids: (1 - ids[1], part(i, ids, 1), 0)),
                pl.BlockSpec((tile, D), lambda i, ids: (i, 0)),
            ],
            out_specs=[
                pl.BlockSpec((rows, tile), lambda i, ids: (0, jnp.minimum(i, steps // 2 - 1))),
                pl.BlockSpec((rows, tile), lambda i, ids: (0, jnp.maximum(i - steps // 2, 0))),
            ]
            + [pl.BlockSpec((rows, tile), lambda i, ids: (0, i))] * 2
            + [
                fixed(rows, D),
                fixed(rows, D),
                fixed(rows, half + 128),
                fixed(rows, half + 128),
                fixed(count, D),
                fixed(count, D),
            ],
            scratch_shapes=[pltpu.VMEM((rows, D), F32), pltpu.VMEM((rows, D), F32)],
        ),
        out_shape=[shape((rows, units // 2), BF)] * 2
        + [shape((rows, units), BF)] * 2
        + [
            shape((rows, D), BF),
            shape((rows, D), F32),
            shape((rows, half + 128), F32),
            shape((rows, half + 128), BF),
            shape((count, D), F32),
            shape((count, D), BF),
        ],
        name="ffn",
        cost_estimate=cost(18),
    )(ids, *small, w_gate_up, came, too, w_down)


def mid_kernel(
    ids,
    near_ref,
    recv_ref,
    mid_ref,
    cot_a,
    cot_b,
    br_ref,
    mod_ref,
    gain_ref,
    w_ref,
    sums_ref,
    gbr_ref,
    near_mid_ref,
    far_mid_ref,
    *refs,
):
    near_refs, far_refs, scratch = refs[:2], refs[2:4], refs[4]
    b, s = ids[0], ids[1]
    half = D // 2
    count = cot_a.shape[0]
    cols = pl.ds(pl.multiple_of(s * half, half), half)
    gate, scale2 = mod_ref[2:3, cols], mod_ref[4:5, cols]
    gain = gain_ref[:, cols]
    middle = mid_ref[...]
    inverse = row_inverse(middle)
    unit = mid_ref[:, cols] * inverse
    parts = jnp.sum(recv_ref[:, half:].astype(F32), axis=-1, keepdims=True)
    mean = (near_ref[:, half : half + 1] + parts) * (1.0 / D)
    grad_in = near_ref[:, :half] + recv_ref[:, :half].astype(F32)
    cot_own, cot_far = cot_a[:, cols].astype(F32), cot_b[:, cols].astype(F32)
    cot = jnp.concatenate(
        [jnp.where(s == 0, cot_own, cot_far), jnp.where(s == 0, cot_far, cot_own)], axis=0
    )
    scaled = grad_in * (1.0 + scale2)
    grad_mid = cot + inverse * (scaled * gain - unit * mean)
    sums_ref[...] = jnp.zeros_like(sums_ref)
    sums_ref[0:1, :] = jnp.sum(grad_mid * br_ref[...].astype(F32), axis=0, keepdims=True)
    sums_ref[1:2, :] = jnp.sum(grad_in, axis=0, keepdims=True)
    sums_ref[2:3, :] = jnp.sum(grad_in * unit, axis=0, keepdims=True) * gain
    sums_ref[3:4, :] = jnp.sum(scaled * unit, axis=0, keepdims=True)
    grad_branch = (grad_mid * gate).astype(BF)
    gbr_ref[...] = grad_branch
    top, low = grad_mid[:count], grad_mid[count:]
    near_mid_ref[...] = jnp.where(s == 0, top, low)
    far_mid_ref[...] = jnp.where(s == 0, low, top).astype(BF)
    scratch[...] = mm(grad_branch, w_ref[...], NN).T
    width = near_refs[0].shape[0] // 2
    for n, k in enumerate(SENDS):
        at = chunk_at(b, k, width)
        to = slice(n % 2 * width, n % 2 * width + width)
        near_refs[n // 2][to, :] = scratch[pl.ds(pl.multiple_of(s * half + at, HD), width), :]
        far_refs[n // 2][to, :] = scratch[
            pl.ds(pl.multiple_of((1 - s) * half + at, HD), width), :
        ].astype(BF)


def mid_back(ids, near, received, middle, cots, branch, mod, gain, w_out):
    rows, half = branch.shape
    width = half // LINE
    count = cots[0].shape[0]
    outs = pl.pallas_call(
        mid_kernel,
        in_specs=[SMEM] + [VMEM] * 9,
        out_specs=[VMEM] * 8,
        out_shape=[
            shape((8, half), F32),
            shape((rows, half), BF),
            shape((count, half), F32),
            shape((count, half), BF),
        ]
        + [shape((2 * width, rows), F32)] * 2
        + [shape((2 * width, rows), BF)] * 2,
        scratch_shapes=[pltpu.VMEM((D, rows), F32)],
        name="mid_back",
        cost_estimate=cost(5.5),
    )(ids, near, received, middle, *cots, branch, mod, gain, w_out)
    return outs[:4], outs[4:6], outs[6:]


def add_pair_kernel(near_ref, recv_ref, a_ref, b_ref):
    width = a_ref.shape[0]
    total = (near_ref[...] + recv_ref[...].astype(F32)).astype(BF)
    a_ref[...] = total[:width]
    b_ref[...] = total[width:]


def add_pair(near, received):
    both, rows = near.shape
    return pl.pallas_call(
        add_pair_kernel,
        in_specs=[VMEM, VMEM],
        out_specs=[VMEM, VMEM],
        out_shape=[shape((both // 2, rows), BF)] * 2,
        name="add_pair",
        cost_estimate=cost(1),
    )(near, received)


def place_row(b, column):
    width = column.shape[0]
    row = jnp.broadcast_to(column, (width, 128)).T[0:1]
    z = b // GROUP
    return jnp.concatenate([jnp.where(z == k, row, 0.0) for k in range(LINE)], axis=1)


def output_kernel(ids, slices, near_ref, recv_ref, mid_ref, cot_ref, mod_ref, sums_ref, out_ref, early_ref):
    s = ids[1]
    count, half = near_ref.shape[0], sums_ref.shape[1]
    clip, _, _ = clip_at(slices, ids[0])
    branch = near_ref[...] + recv_ref[...].astype(F32)
    middle = mid_ref[pl.ds(pl.multiple_of(s * count, count), count), :]
    out_ref[...] = (middle + mod_ref[5:6, :] * branch).astype(BF)
    gate2 = jnp.sum(cot_ref[...].astype(F32) * branch, axis=0, keepdims=True)
    rows = [sums_ref[i : i + 1, :] for i in range(3)] + [gate2[:, :half], gate2[:, half:]]
    early_ref[...] = jnp.zeros_like(early_ref)
    for c in range(CLIPS):
        for i, row in enumerate(rows):
            early_ref[5 * c + i : 5 * c + i + 1, :] = jnp.where(clip == c, row, 0.0)
    early_ref[20:21, :] = sums_ref[3:4, :]


def output_sums(ids, slices, near, received, middle, cot, mod, sums):
    count = near.shape[0]
    return pl.pallas_call(
        output_kernel,
        in_specs=[SMEM, SMEM] + [VMEM] * 6,
        out_specs=[VMEM, VMEM],
        out_shape=[shape((count, D), BF), shape((24, D // 2), F32)],
        name="output_sums",
        cost_estimate=cost(3),
    )(ids, slices, near, received, middle, cot, mod, sums)


def attend_back_kernel(ids, slices, lengths, gates, *refs):
    q_refs, g_refs = refs[:LINE], refs[LINE : 2 * LINE]
    (own_ref, other_ref, stat_ref, qs_ref, ks_ref, pair_ref, cap_ref, gains_ref, cos_ref, sin_ref) = refs[
        2 * LINE : 2 * LINE + 10
    ]
    outs = refs[2 * LINE + 10 :]
    gq_refs = outs[:LINE]
    qgain_ref, keep_ref, send_ref, dgate_ref = outs[LINE : LINE + 4]
    dkv_refs = outs[LINE + 4 : LINE + 4 + GROUP]
    acc_ref, dcap_ref, dq_ref = outs[LINE + 4 + GROUP :]
    b, s = ids[0], ids[1]
    width, rows = q_refs[0].shape
    heads = width // HD
    scale = HD**-0.5
    base = s * LINE * width + b // GROUP * width
    acc_ref[...] = jnp.zeros_like(acc_ref)
    dcap_ref[...] = jnp.zeros_like(dcap_ref)
    dgate_ref[...] = jnp.zeros_like(dgate_ref)
    qgain_ref[...] = jnp.zeros_like(qgain_ref)

    for i in range(LINE):
        slot = slot_of(b, i, 0)
        clip, first, last = clip_at(slices, slot)
        queries, grads, deltas, inverses = [], [], [], []
        tall_q, tall_g, wide = [], [], []
        for h in range(heads):
            at = slice(h * HD, h * HD + HD)
            grad = g_refs[i][at, :]
            queries.append(qs_ref[i, at, :])
            grads.append(grad)
            deltas.append(jnp.sum(grad.astype(F32) * own_ref[i, at, :], axis=0, keepdims=True))
            inverses.append(stat_ref[i, h : h + 1, :])
            blank = jnp.zeros((HD, rows), F32)
            query_pad = jnp.concatenate([queries[h].astype(F32), blank], axis=0)
            grad_pad = jnp.concatenate([blank, grad.astype(F32)], axis=0)
            tall_q.append(query_pad.astype(BF))
            tall_g.append(grad_pad.astype(BF))
            wide.append(jnp.concatenate([query_pad.T, grad_pad.T], axis=0).astype(BF))
        dq_ref[...] = jnp.zeros_like(dq_ref)

        def step(n, carry):
            for h in range(heads):
                at = slice(h * HD, h * HD + HD)
                pair = pair_ref[n, h]
                prob = jnp.exp(mm(pair, tall_q[h], NN)) * inverses[h]
                grad_score = (prob * (mm(pair, tall_g[h], NN) - deltas[h])).astype(BF)
                both = jnp.concatenate([grad_score, prob.astype(BF)], axis=1)
                acc_ref[n, h] += mm(both, wide[h], NN)
                dq_ref[at, :] += mm(ks_ref[n, at, :], grad_score, NN)
            return carry

        lax.fori_loop(first, last, step, 0)
        usable = lax.broadcasted_iota(jnp.int32, (CAP, rows), 0) < lengths[clip]
        cosine, sine = cos_ref[slot - first], sin_ref[slot - first]
        for h in range(heads):
            at = slice(h * HD, h * HD + HD)
            at_value = slice(width + h * HD, width + h * HD + HD)
            gate = gates[(s * LINE + b // GROUP) * heads + h]
            cap_keys, cap_values = cap_ref[clip, at, :], cap_ref[clip, at_value, :]
            grad = grads[h].astype(F32)
            grad_other = (grad * gate).astype(BF)
            prob = (
                jnp.where(usable, jnp.exp(mm(cap_keys, queries[h], TN)), 0.0)
                * stat_ref[i, 4 + h : 5 + h, :]
            )
            grad_prob = mm(cap_values, grad_other, TN)
            inner = jnp.sum(prob * grad_prob, axis=0, keepdims=True)
            grad_score = (prob * (grad_prob - inner)).astype(BF)
            query_grad = (dq_ref[at, :] + mm(cap_keys, grad_score, NN)) * scale
            dcap_ref[clip, at, :] += mm(queries[h], grad_score, NT)
            dcap_ref[clip, at_value, :] += mm(grad_other, prob.astype(BF), NT)
            part = jnp.sum(grad * other_ref[i, at, :], axis=0, keepdims=True)
            dgate_ref[h : h + 1, :] += part * (1.0 - gate * gate)
            gain = gains_ref[pl.ds(pl.multiple_of(base + h * HD, HD), HD), 0:1]
            raw_grad, gain_grad = norm_rope_back(
                query_grad.astype(BF).astype(F32), q_refs[i][at, :].astype(F32), gain, cosine, sine
            )
            gq_refs[i][at, :] = raw_grad.astype(BF)
            qgain_ref[at, :] += gain_grad

    for j, dkv_ref in enumerate(dkv_refs):
        for k in range(LINE):
            slot = slot_of(b, k, j)
            for h in range(heads):
                both = acc_ref[slot, h].T.astype(BF)
                dkv_ref[k, h * HD : h * HD + HD, :] = both[:HD]
                dkv_ref[k, width + h * HD : width + h * HD + HD, :] = both[HD:]
    core = lax.rem(b, 2)
    for i in range(2):
        keep_ref[i] = dcap_ref[2 * i + core]
        send_ref[i] = dcap_ref[2 * i + 1 - core]


def attend_back(ids, slices, lengths, gates, queries, grads, saved, cap_kv, gains, cosine, sine):
    width, rows = queries[0].shape
    outs = pl.pallas_call(
        attend_back_kernel,
        in_specs=[SMEM] * 4 + [VMEM] * (2 * LINE + 10),
        out_specs=[VMEM] * (LINE + 4 + GROUP),
        out_shape=[shape((width, rows), BF)] * LINE
        + [
            shape((width, 1), F32),
            shape((2, 2 * width, CAP), F32),
            shape((2, 2 * width, CAP), F32),
            shape((8, rows), F32),
        ]
        + [shape((LINE, 2 * width, rows), BF)] * GROUP,
        scratch_shapes=[
            pltpu.VMEM((LINE * GROUP, width // HD, rows, 2 * HD), F32),
            pltpu.VMEM((CLIPS, 2 * width, CAP), F32),
            pltpu.VMEM((width, rows), F32),
        ],
        name="attend_back",
        cost_estimate=cost(40),
    )(ids, slices, lengths, gates, *queries, *grads, *saved, cap_kv, gains, cosine, sine)
    return outs[:LINE], outs[LINE : LINE + 4], outs[LINE + 4 :]


def keys_back_kernel(ids, slices, a_ref, c_ref, r_ref, kv_ref, gains_ref, cos_ref, sin_ref, *outs):
    out_refs, gain_ref = outs[:LINE], outs[LINE]
    b, s = ids[0], ids[1]
    width = gain_ref.shape[0]
    base = s * LINE * width + b // GROUP * width
    gain_ref[...] = jnp.zeros_like(gain_ref)
    for i in range(LINE):
        slot = slot_of(b, i, 0)
        _, first, _ = clip_at(slices, slot)
        cosine, sine = cos_ref[slot - first], sin_ref[slot - first]
        total = a_ref[i].astype(F32) + c_ref[i].astype(F32) + r_ref[i].astype(F32)
        total = total.astype(BF)
        for h in range(width // HD):
            at = slice(h * HD, h * HD + HD)
            gain = gains_ref[pl.ds(pl.multiple_of(base + h * HD, HD), HD), 1:2]
            raw_grad, gain_grad = norm_rope_back(
                total[at, :].astype(F32), kv_ref[i, at, :].astype(F32), gain, cosine, sine
            )
            out_refs[i][at, :] = raw_grad.astype(BF)
            gain_ref[at, :] += gain_grad
        out_refs[i][width:, :] = total[width:, :]


def keys_back(ids, slices, part, beside, received, kv, gains, cosine, sine):
    _, both, rows = kv.shape
    outs = pl.pallas_call(
        keys_back_kernel,
        in_specs=[SMEM, SMEM] + [VMEM] * 7,
        out_specs=[VMEM] * (LINE + 1),
        out_shape=[shape((both, rows), BF)] * LINE + [shape((both // 2, 1), F32)],
        name="keys_back",
        cost_estimate=cost(3.7),
    )(ids, slices, part, beside, received, kv, gains, cosine, sine)
    return outs[:LINE], outs[LINE]


def pack_kernel(ids, *refs):
    q_refs, kv_refs = refs[:LINE], refs[LINE : 2 * LINE]
    first_ref, second_ref, send_ref = refs[2 * LINE :]
    b, s = ids[0], ids[1]
    width = q_refs[0].shape[0]
    for k in range(LINE):
        at = chunk_at(b, k, width)

        @pl.when(s == 0)
        def _():
            first_ref[pl.ds(at, width), :] = q_refs[k][...]
            second_ref[pl.ds(at, width), :] = kv_refs[k][:width, :]
            send_ref[pl.ds(at, width), :] = kv_refs[k][width:, :]

        @pl.when(s == 1)
        def _():
            first_ref[pl.ds(at, width), :] = kv_refs[k][:width, :]
            second_ref[pl.ds(at, width), :] = kv_refs[k][width:, :]
            send_ref[pl.ds(at, width), :] = q_refs[k][...]


def pack(ids, grads_q, grads_kv):
    width, rows = grads_q[0].shape
    return pl.pallas_call(
        pack_kernel,
        in_specs=[SMEM] + [VMEM] * (2 * LINE),
        out_specs=[VMEM] * 3,
        out_shape=[shape((LINE * width, rows), BF)] * 3,
        name="pack",
        cost_estimate=cost(2.5),
    )(ids, *grads_q, *grads_kv)


def qkv_back_kernel(ids, first_ref, recv_ref, second_ref, w_ref, near_ref, far_ref, acc_ref):
    step = pl.program_id(0)
    count = near_ref.shape[0]
    s = ids[1]

    for n, ref in enumerate((first_ref, recv_ref, second_ref)):

        @pl.when(step == n)
        def _():
            part = mm(ref[...], w_ref[...], TN)
            acc_ref[...] = part if n == 0 else acc_ref[...] + part

    @pl.when(step == pl.num_programs(0) - 1)
    def _():
        near_ref[...] = acc_ref[pl.ds(pl.multiple_of(s * count, count), count), :]
        far_ref[...] = acc_ref[pl.ds(pl.multiple_of((1 - s) * count, count), count), :].astype(BF)


def qkv_back(ids, first, received, second, w_qkv):
    local, rows = received.shape
    count = rows // 2
    whole = pl.BlockSpec((local, rows), lambda i, ids: (0, 0))
    return pl.pallas_call(
        qkv_back_kernel,
        grid_spec=pltpu.PrefetchScalarGridSpec(
            num_scalar_prefetch=1,
            grid=(3,),
            in_specs=[whole] * 3 + [pl.BlockSpec((local, D), lambda i, ids: (i, 0))],
            out_specs=[pl.BlockSpec((count, D), lambda i, ids: (0, 0))] * 2,
            scratch_shapes=[pltpu.VMEM((rows, D), F32)],
        ),
        out_shape=[shape((count, D), F32), shape((count, D), BF)],
        name="qkv_back",
        cost_estimate=cost(6),
    )(ids, first, received, second, w_qkv)


def tokens_kernel(
    ids, slices, tok_ref, near_ref, recv_ref, mid_near, mid_far, mod_ref, gain_ref, *refs
):
    qgain_ref, kgain_ref, cgain_ref, dgate_ref, early_ref, out_ref, late_ref = refs
    b, s = ids[0], ids[1]
    half = mid_near.shape[1]
    clip, _, _ = clip_at(slices, b)
    values = tok_ref[...].astype(F32)
    inverse = row_inverse(values)
    unit = values * inverse
    scale = 1.0 + mod_ref[1:2, :]
    gain = gain_ref[...]
    grad = near_ref[...] + recv_ref[...].astype(F32)
    scaled = grad * scale
    unit_grad = scaled * gain
    mean = jnp.mean(unit_grad * unit, axis=-1, keepdims=True)
    mid_own, mid_other = mid_near[...], mid_far[...].astype(F32)
    middle = jnp.concatenate(
        [jnp.where(s == 0, mid_own, mid_other), jnp.where(s == 0, mid_other, mid_own)], axis=1
    )
    out_ref[...] = inverse * (unit_grad - unit * mean) + middle
    shift_row = jnp.sum(grad, axis=0, keepdims=True)
    with_unit = grad * unit
    scale_row = jnp.sum(with_unit, axis=0, keepdims=True) * gain
    norm_row = jnp.sum(scaled * unit, axis=0, keepdims=True)
    rows = [shift_row[:, :half], shift_row[:, half:], scale_row[:, :half], scale_row[:, half:]]
    late_ref[...] = jnp.zeros_like(late_ref)
    for c in range(CLIPS):
        for i, row in enumerate(rows):
            late_ref[4 * c + i : 4 * c + i + 1, :] = jnp.where(clip == c, row, 0.0)
    late_ref[16:17, :] = norm_row[:, :half]
    late_ref[17:18, :] = norm_row[:, half:]
    for i, ref in enumerate((qgain_ref, kgain_ref, cgain_ref)):
        late_ref[18 + i : 19 + i, :] = place_row(b, ref[...])
    heads = qgain_ref.shape[0] // HD
    lane = lax.broadcasted_iota(jnp.int32, (1, half), 1)
    gate_row = jnp.zeros((1, half), F32)
    for h in range(heads):
        value = jnp.sum(dgate_ref[h : h + 1, :], axis=1, keepdims=True)
        gate_row = gate_row + jnp.where(lane == b // GROUP * heads + h, value, 0.0)
    late_ref[21:22, :] = gate_row
    late_ref[24:, :] = early_ref[...]


def tokens_back(ids, slices, tok, near, received, mid_near, mid_far, mod, gain, parts):
    return pl.pallas_call(
        tokens_kernel,
        in_specs=[SMEM, SMEM] + [VMEM] * 12,
        out_specs=[VMEM, VMEM],
        out_shape=[shape(tok.shape, F32), shape((48, D // 2), F32)],
        name="tokens_back",
        cost_estimate=cost(3.5),
    )(ids, slices, tok, near, received, mid_near, mid_far, mod, gain, *parts)


def finish_kernel(ids, late_a, late_b, mod_ref, gains_ref):
    s = ids[1]
    early_a, early_b = late_a.at[pl.ds(24, 24)], late_b.at[pl.ds(24, 24)]

    def joined(a, b, i):
        own, other = a[i : i + 1, :], b[i : i + 1, :]
        return jnp.concatenate(
            [jnp.where(s == 0, own, other), jnp.where(s == 0, other, own)], axis=1
        )

    def added(a, b, i):
        both = a[i : i + 2, :] + b[i : i + 2, :]
        return jnp.concatenate([both[0:1], both[1:2]], axis=1)

    for c in range(CLIPS):
        low = [added(late_a, late_b, 4 * c), added(late_a, late_b, 4 * c + 2), joined(early_a, early_b, 5 * c)]
        high = [
            joined(early_a, early_b, 5 * c + 1),
            joined(early_a, early_b, 5 * c + 2),
            added(early_a, early_b, 5 * c + 3),
        ]
        for i in range(3):
            mod_ref[c : c + 1, i * D : (i + 1) * D] = jnp.where(s == 0, low[i], high[i])
    gains_ref[...] = jnp.zeros_like(gains_ref)
    gains_ref[0:1, :] = added(late_a, late_b, 16)
    for i in range(3):
        gains_ref[1 + i : 2 + i, :] = joined(late_a, late_b, 18 + i)
    gains_ref[4:5, :] = joined(early_a, early_b, 20)
    gains_ref[5:6, :] = joined(late_a, late_b, 21)


def finish(ids, late_a, late_b):
    return pl.pallas_call(
        finish_kernel,
        in_specs=[SMEM] + [VMEM] * 2,
        out_specs=[VMEM, VMEM],
        out_shape=[shape((CLIPS, 3 * D), F32), shape((8, D), F32)],
        name="finish",
        cost_estimate=cost(1.7),
    )(ids, late_a, late_b)


def caption_back_kernel(ids, sum_ref, raw_ref, gains_ref, out_ref, gain_ref):
    b, s = ids[0], ids[1]
    width = gain_ref.shape[0]
    base = s * LINE * width + b // GROUP * width
    cols = pl.ds(pl.multiple_of(lax.rem(b, GROUP) * CAP, CAP), CAP)
    for h in range(width // HD):
        at = slice(h * HD, h * HD + HD)
        gain = gains_ref[pl.ds(pl.multiple_of(base + h * HD, HD), HD), 2:3]
        raw = raw_ref[at, cols]
        inverse = lax.rsqrt(jnp.mean(raw * raw, axis=0, keepdims=True) + EPSILON)
        unit = raw * inverse
        grad = sum_ref[at, :]
        gain_ref[at, :] = jnp.sum(grad * unit, axis=1, keepdims=True)
        unit_grad = grad * gain
        out_ref[at, :] = (
            inverse * (unit_grad - unit * jnp.mean(unit_grad * unit, axis=0, keepdims=True))
        ).astype(BF)
    out_ref[width:, :] = sum_ref[width:, :].astype(BF)


def caption_back(ids, total, raw, gains):
    return pl.pallas_call(
        caption_back_kernel,
        in_specs=[SMEM] + [VMEM] * 3,
        out_specs=[VMEM, VMEM],
        out_shape=[shape(total.shape, BF), shape((total.shape[0] // 2, 1), F32)],
        name="caption_back",
        cost_estimate=cost(2.3),
    )(ids, total, raw, gains)


def caption_weight_kernel(ids, *refs):
    raw_refs, cap_ref, out_refs = refs[:GROUP], refs[GROUP], refs[GROUP + 1 :]
    b = ids[0]
    each = out_refs[0].shape[1]
    place = lax.rem(b, GROUP)
    for k in range(LINE):
        at = pl.multiple_of((lax.rem(b // GROUP - k + LINE, LINE) * GROUP + place) * each, each)
        total = None
        for j in range(GROUP):
            rows = pl.ds(pl.multiple_of(jnp.bitwise_xor(place, j) * CAP, CAP), CAP)
            part = mm(raw_refs[j][...], cap_ref[rows, pl.ds(at, each)], NN)
            total = part if total is None else total + part
        out_refs[k][...] = total.astype(BF)


def caption_weights(ids, raws, caption):
    rows = raws[0].shape[0]
    return pl.pallas_call(
        caption_weight_kernel,
        in_specs=[SMEM] + [VMEM] * (GROUP + 1),
        out_specs=[VMEM] * LINE,
        out_shape=[shape((rows, YD // (LINE * GROUP)), BF)] * LINE,
        name="caption_weights",
        cost_estimate=cost(4),
    )(ids, *raws, caption)


def caption_join_kernel(ids, *refs):
    parts, out_ref = refs[:LINE], refs[LINE]
    width = parts[0].shape[0] // 2
    for k in range(LINE):
        at = chunk_at(ids[0], k, width)
        for j in range(2):
            out_ref[j, pl.ds(at, width), :] = parts[k][j * width : (j + 1) * width, :].astype(F32)


def caption_join(ids, parts):
    both, each = parts[0].shape
    return pl.pallas_call(
        caption_join_kernel,
        in_specs=[SMEM] + [VMEM] * LINE,
        out_specs=VMEM,
        out_shape=shape((2, both // 2 * LINE, each), F32),
        name="caption_join",
        cost_estimate=cost(2),
    )(ids, *parts)


def weight_kernel(count, dims, *refs):
    left, right, out_ref = refs[:count], refs[count : 2 * count], refs[-1]
    total = None
    for a_ref, g_ref in zip(left, right):
        block = g_ref[...].reshape(g_ref.shape[-2:])
        part = mm(a_ref[0, 0].reshape(-1, a_ref.shape[-1]), block, dims)
        total = part if total is None else total + part
    out_ref[...] = total.reshape(out_ref.shape).astype(BF)


def weight_grads(left, right, by_rows, tile, kind, total, place, into=None):
    _, _, chunks, columns, tokens = left[0][0].shape
    rows = right[0].shape[-2 if by_rows else -1]
    stack = right[0].shape[0] if right[0].ndim == 3 else 1
    per = rows // tile
    left_specs = [
        pl.BlockSpec((1, 1, chunks, columns, tokens), lambda i, n=n: (n, kind, 0, 0, 0))
        for _, n in left
    ]
    if by_rows:
        right_spec = pl.BlockSpec((tile, tokens), lambda i: (i, 0))
    elif stack == 1:
        right_spec = pl.BlockSpec((tokens, tile), lambda i: (0, i))
    else:
        right_spec = pl.BlockSpec((1, tokens, tile), lambda i: (i // per, 0, i % per))
    args = [a for a, _ in left] + list(right)
    specs = left_specs + [right_spec] * len(right)
    aliases = {}
    if into is not None:
        aliases = {len(args): 0}
        args.append(into)
        specs.append(pl.BlockSpec(memory_space=pl.ANY))
    return pl.pallas_call(
        functools.partial(weight_kernel, len(left), NT if by_rows else NN),
        grid=(stack * per,),
        in_specs=specs,
        out_specs=pl.BlockSpec((chunks, columns, tile), lambda i: (0, 0, place(i))),
        out_shape=shape((chunks, columns, total), BF),
        input_output_aliases=aliases,
        name="weight_grads",
        cost_estimate=cost(5),
    )(*args)


def fast_body(
    tokens,
    cotangent,
    clip_slices,
    caption_lengths,
    caption,
    cond,
    ada_w,
    norm_gain,
    w_qkv,
    q_gain,
    k_gain,
    w_caption,
    ky_gain,
    cross_gate,
    w_out,
    ffn_gain,
    w_gate_up,
    w_down,
):
    bucket_count = LINE * GROUP
    seq_count = lax.axis_size("seq")
    local_width = D // seq_count
    units = FF // seq_count
    b = lax.axis_index(BUCKET)
    s = lax.axis_index("seq")
    z, g, c, y = b // GROUP, b % GROUP, b % 2, (b // 2) % 2
    ids = jnp.stack([b, s]).astype(jnp.int32)

    def xswap(v):
        return lax.ppermute(v, "seq", [(0, 1), (1, 0)])

    def hop(v, to):
        return lax.ppermute(v, BUCKET, [(i, to(i)) for i in range(bucket_count)])

    def cswap(v):
        return hop(v, lambda i: i ^ 1)

    def yswap(v):
        return hop(v, lambda i: i ^ 2)

    def zshift(v, k):
        return hop(v, lambda i: (i + GROUP * k) % bucket_count)

    def after(v, *others):
        return lax.optimization_barrier((v, *others))[0]

    def fence(*values):
        return lax.optimization_barrier(values)

    def pick(v, index):
        return lax.dynamic_index_in_dim(v, index, 0, False)

    def spread(parts):
        return [parts[0]] + [zshift(parts[k], k) for k in range(1, LINE)]

    def unspread(parts):
        return [parts[0]] + [zshift(parts[k], LINE - k) for k in range(1, LINE)]

    half = HD // 2
    rows = tokens.shape[0] * seq_count
    frequency = jnp.exp(jnp.arange(half, dtype=F32) * (-2.0 * math.log(10000.0) / (2 * half)))
    positions = jnp.arange(bucket_count * rows, dtype=F32).reshape(bucket_count, 1, rows)
    angles = positions * frequency[None, :, None]
    cosine, sine = jnp.cos(angles), jnp.sin(angles)
    gains = jnp.stack([q_gain, k_gain, ky_gain], axis=1)
    gates = jnp.tanh(cross_gate)
    norm_row, ffn_row = norm_gain[None], ffn_gain[None]

    tok_far = xswap(tokens)
    activation = jax.nn.silu(cond).astype(BF)
    mod_near = mm(activation, ada_w, NT)
    mod_far = xswap(mod_near)
    each = units // 2
    sent = lax.dynamic_slice_in_dim(w_gate_up, (1 - s) * units + c * each, each, 0)
    tok_far, sent = lax.optimization_barrier((tok_far, sent))
    projected, hidden, mod = pre(
        ids, clip_slices, tokens, tok_far, mod_near, mod_far, norm_row, w_qkv
    )
    local = lax.slice_in_dim(projected, local_width, 2 * local_width, axis=0)
    swapped = xswap(local)
    def scatter(parts):
        return lax.psum_scatter(parts, "z", scatter_dimension=0, tiled=False)

    hid_own, hid_c, hid_y = cut(ids, [hidden], [False])
    swapped, hid_own, hid_c, hid_y, gains = fence(swapped, hid_own, hid_c, hid_y, gains)
    kv_parts, q_parts = route(ids, projected, swapped)
    came = lax.all_gather(after(sent, swapped), "seq", axis=0, tiled=False)
    kv_here = spread(kv_parts)
    q_here = spread(q_parts)
    caption_rows = caption.reshape(CLIPS * CAP, YD)
    cap_raw, cap_kv = caption_keys(ids, w_caption, after(caption_rows, kv_parts[0]), gains)
    cap_raw, cap_kv, cosine, sine, *kv_here = fence(cap_raw, cap_kv, cosine, sine, *kv_here)
    kv_own = jnp.stack(kv_here)
    kv_y = yswap(kv_own)
    kv_c = cswap(kv_own)
    cot_far = xswap(after(cotangent, kv_own))
    kv_y = after(kv_y, kv_c, *q_here[1:], cot_far)
    kv_cy = cswap(kv_y)
    kv_pieces = [kv_own, kv_c, kv_y, kv_cy]
    grad_mlp = (
        jnp.where(
            s == 0,
            jnp.concatenate([cotangent, cot_far], 0),
            jnp.concatenate([cot_far, cotangent], 0),
        ).astype(F32)
        * mod[5:6]
    ).astype(BF)
    q_here[0], hid_y, hid_c = fence(q_here[0], hid_y, hid_c, grad_mlp)[:3]
    hid_came_y, hid_came_c = yswap(hid_y), cswap(hid_c)
    combined, saved = attend(
        ids, clip_slices, caption_lengths, gates, q_here, kv_pieces, cap_kv, gains, cosine, sine
    )
    combined, saved, hid_came_y, hid_came_c = fence(combined, saved, hid_came_y, hid_came_c)
    heads_own = unspread(combined)
    heads_far = [xswap(v) for v in heads_own]
    attention, branch = out_proj(ids, heads_own, heads_far, w_out)
    branch_far = xswap(branch)
    att_own, att_c, att_y = cut(ids, [attention, grad_mlp], [True, False])
    came = after(came, branch)
    too = cswap(came)
    branch_far, att_own, att_c, att_y, too = fence(branch_far, att_own, att_c, att_y, too)
    att_came_y = yswap(att_y)
    att_came_c = cswap(att_c)
    hid_came_yc = cswap(after(hid_came_y, branch_far))
    hid_left = [(hid_own, 0), (hid_came_c, 0), (hid_came_y, 0), (hid_came_yc, 1)]
    inner, inner_2, grad_kept, grad_came, mlp_in, middle, near, far, near_out, far_out = ffn(
        ids, [tokens, tok_far], [branch, branch_far], grad_mlp, mod, ffn_row, w_gate_up, came, too, w_down
    )
    inner, inner_2, grad_kept, grad_came, mlp_in, near, far = fence(
        inner, inner_2, grad_kept, grad_came, mlp_in, near, far
    )
    att_came_y, att_came_c, hid_came_yc, far = fence(att_came_y, att_came_c, hid_came_yc, far)
    hid_left[3] = (hid_came_yc, 1)

    received = xswap(far)
    inner_y = yswap(inner)
    inner_c = cswap(inner)
    kept_c = cswap(grad_kept)
    att_came_yc = cswap(att_came_y)
    att_left = [(att_own, 0), (att_came_c, 0), (att_came_y, 0), (att_came_yc, 1)]
    ffn_own, ffn_c, ffn_y = cut(ids, [mlp_in], [False])
    received, ffn_own, ffn_c, ffn_y, inner_c, inner_y, kept_c, att_came_yc, came_op, inner_op = fence(
        received, ffn_own, ffn_c, ffn_y, inner_c, inner_y, kept_c, att_came_yc, grad_came, inner_2
    )
    att_left[3] = (att_came_yc, 1)
    inner_2y = yswap(inner_op)
    inner_2c = cswap(inner_op)
    inner_yc = cswap(inner_y)
    ffn_came_c = cswap(ffn_c)
    (sums, grad_branch, mid_near, mid_far), near_heads, far_heads = mid_back(
        ids, near, received, middle, [cotangent, cot_far], branch, mod, ffn_row, w_out
    )
    grad_branch, ffn_came_c, inner_yc, inner_2c, *far_heads = fence(
        grad_branch, ffn_came_c, inner_yc, inner_2c, *far_heads
    )
    recv_a = xswap(far_heads[0])
    recv_b = xswap(far_heads[1])
    branch_c = cswap(grad_branch)
    recv_a, branch_c, inner_2y, ffn_y, branch_op, came_op = fence(
        recv_a, branch_c, inner_2y, ffn_y, grad_branch, came_op
    )
    ffn_came_y = yswap(ffn_y)
    inner_2yc = cswap(inner_2y)
    grad_1, grad_2 = add_pair(near_heads[0], recv_a)
    grad_3, grad_0 = add_pair(near_heads[1], after(recv_b, grad_1))
    grad_here = spread([grad_0, grad_1, grad_2, grad_3])
    tile = 512
    per = units // tile
    parts_inner = weight_grads(
        att_left, [after(inner, grad_0), inner_c, inner_y, inner_yc], False, tile, 1, units, lambda i: i
    )
    parts_inner = weight_grads(
        att_left,
        [inner_2, inner_2c, inner_2y, inner_2yc],
        False,
        tile,
        1,
        units,
        lambda i: i + per // 2,
        parts_inner,
    )
    parts_inner, ffn_came_y, *grad_here = fence(parts_inner, ffn_came_y, *grad_here)
    sum_inner = scatter(parts_inner)
    grad_here[0], kept_op, came_op, out_op, mid_op = fence(
        grad_here[0], grad_kept, grad_came, far_out, mid_far
    )
    kept_y = yswap(kept_op)
    came_y = yswap(came_op)
    came_c = cswap(came_op)
    out_recv = xswap(out_op)
    mid_came = xswap(mid_op)
    grads_q, (q_gain_part, cap_keep, cap_send, gate_part), grads_kv = attend_back(
        ids, clip_slices, caption_lengths, gates, q_here, grad_here, saved, cap_kv, gains, cosine, sine
    )
    grads_q, grads_kv, cap_send, kept_y, came_y, came_c, out_recv, mid_came = fence(
        grads_q, grads_kv, cap_send, kept_y, came_y, came_c, out_recv, mid_came
    )

    kv_c3 = cswap(grads_kv[3])
    kv_c1, cap_c = cswap(grads_kv[1]), cswap(cap_send)
    away = (grads_kv[2].astype(F32) + kv_c3.astype(F32)).astype(BF)
    away, kv_c1, cap_c, *grads_q = fence(away, kv_c1, cap_c, *grads_q)
    away_here = yswap(away)
    ffn_came_yc, kept_yc, came_yc = fence(ffn_came_y, kept_y, came_y, away)[:3]
    ffn_came_yc, kept_yc, came_yc = cswap(ffn_came_yc), cswap(kept_yc), cswap(came_yc)
    ffn_came_yc, kept_yc, came_yc, *grads_q = fence(ffn_came_yc, kept_yc, came_yc, *grads_q)
    ffn_left = [(ffn_own, 0), (ffn_came_c, 0), (ffn_came_y, 0), (ffn_came_yc, 1)]
    kept_all = [grad_kept, kept_c, kept_y, kept_yc]
    came_all = [grad_came, came_c, came_y, came_yc]
    back_q = unspread(grads_q)
    pair = cap_keep + cap_c
    parts_a = weight_grads(ffn_left, kept_all, False, tile, 0, 2 * units, lambda i: i)
    parts_a = weight_grads(ffn_left, came_all, False, tile, 0, 2 * units, lambda i: i + per, parts_a)
    away_here, parts_a, pair, sum_inner, *back_q = fence(
        away_here, parts_a, pair, sum_inner, *back_q
    )
    back_kv, k_gain_part = keys_back(
        ids, clip_slices, grads_kv[0], kv_c1, away_here, kv_own, gains, cosine, sine
    )
    back_kv, k_gain_part, branch_op = fence(back_kv, k_gain_part, branch_op)
    branch_y = yswap(branch_op)
    back_kv = unspread(back_kv)
    *back_kv, parts_a, branch_y = fence(*back_kv, parts_a, branch_y)
    sum_a = scatter(parts_a)

    first, second, send = fence(*pack(ids, back_q, back_kv))
    packed_recv = xswap(send)
    first_y = yswap(first)
    first_c = cswap(first)
    branch_all = [grad_branch, branch_c, branch_y, cswap(after(branch_y, first))]
    tile, total = 384, 4 * local_width
    parts_c = weight_grads(att_left, branch_all, False, tile, 0, total, lambda i: i + 6)
    cap_y = yswap(after(pick(pair, 1 - y), first))
    cap_total = pick(pair, y) + cap_y
    raw_cap, cap_gain_part = caption_back(ids, cap_total, cap_raw, gains)
    output, early = output_sums(
        ids, clip_slices, near_out, after(out_recv, first), middle, cotangent, mod, sums
    )
    packed_recv, first_y, first_c, raw_cap, cap_gain_part, second, parts_c, output = fence(
        packed_recv, first_y, first_c, raw_cap, cap_gain_part, second, parts_c, output
    )
    second_y = yswap(second)
    second_c = cswap(second)
    recv_c = cswap(packed_recv)
    first_yc = cswap(first_y)
    tok_near, tok_send = qkv_back(ids, first, packed_recv, second, w_qkv)
    tok_near, tok_send, second_y, second_c, recv_c, first_yc, recv_op, raw_cap = fence(
        tok_near, tok_send, second_y, second_c, recv_c, first_yc, packed_recv, raw_cap
    )
    tok_recv = xswap(tok_send)
    recv_y = yswap(recv_op)
    second_yc = cswap(second_y)
    raw_c = cswap(raw_cap)
    parts_c = weight_grads(
        hid_left, [first, first_c, first_y, first_yc], True, tile, 0, total, lambda i: i, parts_c
    )
    parts_c = weight_grads(
        hid_left, [second, second_c, second_y, second_yc], True, tile, 0, total, lambda i: i + 4, parts_c
    )
    tok_recv, parts_c, recv_y, raw_c = fence(tok_recv, parts_c, recv_y, raw_c)
    recv_yc = cswap(recv_y)
    raw_y = yswap(raw_cap)
    parts_c = weight_grads(
        hid_left, [packed_recv, recv_c, recv_y, recv_yc], True, tile, 0, total, lambda i: i + 2, parts_c
    )
    parts_c, raw_y = fence(parts_c, raw_y)
    sum_c = scatter(parts_c)
    token_grad, late = tokens_back(
        ids,
        clip_slices,
        tokens,
        tok_near,
        tok_recv,
        mid_near,
        mid_came,
        mod,
        norm_row,
        [q_gain_part, k_gain_part, cap_gain_part, gate_part, early],
    )
    raw_yc = cswap(raw_y)
    late = late + cswap(late)
    cap_parts = caption_weights(ids, [raw_cap, raw_c, raw_y, raw_yc], caption_rows)
    late_y = yswap(late)
    late_y, cap_parts = fence(late_y, cap_parts)
    late = late + late_y
    late_z = hop(late, lambda i: i ^ GROUP)
    late_z, sum_a = fence(late_z, sum_a)
    late = late + late_z
    late = late + hop(late, lambda i: i ^ (2 * GROUP))
    late, *cap_parts = fence(late, *cap_parts)
    cap_parts = unspread(cap_parts)
    late_far = xswap(late)
    came_out = xswap(sum_a[:, units:])
    late_sum = late

    mod_grad, gain_rows = finish(ids, late_sum, late_far)
    mod_mine = mod_grad.astype(BF)
    caption_w_grad = caption_join(ids, fence(*cap_parts, mod_mine)[:LINE])
    cols_local = CD // bucket_count
    act_cols = lax.dynamic_slice_in_dim(activation, b * cols_local, cols_local, 1)
    ada_grad = mm(mod_mine, act_cols, TN)
    cond_part = mm(mod_mine, ada_w, NN)
    cond_sigmoid = jax.nn.sigmoid(cond)
    cond_grad = (
        (cond_part + xswap(cond_part)) * cond_sigmoid * (1.0 + cond * (1.0 - cond_sigmoid))
    )
    heads_each = H // seq_count
    cross_out = jnp.concatenate(
        [gain_rows[5, :heads_each], gain_rows[5, local_width : local_width + heads_each]]
    )

    down_out = sum_inner.astype(F32).T
    kept_out = sum_a[:, :units].astype(F32)
    came_out = came_out.astype(F32)
    gate_up_out = jnp.where(
        s == 0,
        jnp.concatenate([kept_out, came_out], 1),
        jnp.concatenate([came_out, kept_out], 1),
    ).T
    sum_c = after(sum_c, gate_up_out)
    return (
        output,
        token_grad,
        cond_grad,
        ada_grad,
        gain_rows[0],
        sum_c[:, : 3 * local_width].astype(F32).T,
        gain_rows[1],
        gain_rows[2],
        caption_w_grad,
        gain_rows[3],
        cross_out,
        sum_c[:, 3 * local_width :].astype(F32).T,
        gain_rows[4],
        gate_up_out,
        down_out,
    )


def project(activations, weight):
    return lax.dot_general(
        activations, weight, (((1,), (1,)), ((), ())), preferred_element_type=jnp.float32
    )


def clip_of(rows, ends):
    return jnp.sum((rows[:, None] >= ends[None, :]).astype(jnp.int32), axis=1)


def head_norm(values, gains, head_count):
    row_count = values.shape[0]
    split = values.reshape(row_count, head_count, -1)
    inverse = lax.rsqrt(jnp.mean(split * split, axis=-1, keepdims=True) + EPSILON)
    unit_rows = split * inverse
    return (unit_rows.reshape(row_count, -1) * gains, unit_rows, inverse)


def head_norm_back(norm_grads, gains, unit_rows, inverse):
    row_count, head_count, head_width = unit_rows.shape
    gain_grad = jnp.sum(norm_grads * unit_rows.reshape(row_count, -1), axis=0)
    unit_grad = (norm_grads * gains).reshape(row_count, head_count, head_width)
    raw_grad = inverse * (
        unit_grad - unit_rows * jnp.mean(unit_grad * unit_rows, axis=-1, keepdims=True)
    )
    return (raw_grad.reshape(row_count, -1), gain_grad)


def rotate(values, positions, head_count):
    row_count = values.shape[0]
    split = values.reshape(row_count, head_count, -1)
    half_width = split.shape[-1] // 2
    frequency = jnp.exp(
        jnp.arange(half_width, dtype=jnp.float32) * (-2.0 * math.log(10000.0) / (2 * half_width))
    )
    angles = positions[:, None] * frequency[None, :]
    cosine = jnp.cos(angles)[:, None, :]
    sine = jnp.sin(angles)[:, None, :]
    first_half = split[..., :half_width]
    second_half = split[..., half_width:]
    turned = jnp.concatenate(
        [first_half * cosine - second_half * sine, first_half * sine + second_half * cosine],
        axis=-1,
    )
    return turned.reshape(row_count, -1)


def block_size(row_count):
    return 512 if row_count % 512 == 0 else row_count


def general_body(
    tokens,
    cotangent,
    clip_slices,
    caption_lengths,
    caption,
    cond,
    ada_w,
    norm_gain,
    w_qkv,
    q_gain,
    k_gain,
    w_caption,
    ky_gain,
    cross_gate,
    w_out,
    ffn_gain,
    w_gate_up,
    w_down,
):
    seq_count = lax.axis_size("seq")
    bucket_count = lax.axis_size("bucket")
    tok_rows = tokens.shape[0]
    slice_rows = tok_rows * seq_count
    total_rows = slice_rows * bucket_count
    local_heads = H // seq_count
    local_width = local_heads * HD
    score_scale = HD ** (-0.5)
    bucket_id = lax.axis_index("bucket")
    seq_id = lax.axis_index("seq")
    ends = jnp.cumsum(clip_slices) * slice_rows
    starts = ends - clip_slices * slice_rows
    my_clip = clip_of(jnp.reshape(bucket_id * slice_rows, (1,)), ends)[0]
    clip_mask = jnp.arange(CLIPS) == my_clip
    clip_start = jnp.sum(jnp.where(clip_mask, starts, 0))
    first_token = (bucket_id * seq_count + seq_id) * tok_rows
    positions = (first_token + jnp.arange(tok_rows, dtype=jnp.int32) - clip_start).astype(
        jnp.float32
    )
    caption_usable = jnp.arange(CAP) < jnp.sum(jnp.where(clip_mask, caption_lengths, 0))
    head_first = seq_id * local_width
    gates_local = jnp.tanh(lax.dynamic_slice_in_dim(cross_gate, seq_id * local_heads, local_heads))
    ky_gain_local = lax.dynamic_slice_in_dim(ky_gain, head_first, local_width)
    activation = jax.nn.silu(cond).astype(jnp.bfloat16)
    cond_row = lax.dynamic_index_in_dim(activation, my_clip, 0, True)
    caption_rows = lax.dynamic_index_in_dim(caption, my_clip, 0, False)
    caption_raw = jnp.einsum(
        "ty,jdy->jtd", caption_rows, w_caption, preferred_element_type=jnp.float32
    )
    caption_norm, caption_unit, caption_inverse = head_norm(
        caption_raw[0], ky_gain_local, local_heads
    )
    caption_keys = caption_norm.astype(jnp.bfloat16).reshape(CAP, local_heads, HD)
    caption_values = caption_raw[1].astype(jnp.bfloat16).reshape(CAP, local_heads, HD)
    inputs = tokens.astype(jnp.float32)

    def key_usable(first_row, row_count):
        return clip_of(first_row + jnp.arange(row_count, dtype=jnp.int32), ends) == my_clip

    def fold_keys(queries3, running, segment, first_row):
        seg_keys, seg_values = segment
        row_count = seg_keys.shape[0]
        key_rows = block_size(row_count)
        steps_count = row_count // key_rows
        usable = key_usable(first_row, row_count).reshape(steps_count, key_rows)
        key_blocks = seg_keys.reshape(steps_count, key_rows, local_heads, HD)
        value_blocks = seg_values.reshape(steps_count, key_rows, local_heads, HD)

        def update(state, item):
            key_block, value_block, usable_block = item

            def update_include(inner):
                row_max, row_total, accum = inner
                scores = (
                    jnp.einsum(
                        "qhd,khd->hqk", queries3, key_block, preferred_element_type=jnp.float32
                    )
                    * score_scale
                )
                scores = jnp.where(usable_block[None, None, :], scores, MASKED)
                new_max = jnp.maximum(row_max, jnp.max(scores, axis=-1))
                factor = jnp.exp(row_max - new_max)
                weights = jnp.exp(scores - new_max[..., None])
                row_total = row_total * factor + jnp.sum(weights, axis=-1)
                accum = accum * factor.T[:, :, None] + jnp.einsum(
                    "hqk,khd->qhd",
                    weights.astype(jnp.bfloat16),
                    value_block,
                    preferred_element_type=jnp.float32,
                )
                return (new_max, row_total, accum)

            return (
                lax.cond(jnp.any(usable_block), update_include, lambda inner: inner, state),
                None,
            )

        running, unused = lax.scan(update, running, (key_blocks, value_blocks, usable))
        return running

    def local_fold(queries3, running, keys_whole):

        def local_visit(state, piece_index):
            first_row = piece_index * slice_rows
            segment = (
                lax.dynamic_slice_in_dim(keys_whole[0], first_row, slice_rows, 0),
                lax.dynamic_slice_in_dim(keys_whole[1], first_row, slice_rows, 0),
            )
            return (fold_keys(queries3, state, segment, first_row), None)

        running, unused = lax.scan(local_visit, running, jnp.arange(bucket_count, dtype=jnp.int32))
        return running

    def forward(qkv_full, out_full, modulation, second):
        shift_vec = modulation[:D]
        scale_vec = modulation[D : 2 * D]
        gate_vec = modulation[2 * D : 3 * D]
        inverse = lax.rsqrt(jnp.mean(inputs * inputs, axis=-1, keepdims=True) + EPSILON)
        unit_rows = inputs * inverse
        hidden = (unit_rows * norm_gain * (1.0 + scale_vec) + shift_vec).astype(jnp.bfloat16)
        projected = project(hidden, qkv_full)
        query_norm, query_unit, query_inverse = head_norm(projected[:, :D], q_gain, H)
        key_norm, key_unit, key_inverse = head_norm(projected[:, D : 2 * D], k_gain, H)
        queries = rotate(query_norm, positions, H).astype(jnp.bfloat16)
        keys_tok = rotate(key_norm, positions, H).astype(jnp.bfloat16)
        values_tok = projected[:, 2 * D :].astype(jnp.bfloat16)
        head_queries, head_keys, head_values = (
            lax.all_to_all(queries, "seq", split_axis=1, concat_axis=0, tiled=True),
            lax.all_to_all(keys_tok, "seq", split_axis=1, concat_axis=0, tiled=True),
            lax.all_to_all(values_tok, "seq", split_axis=1, concat_axis=0, tiled=True),
        )
        queries3 = head_queries.reshape(slice_rows, local_heads, HD)
        start_state = (
            jnp.full((local_heads, slice_rows), MASKED, jnp.float32),
            jnp.zeros((local_heads, slice_rows), jnp.float32),
            jnp.zeros((slice_rows, local_heads, HD), jnp.float32),
        )
        folder = functools.partial(fold_keys, queries3)
        if second:
            keys_whole = (
                lax.all_gather(head_keys, "bucket", axis=0, tiled=True),
                lax.all_gather(head_values, "bucket", axis=0, tiled=True),
            )
            final_state = local_fold(queries3, start_state, keys_whole)
        else:
            keys_whole = None
            final_state = folder(
                start_state,
                (
                    lax.all_gather(head_keys, "bucket", axis=0, tiled=True),
                    lax.all_gather(head_values, "bucket", axis=0, tiled=True),
                ),
                jnp.int32(0),
            )
        row_max, row_total, accum = final_state
        own = accum / row_total.T[:, :, None]
        cross_scores = (
            jnp.einsum("qhd,khd->hqk", queries3, caption_keys, preferred_element_type=jnp.float32)
            * score_scale
        )
        cross_prob = jax.nn.softmax(
            jnp.where(caption_usable[None, None, :], cross_scores, MASKED), axis=-1
        )
        other = jnp.einsum(
            "hqk,khd->qhd",
            cross_prob.astype(jnp.bfloat16),
            caption_values,
            preferred_element_type=jnp.float32,
        )
        combined = (
            (own + gates_local[None, :, None] * other)
            .reshape(slice_rows, local_width)
            .astype(jnp.bfloat16)
        )
        attention = lax.all_to_all(combined, "seq", split_axis=0, concat_axis=1, tiled=True)
        branch = project(attention, out_full)
        return dict(
            gate_vec=gate_vec,
            scale_vec=scale_vec,
            inverse=inverse,
            unit_rows=unit_rows,
            hidden=hidden,
            query_unit=query_unit,
            query_inverse=query_inverse,
            key_unit=key_unit,
            key_inverse=key_inverse,
            queries3=queries3,
            own_keys3=head_keys.reshape(slice_rows, local_heads, HD),
            own_values3=head_values.reshape(slice_rows, local_heads, HD),
            keys_whole=keys_whole,
            row_log=row_max + jnp.log(row_total),
            own=own,
            other=other,
            cross_prob=cross_prob,
            attention=attention,
            branch=branch,
            output=inputs + gate_vec * branch,
        )

    gathered = (
        lax.all_gather(ada_w, "seq", axis=0, tiled=True),
        lax.all_gather(w_qkv, "seq", axis=0, tiled=True),
        lax.all_gather(w_out, "seq", axis=0, tiled=True),
        lax.all_gather(w_gate_up, "seq", axis=0, tiled=True),
        lax.all_gather(w_down, "seq", axis=0, tiled=True),
    )
    modulation = project(cond_row, gathered[0])[0]
    first_pass = forward(gathered[1], gathered[2], modulation, False)
    middle = first_pass["output"]
    shift_mlp = modulation[3 * D : 4 * D]
    scale_mlp = modulation[4 * D : 5 * D]
    gate_mlp = modulation[5 * D :]
    mid_inverse = lax.rsqrt(jnp.mean(middle * middle, axis=-1, keepdims=True) + EPSILON)
    mid_unit = middle * mid_inverse
    mlp_in = (mid_unit * ffn_gain * (1.0 + scale_mlp) + shift_mlp).astype(jnp.bfloat16)
    gate_up = project(mlp_in, gathered[3])
    gate_half = gate_up[:, :FF]
    up_half = gate_up[:, FF:]
    gate_sigmoid = jax.nn.sigmoid(gate_half)
    silu_gate = gate_half * gate_sigmoid
    inner = (silu_gate * up_half).astype(jnp.bfloat16)
    mlp_branch = jnp.dot(inner, gathered[4], preferred_element_type=jnp.float32)
    output = (middle + gate_mlp * mlp_branch).astype(jnp.bfloat16)
    regathered = (
        lax.all_gather(ada_w, "seq", axis=0, tiled=True),
        lax.all_gather(w_qkv, "seq", axis=0, tiled=True),
        lax.all_gather(w_out, "seq", axis=0, tiled=True),
        lax.all_gather(w_gate_up, "seq", axis=0, tiled=True),
        lax.all_gather(w_down, "seq", axis=0, tiled=True),
    )
    second_pass = forward(regathered[1], regathered[2], modulation, True)
    ada_full, qkv_full, out_full, gate_up_full, down_full = regathered
    grad_out = cotangent.astype(jnp.float32)
    mlp_gate_grad = jnp.sum(grad_out * mlp_branch, axis=0)
    grad_mlp = (grad_out * gate_mlp).astype(jnp.bfloat16)
    grad_inner = lax.dot_general(
        grad_mlp, down_full, (((1,), (1,)), ((), ())), preferred_element_type=jnp.float32
    )
    grad_gate_half = grad_inner * up_half * gate_sigmoid * (1.0 + gate_half * (1.0 - gate_sigmoid))
    grad_up_half = grad_inner * silu_gate
    grad_gate_up = jnp.concatenate([grad_gate_half, grad_up_half], axis=1).astype(jnp.bfloat16)
    mlp_in_grad = jnp.dot(grad_gate_up, gate_up_full, preferred_element_type=jnp.float32)
    ffn_gain_grad = jnp.sum(mlp_in_grad * (1.0 + scale_mlp) * mid_unit, axis=0)
    shift_mlp_grad = jnp.sum(mlp_in_grad, axis=0)
    scale_mlp_grad = jnp.sum(mlp_in_grad * mid_unit * ffn_gain, axis=0)
    mid_unit_grad = mlp_in_grad * ffn_gain * (1.0 + scale_mlp)
    residual_grad = (
        mid_inverse
        * (mid_unit_grad - mid_unit * jnp.mean(mid_unit_grad * mid_unit, axis=-1, keepdims=True))
        + grad_out
    )
    gate_grad = jnp.sum(residual_grad * second_pass["branch"], axis=0)
    grad_branch = (residual_grad * second_pass["gate_vec"]).astype(jnp.bfloat16)
    attention = second_pass["attention"]
    grad_attention = jnp.dot(grad_branch, out_full, preferred_element_type=jnp.float32).astype(
        jnp.bfloat16
    )
    grad_heads = lax.all_to_all(grad_attention, "seq", split_axis=1, concat_axis=0, tiled=True)
    grad_own16 = grad_heads.reshape(slice_rows, local_heads, HD)
    grad_own = grad_own16.astype(jnp.float32)
    queries3 = second_pass["queries3"]
    own = second_pass["own"]
    other = second_pass["other"]
    cross_prob = second_pass["cross_prob"]
    grad_other = (grad_own * gates_local[None, :, None]).astype(jnp.bfloat16)
    gate_grad_local = jnp.sum(grad_own * other, axis=(0, 2)) * (1.0 - gates_local * gates_local)
    grad_cross_prob = jnp.einsum(
        "qhd,khd->hqk", grad_other, caption_values, preferred_element_type=jnp.float32
    )
    grad_cross = (
        cross_prob
        * (grad_cross_prob - jnp.sum(cross_prob * grad_cross_prob, axis=-1, keepdims=True))
    ).astype(jnp.bfloat16)
    cross_query_grad = score_scale * jnp.einsum(
        "hqk,khd->qhd", grad_cross, caption_keys, preferred_element_type=jnp.float32
    )
    caption_key_grad = score_scale * jnp.einsum(
        "hqk,qhd->khd", grad_cross, queries3, preferred_element_type=jnp.float32
    )
    caption_value_grad = jnp.einsum(
        "hqk,qhd->khd",
        cross_prob.astype(jnp.bfloat16),
        grad_other,
        preferred_element_type=jnp.float32,
    )
    row_delta = jnp.sum(grad_own * own, axis=-1).T
    row_log = second_pass["row_log"]
    keys_whole = second_pass["keys_whole"]

    def grad_piece(query_grad, piece_index, with_keys):
        first_row = piece_index * slice_rows
        key_rows = block_size(slice_rows)
        steps_count = slice_rows // key_rows
        key_blocks = lax.dynamic_slice_in_dim(keys_whole[0], first_row, slice_rows, 0).reshape(
            steps_count, key_rows, local_heads, HD
        )
        value_blocks = lax.dynamic_slice_in_dim(keys_whole[1], first_row, slice_rows, 0).reshape(
            steps_count, key_rows, local_heads, HD
        )
        usable = key_usable(first_row, slice_rows).reshape(steps_count, key_rows)

        def grad_visit(accum, item):
            key_block, value_block, usable_block = item

            def grad_include(inner):
                scores = (
                    jnp.einsum(
                        "qhd,khd->hqk", queries3, key_block, preferred_element_type=jnp.float32
                    )
                    * score_scale
                )
                scores = jnp.where(usable_block[None, None, :], scores, MASKED)
                probability = jnp.exp(scores - row_log[..., None])
                grad_prob = jnp.einsum(
                    "qhd,khd->hqk", grad_own16, value_block, preferred_element_type=jnp.float32
                )
                grad_scores = (probability * (grad_prob - row_delta[..., None])).astype(
                    jnp.bfloat16
                )
                updated = inner + score_scale * jnp.einsum(
                    "hqk,khd->qhd", grad_scores, key_block, preferred_element_type=jnp.float32
                )
                key_grad = score_scale * jnp.einsum(
                    "hqk,qhd->khd", grad_scores, queries3, preferred_element_type=jnp.float32
                )
                value_grad = jnp.einsum(
                    "hqk,qhd->khd",
                    probability.astype(jnp.bfloat16),
                    grad_own16,
                    preferred_element_type=jnp.float32,
                )
                return (updated, key_grad, value_grad)

            def skip(inner):
                empty = jnp.zeros((key_rows, local_heads, HD), jnp.float32)
                return (inner, empty, empty)

            updated, key_grad, value_grad = lax.cond(
                jnp.any(usable_block), grad_include, skip, accum
            )
            return (updated, (key_grad, value_grad))

        query_grad, (key_grads, value_grads) = lax.scan(
            grad_visit, query_grad, (key_blocks, value_blocks, usable)
        )
        return (
            query_grad,
            (
                key_grads.reshape(slice_rows, local_width),
                value_grads.reshape(slice_rows, local_width),
            ),
        )

    query_start = jnp.zeros((slice_rows, local_heads, HD), jnp.float32)
    piece_order = jnp.arange(bucket_count, dtype=jnp.int32)
    self_query_grad, (key_terms, value_terms) = lax.scan(
        functools.partial(grad_piece, with_keys=True), query_start, piece_order
    )
    key_sum, value_sum = (
        lax.psum_scatter(
            key_terms.reshape(total_rows, local_width).astype(jnp.bfloat16),
            "bucket",
            scatter_dimension=0,
            tiled=True,
        ).astype(jnp.float32),
        lax.psum_scatter(
            value_terms.reshape(total_rows, local_width).astype(jnp.bfloat16),
            "bucket",
            scatter_dimension=0,
            tiled=True,
        ).astype(jnp.float32),
    )
    query_grad16 = (
        (self_query_grad + cross_query_grad).reshape(slice_rows, local_width).astype(jnp.bfloat16)
    )
    tok_query_grad, tok_key_grad, tok_value_grad = (
        lax.all_to_all(query_grad16, "seq", split_axis=0, concat_axis=1, tiled=True),
        lax.all_to_all(
            key_sum.astype(jnp.bfloat16), "seq", split_axis=0, concat_axis=1, tiled=True
        ),
        lax.all_to_all(
            value_sum.astype(jnp.bfloat16), "seq", split_axis=0, concat_axis=1, tiled=True
        ),
    )
    query_raw_grad, q_gain_grad = head_norm_back(
        rotate(tok_query_grad.astype(jnp.float32), -positions, H),
        q_gain,
        second_pass["query_unit"],
        second_pass["query_inverse"],
    )
    key_raw_grad, k_gain_grad = head_norm_back(
        rotate(tok_key_grad.astype(jnp.float32), -positions, H),
        k_gain,
        second_pass["key_unit"],
        second_pass["key_inverse"],
    )
    projected_grad = jnp.concatenate(
        [query_raw_grad, key_raw_grad, tok_value_grad.astype(jnp.float32)], axis=1
    ).astype(jnp.bfloat16)
    hidden = second_pass["hidden"]
    out_each = D // seq_count
    qkv_each = 3 * D // seq_count
    gate_up_each = 2 * FF // seq_count
    down_each = FF // seq_count
    rows_each = out_each + qkv_each + gate_up_each + down_each
    device_count = rows_each * lax.axis_size("seq") // rows_each
    first_device = jnp.int32(0) // rows_each

    def part(operand, partner, each):
        picked = lax.dynamic_slice_in_dim(operand, first_device * each, device_count * each, 1)
        term = lax.dot_general(
            picked, partner, (((0,), (0,)), ((), ())), preferred_element_type=jnp.float32
        )
        return term.reshape(device_count, each, D)

    terms = [
        part(grad_branch, attention, out_each),
        part(projected_grad, hidden, qkv_each),
        part(grad_gate_up, mlp_in, gate_up_each),
        part(inner, grad_mlp, down_each),
    ]
    weight_grad_seq = lax.psum_scatter(
        jnp.concatenate(terms, axis=1)
        .reshape(rows_each * lax.axis_size("seq"), D)
        .astype(jnp.bfloat16),
        "seq",
        scatter_dimension=0,
        tiled=True,
    )
    hidden_grad = jnp.dot(projected_grad, qkv_full, preferred_element_type=jnp.float32)
    unit_rows = second_pass["unit_rows"]
    scale_vec = second_pass["scale_vec"]
    inverse = second_pass["inverse"]
    norm_gain_grad = jnp.sum(hidden_grad * (1.0 + scale_vec) * unit_rows, axis=0)
    shift_grad = jnp.sum(hidden_grad, axis=0)
    scale_grad = jnp.sum(hidden_grad * unit_rows * norm_gain, axis=0)
    unit_grad = hidden_grad * norm_gain * (1.0 + scale_vec)
    token_grad = (
        inverse * (unit_grad - unit_rows * jnp.mean(unit_grad * unit_rows, axis=-1, keepdims=True))
        + residual_grad
    )
    modulation_grad = jnp.where(
        clip_mask[:, None],
        jnp.concatenate(
            [shift_grad, scale_grad, gate_grad, shift_mlp_grad, scale_mlp_grad, mlp_gate_grad]
        )[None, :],
        0.0,
    )
    ky_gain_part = jnp.sum(
        caption_key_grad.reshape(CAP, local_width) * caption_unit.reshape(CAP, local_width), axis=0
    )
    ky_gain_full = lax.dynamic_update_slice_in_dim(
        jnp.zeros((D,), jnp.float32), ky_gain_part, head_first, 0
    )
    gate_full = lax.dynamic_update_slice_in_dim(
        jnp.zeros((H,), jnp.float32), gate_grad_local, seq_id * local_heads, 0
    )
    caption_part = jnp.stack(
        [caption_key_grad.reshape(CAP, local_width), caption_value_grad.reshape(CAP, local_width)]
    )[None]
    zero_index = jnp.zeros((), jnp.int32)
    caption_full = lax.dynamic_update_slice(
        jnp.zeros((CLIPS, 2, CAP, D), jnp.float32),
        caption_part,
        (my_clip, zero_index, zero_index, head_first),
    )
    reduced = lax.psum(
        (
            norm_gain_grad,
            q_gain_grad,
            k_gain_grad,
            ky_gain_full,
            gate_full,
            modulation_grad,
            caption_full,
            ffn_gain_grad,
        ),
        ("bucket", "seq"),
    )
    modulation_total = reduced[5].astype(jnp.bfloat16)
    rows_local = 6 * D // seq_count
    cols_local = CD // bucket_count
    ada_grad = lax.dot_general(
        lax.dynamic_slice_in_dim(modulation_total, seq_id * rows_local, rows_local, 1),
        lax.dynamic_slice_in_dim(activation, bucket_id * cols_local, cols_local, 1),
        (((0,), (0,)), ((), ())),
        preferred_element_type=jnp.float32,
    )
    cond_sigmoid = jax.nn.sigmoid(cond)
    cond_grad = (
        jnp.dot(modulation_total, ada_full, preferred_element_type=jnp.float32)
        * cond_sigmoid
        * (1.0 + cond * (1.0 - cond_sigmoid))
    )
    caption_total = lax.dynamic_slice_in_dim(reduced[6], head_first, local_width, 3)
    raw_keys_all = jnp.einsum(
        "cty,dy->ctd", caption, w_caption[0], preferred_element_type=jnp.float32
    ).reshape(CLIPS * CAP, local_width)
    ignored, unit_all, inverse_all = head_norm(raw_keys_all, ky_gain_local, local_heads)
    raw_key_grad, unused_gain = head_norm_back(
        caption_total[:, 0].reshape(CLIPS * CAP, local_width), ky_gain_local, unit_all, inverse_all
    )
    raw_grad = jnp.stack(
        [raw_key_grad.reshape(CLIPS, CAP, local_width), caption_total[:, 1]], axis=1
    ).astype(jnp.bfloat16)
    caption_cols = lax.dynamic_slice_in_dim(
        caption, bucket_id * (YD // bucket_count), YD // bucket_count, 2
    )
    caption_w_grad = jnp.einsum(
        "cjtd,cty->jdy", raw_grad, caption_cols, preferred_element_type=jnp.float32
    )
    combined_grads = lax.psum_scatter(
        weight_grad_seq, "bucket", scatter_dimension=1, tiled=True
    ).astype(jnp.float32)
    out_grad_out = combined_grads[:out_each]
    qkv_grad_out = combined_grads[out_each : out_each + qkv_each]
    gate_up_grad_out = combined_grads[out_each + qkv_each : out_each + qkv_each + gate_up_each]
    down_grad_out = combined_grads[out_each + qkv_each + gate_up_each :]
    return (
        output,
        token_grad,
        cond_grad,
        ada_grad,
        reduced[0],
        qkv_grad_out,
        reduced[1],
        reduced[2],
        caption_w_grad,
        reduced[3],
        reduced[4],
        out_grad_out,
        reduced[7],
        gate_up_grad_out,
        down_grad_out,
    )


def solution(mesh):
    fits = mesh.shape["seq"] == 2 and mesh.shape["bucket"] == LINE * GROUP
    bucket = ("bucket",)
    if fits:
        bucket = BUCKET
        mesh = Mesh(mesh.devices.reshape(LINE, 2, GROUP // 2, 2), (*BUCKET, "seq"))
    in_specs = (
        P((*bucket, "seq"), None),
        P((*bucket, "seq"), None),
        P(),
        P(),
        P(),
        P(),
        P("seq", None),
        P(),
        P("seq", None),
        P(),
        P(),
        P(None, "seq", None),
        P(),
        P(),
        P("seq", None),
        P(),
        P("seq", None),
        P("seq", None),
    )
    out_specs = (
        P((*bucket, "seq"), None),
        P((*bucket, "seq"), None),
        P(),
        P("seq", bucket),
        P(),
        P("seq", bucket),
        P(),
        P(),
        P(None, "seq", bucket),
        P(),
        P(),
        P("seq", bucket),
        P(),
        P("seq", bucket),
        P("seq", bucket),
    )
    body = fast_body if fits else general_body
    return jax.shard_map(body, mesh=mesh, in_specs=in_specs, out_specs=out_specs, check_vma=False)
```

```python
import functools
import math

import jax
import jax.numpy as jnp
from jax import lax
from jax.experimental import pallas as pl
from jax.experimental.pallas import tpu as pltpu
from jax.sharding import Mesh, PartitionSpec as P

H = 24
HD = 64
D = 1536
FF = 4096
YD = 4096
CD = 1024
CAP = 128
CLIPS = 4

EPSILON = 1e-06
MASKED = -1e30
BF = jnp.bfloat16
F32 = jnp.float32
NN = (((1,), (0,)), ((), ()))
NT = (((1,), (1,)), ((), ()))
TN = (((0,), (0,)), ((), ()))
GROUP = 4
LINE = 4
BUCKET = ("z", "y", "c")
SENDS = (1, 2, 3, 0)
SMEM = pl.BlockSpec(memory_space=pltpu.SMEM)
VMEM = pl.BlockSpec(memory_space=pltpu.VMEM)
shape = jax.ShapeDtypeStruct


def cost(microseconds):
    return pl.CostEstimate(
        flops=0, transcendentals=0, bytes_accessed=int(microseconds * 20_000)
    )


def mm(a, b, dims):
    return lax.dot_general(a, b, dims, preferred_element_type=F32)


def clip_at(slices, slot):
    ends = [slices[0]]
    for i in range(1, CLIPS):
        ends.append(ends[-1] + slices[i])
    clip = jnp.int32(0)
    first, last = jnp.int32(0), ends[0]
    for i in range(CLIPS - 1):
        later = slot >= ends[i]
        clip = jnp.where(later, i + 1, clip)
        first = jnp.where(later, ends[i], first)
        last = jnp.where(later, ends[i + 1], last)
    return clip, first, last


def slot_of(bucket, k, j):
    return lax.rem(bucket // GROUP - k + LINE, LINE) * GROUP + jnp.bitwise_xor(
        lax.rem(bucket, GROUP), j
    )


def chunk_at(bucket, k, width):
    return pl.multiple_of(lax.rem(bucket // GROUP + k, LINE) * width, HD)


def norm_rope(raw, gain, cosine, sine):
    inverse = lax.rsqrt(jnp.mean(raw * raw, axis=0, keepdims=True) + EPSILON)
    normed = raw * inverse * gain
    half = raw.shape[0] // 2
    first, second = normed[:half], normed[half:]
    return jnp.concatenate(
        [first * cosine - second * sine, first * sine + second * cosine], axis=0
    )


def norm_rope_back(grad, raw, gain, cosine, sine):
    inverse = lax.rsqrt(jnp.mean(raw * raw, axis=0, keepdims=True) + EPSILON)
    unit = raw * inverse
    half = raw.shape[0] // 2
    first, second = grad[:half], grad[half:]
    turned = jnp.concatenate(
        [first * cosine + second * sine, second * cosine - first * sine], axis=0
    )
    gain_grad = jnp.sum(turned * unit, axis=1, keepdims=True)
    unit_grad = turned * gain
    raw_grad = inverse * (unit_grad - unit * jnp.mean(unit_grad * unit, axis=0, keepdims=True))
    return raw_grad, gain_grad


def row_inverse(values):
    return lax.rsqrt(jnp.mean(values * values, axis=-1, keepdims=True) + EPSILON)


def pre_kernel(ids, slices, tok_a, tok_b, mod_a, mod_b, gain_ref, w_ref, p_ref, hid_ref, mod_ref):
    @pl.when(pl.program_id(0) == 0)
    def _():
        s = ids[1]
        clip, _, _ = clip_at(slices, ids[0])
        row_a, row_b = mod_a[pl.ds(clip, 1), :], mod_b[pl.ds(clip, 1), :]
        low, high = jnp.where(s == 0, row_a, row_b), jnp.where(s == 0, row_b, row_a)
        mod_ref[...] = jnp.zeros_like(mod_ref)
        for i in range(3):
            mod_ref[i : i + 1, :] = low[:, i * D : (i + 1) * D]
            mod_ref[3 + i : 4 + i, :] = high[:, i * D : (i + 1) * D]
        shift, scale = mod_ref[0:1, :], mod_ref[1:2, :]
        count = tok_a.shape[0]
        for place, ref in ((s, tok_a), (1 - s, tok_b)):
            values = ref[...].astype(F32)
            hidden = values * row_inverse(values) * gain_ref[...] * (1.0 + scale) + shift
            hid_ref[pl.ds(pl.multiple_of(place * count, count), count), :] = hidden.astype(BF)

    p_ref[...] = mm(w_ref[...], hid_ref[...], NT).astype(BF)


def pre(ids, slices, tok_a, tok_b, mod_a, mod_b, gain, w_qkv):
    rows = 2 * tok_a.shape[0]
    tile = w_qkv.shape[0] // 3
    full = lambda v: pl.BlockSpec(v.shape, lambda i: (0,) * v.ndim)
    return pl.pallas_call(
        pre_kernel,
        grid=(w_qkv.shape[0] // tile,),
        in_specs=[SMEM, SMEM]
        + [full(v) for v in (tok_a, tok_b, mod_a, mod_b, gain)]
        + [pl.BlockSpec((tile, D), lambda i: (i, 0))],
        out_specs=[
            pl.BlockSpec((tile, rows), lambda i: (i, 0)),
            pl.BlockSpec((rows, D), lambda i: (0, 0)),
            pl.BlockSpec((8, D), lambda i: (0, 0)),
        ],
        out_shape=[shape((w_qkv.shape[0], rows), BF), shape((rows, D), BF), shape((8, D), F32)],
        name="pre",
        cost_estimate=cost(6),
    )(ids, slices, tok_a, tok_b, mod_a, mod_b, gain, w_qkv)


def route_kernel(ids, p_ref, r_ref, *outs):
    b, s = ids[0], ids[1]
    local = r_ref.shape[0]
    width = local // LINE
    for k in range(LINE):
        at = chunk_at(b, k, width)
        kv_ref, q_ref = outs[k], outs[LINE + k]

        @pl.when(s == 0)
        def _():
            q_ref[...] = p_ref[pl.ds(at, width), :]
            kv_ref[:width, :] = p_ref[pl.ds(2 * local + at, width), :]
            kv_ref[width:, :] = r_ref[pl.ds(at, width), :]

        @pl.when(s == 1)
        def _():
            q_ref[...] = r_ref[pl.ds(at, width), :]
            kv_ref[:width, :] = p_ref[pl.ds(at, width), :]
            kv_ref[width:, :] = p_ref[pl.ds(2 * local + at, width), :]


def route(ids, projected, received):
    local, rows = received.shape
    width = local // LINE
    outs = pl.pallas_call(
        route_kernel,
        in_specs=[SMEM, VMEM, VMEM],
        out_specs=[VMEM] * (2 * LINE),
        out_shape=[shape((2 * width, rows), BF)] * LINE + [shape((width, rows), BF)] * LINE,
        name="route",
        cost_estimate=cost(2.5),
    )(ids, projected, received)
    return outs[:LINE], outs[LINE:]


def caption_kernel(ids, w_ref, cap_ref, gains_ref, raw_ref, kv_ref):
    step = pl.program_id(0)
    width = w_ref.shape[1]

    @pl.when(step == 0)
    def _():
        raw_ref[...] = jnp.zeros_like(raw_ref)

    for j in range(2):
        raw_ref[j * width : (j + 1) * width, :] += mm(w_ref[j], cap_ref[...], NT)

    @pl.when(step == pl.num_programs(0) - 1)
    def _():
        base = ids[1] * LINE * width + ids[0] // GROUP * width
        for h in range(width // HD):
            at = slice(h * HD, h * HD + HD)
            raw = raw_ref[at, :]
            inverse = lax.rsqrt(jnp.mean(raw * raw, axis=0, keepdims=True) + EPSILON)
            gain = gains_ref[pl.ds(pl.multiple_of(base + h * HD, HD), HD), 2:3]
            keys = (raw * inverse * gain).astype(BF)
            for c in range(CLIPS):
                kv_ref[c, at, :] = keys[:, c * CAP : (c + 1) * CAP]
        for c in range(CLIPS):
            kv_ref[c, width:, :] = raw_ref[width:, c * CAP : (c + 1) * CAP].astype(BF)


def caption_keys(ids, w_caption, caption, gains):
    width = w_caption.shape[1] // LINE
    tile = 1024
    count = caption.shape[0]
    return pl.pallas_call(
        caption_kernel,
        grid_spec=pltpu.PrefetchScalarGridSpec(
            num_scalar_prefetch=1,
            grid=(YD // tile,),
            in_specs=[
                pl.BlockSpec((2, width, tile), lambda i, ids: (0, ids[0] // GROUP, i)),
                pl.BlockSpec((count, tile), lambda i, ids: (0, i)),
                pl.BlockSpec(gains.shape, lambda i, ids: (0, 0)),
            ],
            out_specs=[
                pl.BlockSpec((2 * width, count), lambda i, ids: (0, 0)),
                pl.BlockSpec((CLIPS, 2 * width, CAP), lambda i, ids: (0, 0, 0)),
            ],
        ),
        out_shape=[shape((2 * width, count), F32), shape((CLIPS, 2 * width, CAP), BF)],
        name="caption_keys",
        cost_estimate=cost(8),
    )(ids, w_caption, caption, gains)


def attend_kernel(ids, slices, lengths, gates, *refs):
    q_refs = refs[:LINE]
    kv_refs = refs[LINE : LINE + GROUP]
    cap_ref, gains_ref, cos_ref, sin_ref = refs[LINE + GROUP : LINE + GROUP + 4]
    outs = refs[LINE + GROUP + 4 :]
    comb_refs = outs[:LINE]
    own_ref, other_ref, stat_ref, qs_ref, ks_ref, pair_ref = outs[LINE : LINE + 6]
    value_ref, cap_value_ref, sum_ref = outs[LINE + 6 :]
    b, s = ids[0], ids[1]
    width, rows = q_refs[0].shape
    heads = width // HD
    scale = HD**-0.5
    base = s * LINE * width + b // GROUP * width

    def gain_of(h, column):
        return gains_ref[pl.ds(pl.multiple_of(base + h * HD, HD), HD), column : column + 1]

    key_gains = [gain_of(h, 1) for h in range(heads)]
    query_gains = [gain_of(h, 0) for h in range(heads)]
    is_one = lax.broadcasted_iota(jnp.int32, (rows, 2 * HD), 1) < HD
    for j, kv_ref in enumerate(kv_refs):
        for k in range(LINE):
            slot = slot_of(b, k, j)
            _, start, _ = clip_at(slices, slot)
            cosine, sine = cos_ref[slot - start], sin_ref[slot - start]
            for h in range(heads):
                at = slice(h * HD, h * HD + HD)
                raw = kv_ref[k, at, :].astype(F32)
                keys = norm_rope(raw, key_gains[h], cosine, sine)
                values = kv_ref[k, width + h * HD : width + h * HD + HD, :].astype(F32)
                ks_ref[slot, at, :] = keys.astype(BF)
                pair = jnp.concatenate([keys, values], axis=0).T
                pair_ref[slot, h] = pair.astype(BF)
                value_ref[slot, h] = jnp.where(is_one, 1.0, pair).astype(BF)
    cap_one = is_one[:CAP]
    for c in range(CLIPS):
        for h in range(heads):
            values = cap_ref[c, width + h * HD : width + h * HD + HD, :].astype(F32)
            both = jnp.concatenate([values, values], axis=0).T
            cap_value_ref[c, h] = jnp.where(cap_one, 1.0, both).astype(BF)

    for i in range(LINE):
        slot = slot_of(b, i, 0)
        clip, first, last = clip_at(slices, slot)
        cosine, sine = cos_ref[slot - first], sin_ref[slot - first]
        queries = []
        for h in range(heads):
            at = slice(h * HD, h * HD + HD)
            raw = q_refs[i][at, :].astype(F32)
            turned = norm_rope(raw, query_gains[h], cosine, sine).astype(BF).astype(F32) * scale
            qs_ref[i, at, :] = turned.astype(BF)
            queries.append(turned.T.astype(BF))
        sum_ref[...] = jnp.zeros_like(sum_ref)

        def step(n, carry):
            for h in range(heads):
                at = slice(h * HD, h * HD + HD)
                weights = jnp.exp(mm(queries[h], ks_ref[n, at, :], NN))
                sum_ref[h] += mm(weights.astype(BF), value_ref[n, h], NN)
            return carry

        lax.fori_loop(first, last, step, 0)
        usable = lax.broadcasted_iota(jnp.int32, (rows, CAP), 1) < lengths[clip]
        for h in range(heads):
            at = slice(h * HD, h * HD + HD)
            total = sum_ref[h].T
            inverse = 1.0 / total[0:1]
            own = total[HD:] * inverse
            weights = jnp.where(usable, jnp.exp(mm(queries[h], cap_ref[clip, at, :], NN)), 0.0)
            cap_total = mm(weights.astype(BF), cap_value_ref[clip, h], NN).T
            cap_inverse = 1.0 / cap_total[0:1]
            other = cap_total[HD:] * cap_inverse
            own_ref[i, at, :] = own
            other_ref[i, at, :] = other
            gate = gates[(s * LINE + b // GROUP) * heads + h]
            comb_refs[i][at, :] = (own + gate * other).astype(BF)
            stat_ref[i, h : h + 1, :] = inverse
            stat_ref[i, 4 + h : 5 + h, :] = cap_inverse


def attend(ids, slices, lengths, gates, queries, kv_pieces, cap_kv, gains, cosine, sine):
    width, rows = queries[0].shape
    slots = LINE * GROUP
    heads = width // HD
    outs = pl.pallas_call(
        attend_kernel,
        in_specs=[SMEM] * 4 + [VMEM] * (LINE + GROUP + 4),
        out_specs=[VMEM] * (LINE + 6),
        out_shape=[shape((width, rows), BF)] * LINE
        + [
            shape((LINE, width, rows), F32),
            shape((LINE, width, rows), F32),
            shape((LINE, 8, rows), F32),
            shape((LINE, width, rows), BF),
            shape((slots, width, rows), BF),
            shape((slots, heads, rows, 2 * HD), BF),
        ],
        scratch_shapes=[
            pltpu.VMEM((slots, heads, rows, 2 * HD), BF),
            pltpu.VMEM((CLIPS, heads, CAP, 2 * HD), BF),
            pltpu.VMEM((heads, rows, 2 * HD), F32),
        ],
        name="attend",
        cost_estimate=cost(33),
    )(ids, slices, lengths, gates, *queries, *kv_pieces, cap_kv, gains, cosine, sine)
    return outs[:LINE], outs[LINE:]


def out_kernel(ids, *refs):
    own, other = refs[:LINE], refs[LINE : 2 * LINE]
    w_ref, att_ref, branch_ref = refs[2 * LINE :]
    b, s = ids[0], ids[1]
    width = own[0].shape[0]
    for k in range(LINE):
        at = chunk_at(b, k, width)
        att_ref[pl.ds(pl.multiple_of(s * LINE * width + at, HD), width), :] = own[k][...]
        att_ref[pl.ds(pl.multiple_of((1 - s) * LINE * width + at, HD), width), :] = other[k][...]
    branch_ref[...] = mm(w_ref[...], att_ref[...], NN).T.astype(BF)


def out_proj(ids, own, other, w_out):
    rows = own[0].shape[1]
    return pl.pallas_call(
        out_kernel,
        in_specs=[SMEM] + [VMEM] * (2 * LINE + 1),
        out_specs=[VMEM, VMEM],
        out_shape=[shape((D, rows), BF), shape((rows, w_out.shape[0]), BF)],
        name="out_proj",
        cost_estimate=cost(3.5),
    )(ids, *own, *other, w_out)


def cut_kernel(turned, ids, *refs):
    count = len(turned)
    ins = refs[:count]
    own_ref, c_ref, y_ref, scratch = refs[count:]
    place = lax.rem(ids[0], GROUP)
    columns = own_ref.shape[3]
    for n in range(count):
        if turned[n]:
            source = ins[n]
        else:
            scratch[...] = ins[n][...].astype(F32).T
            source = scratch
        for k in range(LINE):
            for j, (ref, i) in enumerate(((own_ref, 0), (c_ref, 0), (y_ref, 0), (y_ref, 1))):
                at = (k * GROUP + jnp.bitwise_xor(place, j)) * columns
                ref[i, n, k] = source[pl.ds(pl.multiple_of(at, 32), columns), :].astype(BF)


def cut(ids, values, turned):
    rows = values[0].shape[1 if turned[0] else 0]
    columns = D // (LINE * GROUP)
    count = len(values)
    return pl.pallas_call(
        functools.partial(cut_kernel, tuple(turned)),
        in_specs=[SMEM] + [VMEM] * count,
        out_specs=[VMEM] * 3,
        out_shape=[shape((n, count, LINE, columns, rows), BF) for n in (1, 1, 2)],
        scratch_shapes=[pltpu.VMEM((D, rows), F32)],
        name="cut",
        cost_estimate=cost(2.4),
    )(ids, *values)


def ffn_kernel(
    ids,
    tok_a,
    tok_b,
    br_a,
    br_b,
    out16_ref,
    mod_ref,
    gain_ref,
    kept_ref,
    came_ref,
    too_ref,
    down_ref,
    inner_a_ref,
    inner_b_ref,
    gcame_a_ref,
    gcame_b_ref,
    gkept_ref,
    in16_ref,
    mid_ref,
    near_ref,
    far_ref,
    near_out_ref,
    far_out_ref,
    acc_in,
    acc_out,
):
    step = pl.program_id(0)
    steps = pl.num_programs(0)
    s = ids[1]
    count = tok_a.shape[0]
    half = br_a.shape[1]
    gate, shift2, scale2 = [mod_ref[i : i + 1, :] for i in (2, 3, 4)]
    mlp_gain = gain_ref[...] * (1.0 + scale2)

    @pl.when(step == 0)
    def _():
        for place, tok in ((s, tok_a), (1 - s, tok_b)):
            at = pl.ds(pl.multiple_of(place * count, count), count)
            mid_ref[at, :] = tok[...].astype(F32)
        low = jnp.where(s == 0, br_a[...].astype(F32), br_b[...].astype(F32))
        high = jnp.where(s == 0, br_b[...].astype(F32), br_a[...].astype(F32))
        mid_ref[:, :half] += gate[:, :half] * low
        mid_ref[:, half:] += gate[:, half:] * high
        middle = mid_ref[...]
        in16_ref[...] = (middle * row_inverse(middle) * mlp_gain + shift2).astype(BF)
        acc_in[...] = jnp.zeros_like(acc_in)
        acc_out[...] = jnp.zeros_like(acc_out)

    w_kept, w_down = kept_ref[...], down_ref[...]
    mine = step // (steps // 2) == lax.rem(ids[0], 2)
    w_came = jnp.where(mine, came_ref[0], too_ref[0])
    kept = mm(in16_ref[...], w_kept, NT)
    other = mm(in16_ref[...], w_came, NT)
    grad_inner = mm(out16_ref[...], w_down, NT)
    gate_half = jnp.where(s == 0, kept, other)
    up_half = jnp.where(s == 0, other, kept)
    sigmoid = jax.nn.sigmoid(gate_half)
    silu = gate_half * sigmoid
    inner = (silu * up_half).astype(BF)
    grad_gate = grad_inner * up_half * sigmoid * (1.0 + gate_half * (1.0 - sigmoid))
    grad_up = grad_inner * silu
    grad_kept = jnp.where(s == 0, grad_gate, grad_up).astype(BF)
    grad_came = jnp.where(s == 0, grad_up, grad_gate).astype(BF)
    @pl.when(step < steps // 2)
    def _():
        inner_a_ref[...] = inner
        gcame_a_ref[...] = grad_came

    @pl.when(step >= steps // 2)
    def _():
        inner_b_ref[...] = inner
        gcame_b_ref[...] = grad_came

    gkept_ref[...] = grad_kept
    acc_in[...] += mm(grad_kept, w_kept, NN) + mm(grad_came, w_came, NN)
    acc_out[...] += mm(inner, w_down, NN)

    @pl.when(step == steps - 1)
    def _():
        middle = mid_ref[...]
        part = jnp.sum(
            acc_in[...] * mlp_gain * (middle * row_inverse(middle)), axis=-1, keepdims=True
        )
        near_ref[:, :half] = acc_in[:, pl.ds(pl.multiple_of(s * half, half), half)]
        near_ref[:, half:] = jnp.broadcast_to(part, (part.shape[0], 128))
        far_ref[:, :half] = acc_in[:, pl.ds(pl.multiple_of((1 - s) * half, half), half)].astype(BF)
        high = part.astype(BF).astype(F32)
        middle_part = (part - high).astype(BF).astype(F32)
        low_part = part - high - middle_part
        lane = lax.broadcasted_iota(jnp.int32, (part.shape[0], 128), 1)
        spread = jnp.where(lane == 0, high, jnp.where(lane == 1, middle_part, jnp.where(lane == 2, low_part, 0.0)))
        far_ref[:, half:] = spread.astype(BF)
        near_out_ref[...] = acc_out[pl.ds(pl.multiple_of(s * count, count), count), :]
        far_out_ref[...] = acc_out[pl.ds(pl.multiple_of((1 - s) * count, count), count), :].astype(BF)


def ffn(ids, toks, branches, grad_mlp, mod, gain, w_gate_up, came, too, w_down):
    count = toks[0].shape[0]
    rows = 2 * count
    half = D // 2
    units = w_down.shape[0]
    tile = 512
    steps = units // tile
    full = lambda v: pl.BlockSpec(v.shape, lambda i, ids: (0,) * v.ndim)

    def fixed(r, c):
        return pl.BlockSpec((r, c), lambda i, ids: (0, 0))

    def part(i, ids, flip):
        core = jnp.bitwise_xor(lax.rem(ids[0], 2), flip)
        return jnp.clip(i - core * (steps // 2), 0, steps // 2 - 1)

    small = [*toks, *branches, grad_mlp, mod, gain]
    return pl.pallas_call(
        ffn_kernel,
        grid_spec=pltpu.PrefetchScalarGridSpec(
            num_scalar_prefetch=1,
            grid=(steps,),
            in_specs=[full(v) for v in small]
            + [
                pl.BlockSpec((tile, D), lambda i, ids: (ids[1] * steps + i, 0)),
                pl.BlockSpec((1, tile, D), lambda i, ids: (1 - ids[1], part(i, ids, 0), 0)),
                pl.BlockSpec((1, tile, D), lambda i, ids: (1 - ids[1], part(i, ids, 1), 0)),
                pl.BlockSpec((tile, D), lambda i, ids: (i, 0)),
            ],
            out_specs=[
                pl.BlockSpec((rows, tile), lambda i, ids: (0, jnp.minimum(i, steps // 2 - 1))),
                pl.BlockSpec((rows, tile), lambda i, ids: (0, jnp.maximum(i - steps // 2, 0))),
            ]
            * 2
            + [pl.BlockSpec((rows, tile), lambda i, ids: (0, i))]
            + [
                fixed(rows, D),
                fixed(rows, D),
                fixed(rows, half + 128),
                fixed(rows, half + 128),
                fixed(count, D),
                fixed(count, D),
            ],
            scratch_shapes=[pltpu.VMEM((rows, D), F32), pltpu.VMEM((rows, D), F32)],
        ),
        out_shape=[shape((rows, units // 2), BF)] * 4
        + [shape((rows, units), BF)]
        + [
            shape((rows, D), BF),
            shape((rows, D), F32),
            shape((rows, half + 128), F32),
            shape((rows, half + 128), BF),
            shape((count, D), F32),
            shape((count, D), BF),
        ],
        name="ffn",
        cost_estimate=cost(18),
    )(ids, *small, w_gate_up, came, too, w_down)


def mid_kernel(
    ids,
    near_ref,
    recv_ref,
    mid_ref,
    cot_a,
    cot_b,
    br_ref,
    mod_ref,
    gain_ref,
    w_ref,
    sums_ref,
    gbr_ref,
    near_mid_ref,
    far_mid_ref,
    *refs,
):
    near_refs, far_refs, scratch = refs[:2], refs[2:4], refs[4]
    b, s = ids[0], ids[1]
    half = D // 2
    count = cot_a.shape[0]
    cols = pl.ds(pl.multiple_of(s * half, half), half)
    gate, scale2 = mod_ref[2:3, cols], mod_ref[4:5, cols]
    gain = gain_ref[:, cols]
    middle = mid_ref[...]
    inverse = row_inverse(middle)
    unit = mid_ref[:, cols] * inverse
    parts = jnp.sum(recv_ref[:, half:].astype(F32), axis=-1, keepdims=True)
    mean = (near_ref[:, half : half + 1] + parts) * (1.0 / D)
    grad_in = near_ref[:, :half] + recv_ref[:, :half].astype(F32)
    cot_own, cot_far = cot_a[:, cols].astype(F32), cot_b[:, cols].astype(F32)
    cot = jnp.concatenate(
        [jnp.where(s == 0, cot_own, cot_far), jnp.where(s == 0, cot_far, cot_own)], axis=0
    )
    scaled = grad_in * (1.0 + scale2)
    grad_mid = cot + inverse * (scaled * gain - unit * mean)
    sums_ref[...] = jnp.zeros_like(sums_ref)
    sums_ref[0:1, :] = jnp.sum(grad_mid * br_ref[...].astype(F32), axis=0, keepdims=True)
    sums_ref[1:2, :] = jnp.sum(grad_in, axis=0, keepdims=True)
    sums_ref[2:3, :] = jnp.sum(grad_in * unit, axis=0, keepdims=True) * gain
    sums_ref[3:4, :] = jnp.sum(scaled * unit, axis=0, keepdims=True)
    grad_branch = (grad_mid * gate).astype(BF)
    gbr_ref[...] = grad_branch
    top, low = grad_mid[:count], grad_mid[count:]
    near_mid_ref[...] = jnp.where(s == 0, top, low)
    far_mid_ref[...] = jnp.where(s == 0, low, top).astype(BF)
    scratch[...] = mm(grad_branch, w_ref[...], NN).T
    width = near_refs[0].shape[0] // 2
    for n, k in enumerate(SENDS):
        at = chunk_at(b, k, width)
        to = slice(n % 2 * width, n % 2 * width + width)
        near_refs[n // 2][to, :] = scratch[pl.ds(pl.multiple_of(s * half + at, HD), width), :]
        far_refs[n // 2][to, :] = scratch[
            pl.ds(pl.multiple_of((1 - s) * half + at, HD), width), :
        ].astype(BF)


def mid_back(ids, near, received, middle, cots, branch, mod, gain, w_out):
    rows, half = branch.shape
    width = half // LINE
    count = cots[0].shape[0]
    outs = pl.pallas_call(
        mid_kernel,
        in_specs=[SMEM] + [VMEM] * 9,
        out_specs=[VMEM] * 8,
        out_shape=[
            shape((8, half), F32),
            shape((rows, half), BF),
            shape((count, half), F32),
            shape((count, half), BF),
        ]
        + [shape((2 * width, rows), F32)] * 2
        + [shape((2 * width, rows), BF)] * 2,
        scratch_shapes=[pltpu.VMEM((D, rows), F32)],
        name="mid_back",
        cost_estimate=cost(5.5),
    )(ids, near, received, middle, *cots, branch, mod, gain, w_out)
    return outs[:4], outs[4:6], outs[6:]


def add_pair_kernel(near_ref, recv_ref, a_ref, b_ref):
    width = a_ref.shape[0]
    total = (near_ref[...] + recv_ref[...].astype(F32)).astype(BF)
    a_ref[...] = total[:width]
    b_ref[...] = total[width:]


def add_pair(near, received):
    both, rows = near.shape
    return pl.pallas_call(
        add_pair_kernel,
        in_specs=[VMEM, VMEM],
        out_specs=[VMEM, VMEM],
        out_shape=[shape((both // 2, rows), BF)] * 2,
        name="add_pair",
        cost_estimate=cost(1),
    )(near, received)


def place_row(b, column):
    width = column.shape[0]
    row = jnp.broadcast_to(column, (width, 128)).T[0:1]
    z = b // GROUP
    return jnp.concatenate([jnp.where(z == k, row, 0.0) for k in range(LINE)], axis=1)


def output_kernel(ids, slices, near_ref, recv_ref, mid_ref, cot_ref, mod_ref, sums_ref, out_ref, early_ref):
    s = ids[1]
    count, half = near_ref.shape[0], sums_ref.shape[1]
    clip, _, _ = clip_at(slices, ids[0])
    branch = near_ref[...] + recv_ref[...].astype(F32)
    middle = mid_ref[pl.ds(pl.multiple_of(s * count, count), count), :]
    out_ref[...] = (middle + mod_ref[5:6, :] * branch).astype(BF)
    gate2 = jnp.sum(cot_ref[...].astype(F32) * branch, axis=0, keepdims=True)
    rows = [sums_ref[i : i + 1, :] for i in range(3)] + [gate2[:, :half], gate2[:, half:]]
    early_ref[...] = jnp.zeros_like(early_ref)
    for c in range(CLIPS):
        for i, row in enumerate(rows):
            early_ref[5 * c + i : 5 * c + i + 1, :] = jnp.where(clip == c, row, 0.0)
    early_ref[20:21, :] = sums_ref[3:4, :]


def output_sums(ids, slices, near, received, middle, cot, mod, sums):
    count = near.shape[0]
    return pl.pallas_call(
        output_kernel,
        in_specs=[SMEM, SMEM] + [VMEM] * 6,
        out_specs=[VMEM, VMEM],
        out_shape=[shape((count, D), BF), shape((24, D // 2), F32)],
        name="output_sums",
        cost_estimate=cost(3),
    )(ids, slices, near, received, middle, cot, mod, sums)


def attend_back_kernel(ids, slices, lengths, gates, *refs):
    q_refs, g_refs = refs[:LINE], refs[LINE : 2 * LINE]
    (own_ref, other_ref, stat_ref, qs_ref, ks_ref, pair_ref, cap_ref, gains_ref, cos_ref, sin_ref) = refs[
        2 * LINE : 2 * LINE + 10
    ]
    outs = refs[2 * LINE + 10 :]
    gq_refs = outs[:LINE]
    qgain_ref, keep_ref, send_ref, dgate_ref = outs[LINE : LINE + 4]
    dkv_refs = outs[LINE + 4 : LINE + 4 + GROUP]
    acc_ref, dcap_ref, dq_ref = outs[LINE + 4 + GROUP :]
    b, s = ids[0], ids[1]
    width, rows = q_refs[0].shape
    heads = width // HD
    scale = HD**-0.5
    base = s * LINE * width + b // GROUP * width
    acc_ref[...] = jnp.zeros_like(acc_ref)
    dcap_ref[...] = jnp.zeros_like(dcap_ref)
    dgate_ref[...] = jnp.zeros_like(dgate_ref)
    qgain_ref[...] = jnp.zeros_like(qgain_ref)

    for i in range(LINE):
        slot = slot_of(b, i, 0)
        clip, first, last = clip_at(slices, slot)
        queries, grads, deltas, inverses = [], [], [], []
        tall_q, tall_g, wide = [], [], []
        for h in range(heads):
            at = slice(h * HD, h * HD + HD)
            grad = g_refs[i][at, :]
            queries.append(qs_ref[i, at, :])
            grads.append(grad)
            deltas.append(jnp.sum(grad.astype(F32) * own_ref[i, at, :], axis=0, keepdims=True))
            inverses.append(stat_ref[i, h : h + 1, :])
            blank = jnp.zeros((HD, rows), F32)
            query_pad = jnp.concatenate([queries[h].astype(F32), blank], axis=0)
            grad_pad = jnp.concatenate([blank, grad.astype(F32)], axis=0)
            tall_q.append(query_pad.astype(BF))
            tall_g.append(grad_pad.astype(BF))
            wide.append(jnp.concatenate([query_pad.T, grad_pad.T], axis=0).astype(BF))
        dq_ref[...] = jnp.zeros_like(dq_ref)

        def step(n, carry):
            for h in range(heads):
                at = slice(h * HD, h * HD + HD)
                pair = pair_ref[n, h]
                prob = jnp.exp(mm(pair, tall_q[h], NN)) * inverses[h]
                grad_score = (prob * (mm(pair, tall_g[h], NN) - deltas[h])).astype(BF)
                both = jnp.concatenate([grad_score, prob.astype(BF)], axis=1)
                acc_ref[n, h] += mm(both, wide[h], NN)
                dq_ref[at, :] += mm(ks_ref[n, at, :], grad_score, NN)
            return carry

        lax.fori_loop(first, last, step, 0)
        usable = lax.broadcasted_iota(jnp.int32, (CAP, rows), 0) < lengths[clip]
        cosine, sine = cos_ref[slot - first], sin_ref[slot - first]
        for h in range(heads):
            at = slice(h * HD, h * HD + HD)
            at_value = slice(width + h * HD, width + h * HD + HD)
            gate = gates[(s * LINE + b // GROUP) * heads + h]
            cap_keys, cap_values = cap_ref[clip, at, :], cap_ref[clip, at_value, :]
            grad = grads[h].astype(F32)
            grad_other = (grad * gate).astype(BF)
            prob = (
                jnp.where(usable, jnp.exp(mm(cap_keys, queries[h], TN)), 0.0)
                * stat_ref[i, 4 + h : 5 + h, :]
            )
            grad_prob = mm(cap_values, grad_other, TN)
            inner = jnp.sum(prob * grad_prob, axis=0, keepdims=True)
            grad_score = (prob * (grad_prob - inner)).astype(BF)
            query_grad = (dq_ref[at, :] + mm(cap_keys, grad_score, NN)) * scale
            dcap_ref[clip, at, :] += mm(queries[h], grad_score, NT)
            dcap_ref[clip, at_value, :] += mm(grad_other, prob.astype(BF), NT)
            part = jnp.sum(grad * other_ref[i, at, :], axis=0, keepdims=True)
            dgate_ref[h : h + 1, :] += part * (1.0 - gate * gate)
            gain = gains_ref[pl.ds(pl.multiple_of(base + h * HD, HD), HD), 0:1]
            raw_grad, gain_grad = norm_rope_back(
                query_grad.astype(BF).astype(F32), q_refs[i][at, :].astype(F32), gain, cosine, sine
            )
            gq_refs[i][at, :] = raw_grad.astype(BF)
            qgain_ref[at, :] += gain_grad

    for j, dkv_ref in enumerate(dkv_refs):
        for k in range(LINE):
            slot = slot_of(b, k, j)
            for h in range(heads):
                both = acc_ref[slot, h].T.astype(BF)
                dkv_ref[k, h * HD : h * HD + HD, :] = both[:HD]
                dkv_ref[k, width + h * HD : width + h * HD + HD, :] = both[HD:]
    core = lax.rem(b, 2)
    for i in range(2):
        keep_ref[i] = dcap_ref[2 * i + core]
        send_ref[i] = dcap_ref[2 * i + 1 - core]


def attend_back(ids, slices, lengths, gates, queries, grads, saved, cap_kv, gains, cosine, sine):
    width, rows = queries[0].shape
    outs = pl.pallas_call(
        attend_back_kernel,
        in_specs=[SMEM] * 4 + [VMEM] * (2 * LINE + 10),
        out_specs=[VMEM] * (LINE + 4 + GROUP),
        out_shape=[shape((width, rows), BF)] * LINE
        + [
            shape((width, 1), F32),
            shape((2, 2 * width, CAP), F32),
            shape((2, 2 * width, CAP), F32),
            shape((8, rows), F32),
        ]
        + [shape((LINE, 2 * width, rows), BF)] * GROUP,
        scratch_shapes=[
            pltpu.VMEM((LINE * GROUP, width // HD, rows, 2 * HD), F32),
            pltpu.VMEM((CLIPS, 2 * width, CAP), F32),
            pltpu.VMEM((width, rows), F32),
        ],
        name="attend_back",
        cost_estimate=cost(40),
    )(ids, slices, lengths, gates, *queries, *grads, *saved, cap_kv, gains, cosine, sine)
    return outs[:LINE], outs[LINE : LINE + 4], outs[LINE + 4 :]


def keys_back_kernel(ids, slices, a_ref, c_ref, r_ref, kv_ref, gains_ref, cos_ref, sin_ref, *outs):
    out_refs, gain_ref = outs[:LINE], outs[LINE]
    b, s = ids[0], ids[1]
    width = gain_ref.shape[0]
    base = s * LINE * width + b // GROUP * width
    gain_ref[...] = jnp.zeros_like(gain_ref)
    for i in range(LINE):
        slot = slot_of(b, i, 0)
        _, first, _ = clip_at(slices, slot)
        cosine, sine = cos_ref[slot - first], sin_ref[slot - first]
        total = a_ref[i].astype(F32) + c_ref[i].astype(F32) + r_ref[i].astype(F32)
        total = total.astype(BF)
        for h in range(width // HD):
            at = slice(h * HD, h * HD + HD)
            gain = gains_ref[pl.ds(pl.multiple_of(base + h * HD, HD), HD), 1:2]
            raw_grad, gain_grad = norm_rope_back(
                total[at, :].astype(F32), kv_ref[i, at, :].astype(F32), gain, cosine, sine
            )
            out_refs[i][at, :] = raw_grad.astype(BF)
            gain_ref[at, :] += gain_grad
        out_refs[i][width:, :] = total[width:, :]


def keys_back(ids, slices, part, beside, received, kv, gains, cosine, sine):
    _, both, rows = kv.shape
    outs = pl.pallas_call(
        keys_back_kernel,
        in_specs=[SMEM, SMEM] + [VMEM] * 7,
        out_specs=[VMEM] * (LINE + 1),
        out_shape=[shape((both, rows), BF)] * LINE + [shape((both // 2, 1), F32)],
        name="keys_back",
        cost_estimate=cost(3.7),
    )(ids, slices, part, beside, received, kv, gains, cosine, sine)
    return outs[:LINE], outs[LINE]


def pack_kernel(ids, *refs):
    q_refs, kv_refs = refs[:LINE], refs[LINE : 2 * LINE]
    first_ref, second_ref, send_ref = refs[2 * LINE :]
    b, s = ids[0], ids[1]
    width = q_refs[0].shape[0]
    for k in range(LINE):
        at = chunk_at(b, k, width)

        @pl.when(s == 0)
        def _():
            first_ref[pl.ds(at, width), :] = q_refs[k][...]
            second_ref[pl.ds(at, width), :] = kv_refs[k][:width, :]
            send_ref[pl.ds(at, width), :] = kv_refs[k][width:, :]

        @pl.when(s == 1)
        def _():
            first_ref[pl.ds(at, width), :] = kv_refs[k][:width, :]
            second_ref[pl.ds(at, width), :] = kv_refs[k][width:, :]
            send_ref[pl.ds(at, width), :] = q_refs[k][...]


def pack(ids, grads_q, grads_kv):
    width, rows = grads_q[0].shape
    return pl.pallas_call(
        pack_kernel,
        in_specs=[SMEM] + [VMEM] * (2 * LINE),
        out_specs=[VMEM] * 3,
        out_shape=[shape((LINE * width, rows), BF)] * 3,
        name="pack",
        cost_estimate=cost(2.5),
    )(ids, *grads_q, *grads_kv)


def qkv_back_kernel(ids, first_ref, recv_ref, second_ref, w_ref, near_ref, far_ref, acc_ref):
    step = pl.program_id(0)
    count = near_ref.shape[0]
    s = ids[1]

    for n, ref in enumerate((first_ref, recv_ref, second_ref)):

        @pl.when(step == n)
        def _():
            part = mm(ref[...], w_ref[...], TN)
            acc_ref[...] = part if n == 0 else acc_ref[...] + part

    @pl.when(step == pl.num_programs(0) - 1)
    def _():
        near_ref[...] = acc_ref[pl.ds(pl.multiple_of(s * count, count), count), :]
        far_ref[...] = acc_ref[pl.ds(pl.multiple_of((1 - s) * count, count), count), :].astype(BF)


def qkv_back(ids, first, received, second, w_qkv):
    local, rows = received.shape
    count = rows // 2
    whole = pl.BlockSpec((local, rows), lambda i, ids: (0, 0))
    return pl.pallas_call(
        qkv_back_kernel,
        grid_spec=pltpu.PrefetchScalarGridSpec(
            num_scalar_prefetch=1,
            grid=(3,),
            in_specs=[whole] * 3 + [pl.BlockSpec((local, D), lambda i, ids: (i, 0))],
            out_specs=[pl.BlockSpec((count, D), lambda i, ids: (0, 0))] * 2,
            scratch_shapes=[pltpu.VMEM((rows, D), F32)],
        ),
        out_shape=[shape((count, D), F32), shape((count, D), BF)],
        name="qkv_back",
        cost_estimate=cost(6),
    )(ids, first, received, second, w_qkv)


def tokens_kernel(
    ids, slices, tok_ref, near_ref, recv_ref, mid_near, mid_far, mod_ref, gain_ref, *refs
):
    qgain_ref, kgain_ref, cgain_ref, dgate_ref, early_ref, out_ref, late_ref = refs
    b, s = ids[0], ids[1]
    half = mid_near.shape[1]
    clip, _, _ = clip_at(slices, b)
    values = tok_ref[...].astype(F32)
    inverse = row_inverse(values)
    unit = values * inverse
    scale = 1.0 + mod_ref[1:2, :]
    gain = gain_ref[...]
    grad = near_ref[...] + recv_ref[...].astype(F32)
    scaled = grad * scale
    unit_grad = scaled * gain
    mean = jnp.mean(unit_grad * unit, axis=-1, keepdims=True)
    mid_own, mid_other = mid_near[...], mid_far[...].astype(F32)
    middle = jnp.concatenate(
        [jnp.where(s == 0, mid_own, mid_other), jnp.where(s == 0, mid_other, mid_own)], axis=1
    )
    out_ref[...] = inverse * (unit_grad - unit * mean) + middle
    shift_row = jnp.sum(grad, axis=0, keepdims=True)
    with_unit = grad * unit
    scale_row = jnp.sum(with_unit, axis=0, keepdims=True) * gain
    norm_row = jnp.sum(scaled * unit, axis=0, keepdims=True)
    rows = [shift_row[:, :half], shift_row[:, half:], scale_row[:, :half], scale_row[:, half:]]
    late_ref[...] = jnp.zeros_like(late_ref)
    for c in range(CLIPS):
        for i, row in enumerate(rows):
            late_ref[4 * c + i : 4 * c + i + 1, :] = jnp.where(clip == c, row, 0.0)
    late_ref[16:17, :] = norm_row[:, :half]
    late_ref[17:18, :] = norm_row[:, half:]
    for i, ref in enumerate((qgain_ref, kgain_ref, cgain_ref)):
        late_ref[18 + i : 19 + i, :] = place_row(b, ref[...])
    heads = qgain_ref.shape[0] // HD
    lane = lax.broadcasted_iota(jnp.int32, (1, half), 1)
    gate_row = jnp.zeros((1, half), F32)
    for h in range(heads):
        value = jnp.sum(dgate_ref[h : h + 1, :], axis=1, keepdims=True)
        gate_row = gate_row + jnp.where(lane == b // GROUP * heads + h, value, 0.0)
    late_ref[21:22, :] = gate_row
    late_ref[24:, :] = early_ref[...]


def tokens_back(ids, slices, tok, near, received, mid_near, mid_far, mod, gain, parts):
    return pl.pallas_call(
        tokens_kernel,
        in_specs=[SMEM, SMEM] + [VMEM] * 12,
        out_specs=[VMEM, VMEM],
        out_shape=[shape(tok.shape, F32), shape((48, D // 2), F32)],
        name="tokens_back",
        cost_estimate=cost(3.5),
    )(ids, slices, tok, near, received, mid_near, mid_far, mod, gain, *parts)


def finish_kernel(ids, late_a, late_b, mod_ref, gains_ref):
    s = ids[1]
    early_a, early_b = late_a.at[pl.ds(24, 24)], late_b.at[pl.ds(24, 24)]

    def joined(a, b, i):
        own, other = a[i : i + 1, :], b[i : i + 1, :]
        return jnp.concatenate(
            [jnp.where(s == 0, own, other), jnp.where(s == 0, other, own)], axis=1
        )

    def added(a, b, i):
        both = a[i : i + 2, :] + b[i : i + 2, :]
        return jnp.concatenate([both[0:1], both[1:2]], axis=1)

    for c in range(CLIPS):
        low = [added(late_a, late_b, 4 * c), added(late_a, late_b, 4 * c + 2), joined(early_a, early_b, 5 * c)]
        high = [
            joined(early_a, early_b, 5 * c + 1),
            joined(early_a, early_b, 5 * c + 2),
            added(early_a, early_b, 5 * c + 3),
        ]
        for i in range(3):
            mod_ref[c : c + 1, i * D : (i + 1) * D] = jnp.where(s == 0, low[i], high[i])
    gains_ref[...] = jnp.zeros_like(gains_ref)
    gains_ref[0:1, :] = added(late_a, late_b, 16)
    for i in range(3):
        gains_ref[1 + i : 2 + i, :] = joined(late_a, late_b, 18 + i)
    gains_ref[4:5, :] = joined(early_a, early_b, 20)
    gains_ref[5:6, :] = joined(late_a, late_b, 21)


def finish(ids, late_a, late_b):
    return pl.pallas_call(
        finish_kernel,
        in_specs=[SMEM] + [VMEM] * 2,
        out_specs=[VMEM, VMEM],
        out_shape=[shape((CLIPS, 3 * D), F32), shape((8, D), F32)],
        name="finish",
        cost_estimate=cost(1.7),
    )(ids, late_a, late_b)


def caption_back_kernel(ids, sum_ref, raw_ref, gains_ref, out_ref, gain_ref):
    b, s = ids[0], ids[1]
    width = gain_ref.shape[0]
    base = s * LINE * width + b // GROUP * width
    cols = pl.ds(pl.multiple_of(lax.rem(b, GROUP) * CAP, CAP), CAP)
    for h in range(width // HD):
        at = slice(h * HD, h * HD + HD)
        gain = gains_ref[pl.ds(pl.multiple_of(base + h * HD, HD), HD), 2:3]
        raw = raw_ref[at, cols]
        inverse = lax.rsqrt(jnp.mean(raw * raw, axis=0, keepdims=True) + EPSILON)
        unit = raw * inverse
        grad = sum_ref[at, :]
        gain_ref[at, :] = jnp.sum(grad * unit, axis=1, keepdims=True)
        unit_grad = grad * gain
        out_ref[at, :] = (
            inverse * (unit_grad - unit * jnp.mean(unit_grad * unit, axis=0, keepdims=True))
        ).astype(BF)
    out_ref[width:, :] = sum_ref[width:, :].astype(BF)


def caption_back(ids, total, raw, gains):
    return pl.pallas_call(
        caption_back_kernel,
        in_specs=[SMEM] + [VMEM] * 3,
        out_specs=[VMEM, VMEM],
        out_shape=[shape(total.shape, BF), shape((total.shape[0] // 2, 1), F32)],
        name="caption_back",
        cost_estimate=cost(2.3),
    )(ids, total, raw, gains)


def caption_weight_kernel(ids, *refs):
    raw_refs, cap_ref, out_refs = refs[:GROUP], refs[GROUP], refs[GROUP + 1 :]
    b = ids[0]
    each = out_refs[0].shape[1]
    place = lax.rem(b, GROUP)
    for k in range(LINE):
        at = pl.multiple_of((lax.rem(b // GROUP - k + LINE, LINE) * GROUP + place) * each, each)
        total = None
        for j in range(GROUP):
            rows = pl.ds(pl.multiple_of(jnp.bitwise_xor(place, j) * CAP, CAP), CAP)
            part = mm(raw_refs[j][...], cap_ref[rows, pl.ds(at, each)], NN)
            total = part if total is None else total + part
        out_refs[k][...] = total.astype(BF)


def caption_weights(ids, raws, caption):
    rows = raws[0].shape[0]
    return pl.pallas_call(
        caption_weight_kernel,
        in_specs=[SMEM] + [VMEM] * (GROUP + 1),
        out_specs=[VMEM] * LINE,
        out_shape=[shape((rows, YD // (LINE * GROUP)), BF)] * LINE,
        name="caption_weights",
        cost_estimate=cost(4),
    )(ids, *raws, caption)


def caption_join_kernel(ids, *refs):
    parts, out_ref = refs[:LINE], refs[LINE]
    width = parts[0].shape[0] // 2
    for k in range(LINE):
        at = chunk_at(ids[0], k, width)
        for j in range(2):
            out_ref[j, pl.ds(at, width), :] = parts[k][j * width : (j + 1) * width, :].astype(F32)


def caption_join(ids, parts):
    both, each = parts[0].shape
    return pl.pallas_call(
        caption_join_kernel,
        in_specs=[SMEM] + [VMEM] * LINE,
        out_specs=VMEM,
        out_shape=shape((2, both // 2 * LINE, each), F32),
        name="caption_join",
        cost_estimate=cost(2),
    )(ids, *parts)


def weight_kernel(count, dims, *refs):
    left, right, out_ref = refs[:count], refs[count : 2 * count], refs[-1]
    total = None
    for a_ref, g_ref in zip(left, right):
        block = g_ref[...].reshape(g_ref.shape[-2:])
        part = mm(a_ref[0, 0].reshape(-1, a_ref.shape[-1]), block, dims)
        total = part if total is None else total + part
    out_ref[...] = total.reshape(out_ref.shape).astype(BF)


def weight_grads(left, right, by_rows, tile, kind, total, place, into=None):
    _, _, chunks, columns, tokens = left[0][0].shape
    rows = right[0].shape[-2 if by_rows else -1]
    stack = right[0].shape[0] if right[0].ndim == 3 else 1
    per = rows // tile
    left_specs = [
        pl.BlockSpec((1, 1, chunks, columns, tokens), lambda i, n=n: (n, kind, 0, 0, 0))
        for _, n in left
    ]
    if by_rows:
        right_spec = pl.BlockSpec((tile, tokens), lambda i: (i, 0))
    elif stack == 1:
        right_spec = pl.BlockSpec((tokens, tile), lambda i: (0, i))
    else:
        right_spec = pl.BlockSpec((1, tokens, tile), lambda i: (i // per, 0, i % per))
    args = [a for a, _ in left] + list(right)
    specs = left_specs + [right_spec] * len(right)
    aliases = {}
    if into is not None:
        aliases = {len(args): 0}
        args.append(into)
        specs.append(pl.BlockSpec(memory_space=pl.ANY))
    return pl.pallas_call(
        functools.partial(weight_kernel, len(left), NT if by_rows else NN),
        grid=(stack * per,),
        in_specs=specs,
        out_specs=pl.BlockSpec((chunks, columns, tile), lambda i: (0, 0, place(i))),
        out_shape=shape((chunks, columns, total), BF),
        input_output_aliases=aliases,
        name="weight_grads",
        cost_estimate=cost(5),
    )(*args)


def fast_body(
    tokens,
    cotangent,
    clip_slices,
    caption_lengths,
    caption,
    cond,
    ada_w,
    norm_gain,
    w_qkv,
    q_gain,
    k_gain,
    w_caption,
    ky_gain,
    cross_gate,
    w_out,
    ffn_gain,
    w_gate_up,
    w_down,
):
    bucket_count = LINE * GROUP
    seq_count = lax.axis_size("seq")
    local_width = D // seq_count
    units = FF // seq_count
    b = lax.axis_index(BUCKET)
    s = lax.axis_index("seq")
    z, g, c, y = b // GROUP, b % GROUP, b % 2, (b // 2) % 2
    ids = jnp.stack([b, s]).astype(jnp.int32)

    def xswap(v):
        return lax.ppermute(v, "seq", [(0, 1), (1, 0)])

    def hop(v, to):
        return lax.ppermute(v, BUCKET, [(i, to(i)) for i in range(bucket_count)])

    def cswap(v):
        return hop(v, lambda i: i ^ 1)

    def yswap(v):
        return hop(v, lambda i: i ^ 2)

    def zshift(v, k):
        return hop(v, lambda i: (i + GROUP * k) % bucket_count)

    def after(v, *others):
        return lax.optimization_barrier((v, *others))[0]

    def fence(*values):
        return lax.optimization_barrier(values)

    def pick(v, index):
        return lax.dynamic_index_in_dim(v, index, 0, False)

    def spread(parts):
        return [parts[0]] + [zshift(parts[k], k) for k in range(1, LINE)]

    def unspread(parts):
        return [parts[0]] + [zshift(parts[k], LINE - k) for k in range(1, LINE)]

    half = HD // 2
    rows = tokens.shape[0] * seq_count
    frequency = jnp.exp(jnp.arange(half, dtype=F32) * (-2.0 * math.log(10000.0) / (2 * half)))
    positions = jnp.arange(bucket_count * rows, dtype=F32).reshape(bucket_count, 1, rows)
    angles = positions * frequency[None, :, None]
    cosine, sine = jnp.cos(angles), jnp.sin(angles)
    gains = jnp.stack([q_gain, k_gain, ky_gain], axis=1)
    gates = jnp.tanh(cross_gate)
    norm_row, ffn_row = norm_gain[None], ffn_gain[None]

    tok_far = xswap(tokens)
    activation = jax.nn.silu(cond).astype(BF)
    mod_near = mm(activation, ada_w, NT)
    mod_far = xswap(mod_near)
    each = units // 2
    sent = lax.dynamic_slice_in_dim(w_gate_up, (1 - s) * units + c * each, each, 0)
    tok_far, sent = lax.optimization_barrier((tok_far, sent))
    projected, hidden, mod = pre(
        ids, clip_slices, tokens, tok_far, mod_near, mod_far, norm_row, w_qkv
    )
    local = lax.slice_in_dim(projected, local_width, 2 * local_width, axis=0)
    swapped = xswap(local)
    def scatter(parts):
        return lax.psum_scatter(parts, "z", scatter_dimension=0, tiled=False)

    hid_own, hid_c, hid_y = cut(ids, [hidden], [False])
    swapped, hid_own, hid_c, hid_y, gains = fence(swapped, hid_own, hid_c, hid_y, gains)
    kv_parts, q_parts = route(ids, projected, swapped)
    came = lax.all_gather(after(sent, swapped), "seq", axis=0, tiled=False)
    kv_here = spread(kv_parts)
    q_here = spread(q_parts)
    caption_rows = caption.reshape(CLIPS * CAP, YD)
    cap_raw, cap_kv = caption_keys(ids, w_caption, after(caption_rows, kv_parts[0]), gains)
    cap_raw, cap_kv, cosine, sine, *kv_here = fence(cap_raw, cap_kv, cosine, sine, *kv_here)
    kv_own = jnp.stack(kv_here)
    kv_y = yswap(kv_own)
    kv_c = cswap(kv_own)
    cot_far = xswap(after(cotangent, kv_own))
    kv_y = after(kv_y, kv_c, *q_here[1:], cot_far)
    kv_cy = cswap(kv_y)
    kv_pieces = [kv_own, kv_c, kv_y, kv_cy]
    grad_mlp = (
        jnp.where(
            s == 0,
            jnp.concatenate([cotangent, cot_far], 0),
            jnp.concatenate([cot_far, cotangent], 0),
        ).astype(F32)
        * mod[5:6]
    ).astype(BF)
    q_here[0], hid_y, hid_c = fence(q_here[0], hid_y, hid_c, grad_mlp)[:3]
    hid_came_y, hid_came_c = yswap(hid_y), cswap(hid_c)
    combined, saved = attend(
        ids, clip_slices, caption_lengths, gates, q_here, kv_pieces, cap_kv, gains, cosine, sine
    )
    combined, saved, hid_came_y, hid_came_c = fence(combined, saved, hid_came_y, hid_came_c)
    heads_own = unspread(combined)
    heads_far = [xswap(v) for v in heads_own]
    attention, branch = out_proj(ids, heads_own, heads_far, w_out)
    branch_far = xswap(branch)
    att_own, att_c, att_y = cut(ids, [attention, grad_mlp], [True, False])
    came = after(came, branch)
    too = cswap(came)
    branch_far, att_own, att_c, att_y, too = fence(branch_far, att_own, att_c, att_y, too)
    att_came_y = yswap(att_y)
    att_came_c = cswap(att_c)
    hid_came_yc = cswap(after(hid_came_y, branch_far))
    hid_left = [(hid_own, 0), (hid_came_c, 0), (hid_came_y, 0), (hid_came_yc, 1)]
    inner, inner_2, came_1, came_2, grad_kept, mlp_in, middle, near, far, near_out, far_out = ffn(
        ids, [tokens, tok_far], [branch, branch_far], grad_mlp, mod, ffn_row, w_gate_up, came, too, w_down
    )
    inner, inner_2, grad_kept, came_1, came_2, mlp_in, near, far = fence(
        inner, inner_2, grad_kept, came_1, came_2, mlp_in, near, far
    )
    att_came_y, att_came_c, hid_came_yc, far = fence(att_came_y, att_came_c, hid_came_yc, far)
    hid_left[3] = (hid_came_yc, 1)

    received = xswap(far)
    inner_y = yswap(inner)
    inner_c = cswap(inner)
    kept_c = cswap(grad_kept)
    att_came_yc = cswap(att_came_y)
    att_left = [(att_own, 0), (att_came_c, 0), (att_came_y, 0), (att_came_yc, 1)]
    ffn_own, ffn_c, ffn_y = cut(ids, [mlp_in], [False])
    received, ffn_own, ffn_c, ffn_y, inner_c, inner_y, kept_c, att_came_yc, came_op, inner_op = fence(
        received, ffn_own, ffn_c, ffn_y, inner_c, inner_y, kept_c, att_came_yc, came_1, inner_2
    )
    came_1c = cswap(came_op)
    att_left[3] = (att_came_yc, 1)
    inner_2y = yswap(inner_op)
    inner_2c = cswap(inner_op)
    inner_yc = cswap(inner_y)
    ffn_came_c = cswap(ffn_c)
    (sums, grad_branch, mid_near, mid_far), near_heads, far_heads = mid_back(
        ids, near, received, middle, [cotangent, cot_far], branch, mod, ffn_row, w_out
    )
    grad_branch, ffn_came_c, inner_yc, inner_2c, came_1c, *far_heads = fence(
        grad_branch, ffn_came_c, inner_yc, inner_2c, came_1c, *far_heads
    )
    recv_a = xswap(far_heads[0])
    recv_b = xswap(far_heads[1])
    branch_c = cswap(grad_branch)
    tile = 512
    per = units // tile
    parts_inner = weight_grads(
        att_left, [inner, inner_c, inner_y, inner_yc], False, tile, 1, units, lambda i: i
    )
    recv_a, parts_inner, branch_c, inner_2y, ffn_y, branch_op, came_op = fence(
        recv_a, parts_inner, branch_c, inner_2y, ffn_y, grad_branch, came_op
    )
    ffn_came_y = yswap(ffn_y)
    came_1y = yswap(came_op)
    inner_2yc = cswap(inner_2y)
    grad_1, grad_2 = add_pair(near_heads[0], recv_a)
    grad_3, grad_0 = add_pair(near_heads[1], after(recv_b, grad_1))
    grad_here = spread([grad_0, grad_1, grad_2, grad_3])
    parts_inner = weight_grads(
        att_left,
        [after(inner_2, grad_0), inner_2c, inner_2y, inner_2yc],
        False,
        tile,
        1,
        units,
        lambda i: i + per // 2,
        parts_inner,
    )
    parts_inner, ffn_came_y, came_1y, *grad_here = fence(
        parts_inner, ffn_came_y, came_1y, *grad_here
    )
    sum_inner = scatter(parts_inner)
    grad_here[0], kept_op, came_op, ffn_y = fence(grad_here[0], grad_kept, came_2, ffn_came_y)
    kept_y = yswap(kept_op)
    came_2y = yswap(came_op)
    came_2c = cswap(came_op)
    ffn_came_yc = cswap(ffn_y)
    came_1yc = cswap(came_1y)
    grads_q, (q_gain_part, cap_keep, cap_send, gate_part), grads_kv = attend_back(
        ids, clip_slices, caption_lengths, gates, q_here, grad_here, saved, cap_kv, gains, cosine, sine
    )
    grads_q, grads_kv, cap_send, kept_y, came_2y, came_2c, ffn_came_yc, came_1yc = fence(
        grads_q, grads_kv, cap_send, kept_y, came_2y, came_2c, ffn_came_yc, came_1yc
    )

    kv_c3 = cswap(grads_kv[3])
    kv_c1, cap_c = cswap(grads_kv[1]), cswap(cap_send)
    away = (grads_kv[2].astype(F32) + kv_c3.astype(F32)).astype(BF)
    away, kv_c1, cap_c, *grads_q = fence(away, kv_c1, cap_c, *grads_q)
    away_here = yswap(away)
    kept_yc, came_2yc = fence(kept_y, came_2y, away)[:2]
    kept_yc, came_2yc = cswap(kept_yc), cswap(came_2yc)
    kept_yc, came_2yc, *grads_q = fence(kept_yc, came_2yc, *grads_q)
    ffn_left = [(ffn_own, 0), (ffn_came_c, 0), (ffn_came_y, 0), (ffn_came_yc, 1)]
    back_q = unspread(grads_q)
    pair = cap_keep + cap_c
    parts_a = None
    for right, first_tile in (
        ([grad_kept, kept_c, kept_y, kept_yc], 0),
        ([came_1, came_1c, came_1y, came_1yc], per),
        ([came_2, came_2c, came_2y, came_2yc], per + per // 2),
    ):
        parts_a = weight_grads(
            ffn_left, right, False, tile, 0, 2 * units, lambda i, n=first_tile: i + n, parts_a
        )
    away_here, parts_a, pair, sum_inner, *back_q = fence(
        away_here, parts_a, pair, sum_inner, *back_q
    )
    back_kv, k_gain_part = keys_back(
        ids, clip_slices, grads_kv[0], kv_c1, away_here, kv_own, gains, cosine, sine
    )
    back_kv, k_gain_part, branch_op, out_op = fence(back_kv, k_gain_part, branch_op, far_out)
    branch_y = yswap(branch_op)
    out_recv = xswap(out_op)
    back_kv = unspread(back_kv)
    *back_kv, parts_a, branch_y, out_recv = fence(*back_kv, parts_a, branch_y, out_recv)
    sum_a = scatter(parts_a)

    first, second, send = fence(*pack(ids, back_q, back_kv))
    packed_recv = xswap(send)
    first_y = yswap(first)
    first_c = cswap(first)
    branch_all = [grad_branch, branch_c, branch_y, cswap(after(branch_y, first))]
    tile, total = 384, 4 * local_width
    parts_c = weight_grads(att_left, branch_all, False, tile, 0, total, lambda i: i + 6)
    cap_y = yswap(after(pick(pair, 1 - y), first))
    cap_total = pick(pair, y) + cap_y
    raw_cap, cap_gain_part = caption_back(ids, cap_total, cap_raw, gains)
    output, early = output_sums(
        ids, clip_slices, near_out, after(out_recv, first), middle, cotangent, mod, sums
    )
    packed_recv, first_y, first_c, raw_cap, cap_gain_part, second, parts_c, output = fence(
        packed_recv, first_y, first_c, raw_cap, cap_gain_part, second, parts_c, output
    )
    second_y = yswap(second)
    second_c = cswap(second)
    recv_c = cswap(packed_recv)
    first_yc = cswap(first_y)
    tok_near, tok_send = qkv_back(ids, first, packed_recv, second, w_qkv)
    mid_came = xswap(after(mid_far, packed_recv))
    tok_near, tok_send, second_y, second_c, recv_c, first_yc, recv_op, raw_cap, mid_came = fence(
        tok_near, tok_send, second_y, second_c, recv_c, first_yc, packed_recv, raw_cap, mid_came
    )
    tok_recv = xswap(tok_send)
    recv_y = yswap(recv_op)
    second_yc = cswap(second_y)
    raw_c = cswap(raw_cap)
    parts_c = weight_grads(
        hid_left, [first, first_c, first_y, first_yc], True, tile, 0, total, lambda i: i, parts_c
    )
    parts_c = weight_grads(
        hid_left, [second, second_c, second_y, second_yc], True, tile, 0, total, lambda i: i + 4, parts_c
    )
    tok_recv, parts_c, recv_y, raw_c = fence(tok_recv, parts_c, recv_y, raw_c)
    recv_yc = cswap(recv_y)
    raw_y = yswap(raw_cap)
    parts_c = weight_grads(
        hid_left, [packed_recv, recv_c, recv_y, recv_yc], True, tile, 0, total, lambda i: i + 2, parts_c
    )
    parts_c, raw_y = fence(parts_c, raw_y)
    sum_c = scatter(parts_c)
    token_grad, late = tokens_back(
        ids,
        clip_slices,
        tokens,
        tok_near,
        tok_recv,
        mid_near,
        mid_came,
        mod,
        norm_row,
        [q_gain_part, k_gain_part, cap_gain_part, gate_part, early],
    )
    raw_yc = cswap(raw_y)
    late = late + cswap(late)
    cap_parts = caption_weights(ids, [raw_cap, raw_c, raw_y, raw_yc], caption_rows)
    late_y = yswap(late)
    late_y, cap_parts = fence(late_y, cap_parts)
    late = late + late_y
    late_z = hop(late, lambda i: i ^ GROUP)
    late_z, sum_a = fence(late_z, sum_a)
    late = late + late_z
    late = late + hop(late, lambda i: i ^ (2 * GROUP))
    late, *cap_parts = fence(late, *cap_parts)
    cap_parts = unspread(cap_parts)
    late_far = xswap(late)
    came_out = xswap(sum_a[:, units:])
    late_sum = late

    mod_grad, gain_rows = finish(ids, late_sum, late_far)
    mod_mine = mod_grad.astype(BF)
    caption_w_grad = caption_join(ids, fence(*cap_parts, mod_mine)[:LINE])
    cols_local = CD // bucket_count
    act_cols = lax.dynamic_slice_in_dim(activation, b * cols_local, cols_local, 1)
    ada_grad = mm(mod_mine, act_cols, TN)
    cond_part = mm(mod_mine, ada_w, NN)
    cond_sigmoid = jax.nn.sigmoid(cond)
    cond_grad = (
        (cond_part + xswap(cond_part)) * cond_sigmoid * (1.0 + cond * (1.0 - cond_sigmoid))
    )
    heads_each = H // seq_count
    cross_out = jnp.concatenate(
        [gain_rows[5, :heads_each], gain_rows[5, local_width : local_width + heads_each]]
    )

    down_out = sum_inner.astype(F32).T
    kept_out = sum_a[:, :units].astype(F32)
    came_out = came_out.astype(F32)
    gate_up_out = jnp.where(
        s == 0,
        jnp.concatenate([kept_out, came_out], 1),
        jnp.concatenate([came_out, kept_out], 1),
    ).T
    sum_c = after(sum_c, gate_up_out)
    return (
        output,
        token_grad,
        cond_grad,
        ada_grad,
        gain_rows[0],
        sum_c[:, : 3 * local_width].astype(F32).T,
        gain_rows[1],
        gain_rows[2],
        caption_w_grad,
        gain_rows[3],
        cross_out,
        sum_c[:, 3 * local_width :].astype(F32).T,
        gain_rows[4],
        gate_up_out,
        down_out,
    )


def project(activations, weight):
    return lax.dot_general(
        activations, weight, (((1,), (1,)), ((), ())), preferred_element_type=jnp.float32
    )


def clip_of(rows, ends):
    return jnp.sum((rows[:, None] >= ends[None, :]).astype(jnp.int32), axis=1)


def head_norm(values, gains, head_count):
    row_count = values.shape[0]
    split = values.reshape(row_count, head_count, -1)
    inverse = lax.rsqrt(jnp.mean(split * split, axis=-1, keepdims=True) + EPSILON)
    unit_rows = split * inverse
    return (unit_rows.reshape(row_count, -1) * gains, unit_rows, inverse)


def head_norm_back(norm_grads, gains, unit_rows, inverse):
    row_count, head_count, head_width = unit_rows.shape
    gain_grad = jnp.sum(norm_grads * unit_rows.reshape(row_count, -1), axis=0)
    unit_grad = (norm_grads * gains).reshape(row_count, head_count, head_width)
    raw_grad = inverse * (
        unit_grad - unit_rows * jnp.mean(unit_grad * unit_rows, axis=-1, keepdims=True)
    )
    return (raw_grad.reshape(row_count, -1), gain_grad)


def rotate(values, positions, head_count):
    row_count = values.shape[0]
    split = values.reshape(row_count, head_count, -1)
    half_width = split.shape[-1] // 2
    frequency = jnp.exp(
        jnp.arange(half_width, dtype=jnp.float32) * (-2.0 * math.log(10000.0) / (2 * half_width))
    )
    angles = positions[:, None] * frequency[None, :]
    cosine = jnp.cos(angles)[:, None, :]
    sine = jnp.sin(angles)[:, None, :]
    first_half = split[..., :half_width]
    second_half = split[..., half_width:]
    turned = jnp.concatenate(
        [first_half * cosine - second_half * sine, first_half * sine + second_half * cosine],
        axis=-1,
    )
    return turned.reshape(row_count, -1)


def block_size(row_count):
    return 512 if row_count % 512 == 0 else row_count


def general_body(
    tokens,
    cotangent,
    clip_slices,
    caption_lengths,
    caption,
    cond,
    ada_w,
    norm_gain,
    w_qkv,
    q_gain,
    k_gain,
    w_caption,
    ky_gain,
    cross_gate,
    w_out,
    ffn_gain,
    w_gate_up,
    w_down,
):
    seq_count = lax.axis_size("seq")
    bucket_count = lax.axis_size("bucket")
    tok_rows = tokens.shape[0]
    slice_rows = tok_rows * seq_count
    total_rows = slice_rows * bucket_count
    local_heads = H // seq_count
    local_width = local_heads * HD
    score_scale = HD ** (-0.5)
    bucket_id = lax.axis_index("bucket")
    seq_id = lax.axis_index("seq")
    ends = jnp.cumsum(clip_slices) * slice_rows
    starts = ends - clip_slices * slice_rows
    my_clip = clip_of(jnp.reshape(bucket_id * slice_rows, (1,)), ends)[0]
    clip_mask = jnp.arange(CLIPS) == my_clip
    clip_start = jnp.sum(jnp.where(clip_mask, starts, 0))
    first_token = (bucket_id * seq_count + seq_id) * tok_rows
    positions = (first_token + jnp.arange(tok_rows, dtype=jnp.int32) - clip_start).astype(
        jnp.float32
    )
    caption_usable = jnp.arange(CAP) < jnp.sum(jnp.where(clip_mask, caption_lengths, 0))
    head_first = seq_id * local_width
    gates_local = jnp.tanh(lax.dynamic_slice_in_dim(cross_gate, seq_id * local_heads, local_heads))
    ky_gain_local = lax.dynamic_slice_in_dim(ky_gain, head_first, local_width)
    activation = jax.nn.silu(cond).astype(jnp.bfloat16)
    cond_row = lax.dynamic_index_in_dim(activation, my_clip, 0, True)
    caption_rows = lax.dynamic_index_in_dim(caption, my_clip, 0, False)
    caption_raw = jnp.einsum(
        "ty,jdy->jtd", caption_rows, w_caption, preferred_element_type=jnp.float32
    )
    caption_norm, caption_unit, caption_inverse = head_norm(
        caption_raw[0], ky_gain_local, local_heads
    )
    caption_keys = caption_norm.astype(jnp.bfloat16).reshape(CAP, local_heads, HD)
    caption_values = caption_raw[1].astype(jnp.bfloat16).reshape(CAP, local_heads, HD)
    inputs = tokens.astype(jnp.float32)

    def key_usable(first_row, row_count):
        return clip_of(first_row + jnp.arange(row_count, dtype=jnp.int32), ends) == my_clip

    def fold_keys(queries3, running, segment, first_row):
        seg_keys, seg_values = segment
        row_count = seg_keys.shape[0]
        key_rows = block_size(row_count)
        steps_count = row_count // key_rows
        usable = key_usable(first_row, row_count).reshape(steps_count, key_rows)
        key_blocks = seg_keys.reshape(steps_count, key_rows, local_heads, HD)
        value_blocks = seg_values.reshape(steps_count, key_rows, local_heads, HD)

        def update(state, item):
            key_block, value_block, usable_block = item

            def update_include(inner):
                row_max, row_total, accum = inner
                scores = (
                    jnp.einsum(
                        "qhd,khd->hqk", queries3, key_block, preferred_element_type=jnp.float32
                    )
                    * score_scale
                )
                scores = jnp.where(usable_block[None, None, :], scores, MASKED)
                new_max = jnp.maximum(row_max, jnp.max(scores, axis=-1))
                factor = jnp.exp(row_max - new_max)
                weights = jnp.exp(scores - new_max[..., None])
                row_total = row_total * factor + jnp.sum(weights, axis=-1)
                accum = accum * factor.T[:, :, None] + jnp.einsum(
                    "hqk,khd->qhd",
                    weights.astype(jnp.bfloat16),
                    value_block,
                    preferred_element_type=jnp.float32,
                )
                return (new_max, row_total, accum)

            return (
                lax.cond(jnp.any(usable_block), update_include, lambda inner: inner, state),
                None,
            )

        running, unused = lax.scan(update, running, (key_blocks, value_blocks, usable))
        return running

    def local_fold(queries3, running, keys_whole):

        def local_visit(state, piece_index):
            first_row = piece_index * slice_rows
            segment = (
                lax.dynamic_slice_in_dim(keys_whole[0], first_row, slice_rows, 0),
                lax.dynamic_slice_in_dim(keys_whole[1], first_row, slice_rows, 0),
            )
            return (fold_keys(queries3, state, segment, first_row), None)

        running, unused = lax.scan(local_visit, running, jnp.arange(bucket_count, dtype=jnp.int32))
        return running

    def forward(qkv_full, out_full, modulation, second):
        shift_vec = modulation[:D]
        scale_vec = modulation[D : 2 * D]
        gate_vec = modulation[2 * D : 3 * D]
        inverse = lax.rsqrt(jnp.mean(inputs * inputs, axis=-1, keepdims=True) + EPSILON)
        unit_rows = inputs * inverse
        hidden = (unit_rows * norm_gain * (1.0 + scale_vec) + shift_vec).astype(jnp.bfloat16)
        projected = project(hidden, qkv_full)
        query_norm, query_unit, query_inverse = head_norm(projected[:, :D], q_gain, H)
        key_norm, key_unit, key_inverse = head_norm(projected[:, D : 2 * D], k_gain, H)
        queries = rotate(query_norm, positions, H).astype(jnp.bfloat16)
        keys_tok = rotate(key_norm, positions, H).astype(jnp.bfloat16)
        values_tok = projected[:, 2 * D :].astype(jnp.bfloat16)
        head_queries, head_keys, head_values = (
            lax.all_to_all(queries, "seq", split_axis=1, concat_axis=0, tiled=True),
            lax.all_to_all(keys_tok, "seq", split_axis=1, concat_axis=0, tiled=True),
            lax.all_to_all(values_tok, "seq", split_axis=1, concat_axis=0, tiled=True),
        )
        queries3 = head_queries.reshape(slice_rows, local_heads, HD)
        start_state = (
            jnp.full((local_heads, slice_rows), MASKED, jnp.float32),
            jnp.zeros((local_heads, slice_rows), jnp.float32),
            jnp.zeros((slice_rows, local_heads, HD), jnp.float32),
        )
        folder = functools.partial(fold_keys, queries3)
        if second:
            keys_whole = (
                lax.all_gather(head_keys, "bucket", axis=0, tiled=True),
                lax.all_gather(head_values, "bucket", axis=0, tiled=True),
            )
            final_state = local_fold(queries3, start_state, keys_whole)
        else:
            keys_whole = None
            final_state = folder(
                start_state,
                (
                    lax.all_gather(head_keys, "bucket", axis=0, tiled=True),
                    lax.all_gather(head_values, "bucket", axis=0, tiled=True),
                ),
                jnp.int32(0),
            )
        row_max, row_total, accum = final_state
        own = accum / row_total.T[:, :, None]
        cross_scores = (
            jnp.einsum("qhd,khd->hqk", queries3, caption_keys, preferred_element_type=jnp.float32)
            * score_scale
        )
        cross_prob = jax.nn.softmax(
            jnp.where(caption_usable[None, None, :], cross_scores, MASKED), axis=-1
        )
        other = jnp.einsum(
            "hqk,khd->qhd",
            cross_prob.astype(jnp.bfloat16),
            caption_values,
            preferred_element_type=jnp.float32,
        )
        combined = (
            (own + gates_local[None, :, None] * other)
            .reshape(slice_rows, local_width)
            .astype(jnp.bfloat16)
        )
        attention = lax.all_to_all(combined, "seq", split_axis=0, concat_axis=1, tiled=True)
        branch = project(attention, out_full)
        return dict(
            gate_vec=gate_vec,
            scale_vec=scale_vec,
            inverse=inverse,
            unit_rows=unit_rows,
            hidden=hidden,
            query_unit=query_unit,
            query_inverse=query_inverse,
            key_unit=key_unit,
            key_inverse=key_inverse,
            queries3=queries3,
            own_keys3=head_keys.reshape(slice_rows, local_heads, HD),
            own_values3=head_values.reshape(slice_rows, local_heads, HD),
            keys_whole=keys_whole,
            row_log=row_max + jnp.log(row_total),
            own=own,
            other=other,
            cross_prob=cross_prob,
            attention=attention,
            branch=branch,
            output=inputs + gate_vec * branch,
        )

    gathered = (
        lax.all_gather(ada_w, "seq", axis=0, tiled=True),
        lax.all_gather(w_qkv, "seq", axis=0, tiled=True),
        lax.all_gather(w_out, "seq", axis=0, tiled=True),
        lax.all_gather(w_gate_up, "seq", axis=0, tiled=True),
        lax.all_gather(w_down, "seq", axis=0, tiled=True),
    )
    modulation = project(cond_row, gathered[0])[0]
    first_pass = forward(gathered[1], gathered[2], modulation, False)
    middle = first_pass["output"]
    shift_mlp = modulation[3 * D : 4 * D]
    scale_mlp = modulation[4 * D : 5 * D]
    gate_mlp = modulation[5 * D :]
    mid_inverse = lax.rsqrt(jnp.mean(middle * middle, axis=-1, keepdims=True) + EPSILON)
    mid_unit = middle * mid_inverse
    mlp_in = (mid_unit * ffn_gain * (1.0 + scale_mlp) + shift_mlp).astype(jnp.bfloat16)
    gate_up = project(mlp_in, gathered[3])
    gate_half = gate_up[:, :FF]
    up_half = gate_up[:, FF:]
    gate_sigmoid = jax.nn.sigmoid(gate_half)
    silu_gate = gate_half * gate_sigmoid
    inner = (silu_gate * up_half).astype(jnp.bfloat16)
    mlp_branch = jnp.dot(inner, gathered[4], preferred_element_type=jnp.float32)
    output = (middle + gate_mlp * mlp_branch).astype(jnp.bfloat16)
    regathered = (
        lax.all_gather(ada_w, "seq", axis=0, tiled=True),
        lax.all_gather(w_qkv, "seq", axis=0, tiled=True),
        lax.all_gather(w_out, "seq", axis=0, tiled=True),
        lax.all_gather(w_gate_up, "seq", axis=0, tiled=True),
        lax.all_gather(w_down, "seq", axis=0, tiled=True),
    )
    second_pass = forward(regathered[1], regathered[2], modulation, True)
    ada_full, qkv_full, out_full, gate_up_full, down_full = regathered
    grad_out = cotangent.astype(jnp.float32)
    mlp_gate_grad = jnp.sum(grad_out * mlp_branch, axis=0)
    grad_mlp = (grad_out * gate_mlp).astype(jnp.bfloat16)
    grad_inner = lax.dot_general(
        grad_mlp, down_full, (((1,), (1,)), ((), ())), preferred_element_type=jnp.float32
    )
    grad_gate_half = grad_inner * up_half * gate_sigmoid * (1.0 + gate_half * (1.0 - gate_sigmoid))
    grad_up_half = grad_inner * silu_gate
    grad_gate_up = jnp.concatenate([grad_gate_half, grad_up_half], axis=1).astype(jnp.bfloat16)
    mlp_in_grad = jnp.dot(grad_gate_up, gate_up_full, preferred_element_type=jnp.float32)
    ffn_gain_grad = jnp.sum(mlp_in_grad * (1.0 + scale_mlp) * mid_unit, axis=0)
    shift_mlp_grad = jnp.sum(mlp_in_grad, axis=0)
    scale_mlp_grad = jnp.sum(mlp_in_grad * mid_unit * ffn_gain, axis=0)
    mid_unit_grad = mlp_in_grad * ffn_gain * (1.0 + scale_mlp)
    residual_grad = (
        mid_inverse
        * (mid_unit_grad - mid_unit * jnp.mean(mid_unit_grad * mid_unit, axis=-1, keepdims=True))
        + grad_out
    )
    gate_grad = jnp.sum(residual_grad * second_pass["branch"], axis=0)
    grad_branch = (residual_grad * second_pass["gate_vec"]).astype(jnp.bfloat16)
    attention = second_pass["attention"]
    grad_attention = jnp.dot(grad_branch, out_full, preferred_element_type=jnp.float32).astype(
        jnp.bfloat16
    )
    grad_heads = lax.all_to_all(grad_attention, "seq", split_axis=1, concat_axis=0, tiled=True)
    grad_own16 = grad_heads.reshape(slice_rows, local_heads, HD)
    grad_own = grad_own16.astype(jnp.float32)
    queries3 = second_pass["queries3"]
    own = second_pass["own"]
    other = second_pass["other"]
    cross_prob = second_pass["cross_prob"]
    grad_other = (grad_own * gates_local[None, :, None]).astype(jnp.bfloat16)
    gate_grad_local = jnp.sum(grad_own * other, axis=(0, 2)) * (1.0 - gates_local * gates_local)
    grad_cross_prob = jnp.einsum(
        "qhd,khd->hqk", grad_other, caption_values, preferred_element_type=jnp.float32
    )
    grad_cross = (
        cross_prob
        * (grad_cross_prob - jnp.sum(cross_prob * grad_cross_prob, axis=-1, keepdims=True))
    ).astype(jnp.bfloat16)
    cross_query_grad = score_scale * jnp.einsum(
        "hqk,khd->qhd", grad_cross, caption_keys, preferred_element_type=jnp.float32
    )
    caption_key_grad = score_scale * jnp.einsum(
        "hqk,qhd->khd", grad_cross, queries3, preferred_element_type=jnp.float32
    )
    caption_value_grad = jnp.einsum(
        "hqk,qhd->khd",
        cross_prob.astype(jnp.bfloat16),
        grad_other,
        preferred_element_type=jnp.float32,
    )
    row_delta = jnp.sum(grad_own * own, axis=-1).T
    row_log = second_pass["row_log"]
    keys_whole = second_pass["keys_whole"]

    def grad_piece(query_grad, piece_index, with_keys):
        first_row = piece_index * slice_rows
        key_rows = block_size(slice_rows)
        steps_count = slice_rows // key_rows
        key_blocks = lax.dynamic_slice_in_dim(keys_whole[0], first_row, slice_rows, 0).reshape(
            steps_count, key_rows, local_heads, HD
        )
        value_blocks = lax.dynamic_slice_in_dim(keys_whole[1], first_row, slice_rows, 0).reshape(
            steps_count, key_rows, local_heads, HD
        )
        usable = key_usable(first_row, slice_rows).reshape(steps_count, key_rows)

        def grad_visit(accum, item):
            key_block, value_block, usable_block = item

            def grad_include(inner):
                scores = (
                    jnp.einsum(
                        "qhd,khd->hqk", queries3, key_block, preferred_element_type=jnp.float32
                    )
                    * score_scale
                )
                scores = jnp.where(usable_block[None, None, :], scores, MASKED)
                probability = jnp.exp(scores - row_log[..., None])
                grad_prob = jnp.einsum(
                    "qhd,khd->hqk", grad_own16, value_block, preferred_element_type=jnp.float32
                )
                grad_scores = (probability * (grad_prob - row_delta[..., None])).astype(
                    jnp.bfloat16
                )
                updated = inner + score_scale * jnp.einsum(
                    "hqk,khd->qhd", grad_scores, key_block, preferred_element_type=jnp.float32
                )
                key_grad = score_scale * jnp.einsum(
                    "hqk,qhd->khd", grad_scores, queries3, preferred_element_type=jnp.float32
                )
                value_grad = jnp.einsum(
                    "hqk,qhd->khd",
                    probability.astype(jnp.bfloat16),
                    grad_own16,
                    preferred_element_type=jnp.float32,
                )
                return (updated, key_grad, value_grad)

            def skip(inner):
                empty = jnp.zeros((key_rows, local_heads, HD), jnp.float32)
                return (inner, empty, empty)

            updated, key_grad, value_grad = lax.cond(
                jnp.any(usable_block), grad_include, skip, accum
            )
            return (updated, (key_grad, value_grad))

        query_grad, (key_grads, value_grads) = lax.scan(
            grad_visit, query_grad, (key_blocks, value_blocks, usable)
        )
        return (
            query_grad,
            (
                key_grads.reshape(slice_rows, local_width),
                value_grads.reshape(slice_rows, local_width),
            ),
        )

    query_start = jnp.zeros((slice_rows, local_heads, HD), jnp.float32)
    piece_order = jnp.arange(bucket_count, dtype=jnp.int32)
    self_query_grad, (key_terms, value_terms) = lax.scan(
        functools.partial(grad_piece, with_keys=True), query_start, piece_order
    )
    key_sum, value_sum = (
        lax.psum_scatter(
            key_terms.reshape(total_rows, local_width).astype(jnp.bfloat16),
            "bucket",
            scatter_dimension=0,
            tiled=True,
        ).astype(jnp.float32),
        lax.psum_scatter(
            value_terms.reshape(total_rows, local_width).astype(jnp.bfloat16),
            "bucket",
            scatter_dimension=0,
            tiled=True,
        ).astype(jnp.float32),
    )
    query_grad16 = (
        (self_query_grad + cross_query_grad).reshape(slice_rows, local_width).astype(jnp.bfloat16)
    )
    tok_query_grad, tok_key_grad, tok_value_grad = (
        lax.all_to_all(query_grad16, "seq", split_axis=0, concat_axis=1, tiled=True),
        lax.all_to_all(
            key_sum.astype(jnp.bfloat16), "seq", split_axis=0, concat_axis=1, tiled=True
        ),
        lax.all_to_all(
            value_sum.astype(jnp.bfloat16), "seq", split_axis=0, concat_axis=1, tiled=True
        ),
    )
    query_raw_grad, q_gain_grad = head_norm_back(
        rotate(tok_query_grad.astype(jnp.float32), -positions, H),
        q_gain,
        second_pass["query_unit"],
        second_pass["query_inverse"],
    )
    key_raw_grad, k_gain_grad = head_norm_back(
        rotate(tok_key_grad.astype(jnp.float32), -positions, H),
        k_gain,
        second_pass["key_unit"],
        second_pass["key_inverse"],
    )
    projected_grad = jnp.concatenate(
        [query_raw_grad, key_raw_grad, tok_value_grad.astype(jnp.float32)], axis=1
    ).astype(jnp.bfloat16)
    hidden = second_pass["hidden"]
    out_each = D // seq_count
    qkv_each = 3 * D // seq_count
    gate_up_each = 2 * FF // seq_count
    down_each = FF // seq_count
    rows_each = out_each + qkv_each + gate_up_each + down_each
    device_count = rows_each * lax.axis_size("seq") // rows_each
    first_device = jnp.int32(0) // rows_each

    def part(operand, partner, each):
        picked = lax.dynamic_slice_in_dim(operand, first_device * each, device_count * each, 1)
        term = lax.dot_general(
            picked, partner, (((0,), (0,)), ((), ())), preferred_element_type=jnp.float32
        )
        return term.reshape(device_count, each, D)

    terms = [
        part(grad_branch, attention, out_each),
        part(projected_grad, hidden, qkv_each),
        part(grad_gate_up, mlp_in, gate_up_each),
        part(inner, grad_mlp, down_each),
    ]
    weight_grad_seq = lax.psum_scatter(
        jnp.concatenate(terms, axis=1)
        .reshape(rows_each * lax.axis_size("seq"), D)
        .astype(jnp.bfloat16),
        "seq",
        scatter_dimension=0,
        tiled=True,
    )
    hidden_grad = jnp.dot(projected_grad, qkv_full, preferred_element_type=jnp.float32)
    unit_rows = second_pass["unit_rows"]
    scale_vec = second_pass["scale_vec"]
    inverse = second_pass["inverse"]
    norm_gain_grad = jnp.sum(hidden_grad * (1.0 + scale_vec) * unit_rows, axis=0)
    shift_grad = jnp.sum(hidden_grad, axis=0)
    scale_grad = jnp.sum(hidden_grad * unit_rows * norm_gain, axis=0)
    unit_grad = hidden_grad * norm_gain * (1.0 + scale_vec)
    token_grad = (
        inverse * (unit_grad - unit_rows * jnp.mean(unit_grad * unit_rows, axis=-1, keepdims=True))
        + residual_grad
    )
    modulation_grad = jnp.where(
        clip_mask[:, None],
        jnp.concatenate(
            [shift_grad, scale_grad, gate_grad, shift_mlp_grad, scale_mlp_grad, mlp_gate_grad]
        )[None, :],
        0.0,
    )
    ky_gain_part = jnp.sum(
        caption_key_grad.reshape(CAP, local_width) * caption_unit.reshape(CAP, local_width), axis=0
    )
    ky_gain_full = lax.dynamic_update_slice_in_dim(
        jnp.zeros((D,), jnp.float32), ky_gain_part, head_first, 0
    )
    gate_full = lax.dynamic_update_slice_in_dim(
        jnp.zeros((H,), jnp.float32), gate_grad_local, seq_id * local_heads, 0
    )
    caption_part = jnp.stack(
        [caption_key_grad.reshape(CAP, local_width), caption_value_grad.reshape(CAP, local_width)]
    )[None]
    zero_index = jnp.zeros((), jnp.int32)
    caption_full = lax.dynamic_update_slice(
        jnp.zeros((CLIPS, 2, CAP, D), jnp.float32),
        caption_part,
        (my_clip, zero_index, zero_index, head_first),
    )
    reduced = lax.psum(
        (
            norm_gain_grad,
            q_gain_grad,
            k_gain_grad,
            ky_gain_full,
            gate_full,
            modulation_grad,
            caption_full,
            ffn_gain_grad,
        ),
        ("bucket", "seq"),
    )
    modulation_total = reduced[5].astype(jnp.bfloat16)
    rows_local = 6 * D // seq_count
    cols_local = CD // bucket_count
    ada_grad = lax.dot_general(
        lax.dynamic_slice_in_dim(modulation_total, seq_id * rows_local, rows_local, 1),
        lax.dynamic_slice_in_dim(activation, bucket_id * cols_local, cols_local, 1),
        (((0,), (0,)), ((), ())),
        preferred_element_type=jnp.float32,
    )
    cond_sigmoid = jax.nn.sigmoid(cond)
    cond_grad = (
        jnp.dot(modulation_total, ada_full, preferred_element_type=jnp.float32)
        * cond_sigmoid
        * (1.0 + cond * (1.0 - cond_sigmoid))
    )
    caption_total = lax.dynamic_slice_in_dim(reduced[6], head_first, local_width, 3)
    raw_keys_all = jnp.einsum(
        "cty,dy->ctd", caption, w_caption[0], preferred_element_type=jnp.float32
    ).reshape(CLIPS * CAP, local_width)
    ignored, unit_all, inverse_all = head_norm(raw_keys_all, ky_gain_local, local_heads)
    raw_key_grad, unused_gain = head_norm_back(
        caption_total[:, 0].reshape(CLIPS * CAP, local_width), ky_gain_local, unit_all, inverse_all
    )
    raw_grad = jnp.stack(
        [raw_key_grad.reshape(CLIPS, CAP, local_width), caption_total[:, 1]], axis=1
    ).astype(jnp.bfloat16)
    caption_cols = lax.dynamic_slice_in_dim(
        caption, bucket_id * (YD // bucket_count), YD // bucket_count, 2
    )
    caption_w_grad = jnp.einsum(
        "cjtd,cty->jdy", raw_grad, caption_cols, preferred_element_type=jnp.float32
    )
    combined_grads = lax.psum_scatter(
        weight_grad_seq, "bucket", scatter_dimension=1, tiled=True
    ).astype(jnp.float32)
    out_grad_out = combined_grads[:out_each]
    qkv_grad_out = combined_grads[out_each : out_each + qkv_each]
    gate_up_grad_out = combined_grads[out_each + qkv_each : out_each + qkv_each + gate_up_each]
    down_grad_out = combined_grads[out_each + qkv_each + gate_up_each :]
    return (
        output,
        token_grad,
        cond_grad,
        ada_grad,
        reduced[0],
        qkv_grad_out,
        reduced[1],
        reduced[2],
        caption_w_grad,
        reduced[3],
        reduced[4],
        out_grad_out,
        reduced[7],
        gate_up_grad_out,
        down_grad_out,
    )


def solution(mesh):
    fits = mesh.shape["seq"] == 2 and mesh.shape["bucket"] == LINE * GROUP
    bucket = ("bucket",)
    if fits:
        bucket = BUCKET
        mesh = Mesh(mesh.devices.reshape(LINE, 2, GROUP // 2, 2), (*BUCKET, "seq"))
    in_specs = (
        P((*bucket, "seq"), None),
        P((*bucket, "seq"), None),
        P(),
        P(),
        P(),
        P(),
        P("seq", None),
        P(),
        P("seq", None),
        P(),
        P(),
        P(None, "seq", None),
        P(),
        P(),
        P("seq", None),
        P(),
        P("seq", None),
        P("seq", None),
    )
    out_specs = (
        P((*bucket, "seq"), None),
        P((*bucket, "seq"), None),
        P(),
        P("seq", bucket),
        P(),
        P("seq", bucket),
        P(),
        P(),
        P(None, "seq", bucket),
        P(),
        P(),
        P("seq", bucket),
        P(),
        P("seq", bucket),
        P("seq", bucket),
    )
    body = fast_body if fits else general_body
    return jax.shard_map(body, mesh=mesh, in_specs=in_specs, out_specs=out_specs, check_vma=False)
```

```python
import functools
import math

import jax
import jax.numpy as jnp
from jax import lax
from jax.experimental import pallas as pl
from jax.experimental.pallas import tpu as pltpu
from jax.sharding import Mesh, PartitionSpec as P

H = 24
HD = 64
D = 1536
FF = 4096
YD = 4096
CD = 1024
CAP = 128
CLIPS = 4

EPSILON = 1e-06
MASKED = -1e30
BF = jnp.bfloat16
F32 = jnp.float32
NN = (((1,), (0,)), ((), ()))
NT = (((1,), (1,)), ((), ()))
TN = (((0,), (0,)), ((), ()))
GROUP = 4
LINE = 4
BUCKET = ("z", "y", "c")
SENDS = (1, 2, 3, 0)
SMEM = pl.BlockSpec(memory_space=pltpu.SMEM)
VMEM = pl.BlockSpec(memory_space=pltpu.VMEM)
shape = jax.ShapeDtypeStruct


def cost(microseconds):
    return pl.CostEstimate(
        flops=0, transcendentals=0, bytes_accessed=int(microseconds * 20_000)
    )


def mm(a, b, dims):
    return lax.dot_general(a, b, dims, preferred_element_type=F32)


def clip_at(slices, slot):
    ends = [slices[0]]
    for i in range(1, CLIPS):
        ends.append(ends[-1] + slices[i])
    clip = jnp.int32(0)
    first, last = jnp.int32(0), ends[0]
    for i in range(CLIPS - 1):
        later = slot >= ends[i]
        clip = jnp.where(later, i + 1, clip)
        first = jnp.where(later, ends[i], first)
        last = jnp.where(later, ends[i + 1], last)
    return clip, first, last


def slot_of(bucket, k, j):
    return lax.rem(bucket // GROUP - k + LINE, LINE) * GROUP + jnp.bitwise_xor(
        lax.rem(bucket, GROUP), j
    )


def chunk_at(bucket, k, width):
    return pl.multiple_of(lax.rem(bucket // GROUP + k, LINE) * width, HD)


def norm_rope(raw, gain, cosine, sine):
    inverse = lax.rsqrt(jnp.mean(raw * raw, axis=0, keepdims=True) + EPSILON)
    normed = raw * inverse * gain
    half = raw.shape[0] // 2
    first, second = normed[:half], normed[half:]
    return jnp.concatenate(
        [first * cosine - second * sine, first * sine + second * cosine], axis=0
    )


def norm_rope_back(grad, raw, gain, cosine, sine):
    inverse = lax.rsqrt(jnp.mean(raw * raw, axis=0, keepdims=True) + EPSILON)
    unit = raw * inverse
    half = raw.shape[0] // 2
    first, second = grad[:half], grad[half:]
    turned = jnp.concatenate(
        [first * cosine + second * sine, second * cosine - first * sine], axis=0
    )
    gain_grad = jnp.sum(turned * unit, axis=1, keepdims=True)
    unit_grad = turned * gain
    raw_grad = inverse * (unit_grad - unit * jnp.mean(unit_grad * unit, axis=0, keepdims=True))
    return raw_grad, gain_grad


def row_inverse(values):
    return lax.rsqrt(jnp.mean(values * values, axis=-1, keepdims=True) + EPSILON)


def pre_kernel(ids, slices, tok_a, tok_b, mod_a, mod_b, gain_ref, w_ref, p_ref, hid_ref, mod_ref):
    @pl.when(pl.program_id(0) == 0)
    def _():
        s = ids[1]
        clip, _, _ = clip_at(slices, ids[0])
        row_a, row_b = mod_a[pl.ds(clip, 1), :], mod_b[pl.ds(clip, 1), :]
        low, high = jnp.where(s == 0, row_a, row_b), jnp.where(s == 0, row_b, row_a)
        mod_ref[...] = jnp.zeros_like(mod_ref)
        for i in range(3):
            mod_ref[i : i + 1, :] = low[:, i * D : (i + 1) * D]
            mod_ref[3 + i : 4 + i, :] = high[:, i * D : (i + 1) * D]
        shift, scale = mod_ref[0:1, :], mod_ref[1:2, :]
        count = tok_a.shape[0]
        for place, ref in ((s, tok_a), (1 - s, tok_b)):
            values = ref[...].astype(F32)
            hidden = values * row_inverse(values) * gain_ref[...] * (1.0 + scale) + shift
            hid_ref[pl.ds(pl.multiple_of(place * count, count), count), :] = hidden.astype(BF)

    p_ref[...] = mm(w_ref[...], hid_ref[...], NT).astype(BF)


def pre(ids, slices, tok_a, tok_b, mod_a, mod_b, gain, w_qkv):
    rows = 2 * tok_a.shape[0]
    tile = w_qkv.shape[0] // 3
    full = lambda v: pl.BlockSpec(v.shape, lambda i: (0,) * v.ndim)
    return pl.pallas_call(
        pre_kernel,
        grid=(w_qkv.shape[0] // tile,),
        in_specs=[SMEM, SMEM]
        + [full(v) for v in (tok_a, tok_b, mod_a, mod_b, gain)]
        + [pl.BlockSpec((tile, D), lambda i: (i, 0))],
        out_specs=[
            pl.BlockSpec((tile, rows), lambda i: (i, 0)),
            pl.BlockSpec((rows, D), lambda i: (0, 0)),
            pl.BlockSpec((8, D), lambda i: (0, 0)),
        ],
        out_shape=[shape((w_qkv.shape[0], rows), BF), shape((rows, D), BF), shape((8, D), F32)],
        name="pre",
        cost_estimate=cost(6),
    )(ids, slices, tok_a, tok_b, mod_a, mod_b, gain, w_qkv)


def route_kernel(ids, p_ref, r_ref, *outs):
    b, s = ids[0], ids[1]
    local = r_ref.shape[0]
    width = local // LINE
    for k in range(LINE):
        at = chunk_at(b, k, width)
        kv_ref, q_ref = outs[k], outs[LINE + k]

        @pl.when(s == 0)
        def _():
            q_ref[...] = p_ref[pl.ds(at, width), :]
            kv_ref[:width, :] = p_ref[pl.ds(2 * local + at, width), :]
            kv_ref[width:, :] = r_ref[pl.ds(at, width), :]

        @pl.when(s == 1)
        def _():
            q_ref[...] = r_ref[pl.ds(at, width), :]
            kv_ref[:width, :] = p_ref[pl.ds(at, width), :]
            kv_ref[width:, :] = p_ref[pl.ds(2 * local + at, width), :]


def route(ids, projected, received):
    local, rows = received.shape
    width = local // LINE
    outs = pl.pallas_call(
        route_kernel,
        in_specs=[SMEM, VMEM, VMEM],
        out_specs=[VMEM] * (2 * LINE),
        out_shape=[shape((2 * width, rows), BF)] * LINE + [shape((width, rows), BF)] * LINE,
        name="route",
        cost_estimate=cost(2.5),
    )(ids, projected, received)
    return outs[:LINE], outs[LINE:]


def caption_kernel(ids, w_ref, cap_ref, gains_ref, raw_ref, kv_ref):
    step = pl.program_id(0)
    width = w_ref.shape[1]

    @pl.when(step == 0)
    def _():
        raw_ref[...] = jnp.zeros_like(raw_ref)

    for j in range(2):
        raw_ref[j * width : (j + 1) * width, :] += mm(w_ref[j], cap_ref[...], NT)

    @pl.when(step == pl.num_programs(0) - 1)
    def _():
        base = ids[1] * LINE * width + ids[0] // GROUP * width
        for h in range(width // HD):
            at = slice(h * HD, h * HD + HD)
            raw = raw_ref[at, :]
            inverse = lax.rsqrt(jnp.mean(raw * raw, axis=0, keepdims=True) + EPSILON)
            gain = gains_ref[pl.ds(pl.multiple_of(base + h * HD, HD), HD), 2:3]
            keys = (raw * inverse * gain).astype(BF)
            for c in range(CLIPS):
                kv_ref[c, at, :] = keys[:, c * CAP : (c + 1) * CAP]
        for c in range(CLIPS):
            kv_ref[c, width:, :] = raw_ref[width:, c * CAP : (c + 1) * CAP].astype(BF)


def caption_keys(ids, w_caption, caption, gains):
    width = w_caption.shape[1] // LINE
    tile = 1024
    count = caption.shape[0]
    return pl.pallas_call(
        caption_kernel,
        grid_spec=pltpu.PrefetchScalarGridSpec(
            num_scalar_prefetch=1,
            grid=(YD // tile,),
            in_specs=[
                pl.BlockSpec((2, width, tile), lambda i, ids: (0, ids[0] // GROUP, i)),
                pl.BlockSpec((count, tile), lambda i, ids: (0, i)),
                pl.BlockSpec(gains.shape, lambda i, ids: (0, 0)),
            ],
            out_specs=[
                pl.BlockSpec((2 * width, count), lambda i, ids: (0, 0)),
                pl.BlockSpec((CLIPS, 2 * width, CAP), lambda i, ids: (0, 0, 0)),
            ],
        ),
        out_shape=[shape((2 * width, count), F32), shape((CLIPS, 2 * width, CAP), BF)],
        name="caption_keys",
        cost_estimate=cost(8),
    )(ids, w_caption, caption, gains)


def attend_kernel(ids, slices, lengths, gates, *refs):
    q_refs = refs[:LINE]
    kv_refs = refs[LINE : LINE + GROUP]
    cap_ref, gains_ref, cos_ref, sin_ref = refs[LINE + GROUP : LINE + GROUP + 4]
    outs = refs[LINE + GROUP + 4 :]
    comb_refs = outs[:LINE]
    own_ref, other_ref, stat_ref, qs_ref, ks_ref, pair_ref = outs[LINE : LINE + 6]
    value_ref, cap_value_ref, sum_ref = outs[LINE + 6 :]
    b, s = ids[0], ids[1]
    width, rows = q_refs[0].shape
    heads = width // HD
    scale = HD**-0.5
    base = s * LINE * width + b // GROUP * width

    def gain_of(h, column):
        return gains_ref[pl.ds(pl.multiple_of(base + h * HD, HD), HD), column : column + 1]

    key_gains = [gain_of(h, 1) for h in range(heads)]
    query_gains = [gain_of(h, 0) for h in range(heads)]
    is_one = lax.broadcasted_iota(jnp.int32, (rows, 2 * HD), 1) < HD
    for j, kv_ref in enumerate(kv_refs):
        for k in range(LINE):
            slot = slot_of(b, k, j)
            _, start, _ = clip_at(slices, slot)
            cosine, sine = cos_ref[slot - start], sin_ref[slot - start]
            for h in range(heads):
                at = slice(h * HD, h * HD + HD)
                raw = kv_ref[k, at, :].astype(F32)
                keys = norm_rope(raw, key_gains[h], cosine, sine)
                values = kv_ref[k, width + h * HD : width + h * HD + HD, :].astype(F32)
                ks_ref[slot, at, :] = keys.astype(BF)
                pair = jnp.concatenate([keys, values], axis=0).T
                pair_ref[slot, h] = pair.astype(BF)
                value_ref[slot, h] = jnp.where(is_one, 1.0, pair).astype(BF)
    cap_one = is_one[:CAP]
    for c in range(CLIPS):
        for h in range(heads):
            values = cap_ref[c, width + h * HD : width + h * HD + HD, :].astype(F32)
            both = jnp.concatenate([values, values], axis=0).T
            cap_value_ref[c, h] = jnp.where(cap_one, 1.0, both).astype(BF)

    for i in range(LINE):
        slot = slot_of(b, i, 0)
        clip, first, last = clip_at(slices, slot)
        cosine, sine = cos_ref[slot - first], sin_ref[slot - first]
        queries = []
        for h in range(heads):
            at = slice(h * HD, h * HD + HD)
            raw = q_refs[i][at, :].astype(F32)
            turned = norm_rope(raw, query_gains[h], cosine, sine).astype(BF).astype(F32) * scale
            qs_ref[i, at, :] = turned.astype(BF)
            queries.append(turned.T.astype(BF))
        sum_ref[...] = jnp.zeros_like(sum_ref)

        def step(n, carry):
            for h in range(heads):
                at = slice(h * HD, h * HD + HD)
                weights = jnp.exp(mm(queries[h], ks_ref[n, at, :], NN))
                sum_ref[h] += mm(weights.astype(BF), value_ref[n, h], NN)
            return carry

        lax.fori_loop(first, last, step, 0)
        usable = lax.broadcasted_iota(jnp.int32, (rows, CAP), 1) < lengths[clip]
        for h in range(heads):
            at = slice(h * HD, h * HD + HD)
            total = sum_ref[h].T
            inverse = 1.0 / total[0:1]
            own = total[HD:] * inverse
            weights = jnp.where(usable, jnp.exp(mm(queries[h], cap_ref[clip, at, :], NN)), 0.0)
            cap_total = mm(weights.astype(BF), cap_value_ref[clip, h], NN).T
            cap_inverse = 1.0 / cap_total[0:1]
            other = cap_total[HD:] * cap_inverse
            own_ref[i, at, :] = own
            other_ref[i, at, :] = other
            gate = gates[(s * LINE + b // GROUP) * heads + h]
            comb_refs[i][at, :] = (own + gate * other).astype(BF)
            stat_ref[i, h : h + 1, :] = inverse
            stat_ref[i, 4 + h : 5 + h, :] = cap_inverse


def attend(ids, slices, lengths, gates, queries, kv_pieces, cap_kv, gains, cosine, sine):
    width, rows = queries[0].shape
    slots = LINE * GROUP
    heads = width // HD
    outs = pl.pallas_call(
        attend_kernel,
        in_specs=[SMEM] * 4 + [VMEM] * (LINE + GROUP + 4),
        out_specs=[VMEM] * (LINE + 6),
        out_shape=[shape((width, rows), BF)] * LINE
        + [
            shape((LINE, width, rows), F32),
            shape((LINE, width, rows), F32),
            shape((LINE, 8, rows), F32),
            shape((LINE, width, rows), BF),
            shape((slots, width, rows), BF),
            shape((slots, heads, rows, 2 * HD), BF),
        ],
        scratch_shapes=[
            pltpu.VMEM((slots, heads, rows, 2 * HD), BF),
            pltpu.VMEM((CLIPS, heads, CAP, 2 * HD), BF),
            pltpu.VMEM((heads, rows, 2 * HD), F32),
        ],
        name="attend",
        cost_estimate=cost(33),
    )(ids, slices, lengths, gates, *queries, *kv_pieces, cap_kv, gains, cosine, sine)
    return outs[:LINE], outs[LINE:]


def out_kernel(ids, *refs):
    own, other_ref, rest_ref = refs[:LINE], refs[LINE], refs[LINE + 1]
    w_ref, att_ref, branch_ref = refs[LINE + 2 :]
    b, s = ids[0], ids[1]
    width = own[0].shape[0]
    for k in range(LINE):
        at = chunk_at(b, k, width)
        att_ref[pl.ds(pl.multiple_of(s * LINE * width + at, HD), width), :] = own[k][...]
        far = other_ref[...] if k == 0 else rest_ref[(k - 1) * width : k * width, :]
        att_ref[pl.ds(pl.multiple_of((1 - s) * LINE * width + at, HD), width), :] = far
    branch_ref[...] = mm(w_ref[...], att_ref[...], NN).T.astype(BF)


def out_proj(ids, own, other, rest, w_out):
    rows = own[0].shape[1]
    return pl.pallas_call(
        out_kernel,
        in_specs=[SMEM] + [VMEM] * (LINE + 3),
        out_specs=[VMEM, VMEM],
        out_shape=[shape((D, rows), BF), shape((rows, w_out.shape[0]), BF)],
        name="out_proj",
        cost_estimate=cost(3.5),
    )(ids, *own, other, rest, w_out)


def cut_kernel(turned, ids, *refs):
    count = len(turned)
    ins = refs[:count]
    own_ref, c_ref, y_ref, scratch = refs[count:]
    place = lax.rem(ids[0], GROUP)
    columns = own_ref.shape[3]
    for n in range(count):
        if turned[n]:
            source = ins[n]
        else:
            scratch[...] = ins[n][...].astype(F32).T
            source = scratch
        for k in range(LINE):
            for j, (ref, i) in enumerate(((own_ref, 0), (c_ref, 0), (y_ref, 0), (y_ref, 1))):
                at = (k * GROUP + jnp.bitwise_xor(place, j)) * columns
                ref[i, n, k] = source[pl.ds(pl.multiple_of(at, 32), columns), :].astype(BF)


def cut(ids, values, turned):
    rows = values[0].shape[1 if turned[0] else 0]
    columns = D // (LINE * GROUP)
    count = len(values)
    return pl.pallas_call(
        functools.partial(cut_kernel, tuple(turned)),
        in_specs=[SMEM] + [VMEM] * count,
        out_specs=[VMEM] * 3,
        out_shape=[shape((n, count, LINE, columns, rows), BF) for n in (1, 1, 2)],
        scratch_shapes=[pltpu.VMEM((D, rows), F32)],
        name="cut",
        cost_estimate=cost(2.4),
    )(ids, *values)


def ffn_kernel(
    ids,
    tok_a,
    tok_b,
    br_a,
    br_b,
    out16_ref,
    mod_ref,
    gain_ref,
    kept_ref,
    came_ref,
    too_ref,
    down_ref,
    inner_a_ref,
    inner_b_ref,
    gcame_a_ref,
    gcame_b_ref,
    gkept_ref,
    in16_ref,
    mid_ref,
    near_ref,
    far_ref,
    near_out_ref,
    far_out_ref,
    acc_in,
    acc_out,
):
    step = pl.program_id(0)
    steps = pl.num_programs(0)
    s = ids[1]
    count = tok_a.shape[0]
    half = br_a.shape[1]
    gate, shift2, scale2 = [mod_ref[i : i + 1, :] for i in (2, 3, 4)]
    mlp_gain = gain_ref[...] * (1.0 + scale2)

    @pl.when(step == 0)
    def _():
        for place, tok in ((s, tok_a), (1 - s, tok_b)):
            at = pl.ds(pl.multiple_of(place * count, count), count)
            mid_ref[at, :] = tok[...].astype(F32)
        low = jnp.where(s == 0, br_a[...].astype(F32), br_b[...].astype(F32))
        high = jnp.where(s == 0, br_b[...].astype(F32), br_a[...].astype(F32))
        mid_ref[:, :half] += gate[:, :half] * low
        mid_ref[:, half:] += gate[:, half:] * high
        middle = mid_ref[...]
        in16_ref[...] = (middle * row_inverse(middle) * mlp_gain + shift2).astype(BF)
        acc_in[...] = jnp.zeros_like(acc_in)
        acc_out[...] = jnp.zeros_like(acc_out)

    w_kept, w_down = kept_ref[...], down_ref[...]
    mine = step // (steps // 2) == lax.rem(ids[0], 2)
    w_came = jnp.where(mine, came_ref[0], too_ref[0])
    kept = mm(in16_ref[...], w_kept, NT)
    other = mm(in16_ref[...], w_came, NT)
    grad_inner = mm(out16_ref[...], w_down, NT)
    gate_half = jnp.where(s == 0, kept, other)
    up_half = jnp.where(s == 0, other, kept)
    sigmoid = jax.nn.sigmoid(gate_half)
    silu = gate_half * sigmoid
    inner = (silu * up_half).astype(BF)
    grad_gate = grad_inner * up_half * sigmoid * (1.0 + gate_half * (1.0 - sigmoid))
    grad_up = grad_inner * silu
    grad_kept = jnp.where(s == 0, grad_gate, grad_up).astype(BF)
    grad_came = jnp.where(s == 0, grad_up, grad_gate).astype(BF)
    @pl.when(step < steps // 2)
    def _():
        inner_a_ref[...] = inner
        gcame_a_ref[...] = grad_came

    @pl.when(step >= steps // 2)
    def _():
        inner_b_ref[...] = inner
        gcame_b_ref[...] = grad_came

    gkept_ref[...] = grad_kept
    acc_in[...] += mm(grad_kept, w_kept, NN) + mm(grad_came, w_came, NN)
    acc_out[...] += mm(inner, w_down, NN)

    @pl.when(step == steps - 1)
    def _():
        middle = mid_ref[...]
        part = jnp.sum(
            acc_in[...] * mlp_gain * (middle * row_inverse(middle)), axis=-1, keepdims=True
        )
        near_ref[:, :half] = acc_in[:, pl.ds(pl.multiple_of(s * half, half), half)]
        near_ref[:, half:] = jnp.broadcast_to(part, (part.shape[0], 128))
        far_ref[:, :half] = acc_in[:, pl.ds(pl.multiple_of((1 - s) * half, half), half)].astype(BF)
        high = part.astype(BF).astype(F32)
        middle_part = (part - high).astype(BF).astype(F32)
        low_part = part - high - middle_part
        lane = lax.broadcasted_iota(jnp.int32, (part.shape[0], 128), 1)
        spread = jnp.where(lane == 0, high, jnp.where(lane == 1, middle_part, jnp.where(lane == 2, low_part, 0.0)))
        far_ref[:, half:] = spread.astype(BF)
        near_out_ref[...] = acc_out[pl.ds(pl.multiple_of(s * count, count), count), :]
        far_out_ref[...] = acc_out[pl.ds(pl.multiple_of((1 - s) * count, count), count), :].astype(BF)


def ffn(ids, toks, branches, grad_mlp, mod, gain, w_gate_up, came, too, w_down):
    count = toks[0].shape[0]
    rows = 2 * count
    half = D // 2
    units = w_down.shape[0]
    tile = 512
    steps = units // tile
    full = lambda v: pl.BlockSpec(v.shape, lambda i, ids: (0,) * v.ndim)

    def fixed(r, c):
        return pl.BlockSpec((r, c), lambda i, ids: (0, 0))

    def part(i, ids, flip):
        core = jnp.bitwise_xor(lax.rem(ids[0], 2), flip)
        return jnp.clip(i - core * (steps // 2), 0, steps // 2 - 1)

    small = [*toks, *branches, grad_mlp, mod, gain]
    return pl.pallas_call(
        ffn_kernel,
        grid_spec=pltpu.PrefetchScalarGridSpec(
            num_scalar_prefetch=1,
            grid=(steps,),
            in_specs=[full(v) for v in small]
            + [
                pl.BlockSpec((tile, D), lambda i, ids: (ids[1] * steps + i, 0)),
                pl.BlockSpec((1, tile, D), lambda i, ids: (1 - ids[1], part(i, ids, 0), 0)),
                pl.BlockSpec((1, tile, D), lambda i, ids: (1 - ids[1], part(i, ids, 1), 0)),
                pl.BlockSpec((tile, D), lambda i, ids: (i, 0)),
            ],
            out_specs=[
                pl.BlockSpec((rows, tile), lambda i, ids: (0, jnp.minimum(i, steps // 2 - 1))),
                pl.BlockSpec((rows, tile), lambda i, ids: (0, jnp.maximum(i - steps // 2, 0))),
            ]
            * 2
            + [pl.BlockSpec((rows, tile), lambda i, ids: (0, i))]
            + [
                fixed(rows, D),
                fixed(rows, D),
                fixed(rows, half + 128),
                fixed(rows, half + 128),
                fixed(count, D),
                fixed(count, D),
            ],
            scratch_shapes=[pltpu.VMEM((rows, D), F32), pltpu.VMEM((rows, D), F32)],
        ),
        out_shape=[shape((rows, units // 2), BF)] * 4
        + [shape((rows, units), BF)]
        + [
            shape((rows, D), BF),
            shape((rows, D), F32),
            shape((rows, half + 128), F32),
            shape((rows, half + 128), BF),
            shape((count, D), F32),
            shape((count, D), BF),
        ],
        name="ffn",
        cost_estimate=cost(18),
    )(ids, *small, w_gate_up, came, too, w_down)


def mid_kernel(
    ids,
    near_ref,
    recv_ref,
    mid_ref,
    cot_a,
    cot_b,
    br_ref,
    mod_ref,
    gain_ref,
    w_ref,
    sums_ref,
    gbr_ref,
    near_mid_ref,
    far_mid_ref,
    *refs,
):
    near_refs, far_refs, scratch = refs[:2], refs[2:4], refs[4]
    b, s = ids[0], ids[1]
    half = D // 2
    count = cot_a.shape[0]
    cols = pl.ds(pl.multiple_of(s * half, half), half)
    gate, scale2 = mod_ref[2:3, cols], mod_ref[4:5, cols]
    gain = gain_ref[:, cols]
    middle = mid_ref[...]
    inverse = row_inverse(middle)
    unit = mid_ref[:, cols] * inverse
    parts = jnp.sum(recv_ref[:, half:].astype(F32), axis=-1, keepdims=True)
    mean = (near_ref[:, half : half + 1] + parts) * (1.0 / D)
    grad_in = near_ref[:, :half] + recv_ref[:, :half].astype(F32)
    cot_own, cot_far = cot_a[:, cols].astype(F32), cot_b[:, cols].astype(F32)
    cot = jnp.concatenate(
        [jnp.where(s == 0, cot_own, cot_far), jnp.where(s == 0, cot_far, cot_own)], axis=0
    )
    scaled = grad_in * (1.0 + scale2)
    grad_mid = cot + inverse * (scaled * gain - unit * mean)
    sums_ref[...] = jnp.zeros_like(sums_ref)
    sums_ref[0:1, :] = jnp.sum(grad_mid * br_ref[...].astype(F32), axis=0, keepdims=True)
    sums_ref[1:2, :] = jnp.sum(grad_in, axis=0, keepdims=True)
    sums_ref[2:3, :] = jnp.sum(grad_in * unit, axis=0, keepdims=True) * gain
    sums_ref[3:4, :] = jnp.sum(scaled * unit, axis=0, keepdims=True)
    grad_branch = (grad_mid * gate).astype(BF)
    gbr_ref[...] = grad_branch
    top, low = grad_mid[:count], grad_mid[count:]
    near_mid_ref[...] = jnp.where(s == 0, top, low)
    far_mid_ref[...] = jnp.where(s == 0, low, top).astype(BF)
    scratch[...] = mm(grad_branch, w_ref[...], NN).T
    width = near_refs[0].shape[0] // 2
    for n, k in enumerate(SENDS):
        at = chunk_at(b, k, width)
        to = slice(n % 2 * width, n % 2 * width + width)
        near_refs[n // 2][to, :] = scratch[pl.ds(pl.multiple_of(s * half + at, HD), width), :]
        far_refs[n // 2][to, :] = scratch[
            pl.ds(pl.multiple_of((1 - s) * half + at, HD), width), :
        ].astype(BF)


def mid_back(ids, near, received, middle, cots, branch, mod, gain, w_out):
    rows, half = branch.shape
    width = half // LINE
    count = cots[0].shape[0]
    outs = pl.pallas_call(
        mid_kernel,
        in_specs=[SMEM] + [VMEM] * 9,
        out_specs=[VMEM] * 8,
        out_shape=[
            shape((8, half), F32),
            shape((rows, half), BF),
            shape((count, half), F32),
            shape((count, half), BF),
        ]
        + [shape((2 * width, rows), F32)] * 2
        + [shape((2 * width, rows), BF)] * 2,
        scratch_shapes=[pltpu.VMEM((D, rows), F32)],
        name="mid_back",
        cost_estimate=cost(5.5),
    )(ids, near, received, middle, *cots, branch, mod, gain, w_out)
    return outs[:4], outs[4:6], outs[6:]


def add_pair_kernel(near_ref, recv_ref, a_ref, b_ref):
    width = a_ref.shape[0]
    total = (near_ref[...] + recv_ref[...].astype(F32)).astype(BF)
    a_ref[...] = total[:width]
    b_ref[...] = total[width:]


def add_pair(near, received):
    both, rows = near.shape
    return pl.pallas_call(
        add_pair_kernel,
        in_specs=[VMEM, VMEM],
        out_specs=[VMEM, VMEM],
        out_shape=[shape((both // 2, rows), BF)] * 2,
        name="add_pair",
        cost_estimate=cost(1),
    )(near, received)


def place_row(b, column):
    width = column.shape[0]
    row = jnp.broadcast_to(column, (width, 128)).T[0:1]
    z = b // GROUP
    return jnp.concatenate([jnp.where(z == k, row, 0.0) for k in range(LINE)], axis=1)


def output_kernel(ids, slices, near_ref, recv_ref, mid_ref, cot_ref, mod_ref, sums_ref, out_ref, early_ref):
    s = ids[1]
    count, half = near_ref.shape[0], sums_ref.shape[1]
    clip, _, _ = clip_at(slices, ids[0])
    branch = near_ref[...] + recv_ref[...].astype(F32)
    middle = mid_ref[pl.ds(pl.multiple_of(s * count, count), count), :]
    out_ref[...] = (middle + mod_ref[5:6, :] * branch).astype(BF)
    gate2 = jnp.sum(cot_ref[...].astype(F32) * branch, axis=0, keepdims=True)
    rows = [sums_ref[i : i + 1, :] for i in range(3)] + [gate2[:, :half], gate2[:, half:]]
    early_ref[...] = jnp.zeros_like(early_ref)
    for c in range(CLIPS):
        for i, row in enumerate(rows):
            early_ref[5 * c + i : 5 * c + i + 1, :] = jnp.where(clip == c, row, 0.0)
    early_ref[20:21, :] = sums_ref[3:4, :]


def output_sums(ids, slices, near, received, middle, cot, mod, sums):
    count = near.shape[0]
    return pl.pallas_call(
        output_kernel,
        in_specs=[SMEM, SMEM] + [VMEM] * 6,
        out_specs=[VMEM, VMEM],
        out_shape=[shape((count, D), BF), shape((24, D // 2), F32)],
        name="output_sums",
        cost_estimate=cost(3),
    )(ids, slices, near, received, middle, cot, mod, sums)


def attend_back_kernel(ids, slices, lengths, gates, *refs):
    q_refs, g_refs = refs[:LINE], refs[LINE : 2 * LINE]
    (own_ref, other_ref, stat_ref, qs_ref, ks_ref, pair_ref, cap_ref, gains_ref, cos_ref, sin_ref) = refs[
        2 * LINE : 2 * LINE + 10
    ]
    outs = refs[2 * LINE + 10 :]
    gq_refs = outs[:LINE]
    qgain_ref, keep_ref, send_ref, dgate_ref = outs[LINE : LINE + 4]
    dkv_refs = outs[LINE + 4 : LINE + 4 + GROUP]
    acc_ref, dcap_ref, dq_ref = outs[LINE + 4 + GROUP :]
    b, s = ids[0], ids[1]
    width, rows = q_refs[0].shape
    heads = width // HD
    scale = HD**-0.5
    base = s * LINE * width + b // GROUP * width
    acc_ref[...] = jnp.zeros_like(acc_ref)
    dcap_ref[...] = jnp.zeros_like(dcap_ref)
    dgate_ref[...] = jnp.zeros_like(dgate_ref)
    qgain_ref[...] = jnp.zeros_like(qgain_ref)

    for i in range(LINE):
        slot = slot_of(b, i, 0)
        clip, first, last = clip_at(slices, slot)
        queries, grads, deltas, inverses = [], [], [], []
        tall_q, tall_g, wide = [], [], []
        for h in range(heads):
            at = slice(h * HD, h * HD + HD)
            grad = g_refs[i][at, :]
            queries.append(qs_ref[i, at, :])
            grads.append(grad)
            deltas.append(jnp.sum(grad.astype(F32) * own_ref[i, at, :], axis=0, keepdims=True))
            inverses.append(stat_ref[i, h : h + 1, :])
            blank = jnp.zeros((HD, rows), F32)
            query_pad = jnp.concatenate([queries[h].astype(F32), blank], axis=0)
            grad_pad = jnp.concatenate([blank, grad.astype(F32)], axis=0)
            tall_q.append(query_pad.astype(BF))
            tall_g.append(grad_pad.astype(BF))
            wide.append(jnp.concatenate([query_pad.T, grad_pad.T], axis=0).astype(BF))
        dq_ref[...] = jnp.zeros_like(dq_ref)

        def step(n, carry):
            for h in range(heads):
                at = slice(h * HD, h * HD + HD)
                pair = pair_ref[n, h]
                prob = jnp.exp(mm(pair, tall_q[h], NN)) * inverses[h]
                grad_score = (prob * (mm(pair, tall_g[h], NN) - deltas[h])).astype(BF)
                both = jnp.concatenate([grad_score, prob.astype(BF)], axis=1)
                acc_ref[n, h] += mm(both, wide[h], NN)
                dq_ref[at, :] += mm(ks_ref[n, at, :], grad_score, NN)
            return carry

        lax.fori_loop(first, last, step, 0)
        usable = lax.broadcasted_iota(jnp.int32, (CAP, rows), 0) < lengths[clip]
        cosine, sine = cos_ref[slot - first], sin_ref[slot - first]
        for h in range(heads):
            at = slice(h * HD, h * HD + HD)
            at_value = slice(width + h * HD, width + h * HD + HD)
            gate = gates[(s * LINE + b // GROUP) * heads + h]
            cap_keys, cap_values = cap_ref[clip, at, :], cap_ref[clip, at_value, :]
            grad = grads[h].astype(F32)
            grad_other = (grad * gate).astype(BF)
            prob = (
                jnp.where(usable, jnp.exp(mm(cap_keys, queries[h], TN)), 0.0)
                * stat_ref[i, 4 + h : 5 + h, :]
            )
            grad_prob = mm(cap_values, grad_other, TN)
            inner = jnp.sum(prob * grad_prob, axis=0, keepdims=True)
            grad_score = (prob * (grad_prob - inner)).astype(BF)
            query_grad = (dq_ref[at, :] + mm(cap_keys, grad_score, NN)) * scale
            dcap_ref[clip, at, :] += mm(queries[h], grad_score, NT)
            dcap_ref[clip, at_value, :] += mm(grad_other, prob.astype(BF), NT)
            part = jnp.sum(grad * other_ref[i, at, :], axis=0, keepdims=True)
            dgate_ref[h : h + 1, :] += part * (1.0 - gate * gate)
            gain = gains_ref[pl.ds(pl.multiple_of(base + h * HD, HD), HD), 0:1]
            raw_grad, gain_grad = norm_rope_back(
                query_grad.astype(BF).astype(F32), q_refs[i][at, :].astype(F32), gain, cosine, sine
            )
            gq_refs[i][at, :] = raw_grad.astype(BF)
            qgain_ref[at, :] += gain_grad

    for j, dkv_ref in enumerate(dkv_refs):
        for k in range(LINE):
            slot = slot_of(b, k, j)
            for h in range(heads):
                both = acc_ref[slot, h].T.astype(BF)
                dkv_ref[k, h * HD : h * HD + HD, :] = both[:HD]
                dkv_ref[k, width + h * HD : width + h * HD + HD, :] = both[HD:]
    core = lax.rem(b, 2)
    for i in range(2):
        keep_ref[i] = dcap_ref[2 * i + core]
        send_ref[i] = dcap_ref[2 * i + 1 - core]


def attend_back(ids, slices, lengths, gates, queries, grads, saved, cap_kv, gains, cosine, sine):
    width, rows = queries[0].shape
    outs = pl.pallas_call(
        attend_back_kernel,
        in_specs=[SMEM] * 4 + [VMEM] * (2 * LINE + 10),
        out_specs=[VMEM] * (LINE + 4 + GROUP),
        out_shape=[shape((width, rows), BF)] * LINE
        + [
            shape((width, 1), F32),
            shape((2, 2 * width, CAP), F32),
            shape((2, 2 * width, CAP), F32),
            shape((8, rows), F32),
        ]
        + [shape((LINE, 2 * width, rows), BF)] * GROUP,
        scratch_shapes=[
            pltpu.VMEM((LINE * GROUP, width // HD, rows, 2 * HD), F32),
            pltpu.VMEM((CLIPS, 2 * width, CAP), F32),
            pltpu.VMEM((width, rows), F32),
        ],
        name="attend_back",
        cost_estimate=cost(40),
    )(ids, slices, lengths, gates, *queries, *grads, *saved, cap_kv, gains, cosine, sine)
    return outs[:LINE], outs[LINE : LINE + 4], outs[LINE + 4 :]


def keys_back_kernel(ids, slices, a_ref, c_ref, r_ref, kv_ref, gains_ref, cos_ref, sin_ref, *outs):
    out_refs, gain_ref = outs[:LINE], outs[LINE]
    b, s = ids[0], ids[1]
    width = gain_ref.shape[0]
    base = s * LINE * width + b // GROUP * width
    gain_ref[...] = jnp.zeros_like(gain_ref)
    for i in range(LINE):
        slot = slot_of(b, i, 0)
        _, first, _ = clip_at(slices, slot)
        cosine, sine = cos_ref[slot - first], sin_ref[slot - first]
        total = a_ref[i].astype(F32) + c_ref[i].astype(F32) + r_ref[i].astype(F32)
        total = total.astype(BF)
        for h in range(width // HD):
            at = slice(h * HD, h * HD + HD)
            gain = gains_ref[pl.ds(pl.multiple_of(base + h * HD, HD), HD), 1:2]
            raw_grad, gain_grad = norm_rope_back(
                total[at, :].astype(F32), kv_ref[i, at, :].astype(F32), gain, cosine, sine
            )
            out_refs[i][at, :] = raw_grad.astype(BF)
            gain_ref[at, :] += gain_grad
        out_refs[i][width:, :] = total[width:, :]


def keys_back(ids, slices, part, beside, received, kv, gains, cosine, sine):
    _, both, rows = kv.shape
    outs = pl.pallas_call(
        keys_back_kernel,
        in_specs=[SMEM, SMEM] + [VMEM] * 7,
        out_specs=[VMEM] * (LINE + 1),
        out_shape=[shape((both, rows), BF)] * LINE + [shape((both // 2, 1), F32)],
        name="keys_back",
        cost_estimate=cost(3.7),
    )(ids, slices, part, beside, received, kv, gains, cosine, sine)
    return outs[:LINE], outs[LINE]


def pack_kernel(ids, *refs):
    q_refs, kv_refs = refs[:LINE], refs[LINE : 2 * LINE]
    first_ref, second_ref, send_ref = refs[2 * LINE :]
    b, s = ids[0], ids[1]
    width = q_refs[0].shape[0]
    for k in range(LINE):
        at = chunk_at(b, k, width)

        @pl.when(s == 0)
        def _():
            first_ref[pl.ds(at, width), :] = q_refs[k][...]
            second_ref[pl.ds(at, width), :] = kv_refs[k][:width, :]
            send_ref[pl.ds(at, width), :] = kv_refs[k][width:, :]

        @pl.when(s == 1)
        def _():
            first_ref[pl.ds(at, width), :] = kv_refs[k][:width, :]
            second_ref[pl.ds(at, width), :] = kv_refs[k][width:, :]
            send_ref[pl.ds(at, width), :] = q_refs[k][...]


def pack(ids, grads_q, grads_kv):
    width, rows = grads_q[0].shape
    return pl.pallas_call(
        pack_kernel,
        in_specs=[SMEM] + [VMEM] * (2 * LINE),
        out_specs=[VMEM] * 3,
        out_shape=[shape((LINE * width, rows), BF)] * 3,
        name="pack",
        cost_estimate=cost(2.5),
    )(ids, *grads_q, *grads_kv)


def qkv_back_kernel(ids, first_ref, recv_ref, second_ref, w_ref, near_ref, far_ref, acc_ref):
    step = pl.program_id(0)
    count = near_ref.shape[0]
    s = ids[1]

    for n, ref in enumerate((first_ref, recv_ref, second_ref)):

        @pl.when(step == n)
        def _():
            part = mm(ref[...], w_ref[...], TN)
            acc_ref[...] = part if n == 0 else acc_ref[...] + part

    @pl.when(step == pl.num_programs(0) - 1)
    def _():
        near_ref[...] = acc_ref[pl.ds(pl.multiple_of(s * count, count), count), :]
        far_ref[...] = acc_ref[pl.ds(pl.multiple_of((1 - s) * count, count), count), :].astype(BF)


def qkv_back(ids, first, received, second, w_qkv):
    local, rows = received.shape
    count = rows // 2
    whole = pl.BlockSpec((local, rows), lambda i, ids: (0, 0))
    return pl.pallas_call(
        qkv_back_kernel,
        grid_spec=pltpu.PrefetchScalarGridSpec(
            num_scalar_prefetch=1,
            grid=(3,),
            in_specs=[whole] * 3 + [pl.BlockSpec((local, D), lambda i, ids: (i, 0))],
            out_specs=[pl.BlockSpec((count, D), lambda i, ids: (0, 0))] * 2,
            scratch_shapes=[pltpu.VMEM((rows, D), F32)],
        ),
        out_shape=[shape((count, D), F32), shape((count, D), BF)],
        name="qkv_back",
        cost_estimate=cost(6),
    )(ids, first, received, second, w_qkv)


def tokens_kernel(
    ids, slices, tok_ref, near_ref, recv_ref, mid_near, mid_far, mod_ref, gain_ref, *refs
):
    qgain_ref, kgain_ref, cgain_ref, dgate_ref, early_ref, out_ref, late_ref = refs
    b, s = ids[0], ids[1]
    half = mid_near.shape[1]
    clip, _, _ = clip_at(slices, b)
    values = tok_ref[...].astype(F32)
    inverse = row_inverse(values)
    unit = values * inverse
    scale = 1.0 + mod_ref[1:2, :]
    gain = gain_ref[...]
    grad = near_ref[...] + recv_ref[...].astype(F32)
    scaled = grad * scale
    unit_grad = scaled * gain
    mean = jnp.mean(unit_grad * unit, axis=-1, keepdims=True)
    mid_own, mid_other = mid_near[...], mid_far[...].astype(F32)
    middle = jnp.concatenate(
        [jnp.where(s == 0, mid_own, mid_other), jnp.where(s == 0, mid_other, mid_own)], axis=1
    )
    out_ref[...] = inverse * (unit_grad - unit * mean) + middle
    shift_row = jnp.sum(grad, axis=0, keepdims=True)
    with_unit = grad * unit
    scale_row = jnp.sum(with_unit, axis=0, keepdims=True) * gain
    norm_row = jnp.sum(scaled * unit, axis=0, keepdims=True)
    rows = [shift_row[:, :half], shift_row[:, half:], scale_row[:, :half], scale_row[:, half:]]
    late_ref[...] = jnp.zeros_like(late_ref)
    for c in range(CLIPS):
        for i, row in enumerate(rows):
            late_ref[4 * c + i : 4 * c + i + 1, :] = jnp.where(clip == c, row, 0.0)
    late_ref[16:17, :] = norm_row[:, :half]
    late_ref[17:18, :] = norm_row[:, half:]
    for i, ref in enumerate((qgain_ref, kgain_ref, cgain_ref)):
        late_ref[18 + i : 19 + i, :] = place_row(b, ref[...])
    heads = qgain_ref.shape[0] // HD
    lane = lax.broadcasted_iota(jnp.int32, (1, half), 1)
    gate_row = jnp.zeros((1, half), F32)
    for h in range(heads):
        value = jnp.sum(dgate_ref[h : h + 1, :], axis=1, keepdims=True)
        gate_row = gate_row + jnp.where(lane == b // GROUP * heads + h, value, 0.0)
    late_ref[21:22, :] = gate_row
    late_ref[24:, :] = early_ref[...]


def tokens_back(ids, slices, tok, near, received, mid_near, mid_far, mod, gain, parts):
    return pl.pallas_call(
        tokens_kernel,
        in_specs=[SMEM, SMEM] + [VMEM] * 12,
        out_specs=[VMEM, VMEM],
        out_shape=[shape(tok.shape, F32), shape((48, D // 2), F32)],
        name="tokens_back",
        cost_estimate=cost(3.5),
    )(ids, slices, tok, near, received, mid_near, mid_far, mod, gain, *parts)


def finish_kernel(ids, late_a, late_b, mod_ref, gains_ref):
    s = ids[1]
    early_a, early_b = late_a.at[pl.ds(24, 24)], late_b.at[pl.ds(24, 24)]

    def joined(a, b, i):
        own, other = a[i : i + 1, :], b[i : i + 1, :]
        return jnp.concatenate(
            [jnp.where(s == 0, own, other), jnp.where(s == 0, other, own)], axis=1
        )

    def added(a, b, i):
        both = a[i : i + 2, :] + b[i : i + 2, :]
        return jnp.concatenate([both[0:1], both[1:2]], axis=1)

    for c in range(CLIPS):
        low = [added(late_a, late_b, 4 * c), added(late_a, late_b, 4 * c + 2), joined(early_a, early_b, 5 * c)]
        high = [
            joined(early_a, early_b, 5 * c + 1),
            joined(early_a, early_b, 5 * c + 2),
            added(early_a, early_b, 5 * c + 3),
        ]
        for i in range(3):
            mod_ref[c : c + 1, i * D : (i + 1) * D] = jnp.where(s == 0, low[i], high[i])
    gains_ref[...] = jnp.zeros_like(gains_ref)
    gains_ref[0:1, :] = added(late_a, late_b, 16)
    for i in range(3):
        gains_ref[1 + i : 2 + i, :] = joined(late_a, late_b, 18 + i)
    gains_ref[4:5, :] = joined(early_a, early_b, 20)
    gains_ref[5:6, :] = joined(late_a, late_b, 21)


def finish(ids, late_a, late_b):
    return pl.pallas_call(
        finish_kernel,
        in_specs=[SMEM] + [VMEM] * 2,
        out_specs=[VMEM, VMEM],
        out_shape=[shape((CLIPS, 3 * D), F32), shape((8, D), F32)],
        name="finish",
        cost_estimate=cost(1.7),
    )(ids, late_a, late_b)


def caption_back_kernel(ids, sum_ref, raw_ref, gains_ref, out_ref, gain_ref):
    b, s = ids[0], ids[1]
    width = gain_ref.shape[0]
    base = s * LINE * width + b // GROUP * width
    cols = pl.ds(pl.multiple_of(lax.rem(b, GROUP) * CAP, CAP), CAP)
    for h in range(width // HD):
        at = slice(h * HD, h * HD + HD)
        gain = gains_ref[pl.ds(pl.multiple_of(base + h * HD, HD), HD), 2:3]
        raw = raw_ref[at, cols]
        inverse = lax.rsqrt(jnp.mean(raw * raw, axis=0, keepdims=True) + EPSILON)
        unit = raw * inverse
        grad = sum_ref[at, :]
        gain_ref[at, :] = jnp.sum(grad * unit, axis=1, keepdims=True)
        unit_grad = grad * gain
        out_ref[at, :] = (
            inverse * (unit_grad - unit * jnp.mean(unit_grad * unit, axis=0, keepdims=True))
        ).astype(BF)
    out_ref[width:, :] = sum_ref[width:, :].astype(BF)


def caption_back(ids, total, raw, gains):
    return pl.pallas_call(
        caption_back_kernel,
        in_specs=[SMEM] + [VMEM] * 3,
        out_specs=[VMEM, VMEM],
        out_shape=[shape(total.shape, BF), shape((total.shape[0] // 2, 1), F32)],
        name="caption_back",
        cost_estimate=cost(2.3),
    )(ids, total, raw, gains)


def caption_weight_kernel(ids, *refs):
    raw_refs, cap_ref, out_refs = refs[:GROUP], refs[GROUP], refs[GROUP + 1 :]
    b = ids[0]
    each = out_refs[0].shape[1]
    place = lax.rem(b, GROUP)
    for k in range(LINE):
        at = pl.multiple_of((lax.rem(b // GROUP - k + LINE, LINE) * GROUP + place) * each, each)
        total = None
        for j in range(GROUP):
            rows = pl.ds(pl.multiple_of(jnp.bitwise_xor(place, j) * CAP, CAP), CAP)
            part = mm(raw_refs[j][...], cap_ref[rows, pl.ds(at, each)], NN)
            total = part if total is None else total + part
        out_refs[k][...] = total.astype(BF)


def caption_weights(ids, raws, caption):
    rows = raws[0].shape[0]
    return pl.pallas_call(
        caption_weight_kernel,
        in_specs=[SMEM] + [VMEM] * (GROUP + 1),
        out_specs=[VMEM] * LINE,
        out_shape=[shape((rows, YD // (LINE * GROUP)), BF)] * LINE,
        name="caption_weights",
        cost_estimate=cost(4),
    )(ids, *raws, caption)


def caption_join_kernel(ids, *refs):
    parts, out_ref = refs[:LINE], refs[LINE]
    width = parts[0].shape[0] // 2
    for k in range(LINE):
        at = chunk_at(ids[0], k, width)
        for j in range(2):
            out_ref[j, pl.ds(at, width), :] = parts[k][j * width : (j + 1) * width, :].astype(F32)


def caption_join(ids, parts):
    both, each = parts[0].shape
    return pl.pallas_call(
        caption_join_kernel,
        in_specs=[SMEM] + [VMEM] * LINE,
        out_specs=VMEM,
        out_shape=shape((2, both // 2 * LINE, each), F32),
        name="caption_join",
        cost_estimate=cost(2),
    )(ids, *parts)


def weight_kernel(count, dims, *refs):
    left, right, out_ref = refs[:count], refs[count : 2 * count], refs[-1]
    total = None
    for a_ref, g_ref in zip(left, right):
        block = g_ref[...].reshape(g_ref.shape[-2:])
        part = mm(a_ref[0, 0].reshape(-1, a_ref.shape[-1]), block, dims)
        total = part if total is None else total + part
    out_ref[...] = total.reshape(out_ref.shape).astype(BF)


def weight_grads(left, right, by_rows, tile, kind, total, place, into=None):
    _, _, chunks, columns, tokens = left[0][0].shape
    rows = right[0].shape[-2 if by_rows else -1]
    stack = right[0].shape[0] if right[0].ndim == 3 else 1
    per = rows // tile
    left_specs = [
        pl.BlockSpec((1, 1, chunks, columns, tokens), lambda i, n=n: (n, kind, 0, 0, 0))
        for _, n in left
    ]
    if by_rows:
        right_spec = pl.BlockSpec((tile, tokens), lambda i: (i, 0))
    elif stack == 1:
        right_spec = pl.BlockSpec((tokens, tile), lambda i: (0, i))
    else:
        right_spec = pl.BlockSpec((1, tokens, tile), lambda i: (i // per, 0, i % per))
    args = [a for a, _ in left] + list(right)
    specs = left_specs + [right_spec] * len(right)
    aliases = {}
    if into is not None:
        aliases = {len(args): 0}
        args.append(into)
        specs.append(pl.BlockSpec(memory_space=pl.ANY))
    return pl.pallas_call(
        functools.partial(weight_kernel, len(left), NT if by_rows else NN),
        grid=(stack * per,),
        in_specs=specs,
        out_specs=pl.BlockSpec((chunks, columns, tile), lambda i: (0, 0, place(i))),
        out_shape=shape((chunks, columns, total), BF),
        input_output_aliases=aliases,
        name="weight_grads",
        cost_estimate=cost(5),
    )(*args)


def fast_body(
    tokens,
    cotangent,
    clip_slices,
    caption_lengths,
    caption,
    cond,
    ada_w,
    norm_gain,
    w_qkv,
    q_gain,
    k_gain,
    w_caption,
    ky_gain,
    cross_gate,
    w_out,
    ffn_gain,
    w_gate_up,
    w_down,
):
    bucket_count = LINE * GROUP
    seq_count = lax.axis_size("seq")
    local_width = D // seq_count
    units = FF // seq_count
    b = lax.axis_index(BUCKET)
    s = lax.axis_index("seq")
    z, g, c, y = b // GROUP, b % GROUP, b % 2, (b // 2) % 2
    ids = jnp.stack([b, s]).astype(jnp.int32)

    def xswap(v):
        return lax.ppermute(v, "seq", [(0, 1), (1, 0)])

    def hop(v, to):
        return lax.ppermute(v, BUCKET, [(i, to(i)) for i in range(bucket_count)])

    def cswap(v):
        return hop(v, lambda i: i ^ 1)

    def yswap(v):
        return hop(v, lambda i: i ^ 2)

    def zshift(v, k):
        return hop(v, lambda i: (i + GROUP * k) % bucket_count)

    def after(v, *others):
        return lax.optimization_barrier((v, *others))[0]

    def fence(*values):
        return lax.optimization_barrier(values)

    def pick(v, index):
        return lax.dynamic_index_in_dim(v, index, 0, False)

    def spread(parts):
        return [parts[0]] + [zshift(parts[k], k) for k in range(1, LINE)]

    def unspread(parts):
        return [parts[0]] + [zshift(parts[k], LINE - k) for k in range(1, LINE)]

    half = HD // 2
    rows = tokens.shape[0] * seq_count
    frequency = jnp.exp(jnp.arange(half, dtype=F32) * (-2.0 * math.log(10000.0) / (2 * half)))
    positions = jnp.arange(bucket_count * rows, dtype=F32).reshape(bucket_count, 1, rows)
    angles = positions * frequency[None, :, None]
    cosine, sine = jnp.cos(angles), jnp.sin(angles)
    gains = jnp.stack([q_gain, k_gain, ky_gain], axis=1)
    gates = jnp.tanh(cross_gate)
    norm_row, ffn_row = norm_gain[None], ffn_gain[None]

    tok_far = xswap(tokens)
    activation = jax.nn.silu(cond).astype(BF)
    mod_near = mm(activation, ada_w, NT)
    mod_far = xswap(mod_near)
    each = units // 2
    sent = lax.dynamic_slice_in_dim(w_gate_up, (1 - s) * units + c * each, each, 0)
    tok_far, sent = lax.optimization_barrier((tok_far, sent))
    projected, hidden, mod = pre(
        ids, clip_slices, tokens, tok_far, mod_near, mod_far, norm_row, w_qkv
    )
    local = lax.slice_in_dim(projected, local_width, 2 * local_width, axis=0)
    swapped = xswap(local)
    def scatter(parts):
        return lax.psum_scatter(parts, "z", scatter_dimension=0, tiled=False)

    hid_own, hid_c, hid_y = cut(ids, [hidden], [False])
    swapped, hid_own, hid_c, hid_y, gains = fence(swapped, hid_own, hid_c, hid_y, gains)
    kv_parts, q_parts = route(ids, projected, swapped)
    came = lax.all_gather(after(sent, swapped), "seq", axis=0, tiled=False)
    kv_here = spread(kv_parts)
    q_here = spread(q_parts)
    caption_rows = caption.reshape(CLIPS * CAP, YD)
    cap_raw, cap_kv = caption_keys(ids, w_caption, after(caption_rows, kv_parts[0]), gains)
    cap_raw, cap_kv, cosine, sine, *kv_here = fence(cap_raw, cap_kv, cosine, sine, *kv_here)
    kv_own = jnp.stack(kv_here)
    kv_y = yswap(kv_own)
    kv_c = cswap(kv_own)
    cot_far = xswap(after(cotangent, kv_own))
    kv_y = after(kv_y, kv_c, *q_here[1:], cot_far)
    kv_cy = cswap(kv_y)
    kv_pieces = [kv_own, kv_c, kv_y, kv_cy]
    grad_mlp = (
        jnp.where(
            s == 0,
            jnp.concatenate([cotangent, cot_far], 0),
            jnp.concatenate([cot_far, cotangent], 0),
        ).astype(F32)
        * mod[5:6]
    ).astype(BF)
    q_here[0], hid_y, hid_c = fence(q_here[0], hid_y, hid_c, grad_mlp)[:3]
    hid_came_y, hid_came_c = yswap(hid_y), cswap(hid_c)
    combined, saved = attend(
        ids, clip_slices, caption_lengths, gates, q_here, kv_pieces, cap_kv, gains, cosine, sine
    )
    combined, saved, hid_came_y, hid_came_c = fence(combined, saved, hid_came_y, hid_came_c)
    heads_own = unspread(combined)
    heads_far = xswap(heads_own[0])
    rest_far = xswap(jnp.concatenate(heads_own[1:], axis=0))
    attention, branch = out_proj(ids, heads_own, heads_far, rest_far, w_out)
    branch_far = xswap(branch)
    att_own, att_c, att_y = cut(ids, [attention, grad_mlp], [True, False])
    came = after(came, branch)
    too = cswap(came)
    branch_far, att_own, att_c, att_y, too = fence(branch_far, att_own, att_c, att_y, too)
    att_came_y = yswap(att_y)
    att_came_c = cswap(att_c)
    hid_came_yc = cswap(after(hid_came_y, branch_far))
    hid_left = [(hid_own, 0), (hid_came_c, 0), (hid_came_y, 0), (hid_came_yc, 1)]
    inner, inner_2, came_1, came_2, grad_kept, mlp_in, middle, near, far, near_out, far_out = ffn(
        ids, [tokens, tok_far], [branch, branch_far], grad_mlp, mod, ffn_row, w_gate_up, came, too, w_down
    )
    inner, inner_2, grad_kept, came_1, came_2, mlp_in, near, far = fence(
        inner, inner_2, grad_kept, came_1, came_2, mlp_in, near, far
    )
    att_came_y, att_came_c, hid_came_yc, far = fence(att_came_y, att_came_c, hid_came_yc, far)
    hid_left[3] = (hid_came_yc, 1)

    received = xswap(far)
    inner_y = yswap(inner)
    inner_c = cswap(inner)
    kept_c = cswap(grad_kept)
    att_came_yc = cswap(att_came_y)
    att_left = [(att_own, 0), (att_came_c, 0), (att_came_y, 0), (att_came_yc, 1)]
    ffn_own, ffn_c, ffn_y = cut(ids, [mlp_in], [False])
    received, ffn_own, ffn_c, ffn_y, inner_c, inner_y, kept_c, att_came_yc, came_op, inner_op = fence(
        received, ffn_own, ffn_c, ffn_y, inner_c, inner_y, kept_c, att_came_yc, came_1, inner_2
    )
    came_1c = cswap(came_op)
    att_left[3] = (att_came_yc, 1)
    inner_2y = yswap(inner_op)
    inner_2c = cswap(inner_op)
    inner_yc = cswap(inner_y)
    ffn_came_c = cswap(ffn_c)
    (sums, grad_branch, mid_near, mid_far), near_heads, far_heads = mid_back(
        ids, near, received, middle, [cotangent, cot_far], branch, mod, ffn_row, w_out
    )
    grad_branch, ffn_came_c, inner_yc, inner_2c, came_1c, *far_heads = fence(
        grad_branch, ffn_came_c, inner_yc, inner_2c, came_1c, *far_heads
    )
    recv_a = xswap(far_heads[0])
    recv_b = xswap(far_heads[1])
    branch_c = cswap(grad_branch)
    tile = 512
    per = units // tile
    parts_inner = weight_grads(
        att_left, [inner, inner_c, inner_y, inner_yc], False, tile, 1, units, lambda i: i
    )
    recv_a, parts_inner, branch_c, inner_2y, ffn_y, branch_op, came_op = fence(
        recv_a, parts_inner, branch_c, inner_2y, ffn_y, grad_branch, came_op
    )
    ffn_came_y = yswap(ffn_y)
    came_1y = yswap(came_op)
    inner_2yc = cswap(inner_2y)
    grad_1, grad_2 = add_pair(near_heads[0], recv_a)
    grad_3, grad_0 = add_pair(near_heads[1], after(recv_b, grad_1))
    grad_here = spread([grad_0, grad_1, grad_2, grad_3])
    parts_inner = weight_grads(
        att_left,
        [after(inner_2, grad_0), inner_2c, inner_2y, inner_2yc],
        False,
        tile,
        1,
        units,
        lambda i: i + per // 2,
        parts_inner,
    )
    parts_inner, ffn_came_y, came_1y, *grad_here = fence(
        parts_inner, ffn_came_y, came_1y, *grad_here
    )
    sum_inner = scatter(parts_inner)
    grad_here[0], kept_op, came_op, ffn_y = fence(grad_here[0], grad_kept, came_2, ffn_came_y)
    kept_y = yswap(kept_op)
    came_2y = yswap(came_op)
    came_2c = cswap(came_op)
    ffn_came_yc = cswap(ffn_y)
    came_1yc = cswap(came_1y)
    grads_q, (q_gain_part, cap_keep, cap_send, gate_part), grads_kv = attend_back(
        ids, clip_slices, caption_lengths, gates, q_here, grad_here, saved, cap_kv, gains, cosine, sine
    )
    grads_q, grads_kv, cap_send, kept_y, came_2y, came_2c, ffn_came_yc, came_1yc = fence(
        grads_q, grads_kv, cap_send, kept_y, came_2y, came_2c, ffn_came_yc, came_1yc
    )

    kv_c3 = cswap(grads_kv[3])
    kv_c1, cap_c = cswap(grads_kv[1]), cswap(cap_send)
    away = (grads_kv[2].astype(F32) + kv_c3.astype(F32)).astype(BF)
    away, kv_c1, cap_c, *grads_q = fence(away, kv_c1, cap_c, *grads_q)
    away_here = yswap(away)
    kept_yc, came_2yc = fence(kept_y, came_2y, away)[:2]
    kept_yc, came_2yc = cswap(kept_yc), cswap(came_2yc)
    kept_yc, came_2yc, *grads_q = fence(kept_yc, came_2yc, *grads_q)
    ffn_left = [(ffn_own, 0), (ffn_came_c, 0), (ffn_came_y, 0), (ffn_came_yc, 1)]
    back_q = unspread(grads_q)
    pair = cap_keep + cap_c
    parts_a = None
    for right, first_tile in (
        ([grad_kept, kept_c, kept_y, kept_yc], 0),
        ([came_1, came_1c, came_1y, came_1yc], per),
        ([came_2, came_2c, came_2y, came_2yc], per + per // 2),
    ):
        parts_a = weight_grads(
            ffn_left, right, False, tile, 0, 2 * units, lambda i, n=first_tile: i + n, parts_a
        )
    away_here, parts_a, pair, sum_inner, *back_q = fence(
        away_here, parts_a, pair, sum_inner, *back_q
    )
    back_kv, k_gain_part = keys_back(
        ids, clip_slices, grads_kv[0], kv_c1, away_here, kv_own, gains, cosine, sine
    )
    back_kv, k_gain_part, branch_op, out_op = fence(back_kv, k_gain_part, branch_op, far_out)
    branch_y = yswap(branch_op)
    out_recv = xswap(out_op)
    back_kv = unspread(back_kv)
    *back_kv, parts_a, branch_y, out_recv = fence(*back_kv, parts_a, branch_y, out_recv)
    sum_a = scatter(parts_a)

    first, second, send = fence(*pack(ids, back_q, back_kv))
    packed_recv = xswap(send)
    first_y = yswap(first)
    first_c = cswap(first)
    branch_all = [grad_branch, branch_c, branch_y, cswap(after(branch_y, first))]
    tile, total = 384, 4 * local_width
    parts_c = weight_grads(att_left, branch_all, False, tile, 0, total, lambda i: i + 6)
    cap_y = yswap(after(pick(pair, 1 - y), first))
    cap_total = pick(pair, y) + cap_y
    raw_cap, cap_gain_part = caption_back(ids, cap_total, cap_raw, gains)
    output, early = output_sums(
        ids, clip_slices, near_out, after(out_recv, first), middle, cotangent, mod, sums
    )
    packed_recv, first_y, first_c, raw_cap, cap_gain_part, second, parts_c, output = fence(
        packed_recv, first_y, first_c, raw_cap, cap_gain_part, second, parts_c, output
    )
    second_y = yswap(second)
    second_c = cswap(second)
    recv_c = cswap(packed_recv)
    first_yc = cswap(first_y)
    tok_near, tok_send = qkv_back(ids, first, packed_recv, second, w_qkv)
    mid_came = xswap(after(mid_far, packed_recv))
    tok_near, tok_send, second_y, second_c, recv_c, first_yc, recv_op, raw_cap, mid_came = fence(
        tok_near, tok_send, second_y, second_c, recv_c, first_yc, packed_recv, raw_cap, mid_came
    )
    tok_recv = xswap(tok_send)
    recv_y = yswap(recv_op)
    second_yc = cswap(second_y)
    raw_c = cswap(raw_cap)
    parts_c = weight_grads(
        hid_left, [first, first_c, first_y, first_yc], True, tile, 0, total, lambda i: i, parts_c
    )
    parts_c = weight_grads(
        hid_left, [second, second_c, second_y, second_yc], True, tile, 0, total, lambda i: i + 4, parts_c
    )
    tok_recv, parts_c, recv_y, raw_c = fence(tok_recv, parts_c, recv_y, raw_c)
    recv_yc = cswap(recv_y)
    raw_y = yswap(raw_cap)
    parts_c = weight_grads(
        hid_left, [packed_recv, recv_c, recv_y, recv_yc], True, tile, 0, total, lambda i: i + 2, parts_c
    )
    parts_c, raw_y = fence(parts_c, raw_y)
    sum_c = scatter(parts_c)
    token_grad, late = tokens_back(
        ids,
        clip_slices,
        tokens,
        tok_near,
        tok_recv,
        mid_near,
        mid_came,
        mod,
        norm_row,
        [q_gain_part, k_gain_part, cap_gain_part, gate_part, early],
    )
    raw_yc = cswap(raw_y)
    late = late + cswap(late)
    cap_parts = caption_weights(ids, [raw_cap, raw_c, raw_y, raw_yc], caption_rows)
    late_y = yswap(late)
    late_y, cap_parts = fence(late_y, cap_parts)
    late = late + late_y
    late_z = hop(late, lambda i: i ^ GROUP)
    late_z, sum_a = fence(late_z, sum_a)
    late = late + late_z
    late = late + hop(late, lambda i: i ^ (2 * GROUP))
    late, *cap_parts = fence(late, *cap_parts)
    cap_parts = unspread(cap_parts)
    late_far = xswap(late)
    came_out = xswap(sum_a[:, units:])
    late_sum = late

    mod_grad, gain_rows = finish(ids, late_sum, late_far)
    mod_mine = mod_grad.astype(BF)
    caption_w_grad = caption_join(ids, fence(*cap_parts, mod_mine)[:LINE])
    cols_local = CD // bucket_count
    act_cols = lax.dynamic_slice_in_dim(activation, b * cols_local, cols_local, 1)
    ada_grad = mm(mod_mine, act_cols, TN)
    cond_part = mm(mod_mine, ada_w, NN)
    cond_sigmoid = jax.nn.sigmoid(cond)
    cond_grad = (
        (cond_part + xswap(cond_part)) * cond_sigmoid * (1.0 + cond * (1.0 - cond_sigmoid))
    )
    heads_each = H // seq_count
    cross_out = jnp.concatenate(
        [gain_rows[5, :heads_each], gain_rows[5, local_width : local_width + heads_each]]
    )

    down_out = sum_inner.astype(F32).T
    kept_out = sum_a[:, :units].astype(F32)
    came_out = came_out.astype(F32)
    gate_up_out = jnp.where(
        s == 0,
        jnp.concatenate([kept_out, came_out], 1),
        jnp.concatenate([came_out, kept_out], 1),
    ).T
    sum_c = after(sum_c, gate_up_out)
    return (
        output,
        token_grad,
        cond_grad,
        ada_grad,
        gain_rows[0],
        sum_c[:, : 3 * local_width].astype(F32).T,
        gain_rows[1],
        gain_rows[2],
        caption_w_grad,
        gain_rows[3],
        cross_out,
        sum_c[:, 3 * local_width :].astype(F32).T,
        gain_rows[4],
        gate_up_out,
        down_out,
    )


def project(activations, weight):
    return lax.dot_general(
        activations, weight, (((1,), (1,)), ((), ())), preferred_element_type=jnp.float32
    )


def clip_of(rows, ends):
    return jnp.sum((rows[:, None] >= ends[None, :]).astype(jnp.int32), axis=1)


def head_norm(values, gains, head_count):
    row_count = values.shape[0]
    split = values.reshape(row_count, head_count, -1)
    inverse = lax.rsqrt(jnp.mean(split * split, axis=-1, keepdims=True) + EPSILON)
    unit_rows = split * inverse
    return (unit_rows.reshape(row_count, -1) * gains, unit_rows, inverse)


def head_norm_back(norm_grads, gains, unit_rows, inverse):
    row_count, head_count, head_width = unit_rows.shape
    gain_grad = jnp.sum(norm_grads * unit_rows.reshape(row_count, -1), axis=0)
    unit_grad = (norm_grads * gains).reshape(row_count, head_count, head_width)
    raw_grad = inverse * (
        unit_grad - unit_rows * jnp.mean(unit_grad * unit_rows, axis=-1, keepdims=True)
    )
    return (raw_grad.reshape(row_count, -1), gain_grad)


def rotate(values, positions, head_count):
    row_count = values.shape[0]
    split = values.reshape(row_count, head_count, -1)
    half_width = split.shape[-1] // 2
    frequency = jnp.exp(
        jnp.arange(half_width, dtype=jnp.float32) * (-2.0 * math.log(10000.0) / (2 * half_width))
    )
    angles = positions[:, None] * frequency[None, :]
    cosine = jnp.cos(angles)[:, None, :]
    sine = jnp.sin(angles)[:, None, :]
    first_half = split[..., :half_width]
    second_half = split[..., half_width:]
    turned = jnp.concatenate(
        [first_half * cosine - second_half * sine, first_half * sine + second_half * cosine],
        axis=-1,
    )
    return turned.reshape(row_count, -1)


def block_size(row_count):
    return 512 if row_count % 512 == 0 else row_count


def general_body(
    tokens,
    cotangent,
    clip_slices,
    caption_lengths,
    caption,
    cond,
    ada_w,
    norm_gain,
    w_qkv,
    q_gain,
    k_gain,
    w_caption,
    ky_gain,
    cross_gate,
    w_out,
    ffn_gain,
    w_gate_up,
    w_down,
):
    seq_count = lax.axis_size("seq")
    bucket_count = lax.axis_size("bucket")
    tok_rows = tokens.shape[0]
    slice_rows = tok_rows * seq_count
    total_rows = slice_rows * bucket_count
    local_heads = H // seq_count
    local_width = local_heads * HD
    score_scale = HD ** (-0.5)
    bucket_id = lax.axis_index("bucket")
    seq_id = lax.axis_index("seq")
    ends = jnp.cumsum(clip_slices) * slice_rows
    starts = ends - clip_slices * slice_rows
    my_clip = clip_of(jnp.reshape(bucket_id * slice_rows, (1,)), ends)[0]
    clip_mask = jnp.arange(CLIPS) == my_clip
    clip_start = jnp.sum(jnp.where(clip_mask, starts, 0))
    first_token = (bucket_id * seq_count + seq_id) * tok_rows
    positions = (first_token + jnp.arange(tok_rows, dtype=jnp.int32) - clip_start).astype(
        jnp.float32
    )
    caption_usable = jnp.arange(CAP) < jnp.sum(jnp.where(clip_mask, caption_lengths, 0))
    head_first = seq_id * local_width
    gates_local = jnp.tanh(lax.dynamic_slice_in_dim(cross_gate, seq_id * local_heads, local_heads))
    ky_gain_local = lax.dynamic_slice_in_dim(ky_gain, head_first, local_width)
    activation = jax.nn.silu(cond).astype(jnp.bfloat16)
    cond_row = lax.dynamic_index_in_dim(activation, my_clip, 0, True)
    caption_rows = lax.dynamic_index_in_dim(caption, my_clip, 0, False)
    caption_raw = jnp.einsum(
        "ty,jdy->jtd", caption_rows, w_caption, preferred_element_type=jnp.float32
    )
    caption_norm, caption_unit, caption_inverse = head_norm(
        caption_raw[0], ky_gain_local, local_heads
    )
    caption_keys = caption_norm.astype(jnp.bfloat16).reshape(CAP, local_heads, HD)
    caption_values = caption_raw[1].astype(jnp.bfloat16).reshape(CAP, local_heads, HD)
    inputs = tokens.astype(jnp.float32)

    def key_usable(first_row, row_count):
        return clip_of(first_row + jnp.arange(row_count, dtype=jnp.int32), ends) == my_clip

    def fold_keys(queries3, running, segment, first_row):
        seg_keys, seg_values = segment
        row_count = seg_keys.shape[0]
        key_rows = block_size(row_count)
        steps_count = row_count // key_rows
        usable = key_usable(first_row, row_count).reshape(steps_count, key_rows)
        key_blocks = seg_keys.reshape(steps_count, key_rows, local_heads, HD)
        value_blocks = seg_values.reshape(steps_count, key_rows, local_heads, HD)

        def update(state, item):
            key_block, value_block, usable_block = item

            def update_include(inner):
                row_max, row_total, accum = inner
                scores = (
                    jnp.einsum(
                        "qhd,khd->hqk", queries3, key_block, preferred_element_type=jnp.float32
                    )
                    * score_scale
                )
                scores = jnp.where(usable_block[None, None, :], scores, MASKED)
                new_max = jnp.maximum(row_max, jnp.max(scores, axis=-1))
                factor = jnp.exp(row_max - new_max)
                weights = jnp.exp(scores - new_max[..., None])
                row_total = row_total * factor + jnp.sum(weights, axis=-1)
                accum = accum * factor.T[:, :, None] + jnp.einsum(
                    "hqk,khd->qhd",
                    weights.astype(jnp.bfloat16),
                    value_block,
                    preferred_element_type=jnp.float32,
                )
                return (new_max, row_total, accum)

            return (
                lax.cond(jnp.any(usable_block), update_include, lambda inner: inner, state),
                None,
            )

        running, unused = lax.scan(update, running, (key_blocks, value_blocks, usable))
        return running

    def local_fold(queries3, running, keys_whole):

        def local_visit(state, piece_index):
            first_row = piece_index * slice_rows
            segment = (
                lax.dynamic_slice_in_dim(keys_whole[0], first_row, slice_rows, 0),
                lax.dynamic_slice_in_dim(keys_whole[1], first_row, slice_rows, 0),
            )
            return (fold_keys(queries3, state, segment, first_row), None)

        running, unused = lax.scan(local_visit, running, jnp.arange(bucket_count, dtype=jnp.int32))
        return running

    def forward(qkv_full, out_full, modulation, second):
        shift_vec = modulation[:D]
        scale_vec = modulation[D : 2 * D]
        gate_vec = modulation[2 * D : 3 * D]
        inverse = lax.rsqrt(jnp.mean(inputs * inputs, axis=-1, keepdims=True) + EPSILON)
        unit_rows = inputs * inverse
        hidden = (unit_rows * norm_gain * (1.0 + scale_vec) + shift_vec).astype(jnp.bfloat16)
        projected = project(hidden, qkv_full)
        query_norm, query_unit, query_inverse = head_norm(projected[:, :D], q_gain, H)
        key_norm, key_unit, key_inverse = head_norm(projected[:, D : 2 * D], k_gain, H)
        queries = rotate(query_norm, positions, H).astype(jnp.bfloat16)
        keys_tok = rotate(key_norm, positions, H).astype(jnp.bfloat16)
        values_tok = projected[:, 2 * D :].astype(jnp.bfloat16)
        head_queries, head_keys, head_values = (
            lax.all_to_all(queries, "seq", split_axis=1, concat_axis=0, tiled=True),
            lax.all_to_all(keys_tok, "seq", split_axis=1, concat_axis=0, tiled=True),
            lax.all_to_all(values_tok, "seq", split_axis=1, concat_axis=0, tiled=True),
        )
        queries3 = head_queries.reshape(slice_rows, local_heads, HD)
        start_state = (
            jnp.full((local_heads, slice_rows), MASKED, jnp.float32),
            jnp.zeros((local_heads, slice_rows), jnp.float32),
            jnp.zeros((slice_rows, local_heads, HD), jnp.float32),
        )
        folder = functools.partial(fold_keys, queries3)
        if second:
            keys_whole = (
                lax.all_gather(head_keys, "bucket", axis=0, tiled=True),
                lax.all_gather(head_values, "bucket", axis=0, tiled=True),
            )
            final_state = local_fold(queries3, start_state, keys_whole)
        else:
            keys_whole = None
            final_state = folder(
                start_state,
                (
                    lax.all_gather(head_keys, "bucket", axis=0, tiled=True),
                    lax.all_gather(head_values, "bucket", axis=0, tiled=True),
                ),
                jnp.int32(0),
            )
        row_max, row_total, accum = final_state
        own = accum / row_total.T[:, :, None]
        cross_scores = (
            jnp.einsum("qhd,khd->hqk", queries3, caption_keys, preferred_element_type=jnp.float32)
            * score_scale
        )
        cross_prob = jax.nn.softmax(
            jnp.where(caption_usable[None, None, :], cross_scores, MASKED), axis=-1
        )
        other = jnp.einsum(
            "hqk,khd->qhd",
            cross_prob.astype(jnp.bfloat16),
            caption_values,
            preferred_element_type=jnp.float32,
        )
        combined = (
            (own + gates_local[None, :, None] * other)
            .reshape(slice_rows, local_width)
            .astype(jnp.bfloat16)
        )
        attention = lax.all_to_all(combined, "seq", split_axis=0, concat_axis=1, tiled=True)
        branch = project(attention, out_full)
        return dict(
            gate_vec=gate_vec,
            scale_vec=scale_vec,
            inverse=inverse,
            unit_rows=unit_rows,
            hidden=hidden,
            query_unit=query_unit,
            query_inverse=query_inverse,
            key_unit=key_unit,
            key_inverse=key_inverse,
            queries3=queries3,
            own_keys3=head_keys.reshape(slice_rows, local_heads, HD),
            own_values3=head_values.reshape(slice_rows, local_heads, HD),
            keys_whole=keys_whole,
            row_log=row_max + jnp.log(row_total),
            own=own,
            other=other,
            cross_prob=cross_prob,
            attention=attention,
            branch=branch,
            output=inputs + gate_vec * branch,
        )

    gathered = (
        lax.all_gather(ada_w, "seq", axis=0, tiled=True),
        lax.all_gather(w_qkv, "seq", axis=0, tiled=True),
        lax.all_gather(w_out, "seq", axis=0, tiled=True),
        lax.all_gather(w_gate_up, "seq", axis=0, tiled=True),
        lax.all_gather(w_down, "seq", axis=0, tiled=True),
    )
    modulation = project(cond_row, gathered[0])[0]
    first_pass = forward(gathered[1], gathered[2], modulation, False)
    middle = first_pass["output"]
    shift_mlp = modulation[3 * D : 4 * D]
    scale_mlp = modulation[4 * D : 5 * D]
    gate_mlp = modulation[5 * D :]
    mid_inverse = lax.rsqrt(jnp.mean(middle * middle, axis=-1, keepdims=True) + EPSILON)
    mid_unit = middle * mid_inverse
    mlp_in = (mid_unit * ffn_gain * (1.0 + scale_mlp) + shift_mlp).astype(jnp.bfloat16)
    gate_up = project(mlp_in, gathered[3])
    gate_half = gate_up[:, :FF]
    up_half = gate_up[:, FF:]
    gate_sigmoid = jax.nn.sigmoid(gate_half)
    silu_gate = gate_half * gate_sigmoid
    inner = (silu_gate * up_half).astype(jnp.bfloat16)
    mlp_branch = jnp.dot(inner, gathered[4], preferred_element_type=jnp.float32)
    output = (middle + gate_mlp * mlp_branch).astype(jnp.bfloat16)
    regathered = (
        lax.all_gather(ada_w, "seq", axis=0, tiled=True),
        lax.all_gather(w_qkv, "seq", axis=0, tiled=True),
        lax.all_gather(w_out, "seq", axis=0, tiled=True),
        lax.all_gather(w_gate_up, "seq", axis=0, tiled=True),
        lax.all_gather(w_down, "seq", axis=0, tiled=True),
    )
    second_pass = forward(regathered[1], regathered[2], modulation, True)
    ada_full, qkv_full, out_full, gate_up_full, down_full = regathered
    grad_out = cotangent.astype(jnp.float32)
    mlp_gate_grad = jnp.sum(grad_out * mlp_branch, axis=0)
    grad_mlp = (grad_out * gate_mlp).astype(jnp.bfloat16)
    grad_inner = lax.dot_general(
        grad_mlp, down_full, (((1,), (1,)), ((), ())), preferred_element_type=jnp.float32
    )
    grad_gate_half = grad_inner * up_half * gate_sigmoid * (1.0 + gate_half * (1.0 - gate_sigmoid))
    grad_up_half = grad_inner * silu_gate
    grad_gate_up = jnp.concatenate([grad_gate_half, grad_up_half], axis=1).astype(jnp.bfloat16)
    mlp_in_grad = jnp.dot(grad_gate_up, gate_up_full, preferred_element_type=jnp.float32)
    ffn_gain_grad = jnp.sum(mlp_in_grad * (1.0 + scale_mlp) * mid_unit, axis=0)
    shift_mlp_grad = jnp.sum(mlp_in_grad, axis=0)
    scale_mlp_grad = jnp.sum(mlp_in_grad * mid_unit * ffn_gain, axis=0)
    mid_unit_grad = mlp_in_grad * ffn_gain * (1.0 + scale_mlp)
    residual_grad = (
        mid_inverse
        * (mid_unit_grad - mid_unit * jnp.mean(mid_unit_grad * mid_unit, axis=-1, keepdims=True))
        + grad_out
    )
    gate_grad = jnp.sum(residual_grad * second_pass["branch"], axis=0)
    grad_branch = (residual_grad * second_pass["gate_vec"]).astype(jnp.bfloat16)
    attention = second_pass["attention"]
    grad_attention = jnp.dot(grad_branch, out_full, preferred_element_type=jnp.float32).astype(
        jnp.bfloat16
    )
    grad_heads = lax.all_to_all(grad_attention, "seq", split_axis=1, concat_axis=0, tiled=True)
    grad_own16 = grad_heads.reshape(slice_rows, local_heads, HD)
    grad_own = grad_own16.astype(jnp.float32)
    queries3 = second_pass["queries3"]
    own = second_pass["own"]
    other = second_pass["other"]
    cross_prob = second_pass["cross_prob"]
    grad_other = (grad_own * gates_local[None, :, None]).astype(jnp.bfloat16)
    gate_grad_local = jnp.sum(grad_own * other, axis=(0, 2)) * (1.0 - gates_local * gates_local)
    grad_cross_prob = jnp.einsum(
        "qhd,khd->hqk", grad_other, caption_values, preferred_element_type=jnp.float32
    )
    grad_cross = (
        cross_prob
        * (grad_cross_prob - jnp.sum(cross_prob * grad_cross_prob, axis=-1, keepdims=True))
    ).astype(jnp.bfloat16)
    cross_query_grad = score_scale * jnp.einsum(
        "hqk,khd->qhd", grad_cross, caption_keys, preferred_element_type=jnp.float32
    )
    caption_key_grad = score_scale * jnp.einsum(
        "hqk,qhd->khd", grad_cross, queries3, preferred_element_type=jnp.float32
    )
    caption_value_grad = jnp.einsum(
        "hqk,qhd->khd",
        cross_prob.astype(jnp.bfloat16),
        grad_other,
        preferred_element_type=jnp.float32,
    )
    row_delta = jnp.sum(grad_own * own, axis=-1).T
    row_log = second_pass["row_log"]
    keys_whole = second_pass["keys_whole"]

    def grad_piece(query_grad, piece_index, with_keys):
        first_row = piece_index * slice_rows
        key_rows = block_size(slice_rows)
        steps_count = slice_rows // key_rows
        key_blocks = lax.dynamic_slice_in_dim(keys_whole[0], first_row, slice_rows, 0).reshape(
            steps_count, key_rows, local_heads, HD
        )
        value_blocks = lax.dynamic_slice_in_dim(keys_whole[1], first_row, slice_rows, 0).reshape(
            steps_count, key_rows, local_heads, HD
        )
        usable = key_usable(first_row, slice_rows).reshape(steps_count, key_rows)

        def grad_visit(accum, item):
            key_block, value_block, usable_block = item

            def grad_include(inner):
                scores = (
                    jnp.einsum(
                        "qhd,khd->hqk", queries3, key_block, preferred_element_type=jnp.float32
                    )
                    * score_scale
                )
                scores = jnp.where(usable_block[None, None, :], scores, MASKED)
                probability = jnp.exp(scores - row_log[..., None])
                grad_prob = jnp.einsum(
                    "qhd,khd->hqk", grad_own16, value_block, preferred_element_type=jnp.float32
                )
                grad_scores = (probability * (grad_prob - row_delta[..., None])).astype(
                    jnp.bfloat16
                )
                updated = inner + score_scale * jnp.einsum(
                    "hqk,khd->qhd", grad_scores, key_block, preferred_element_type=jnp.float32
                )
                key_grad = score_scale * jnp.einsum(
                    "hqk,qhd->khd", grad_scores, queries3, preferred_element_type=jnp.float32
                )
                value_grad = jnp.einsum(
                    "hqk,qhd->khd",
                    probability.astype(jnp.bfloat16),
                    grad_own16,
                    preferred_element_type=jnp.float32,
                )
                return (updated, key_grad, value_grad)

            def skip(inner):
                empty = jnp.zeros((key_rows, local_heads, HD), jnp.float32)
                return (inner, empty, empty)

            updated, key_grad, value_grad = lax.cond(
                jnp.any(usable_block), grad_include, skip, accum
            )
            return (updated, (key_grad, value_grad))

        query_grad, (key_grads, value_grads) = lax.scan(
            grad_visit, query_grad, (key_blocks, value_blocks, usable)
        )
        return (
            query_grad,
            (
                key_grads.reshape(slice_rows, local_width),
                value_grads.reshape(slice_rows, local_width),
            ),
        )

    query_start = jnp.zeros((slice_rows, local_heads, HD), jnp.float32)
    piece_order = jnp.arange(bucket_count, dtype=jnp.int32)
    self_query_grad, (key_terms, value_terms) = lax.scan(
        functools.partial(grad_piece, with_keys=True), query_start, piece_order
    )
    key_sum, value_sum = (
        lax.psum_scatter(
            key_terms.reshape(total_rows, local_width).astype(jnp.bfloat16),
            "bucket",
            scatter_dimension=0,
            tiled=True,
        ).astype(jnp.float32),
        lax.psum_scatter(
            value_terms.reshape(total_rows, local_width).astype(jnp.bfloat16),
            "bucket",
            scatter_dimension=0,
            tiled=True,
        ).astype(jnp.float32),
    )
    query_grad16 = (
        (self_query_grad + cross_query_grad).reshape(slice_rows, local_width).astype(jnp.bfloat16)
    )
    tok_query_grad, tok_key_grad, tok_value_grad = (
        lax.all_to_all(query_grad16, "seq", split_axis=0, concat_axis=1, tiled=True),
        lax.all_to_all(
            key_sum.astype(jnp.bfloat16), "seq", split_axis=0, concat_axis=1, tiled=True
        ),
        lax.all_to_all(
            value_sum.astype(jnp.bfloat16), "seq", split_axis=0, concat_axis=1, tiled=True
        ),
    )
    query_raw_grad, q_gain_grad = head_norm_back(
        rotate(tok_query_grad.astype(jnp.float32), -positions, H),
        q_gain,
        second_pass["query_unit"],
        second_pass["query_inverse"],
    )
    key_raw_grad, k_gain_grad = head_norm_back(
        rotate(tok_key_grad.astype(jnp.float32), -positions, H),
        k_gain,
        second_pass["key_unit"],
        second_pass["key_inverse"],
    )
    projected_grad = jnp.concatenate(
        [query_raw_grad, key_raw_grad, tok_value_grad.astype(jnp.float32)], axis=1
    ).astype(jnp.bfloat16)
    hidden = second_pass["hidden"]
    out_each = D // seq_count
    qkv_each = 3 * D // seq_count
    gate_up_each = 2 * FF // seq_count
    down_each = FF // seq_count
    rows_each = out_each + qkv_each + gate_up_each + down_each
    device_count = rows_each * lax.axis_size("seq") // rows_each
    first_device = jnp.int32(0) // rows_each

    def part(operand, partner, each):
        picked = lax.dynamic_slice_in_dim(operand, first_device * each, device_count * each, 1)
        term = lax.dot_general(
            picked, partner, (((0,), (0,)), ((), ())), preferred_element_type=jnp.float32
        )
        return term.reshape(device_count, each, D)

    terms = [
        part(grad_branch, attention, out_each),
        part(projected_grad, hidden, qkv_each),
        part(grad_gate_up, mlp_in, gate_up_each),
        part(inner, grad_mlp, down_each),
    ]
    weight_grad_seq = lax.psum_scatter(
        jnp.concatenate(terms, axis=1)
        .reshape(rows_each * lax.axis_size("seq"), D)
        .astype(jnp.bfloat16),
        "seq",
        scatter_dimension=0,
        tiled=True,
    )
    hidden_grad = jnp.dot(projected_grad, qkv_full, preferred_element_type=jnp.float32)
    unit_rows = second_pass["unit_rows"]
    scale_vec = second_pass["scale_vec"]
    inverse = second_pass["inverse"]
    norm_gain_grad = jnp.sum(hidden_grad * (1.0 + scale_vec) * unit_rows, axis=0)
    shift_grad = jnp.sum(hidden_grad, axis=0)
    scale_grad = jnp.sum(hidden_grad * unit_rows * norm_gain, axis=0)
    unit_grad = hidden_grad * norm_gain * (1.0 + scale_vec)
    token_grad = (
        inverse * (unit_grad - unit_rows * jnp.mean(unit_grad * unit_rows, axis=-1, keepdims=True))
        + residual_grad
    )
    modulation_grad = jnp.where(
        clip_mask[:, None],
        jnp.concatenate(
            [shift_grad, scale_grad, gate_grad, shift_mlp_grad, scale_mlp_grad, mlp_gate_grad]
        )[None, :],
        0.0,
    )
    ky_gain_part = jnp.sum(
        caption_key_grad.reshape(CAP, local_width) * caption_unit.reshape(CAP, local_width), axis=0
    )
    ky_gain_full = lax.dynamic_update_slice_in_dim(
        jnp.zeros((D,), jnp.float32), ky_gain_part, head_first, 0
    )
    gate_full = lax.dynamic_update_slice_in_dim(
        jnp.zeros((H,), jnp.float32), gate_grad_local, seq_id * local_heads, 0
    )
    caption_part = jnp.stack(
        [caption_key_grad.reshape(CAP, local_width), caption_value_grad.reshape(CAP, local_width)]
    )[None]
    zero_index = jnp.zeros((), jnp.int32)
    caption_full = lax.dynamic_update_slice(
        jnp.zeros((CLIPS, 2, CAP, D), jnp.float32),
        caption_part,
        (my_clip, zero_index, zero_index, head_first),
    )
    reduced = lax.psum(
        (
            norm_gain_grad,
            q_gain_grad,
            k_gain_grad,
            ky_gain_full,
            gate_full,
            modulation_grad,
            caption_full,
            ffn_gain_grad,
        ),
        ("bucket", "seq"),
    )
    modulation_total = reduced[5].astype(jnp.bfloat16)
    rows_local = 6 * D // seq_count
    cols_local = CD // bucket_count
    ada_grad = lax.dot_general(
        lax.dynamic_slice_in_dim(modulation_total, seq_id * rows_local, rows_local, 1),
        lax.dynamic_slice_in_dim(activation, bucket_id * cols_local, cols_local, 1),
        (((0,), (0,)), ((), ())),
        preferred_element_type=jnp.float32,
    )
    cond_sigmoid = jax.nn.sigmoid(cond)
    cond_grad = (
        jnp.dot(modulation_total, ada_full, preferred_element_type=jnp.float32)
        * cond_sigmoid
        * (1.0 + cond * (1.0 - cond_sigmoid))
    )
    caption_total = lax.dynamic_slice_in_dim(reduced[6], head_first, local_width, 3)
    raw_keys_all = jnp.einsum(
        "cty,dy->ctd", caption, w_caption[0], preferred_element_type=jnp.float32
    ).reshape(CLIPS * CAP, local_width)
    ignored, unit_all, inverse_all = head_norm(raw_keys_all, ky_gain_local, local_heads)
    raw_key_grad, unused_gain = head_norm_back(
        caption_total[:, 0].reshape(CLIPS * CAP, local_width), ky_gain_local, unit_all, inverse_all
    )
    raw_grad = jnp.stack(
        [raw_key_grad.reshape(CLIPS, CAP, local_width), caption_total[:, 1]], axis=1
    ).astype(jnp.bfloat16)
    caption_cols = lax.dynamic_slice_in_dim(
        caption, bucket_id * (YD // bucket_count), YD // bucket_count, 2
    )
    caption_w_grad = jnp.einsum(
        "cjtd,cty->jdy", raw_grad, caption_cols, preferred_element_type=jnp.float32
    )
    combined_grads = lax.psum_scatter(
        weight_grad_seq, "bucket", scatter_dimension=1, tiled=True
    ).astype(jnp.float32)
    out_grad_out = combined_grads[:out_each]
    qkv_grad_out = combined_grads[out_each : out_each + qkv_each]
    gate_up_grad_out = combined_grads[out_each + qkv_each : out_each + qkv_each + gate_up_each]
    down_grad_out = combined_grads[out_each + qkv_each + gate_up_each :]
    return (
        output,
        token_grad,
        cond_grad,
        ada_grad,
        reduced[0],
        qkv_grad_out,
        reduced[1],
        reduced[2],
        caption_w_grad,
        reduced[3],
        reduced[4],
        out_grad_out,
        reduced[7],
        gate_up_grad_out,
        down_grad_out,
    )


def solution(mesh):
    fits = mesh.shape["seq"] == 2 and mesh.shape["bucket"] == LINE * GROUP
    bucket = ("bucket",)
    if fits:
        bucket = BUCKET
        mesh = Mesh(mesh.devices.reshape(LINE, 2, GROUP // 2, 2), (*BUCKET, "seq"))
    in_specs = (
        P((*bucket, "seq"), None),
        P((*bucket, "seq"), None),
        P(),
        P(),
        P(),
        P(),
        P("seq", None),
        P(),
        P("seq", None),
        P(),
        P(),
        P(None, "seq", None),
        P(),
        P(),
        P("seq", None),
        P(),
        P("seq", None),
        P("seq", None),
    )
    out_specs = (
        P((*bucket, "seq"), None),
        P((*bucket, "seq"), None),
        P(),
        P("seq", bucket),
        P(),
        P("seq", bucket),
        P(),
        P(),
        P(None, "seq", bucket),
        P(),
        P(),
        P("seq", bucket),
        P(),
        P("seq", bucket),
        P("seq", bucket),
    )
    body = fast_body if fits else general_body
    return jax.shard_map(body, mesh=mesh, in_specs=in_specs, out_specs=out_specs, check_vma=False)
```
